32 devices in a mesh: img: 16 (over z, y, core), seq: 2 (over x).
Axes of the slice: x: 2, y: 2, z: 4, core: 2. Of those that a mesh axis runs over, the one named last changes fastest.
Arguments:
- tokens: bfloat16 [4096, 768], P(('img', 'seq')), may hold values from -6 to 6
- cotangent: bfloat16 [4096, 768], P(('img', 'seq')), may hold values from -6 to 6
- counts: int32 [16], P('img'), may hold values from 129 to 256, as said below
- widths: int32 [16], P('img'), may hold values from 16 to 32
- norm1_gain: bfloat16 [768], P(('img', 'seq')), may hold values from 0.5 to 1.5
- norm1_shift: bfloat16 [768], P(('img', 'seq')), may hold values from -1.75 to 1.75
- w_qkv: bfloat16 [768, 2304], P(('img', 'seq')), may hold values from -0.3125 to 0.3125
- q_bias: bfloat16 [768], P(('img', 'seq')), may hold values from -1.75 to 1.75
- v_bias: bfloat16 [768], P(('img', 'seq')), may hold values from -1.75 to 1.75
- w_proj: bfloat16 [768, 768], P(('img', 'seq')), may hold values from -0.875 to 0.875
- proj_bias: bfloat16 [768], P(('img', 'seq')), may hold values from -1.75 to 1.75
- gamma1: bfloat16 [768], P(('img', 'seq')), may hold values from 0.5 to 2
- norm2_gain: bfloat16 [768], P(('img', 'seq')), may hold values from 0.5 to 1.5
- norm2_shift: bfloat16 [768], P(('img', 'seq')), may hold values from -1.75 to 1.75
- w_fc1: bfloat16 [768, 3072], P(('img', 'seq')), may hold values from -0.21875 to 0.21875
- fc1_bias: bfloat16 [3072], P(('img', 'seq')), may hold values from -1.75 to 1.75
- w_fc2: bfloat16 [3072, 768], P(('img', 'seq')), may hold values from -0.109375 to 0.109375
- fc2_bias: bfloat16 [768], P(('img', 'seq')), may hold values from -1.75 to 1.75
- gamma2: bfloat16 [768], P(('img', 'seq')), may hold values from 0.5 to 2
- bias_table: bfloat16 [1953, 12], replicated, may hold values from -6 to 6
Outputs:
- output: bfloat16 [4096, 768], P(('img', 'seq'))
- grad_tokens: bfloat16 [4096, 768], P(('img', 'seq'))
- grad_norm1_gain: float32 [768], P(('img', 'seq'))
- grad_norm1_shift: float32 [768], P(('img', 'seq'))
- grad_w_qkv: float32 [768, 2304], P(('img', 'seq'))
- grad_q_bias: float32 [768], P(('img', 'seq'))
- grad_v_bias: float32 [768], P(('img', 'seq'))
- grad_w_proj: float32 [768, 768], P(('img', 'seq'))
- grad_proj_bias: float32 [768], P(('img', 'seq'))
- grad_gamma1: float32 [768], P(('img', 'seq'))
- grad_norm2_gain: float32 [768], P(('img', 'seq'))
- grad_norm2_shift: float32 [768], P(('img', 'seq'))
- grad_w_fc1: float32 [768, 3072], P(('img', 'seq'))
- grad_fc1_bias: float32 [3072], P(('img', 'seq'))
- grad_w_fc2: float32 [3072, 768], P(('img', 'seq'))
- grad_fc2_bias: float32 [768], P(('img', 'seq'))
- grad_gamma2: float32 [768], P(('img', 'seq'))
- grad_bias_table: float32 [1953, 12], replicated
The draws below stay inside these ranges and needn't reach their ends.
Inputs may be any that keep to these rules, and one draw needn't show every extreme that they name: Image g's patches are positions 0 to counts[g] - 1 of its 256; the rest are padding. Some image has all 256 positions and some exactly 129.
All inputs are finite; a program needn't handle non-finite values.
Results may differ from the reference program's by a relative error of at most 0.014.
The reference program's roundings to bfloat16 on the way count: a program that leaves them out, or rounds other values in their place, can miss the bound.
Values may be sent and summed in bfloat16 or wider, within the bound.
A program may use at most 128 MiB of HBM per device.

```python
import math
import jax
import jax.numpy as jnp
from jax import lax

D = 768
HEADS = 12
HEAD_DIM = 64
FF = 3072
TOK_DEV = 128
SIDE = 32
SEQ = 256
IMAGES = 16
TOKENS = 4096
ROWS = 16
TABLE = 1953


def draw_counts(key, part):
    key_a, key_b, key_c, key_d, key_e = jax.random.split(jax.random.fold_in(key, 11), 5)
    span = SEQ - TOK_DEV
    first = jax.random.randint(key_a, (IMAGES,), 0, span, dtype=jnp.int32)
    second = jax.random.randint(key_b, (IMAGES,), 0, span, dtype=jnp.int32)
    third = jax.random.randint(key_c, (IMAGES,), 0, span, dtype=jnp.int32)
    extra = jnp.minimum(jnp.minimum(first, second), third)
    counts_drawn = TOK_DEV + 1 + extra
    chosen = jax.random.randint(key_d, (), 0, IMAGES, dtype=jnp.int32)
    other = (chosen + 1 + jax.random.randint(key_e, (), 0, IMAGES - 1, dtype=jnp.int32)) % IMAGES
    places = jnp.arange(IMAGES, dtype=jnp.int32)
    counts_drawn = jnp.where(places == chosen, SEQ, counts_drawn)
    counts_drawn = jnp.where(places == other, TOK_DEV + 1, counts_drawn)
    return counts_drawn.astype(jnp.int32)


def place_ends(array, rng, least, high):
    longest = array.shape.index(max(array.shape))
    spots = []
    for shift in (0, 1):
        where = [jax.random.randint(jax.random.fold_in(rng, axis), (), 0, length) for axis, length in enumerate(array.shape)]
        where[longest] = (where[longest] + shift) % array.shape[longest]
        spots.append(tuple(where))
    return array.at[spots[0]].set(least).at[spots[1]].set(high)


def spiked(values, key, source, target, parts, factor):
    owner, partner = [(jnp.arange(values.shape[dim]) // (values.shape[dim] // parts)).reshape([-1 if axis == dim else 1 for axis in range(values.ndim)]) for dim in (source, target)]
    chosen = jax.random.permutation(key, parts)[partner]
    strong = (owner == chosen) | (owner == (partner + parts // 2) % parts)
    return jnp.where(strong, factor * values, values)


def steps_of(rng, dims, pieces, smallest, top_value):
    loudness, own = 1.0, jax.random.fold_in(rng, 6)
    for dim, parts in pieces:
        steps = jnp.exp(jax.random.uniform(jax.random.fold_in(own, dim), (parts,), jnp.float32, smallest / len(pieces), top_value / len(pieces)))
        loudness = loudness * jnp.repeat(steps, dims[dim] // parts).reshape([-1 if axis == dim else 1 for axis in range(len(dims))])
    return loudness


def bell_draw(own_key, shape, spread, most, cuts=(), kind=jnp.bfloat16):
    entries = jax.random.normal(own_key, shape, jnp.float32) * spread
    if len(cuts) > 0:
        entries = steps_of(own_key, shape, cuts, -0.22, 0.18) * entries
    return jnp.clip(entries, min=-most, max=most).astype(kind)


def bell_draw_with(stream_key, dims, deviation, reach, pieces, heavy, kind=jnp.bfloat16):
    drawn = deviation * jax.random.normal(stream_key, dims, jnp.float32)
    if pieces:
        drawn = drawn * steps_of(stream_key, dims, pieces, -0.22, 0.18)
    return jnp.clip(spiked(drawn, jax.random.fold_in(stream_key, 3), *heavy), -reach, reach).astype(kind)


def setup_inputs(seed: int = 0) -> dict:
    arg_keys = jax.random.split(jax.random.key(seed), 21)
    return {
        "tokens": bell_draw_with(arg_keys[0], (TOKENS, D), 1.0, 6.0, ((0, 32),), (0, 1, 32, 2.75)),
        "cotangent": bell_draw_with(arg_keys[1], (TOKENS, D), 1.0, 6.0, ((0, 32),), (0, 1, 32, 2.75)),
        "counts": draw_counts(jax.random.fold_in(arg_keys[20], 71), 0),
        "widths": place_ends(jax.random.randint(arg_keys[3], (IMAGES,), SIDE // 2, SIDE + 1), jax.random.fold_in(arg_keys[3], 1), SIDE // 2, SIDE).astype(jnp.int32),
        "norm1_gain": jnp.clip(1.0 + 0.1 * jax.random.normal(arg_keys[4], (D,), jnp.float32), 0.5, 1.5).astype(jnp.bfloat16),
        "norm1_shift": bell_draw(arg_keys[5], (D,), 0.3, 1.75, ((0, 32),)),
        "w_qkv": bell_draw(arg_keys[6], (D, 3 * D), (D // 2) ** -0.5, 0.3125, ((0, 32),)),
        "q_bias": bell_draw(arg_keys[7], (D,), 0.3, 1.75, ((0, 32),)),
        "v_bias": bell_draw(arg_keys[8], (D,), 0.3, 1.75, ((0, 32),)),
        "w_proj": bell_draw(arg_keys[9], (D, D), (D // 16) ** -0.5, 0.875, ((0, 32),)),
        "proj_bias": bell_draw(arg_keys[10], (D,), 0.3, 1.75, ((0, 32),)),
        "gamma1": jnp.clip(jnp.exp(math.log(2.0) - 1.3862944 * jax.random.uniform(arg_keys[11], (D,), jnp.float32) ** steps_of(arg_keys[11], (D,), ((0, 32),), -0.2, 0.2)), 0.5, 2.0).astype(jnp.bfloat16),
        "norm2_gain": jnp.clip(1.0 + 0.1 * jax.random.normal(arg_keys[12], (D,), jnp.float32), 0.5, 1.5).astype(jnp.bfloat16),
        "norm2_shift": bell_draw(arg_keys[13], (D,), 0.3, 1.75, ((0, 32),)),
        "w_fc1": bell_draw(arg_keys[14], (D, FF), D ** -0.5, 0.21875, ((0, 32),)),
        "fc1_bias": bell_draw(arg_keys[15], (FF,), 0.3, 1.75, ((0, 32),)),
        "w_fc2": bell_draw(arg_keys[16], (FF, D), FF ** -0.5, 0.109375, ((0, 32),)),
        "fc2_bias": bell_draw(arg_keys[17], (D,), 0.3, 1.75, ((0, 32),)),
        "gamma2": jnp.clip(jnp.exp(math.log(2.0) - 1.3862944 * jax.random.uniform(arg_keys[18], (D,), jnp.float32) ** steps_of(arg_keys[18], (D,), ((0, 32),), -0.2, 0.2)), 0.5, 2.0).astype(jnp.bfloat16),
        "bias_table": bell_draw(arg_keys[19], (TABLE, HEADS), 1.0, 6.0),
    }


@jax.custom_vjp
def low(v):
    return lax.optimization_barrier(v.astype(jnp.bfloat16)).astype(jnp.float32)

@jax.custom_vjp
def low_back(v):
    return v

def low_keep(v):
    return (low(v), None)

def low_pass(kept, grad):
    return (grad,)

def back_keep(v):
    return (v, None)

def back_low(kept, grad):
    return (low(grad),)
low.defvjp(low_keep, low_pass)
low_back.defvjp(back_keep, back_low)
EPSILON = 1e-06
NEG_FILL = -1e+30
HIGH = lax.Precision.HIGHEST

def dense(left, right):
    return jnp.dot(left, right, precision=HIGH, preferred_element_type=jnp.float32)

def layer_norm(values, gain, shift):
    centred = values - lax.optimization_barrier(jnp.mean(values, axis=-1, keepdims=True))
    inv_std = lax.rsqrt(lax.optimization_barrier(jnp.mean(centred * centred, axis=-1, keepdims=True)) + EPSILON)
    return centred * inv_std * gain + shift

def image_layer(params, inputs, count, width):
    gain_one, shift_one, qkv_weight, query_bias, value_bias, proj_weight, proj_shift, scale_one, gain_two, shift_two, fc1_weight, fc1_shift, fc2_weight, fc2_shift, scale_two, table = params
    places = jnp.arange(SEQ, dtype=jnp.int32)
    grid_row = places // width
    grid_col = places % width
    key_valid = (places < count)[None, None, :]
    rel_index = (grid_row[:, None] - grid_row[None, :] + ROWS - 1) * (2 * SIDE - 1) + (grid_col[:, None] - grid_col[None, :] + SIDE - 1)
    normed_one = low(layer_norm(inputs, gain_one, shift_one))
    qkv_shift = jnp.concatenate([query_bias, jnp.zeros((D,), jnp.float32), value_bias])
    projected = low(low_back(dense(normed_one, qkv_weight) + qkv_shift))
    queries = projected[:, :D].reshape(SEQ, HEADS, HEAD_DIM)
    key_rows = projected[:, D:2 * D].reshape(SEQ, HEADS, HEAD_DIM)
    values = projected[:, 2 * D:].reshape(SEQ, HEADS, HEAD_DIM)
    product = low_back(jnp.einsum('qhd,khd->hqk', queries, key_rows, precision=HIGH))
    scores = product * HEAD_DIM ** (-0.5) + jnp.take(table.T, rel_index, axis=1)
    scores = jnp.where(key_valid, scores, NEG_FILL)
    top_val = lax.optimization_barrier(jnp.max(scores, axis=-1, keepdims=True))
    exp_terms = jnp.where(key_valid, jnp.exp(scores - top_val), 0.0)
    probs = exp_terms / lax.optimization_barrier(jnp.sum(exp_terms, axis=-1, keepdims=True))
    mixed = jnp.einsum('hqk,khd->qhd', low(probs), values, precision=HIGH).reshape(SEQ, D)
    mixed = low(low_back(mixed))
    branch_one = low_back(dense(mixed, proj_weight) + proj_shift)
    residual_one = inputs + scale_one * branch_one
    normed_two = low(layer_norm(residual_one, gain_two, shift_two))
    pre_act = low_back(dense(normed_two, fc1_weight) + fc1_shift)
    hidden = low(jax.nn.gelu(pre_act, approximate=False))
    branch_two = low_back(dense(hidden, fc2_weight) + fc2_shift)
    return residual_one + scale_two * branch_two

def reference(tokens, cotangent, counts, widths, norm1_gain, norm1_shift, w_qkv, q_bias, v_bias, w_proj, proj_bias, gamma1, norm2_gain, norm2_shift, w_fc1, fc1_bias, w_fc2, fc2_bias, gamma2, bias_table):
    params = tuple((weight_arg.astype(jnp.float32) for weight_arg in (norm1_gain, norm1_shift, w_qkv, q_bias, v_bias, w_proj, proj_bias, gamma1, norm2_gain, norm2_shift, w_fc1, fc1_bias, w_fc2, fc2_bias, gamma2, bias_table)))

    def forward(inputs, weights):

        def one_image(packed):
            return image_layer(weights, packed[0], packed[1], packed[2])
        stacked = inputs.reshape(IMAGES, SEQ, D)
        result = lax.map(jax.checkpoint(one_image), (stacked, counts, widths))
        return result.reshape(TOKENS, D)
    output, pull_back = jax.vjp(forward, tokens.astype(jnp.float32), params)
    grad_inputs, grad_params = pull_back(cotangent.astype(jnp.float32))
    grad_gain_one, grad_shift_one, grad_qkv_weight, grad_query_bias, grad_value_bias, grad_proj_weight, grad_proj_shift, grad_scale_one, grad_gain_two, grad_shift_two, grad_fc1_weight, grad_fc1_shift, grad_fc2_weight, grad_fc2_shift, grad_scale_two, grad_table = grad_params
    return (output.astype(jnp.bfloat16), grad_inputs.astype(jnp.bfloat16), grad_gain_one, grad_shift_one, grad_qkv_weight, grad_query_bias, grad_value_bias, grad_proj_weight, grad_proj_shift, grad_scale_one, grad_gain_two, grad_shift_two, grad_fc1_weight, grad_fc1_shift, grad_fc2_weight, grad_fc2_shift, grad_scale_two, grad_table)
```

```python
from functools import partial

import jax
import jax.numpy as jnp
from jax import lax
from jax.experimental import pallas as pl
from jax.experimental.pallas import tpu as pltpu
from jax.sharding import PartitionSpec as P

HEADS = 12
HEAD_DIM = 64
SIDE = 32
PAIR = 2 * HEAD_DIM
PAIRS = HEADS // 2
HEAD_ROWS = 16
LANES = 128
F32 = jnp.float32
BF16 = jnp.bfloat16
NT = (((1,), (1,)), ((), ()))
TN = (((0,), (0,)), ((), ()))


EPSILON = 1e-06
NEG_FILL = -1e30


def dot(left, right, dims=(((1,), (0,)), ((), ()))):
    return lax.dot_general(left, right, dims, preferred_element_type=F32)


def iota(shape, dim):
    return lax.broadcasted_iota(jnp.int32, shape, dim)


def floor_div(values, width):
    return jnp.floor((values.astype(F32) + 0.5) / width.astype(F32)).astype(jnp.int32)


def table_index(place, span, rows, row_span, width, offset):
    right = place >= span
    diagonal = offset + rows - 1 - jnp.where(right, place - span, place)
    row = floor_div(diagonal, width)
    col = diagonal - row * width
    row = jnp.where(right, row + 1, row)
    col = jnp.where(right, col - width, col)
    return (row + row_span - 1) * (2 * SIDE - 1) + col + SIDE - 1


def same_side(rows, keys, width, offset):
    query = iota((rows, keys), 0) + offset
    key = iota((rows, keys), 1)
    return (query - floor_div(query, width) * width) >= (key - floor_div(key, width) * width)


def fill_diagonals(table_ref, diag_ref, rows, keys, row_span, width, offset):
    span = rows + keys
    entries = table_ref.shape[1]
    step = 2 * LANES
    index = table_index(iota((step, 2 * span), 1), span, rows, row_span, width, offset)
    entry = iota((step, 2 * span), 0)
    diag_ref[...] = jnp.zeros_like(diag_ref)

    def add(chunk, carry):
        start = pl.multiple_of(chunk * step, step)
        chosen = jnp.where(entry + start == index, 1.0, 0.0).astype(BF16)
        diag_ref[...] += dot(table_ref[:, pl.ds(start, step)], chosen)
        return carry

    lax.fori_loop(0, entries // step, add, 0)


def half_mask(shape, half):
    lane = iota(shape, 1)
    return lane < HEAD_DIM if half == 0 else lane >= HEAD_DIM


def pick(values, half):
    return jnp.where(half_mask(values.shape, half), values, jnp.zeros_like(values))


def attend(query_ref, kv_ref, diag_ref, probs_ref, mixed_ref, width, count, offset):
    rows, model = query_ref.shape
    keys = kv_ref.shape[0]
    span = rows + keys
    same = same_side(rows, keys, width, offset)
    valid = iota((rows, keys), 1) < count

    def one_pair(pair, carry):
        cols = pl.ds(pl.multiple_of(pair * PAIR, PAIR), PAIR)
        value_cols = pl.ds(pl.multiple_of(model + pair * PAIR, PAIR), PAIR)
        query_pair = query_ref[:, cols]
        key_pair = kv_ref[:, cols]
        value_pair = kv_ref[:, value_cols]
        mixed = jnp.zeros((rows, PAIR), F32)
        for half in range(2):
            head = pair * 2 + half
            product = dot(pick(query_pair, half), key_pair, NT)
            shifted = []
            for side in range(2):
                line = diag_ref[pl.ds(head, 1), side * span : (side + 1) * span]
                line = jnp.broadcast_to(line, (rows, span))
                line = pltpu.roll(line, keys + 1, 1, stride=1, stride_axis=0)
                shifted.append(line[:, :keys])
            scores = product * HEAD_DIM**-0.5 + jnp.where(same, shifted[0], shifted[1])
            scores = jnp.where(valid, scores, NEG_FILL)
            terms = jnp.exp(scores - jnp.max(scores, axis=1, keepdims=True))
            terms = jnp.where(valid, terms, 0.0)
            probs = terms / jnp.sum(terms, axis=1, keepdims=True)
            probs_ref[head] = probs
            mixed = mixed + dot(probs.astype(BF16), pick(value_pair, half))
        mixed_ref[:, cols] = mixed.astype(BF16)
        return carry

    lax.fori_loop(0, PAIRS, one_pair, 0)


def fold_rows(values):
    while values.shape[0] > 8:
        half = values.shape[0] // 2
        values = values[half:] + pltpu.roll(values[:half], half, 1)
    return values


def attend_back(
    query_ref, kv_ref, probs_ref, grad_ref, grad_query_ref, grad_kv_ref, fold_ref, width, offset
):
    rows, model = query_ref.shape
    keys = kv_ref.shape[0]
    same = same_side(rows, keys, width, offset)
    fold_ref[...] = jnp.zeros_like(fold_ref)

    def one_pair(pair, carry):
        cols = pl.ds(pl.multiple_of(pair * PAIR, PAIR), PAIR)
        value_cols = pl.ds(pl.multiple_of(model + pair * PAIR, PAIR), PAIR)
        query_pair = query_ref[:, cols]
        key_pair = kv_ref[:, cols]
        value_pair = kv_ref[:, value_cols]
        grad_pair = grad_ref[:, cols]
        grad_query = jnp.zeros((rows, PAIR), F32)
        grad_key = jnp.zeros((keys, PAIR), F32)
        grad_value = jnp.zeros((keys, PAIR), F32)
        for half in range(2):
            head = pair * 2 + half
            probs = probs_ref[head]
            grad_half = pick(grad_pair, half)
            grad_probs = dot(grad_half, value_pair, NT)
            grad_scores = probs * (
                grad_probs - jnp.sum(probs * grad_probs, axis=1, keepdims=True)
            )
            blank = jnp.zeros((rows, rows), F32)
            left = jnp.where(same, grad_scores, 0.0)
            right = jnp.where(same, 0.0, grad_scores)
            for side, part in enumerate((left, right)):
                place = pl.multiple_of((side * HEAD_ROWS + head) * 8, 8)
                folded = fold_rows(jnp.concatenate([part, blank], axis=1))
                for block in range((rows + keys) // LANES):
                    fold_ref[block, pl.ds(place, 8), :] = folded[:, block * LANES : (block + 1) * LANES]
            grad_prod = (grad_scores * HEAD_DIM**-0.5).astype(BF16)
            grad_query = grad_query + dot(grad_prod, pick(key_pair, half))
            grad_key = grad_key + dot(grad_prod, pick(query_pair, half), TN)
            grad_value = grad_value + dot(probs.astype(BF16), grad_half, TN)
        grad_query_ref[:, cols] = grad_query.astype(BF16)
        grad_kv_ref[:, cols] = grad_key.astype(BF16)
        grad_kv_ref[:, value_cols] = grad_value.astype(BF16)
        return carry

    lax.fori_loop(0, PAIRS, one_pair, 0)


def table_gradient(fold_ref, out_ref, rows, keys, row_span, width, offset):
    span = rows + keys
    lines = 2 * HEAD_ROWS
    total = jnp.zeros((lines, span), F32)
    for row in range(8):
        blocks = [fold_ref[block, pl.ds(row, lines, stride=8), :] for block in range(span // LANES)]
        moved = jnp.concatenate(blocks, axis=1)
        total = total + (pltpu.roll(moved, 7 - row, 1) if row < 7 else moved)
    parts = []
    for side in range(2):
        rest = total[side * HEAD_ROWS : (side + 1) * HEAD_ROWS]
        pieces = []
        for _ in range(3):
            piece = rest.astype(BF16)
            rest = rest - piece.astype(F32)
            pieces.append(piece)
        parts.append(jnp.concatenate(pieces, axis=0))
    place = iota((span, LANES), 0)
    index = [
        table_index(place + side * span, span, rows, row_span, width, offset) for side in range(2)
    ]
    entry = iota((span, LANES), 1)

    def put(chunk, carry):
        start = pl.multiple_of(chunk * LANES, LANES)
        sums = jnp.zeros((3 * HEAD_ROWS, LANES), F32)
        for side in range(2):
            chosen = jnp.where(entry + start == index[side], 1.0, 0.0).astype(BF16)
            sums = sums + dot(parts[side], chosen)
        out_ref[:, pl.ds(start, LANES)] = (
            sums[:HEAD_ROWS] + sums[HEAD_ROWS : 2 * HEAD_ROWS] + sums[2 * HEAD_ROWS :]
        )
        return carry

    lax.fori_loop(0, out_ref.shape[1] // LANES, put, 0)


def attend_kernel(row_span, scal_ref, query_ref, kv_ref, table_ref, mixed_ref, probs_ref, diag_ref):
    rows, keys = query_ref.shape[0], kv_ref.shape[0]
    width, count, offset = scal_ref[0], scal_ref[1], scal_ref[2]
    fill_diagonals(table_ref, diag_ref, rows, keys, row_span, width, offset)
    attend(query_ref, kv_ref, diag_ref, probs_ref, mixed_ref, width, count, offset)


def attend_back_kernel(
    row_span, scal_ref, query_ref, kv_ref, probs_ref, grad_ref, grad_query_ref, grad_kv_ref, table_ref, fold_ref
):
    rows, keys = query_ref.shape[0], kv_ref.shape[0]
    width, offset = scal_ref[0], scal_ref[2]
    attend_back(
        query_ref, kv_ref, probs_ref, grad_ref, grad_query_ref, grad_kv_ref, fold_ref, width, offset
    )
    table_gradient(fold_ref, table_ref, rows, keys, row_span, width, offset)


def layer_norm(values, gain, shift):
    centred = values - jnp.mean(values, axis=-1, keepdims=True)
    inv_std = lax.rsqrt(jnp.mean(centred * centred, axis=-1, keepdims=True) + EPSILON)
    normed = centred * inv_std
    return (normed * gain + shift, normed, inv_std)


def norm_back(grad_out, normed, inv_std, gain):
    scaled = grad_out * gain
    return inv_std * (
        scaled
        - jnp.mean(scaled, axis=-1, keepdims=True)
        - normed * jnp.mean(scaled * normed, axis=-1, keepdims=True)
    )


def row_sum(values):
    return jnp.sum(values.astype(jnp.float32), axis=0)


def per_device(
    tokens,
    cotangent,
    counts,
    widths,
    norm1_gain,
    norm1_shift,
    w_qkv,
    q_bias,
    v_bias,
    w_proj,
    proj_bias,
    gamma1,
    norm2_gain,
    norm2_shift,
    w_fc1,
    fc1_bias,
    w_fc2,
    fc2_bias,
    gamma2,
    bias_table,
):
    fetched = (
        lax.all_gather(norm1_gain, ("img", "seq"), axis=0, tiled=True),
        lax.all_gather(norm1_shift, ("img", "seq"), axis=0, tiled=True),
        lax.all_gather(w_qkv, ("img", "seq"), axis=0, tiled=True),
        lax.all_gather(q_bias, ("img", "seq"), axis=0, tiled=True),
        lax.all_gather(v_bias, ("img", "seq"), axis=0, tiled=True),
        lax.all_gather(w_proj, ("img", "seq"), axis=0, tiled=True),
        lax.all_gather(proj_bias, ("img", "seq"), axis=0, tiled=True),
        lax.all_gather(gamma1, ("img", "seq"), axis=0, tiled=True),
        lax.all_gather(norm2_gain, ("img", "seq"), axis=0, tiled=True),
        lax.all_gather(norm2_shift, ("img", "seq"), axis=0, tiled=True),
        lax.all_gather(w_fc1, ("img", "seq"), axis=0, tiled=True),
        lax.all_gather(fc1_bias, ("img", "seq"), axis=0, tiled=True),
        lax.all_gather(w_fc2, ("img", "seq"), axis=0, tiled=True),
        lax.all_gather(fc2_bias, ("img", "seq"), axis=0, tiled=True),
        lax.all_gather(gamma2, ("img", "seq"), axis=0, tiled=True),
    )
    (
        gain_one,
        shift_one,
        qkv_weight,
        query_bias,
        value_bias,
        proj_weight,
        proj_shift,
        scale_one,
        gain_two,
        shift_two,
        fc1_weight,
        fc1_shift,
        fc2_weight,
        fc2_shift,
        scale_two,
    ) = fetched
    gain_one = gain_one.astype(jnp.float32)
    shift_one = shift_one.astype(jnp.float32)
    proj_shift = proj_shift.astype(jnp.float32)
    scale_one = scale_one.astype(jnp.float32)
    gain_two = gain_two.astype(jnp.float32)
    shift_two = shift_two.astype(jnp.float32)
    fc1_shift = fc1_shift.astype(jnp.float32)
    fc2_shift = fc2_shift.astype(jnp.float32)
    scale_two = scale_two.astype(jnp.float32)
    local_rows = tokens.shape[0]
    width_model = tokens.shape[1]
    seq_len = local_rows * lax.axis_size("seq")
    offset = lax.axis_index("seq") * local_rows
    row_span = (seq_len - 1) // (SIDE // 2) + 1
    table_rows = bias_table.shape[0]
    entries = -(-table_rows // (2 * LANES)) * 2 * LANES
    table_lines = jnp.pad(
        bias_table.T, ((0, HEAD_ROWS - HEADS), (0, entries - table_rows))
    )
    scalars = jnp.stack([widths[0], counts[0], offset.astype(jnp.int32)])
    smem = pl.BlockSpec(memory_space=pltpu.SMEM)
    vmem = pl.BlockSpec(memory_space=pltpu.VMEM)
    params = pltpu.CompilerParams(vmem_limit_bytes=40 << 20)

    inputs_f = tokens.astype(jnp.float32)
    normed_full, normed_one, inv_std_one = layer_norm(inputs_f, gain_one, shift_one)
    normed_low = normed_full.astype(jnp.bfloat16)
    qkv_shift = jnp.concatenate(
        [query_bias, jnp.zeros((width_model,), jnp.bfloat16), value_bias]
    ).astype(jnp.float32)
    projected = (
        jnp.dot(normed_low, qkv_weight, preferred_element_type=jnp.float32) + qkv_shift
    ).astype(jnp.bfloat16)
    queries = projected[:, :width_model]
    key_local = projected[:, width_model:]
    keys_all = lax.all_gather(key_local, "seq", axis=0, tiled=True)

    attn_low, probs = pl.pallas_call(
        partial(attend_kernel, row_span),
        out_shape=(
            jax.ShapeDtypeStruct((local_rows, width_model), BF16),
            jax.ShapeDtypeStruct((HEADS, local_rows, seq_len), F32),
        ),
        in_specs=[smem, vmem, vmem, vmem],
        out_specs=(vmem, vmem),
        scratch_shapes=[pltpu.VMEM((HEAD_ROWS, 2 * (local_rows + seq_len)), F32)],
        compiler_params=params,
    )(scalars, queries, keys_all, table_lines)
    branch_one = jnp.dot(attn_low, proj_weight, preferred_element_type=jnp.float32) + proj_shift
    residual_one = inputs_f + scale_one * branch_one
    normed_full_two, normed_two, inv_std_two = layer_norm(residual_one, gain_two, shift_two)
    normed_low_two = normed_full_two.astype(jnp.bfloat16)
    pre_act = jnp.dot(normed_low_two, fc1_weight, preferred_element_type=jnp.float32) + fc1_shift
    activated, gelu_pull = jax.vjp(partial(jax.nn.gelu, approximate=False), pre_act)
    hidden = activated.astype(jnp.bfloat16)
    branch_two = jnp.dot(hidden, fc2_weight, preferred_element_type=jnp.float32) + fc2_shift
    output = (residual_one + scale_two * branch_two).astype(jnp.bfloat16)
    grad_out = cotangent.astype(jnp.float32)
    grad_scale_two = jnp.sum(grad_out * branch_two, axis=0)
    grad_branch_two = (scale_two * grad_out).astype(jnp.bfloat16)
    grad_fc2_weight = jnp.einsum(
        "tf,td->fd", hidden, grad_branch_two, preferred_element_type=jnp.float32
    )
    grad_fc2_shift = row_sum(grad_branch_two)
    grad_hidden = jnp.einsum(
        "td,fd->tf", grad_branch_two, fc2_weight, preferred_element_type=jnp.float32
    )
    grad_pre = gelu_pull(grad_hidden)[0].astype(jnp.bfloat16)
    grad_fc1_weight = jnp.einsum(
        "td,tf->df", normed_low_two, grad_pre, preferred_element_type=jnp.float32
    )
    grad_fc1_shift = row_sum(grad_pre)
    grad_normed_two = jnp.einsum(
        "tf,df->td", grad_pre, fc1_weight, preferred_element_type=jnp.float32
    )
    grad_gain_two = jnp.sum(grad_normed_two * normed_two, axis=0)
    grad_shift_two = jnp.sum(grad_normed_two, axis=0)
    grad_resid = grad_out + norm_back(grad_normed_two, normed_two, inv_std_two, gain_two)
    grad_scale_one = jnp.sum(grad_resid * branch_one, axis=0)
    grad_branch_one = (scale_one * grad_resid).astype(jnp.bfloat16)
    grad_proj_weight = jnp.einsum(
        "td,te->de", attn_low, grad_branch_one, preferred_element_type=jnp.float32
    )
    grad_proj_shift = row_sum(grad_branch_one)
    grad_attn = jnp.einsum(
        "te,de->td", grad_branch_one, proj_weight, preferred_element_type=jnp.float32
    ).astype(jnp.bfloat16)
    grad_query, key_terms, table_grad = pl.pallas_call(
        partial(attend_back_kernel, row_span),
        out_shape=(
            jax.ShapeDtypeStruct((local_rows, width_model), BF16),
            jax.ShapeDtypeStruct((seq_len, 2 * width_model), BF16),
            jax.ShapeDtypeStruct((HEAD_ROWS, entries), F32),
        ),
        in_specs=[smem, vmem, vmem, vmem, vmem],
        out_specs=(vmem, vmem, vmem),
        scratch_shapes=[
            pltpu.VMEM(((local_rows + seq_len) // LANES, 2 * HEAD_ROWS * 8, LANES), F32)
        ],
        compiler_params=params,
    )(scalars, queries, keys_all, probs, grad_attn)
    own_terms = lax.psum_scatter(key_terms, "seq", scatter_dimension=0, tiled=True)
    grad_qkv = jnp.concatenate([grad_query, own_terms], axis=1)
    grad_qkv_weight = jnp.einsum(
        "td,te->de", normed_low, grad_qkv, preferred_element_type=jnp.float32
    )
    grad_query_bias = row_sum(grad_qkv[:, :width_model])
    grad_value_bias = row_sum(grad_qkv[:, 2 * width_model :])
    grad_normed_one = jnp.einsum(
        "te,de->td", grad_qkv, qkv_weight, preferred_element_type=jnp.float32
    )
    grad_gain_one = jnp.sum(grad_normed_one * normed_one, axis=0)
    grad_shift_one = jnp.sum(grad_normed_one, axis=0)
    grad_inputs = (
        grad_resid + norm_back(grad_normed_one, normed_one, inv_std_one, gain_one)
    ).astype(jnp.bfloat16)
    summed = (
        lax.psum_scatter(grad_gain_one, ("img", "seq"), scatter_dimension=0, tiled=True),
        lax.psum_scatter(grad_shift_one, ("img", "seq"), scatter_dimension=0, tiled=True),
        lax.psum_scatter(grad_qkv_weight, ("img", "seq"), scatter_dimension=0, tiled=True),
        lax.psum_scatter(grad_query_bias, ("img", "seq"), scatter_dimension=0, tiled=True),
        lax.psum_scatter(grad_value_bias, ("img", "seq"), scatter_dimension=0, tiled=True),
        lax.psum_scatter(grad_proj_weight, ("img", "seq"), scatter_dimension=0, tiled=True),
        lax.psum_scatter(grad_proj_shift, ("img", "seq"), scatter_dimension=0, tiled=True),
        lax.psum_scatter(grad_scale_one, ("img", "seq"), scatter_dimension=0, tiled=True),
        lax.psum_scatter(grad_gain_two, ("img", "seq"), scatter_dimension=0, tiled=True),
        lax.psum_scatter(grad_shift_two, ("img", "seq"), scatter_dimension=0, tiled=True),
        lax.psum_scatter(grad_fc1_weight, ("img", "seq"), scatter_dimension=0, tiled=True),
        lax.psum_scatter(grad_fc1_shift, ("img", "seq"), scatter_dimension=0, tiled=True),
        lax.psum_scatter(grad_fc2_weight, ("img", "seq"), scatter_dimension=0, tiled=True),
        lax.psum_scatter(grad_fc2_shift, ("img", "seq"), scatter_dimension=0, tiled=True),
        lax.psum_scatter(grad_scale_two, ("img", "seq"), scatter_dimension=0, tiled=True),
    )
    table_total = lax.psum(table_grad, ("img", "seq"))[:HEADS, :table_rows].T
    return (output, grad_inputs) + tuple(summed) + (table_total,)


def solution(mesh):
    return jax.shard_map(
        per_device,
        mesh=mesh,
        in_specs=(
            P(("img", "seq"), None),
            P(("img", "seq"), None),
            P("img"),
            P("img"),
            P(("img", "seq")),
            P(("img", "seq")),
            P(("img", "seq"), None),
            P(("img", "seq")),
            P(("img", "seq")),
            P(("img", "seq"), None),
            P(("img", "seq")),
            P(("img", "seq")),
            P(("img", "seq")),
            P(("img", "seq")),
            P(("img", "seq"), None),
            P(("img", "seq")),
            P(("img", "seq"), None),
            P(("img", "seq")),
            P(("img", "seq")),
            P(),
        ),
        out_specs=(
            P(("img", "seq"), None),
            P(("img", "seq"), None),
            P(("img", "seq")),
            P(("img", "seq")),
            P(("img", "seq"), None),
            P(("img", "seq")),
            P(("img", "seq")),
            P(("img", "seq"), None),
            P(("img", "seq")),
            P(("img", "seq")),
            P(("img", "seq")),
            P(("img", "seq")),
            P(("img", "seq"), None),
            P(("img", "seq")),
            P(("img", "seq"), None),
            P(("img", "seq")),
            P(("img", "seq")),
            P(),
        ),
        check_vma=False,
    )
```

```python
from functools import partial

import jax
import jax.numpy as jnp
from jax import lax
from jax.experimental import pallas as pl
from jax.experimental.pallas import tpu as pltpu
from jax.sharding import PartitionSpec as P

HEADS = 12
HEAD_DIM = 64
SIDE = 32
PAIR = 2 * HEAD_DIM
PAIRS = HEADS // 2
HEAD_ROWS = 16
LANES = 128
F32 = jnp.float32
BF16 = jnp.bfloat16
NT = (((1,), (1,)), ((), ()))
TN = (((0,), (0,)), ((), ()))


EPSILON = 1e-06
NEG_FILL = -1e30


def dot(left, right, dims=(((1,), (0,)), ((), ()))):
    return lax.dot_general(left, right, dims, preferred_element_type=F32)


def iota(shape, dim):
    return lax.broadcasted_iota(jnp.int32, shape, dim)


def floor_div(values, width):
    return jnp.floor((values.astype(F32) + 0.5) / width.astype(F32)).astype(jnp.int32)


def table_index(place, span, rows, row_span, width, offset):
    right = place >= span
    diagonal = offset + rows - 1 - jnp.where(right, place - span, place)
    row = floor_div(diagonal, width)
    col = diagonal - row * width
    row = jnp.where(right, row + 1, row)
    col = jnp.where(right, col - width, col)
    return (row + row_span - 1) * (2 * SIDE - 1) + col + SIDE - 1


def same_side(rows, keys, width, offset):
    query = iota((rows, keys), 0) + offset
    key = iota((rows, keys), 1)
    return (query - floor_div(query, width) * width) >= (key - floor_div(key, width) * width)


def fill_diagonals(table_ref, diag_ref, rows, keys, row_span, width, offset):
    span = rows + keys
    entries = table_ref.shape[1]
    step = 2 * LANES
    index = table_index(iota((step, 2 * span), 1), span, rows, row_span, width, offset)
    entry = iota((step, 2 * span), 0)
    diag_ref[...] = jnp.zeros_like(diag_ref)

    def add(chunk, carry):
        start = pl.multiple_of(chunk * step, step)
        chosen = jnp.where(entry + start == index, 1.0, 0.0).astype(BF16)
        diag_ref[...] += dot(table_ref[:, pl.ds(start, step)], chosen)
        return carry

    lax.fori_loop(0, entries // step, add, 0)


def half_mask(shape, half):
    lane = iota(shape, 1)
    return lane < HEAD_DIM if half == 0 else lane >= HEAD_DIM


def pick(values, half):
    return jnp.where(half_mask(values.shape, half), values, jnp.zeros_like(values))


def attend(query_ref, kv_ref, diag_ref, probs_ref, mixed_ref, width, count, offset):
    rows, model = query_ref.shape
    keys = kv_ref.shape[0]
    span = rows + keys
    same = same_side(rows, keys, width, offset)
    valid = iota((rows, keys), 1) < count

    def one_pair(pair, carry):
        cols = pl.ds(pl.multiple_of(pair * PAIR, PAIR), PAIR)
        value_cols = pl.ds(pl.multiple_of(model + pair * PAIR, PAIR), PAIR)
        query_pair = query_ref[:, cols]
        key_pair = kv_ref[:, cols]
        value_pair = kv_ref[:, value_cols]
        mixed = jnp.zeros((rows, PAIR), F32)
        for half in range(2):
            head = pair * 2 + half
            product = dot(pick(query_pair, half), key_pair, NT)
            shifted = []
            for side in range(2):
                line = diag_ref[pl.ds(head, 1), side * span : (side + 1) * span]
                line = jnp.broadcast_to(line, (rows, span))
                line = pltpu.roll(line, keys + 1, 1, stride=1, stride_axis=0)
                shifted.append(line[:, :keys])
            scores = product * HEAD_DIM**-0.5 + jnp.where(same, shifted[0], shifted[1])
            scores = jnp.where(valid, scores, NEG_FILL)
            terms = jnp.exp(scores - jnp.max(scores, axis=1, keepdims=True))
            terms = jnp.where(valid, terms, 0.0)
            probs = terms / jnp.sum(terms, axis=1, keepdims=True)
            probs_ref[head] = probs
            mixed = mixed + dot(probs.astype(BF16), pick(value_pair, half))
        mixed_ref[:, cols] = mixed.astype(BF16)
        return carry

    lax.fori_loop(0, PAIRS, one_pair, 0)


def fold_rows(values):
    while values.shape[0] > 8:
        half = values.shape[0] // 2
        values = values[half:] + pltpu.roll(values[:half], half, 1)
    return values


def attend_back(
    query_ref, kv_ref, probs_ref, grad_ref, grad_query_ref, grad_kv_ref, fold_ref, width, offset
):
    rows, model = query_ref.shape
    keys = kv_ref.shape[0]
    same = same_side(rows, keys, width, offset)
    fold_ref[...] = jnp.zeros_like(fold_ref)

    def one_pair(pair, carry):
        cols = pl.ds(pl.multiple_of(pair * PAIR, PAIR), PAIR)
        value_cols = pl.ds(pl.multiple_of(model + pair * PAIR, PAIR), PAIR)
        query_pair = query_ref[:, cols]
        key_pair = kv_ref[:, cols]
        value_pair = kv_ref[:, value_cols]
        grad_pair = grad_ref[:, cols]
        grad_query = jnp.zeros((rows, PAIR), F32)
        grad_key = jnp.zeros((keys, PAIR), F32)
        grad_value = jnp.zeros((keys, PAIR), F32)
        for half in range(2):
            head = pair * 2 + half
            probs = probs_ref[head]
            grad_half = pick(grad_pair, half)
            grad_probs = dot(grad_half, value_pair, NT)
            grad_scores = probs * (
                grad_probs - jnp.sum(probs * grad_probs, axis=1, keepdims=True)
            )
            blank = jnp.zeros((rows, rows), F32)
            left = jnp.where(same, grad_scores, 0.0)
            right = jnp.where(same, 0.0, grad_scores)
            for side, part in enumerate((left, right)):
                place = pl.multiple_of((side * HEAD_ROWS + head) * 8, 8)
                folded = fold_rows(jnp.concatenate([part, blank], axis=1))
                for block in range((rows + keys) // LANES):
                    fold_ref[block, pl.ds(place, 8), :] = folded[:, block * LANES : (block + 1) * LANES]
            grad_prod = (grad_scores * HEAD_DIM**-0.5).astype(BF16)
            grad_query = grad_query + dot(grad_prod, pick(key_pair, half))
            grad_key = grad_key + dot(grad_prod, pick(query_pair, half), TN)
            grad_value = grad_value + dot(probs.astype(BF16), grad_half, TN)
        grad_query_ref[:, cols] = grad_query.astype(BF16)
        grad_kv_ref[:, cols] = grad_key.astype(BF16)
        grad_kv_ref[:, value_cols] = grad_value.astype(BF16)
        return carry

    lax.fori_loop(0, PAIRS, one_pair, 0)


def table_gradient(fold_ref, out_ref, rows, keys, row_span, width, offset):
    span = rows + keys
    lines = 2 * HEAD_ROWS
    total = jnp.zeros((lines, span), F32)
    for row in range(8):
        blocks = [fold_ref[block, pl.ds(row, lines, stride=8), :] for block in range(span // LANES)]
        moved = jnp.concatenate(blocks, axis=1)
        total = total + (pltpu.roll(moved, 7 - row, 1) if row < 7 else moved)
    parts = []
    for side in range(2):
        rest = total[side * HEAD_ROWS : (side + 1) * HEAD_ROWS]
        pieces = []
        for _ in range(3):
            piece = rest.astype(BF16)
            rest = rest - piece.astype(F32)
            pieces.append(piece)
        parts.append(jnp.concatenate(pieces, axis=0))
    place = iota((span, LANES), 0)
    index = [
        table_index(place + side * span, span, rows, row_span, width, offset) for side in range(2)
    ]
    entry = iota((span, LANES), 1)

    def put(chunk, carry):
        start = pl.multiple_of(chunk * LANES, LANES)
        sums = jnp.zeros((3 * HEAD_ROWS, LANES), F32)
        for side in range(2):
            chosen = jnp.where(entry + start == index[side], 1.0, 0.0).astype(BF16)
            sums = sums + dot(parts[side], chosen)
        out_ref[:, pl.ds(start, LANES)] = (
            sums[:HEAD_ROWS] + sums[HEAD_ROWS : 2 * HEAD_ROWS] + sums[2 * HEAD_ROWS :]
        )
        return carry

    lax.fori_loop(0, out_ref.shape[1] // LANES, put, 0)


def attend_kernel(row_span, scal_ref, query_ref, kv_ref, table_ref, mixed_ref, probs_ref, diag_ref):
    rows, keys = query_ref.shape[0], kv_ref.shape[0]
    width, count, offset = scal_ref[0], scal_ref[1], scal_ref[2]
    fill_diagonals(table_ref, diag_ref, rows, keys, row_span, width, offset)
    attend(query_ref, kv_ref, diag_ref, probs_ref, mixed_ref, width, count, offset)


def attend_back_kernel(
    row_span, scal_ref, query_ref, kv_ref, probs_ref, grad_ref, grad_query_ref, grad_kv_ref, table_ref, fold_ref
):
    rows, keys = query_ref.shape[0], kv_ref.shape[0]
    width, offset = scal_ref[0], scal_ref[2]
    attend_back(
        query_ref, kv_ref, probs_ref, grad_ref, grad_query_ref, grad_kv_ref, fold_ref, width, offset
    )
    table_gradient(fold_ref, table_ref, rows, keys, row_span, width, offset)


MESH = pl.DeviceIdType.MESH
Z_SIZE = 4


class Place:
    def __init__(self):
        img = lax.axis_index("img")
        self.x = lax.axis_index("seq")
        self.c = lax.rem(img, 2)
        self.y = lax.rem(img // 2, 2)
        self.z = img // 4

    def at(self, z=None, y=None, c=None, x=None):
        z = self.z if z is None else z
        y = self.y if y is None else y
        c = self.c if c is None else c
        x = self.x if x is None else x
        return {"img": (z * 2 + y) * 2 + c, "seq": x}

    def sibling(self):
        return self.at(c=1 - self.c)

    def over_x(self):
        return self.at(x=1 - self.x)

    def over_y(self):
        return self.at(y=1 - self.y)

    def z_of(self, step):
        return lax.rem(self.z + step, Z_SIZE)

    def partners(self):
        return [self.sibling(), self.over_x(), self.over_y()] + [
            self.at(z=self.z_of(step)) for step in range(1, Z_SIZE)
        ]


def meet(place):
    barrier = pltpu.get_barrier_semaphore()
    partners = place.partners()
    for partner in partners:
        pl.semaphore_signal(barrier, inc=1, device_id=partner, device_id_type=MESH)
    pl.semaphore_wait(barrier, len(partners))


class Sems:
    def __init__(self, send, recv):
        self.send, self.recv, self.used = send, recv, 0

    def copy(self, src, dst, device):
        index = self.used
        self.used += 1
        return pltpu.make_async_remote_copy(
            src_ref=src,
            dst_ref=dst,
            send_sem=self.send.at[index],
            recv_sem=self.recv.at[index],
            device_id=device,
            device_id_type=MESH,
        )


GATHER_COPIES = 10


class Gather:
    def __init__(self, place, src, slots, cols, x_last, sems, local_sem):
        z, y, c, x = place.z, place.y, place.c, place.x
        every = slice(None)

        def part(a, b, d, e):
            return slots.at[a, b, d, e, :, cols]

        own = part(z, y, c, x)
        self.local = pltpu.make_async_copy(src.at[:, cols], own, local_sem)
        self.along_z = [
            sems.copy(src.at[:, cols], own, place.at(z=place.z_of(step)))
            for step in range(1, Z_SIZE)
        ]
        line = part(every, y, c, x)
        mid_line = part(every, 1 - y, c, x) if x_last else part(every, y, c, 1 - x)
        mid, last = place.over_y(), place.over_x()
        if not x_last:
            mid, last = last, mid
        sibling = place.sibling()
        far_line = part(every, y, c, 1 - x) if x_last else part(every, 1 - y, c, x)
        cross_line = part(every, 1 - y, c, 1 - x)
        self.line_mid = sems.copy(line, line, mid)
        self.line_last = sems.copy(line, line, last)
        self.line_core = sems.copy(line, line, sibling)
        self.mid_last = sems.copy(mid_line, mid_line, last)
        self.mid_core = sems.copy(mid_line, mid_line, sibling)
        self.far_core = sems.copy(far_line, far_line, sibling)
        self.cross_core = sems.copy(cross_line, cross_line, sibling)

    def begin(self):
        self.local.start()
        for copy in self.along_z:
            copy.start()

    def second(self):
        self.local.wait()
        for copy in self.along_z:
            copy.wait_recv()
        self.line_mid.start()
        self.line_last.start()
        self.line_core.start()

    def third(self):
        self.line_mid.wait_recv()
        self.mid_last.start()
        self.mid_core.start()

    def fourth(self):
        self.line_last.wait_recv()
        self.far_core.start()
        self.mid_last.wait_recv()
        self.cross_core.start()

    def arrive(self):
        for copy in (self.line_core, self.mid_core, self.far_core, self.cross_core):
            copy.wait_recv()

    def settle(self):
        for copy in self.along_z + [
            self.line_mid,
            self.line_last,
            self.line_core,
            self.mid_last,
            self.mid_core,
            self.far_core,
            self.cross_core,
        ]:
            copy.wait_send()


def halves(width):
    middle = width // 2 // LANES * LANES
    return [(0, middle), (middle, width - middle)]


def gather_kernel(count, *refs):
    sources, slots = refs[:count], refs[count : 2 * count]
    send, recv, local = refs[2 * count :]
    place = Place()
    meet(place)
    sems = Sems(send, recv)
    chunks = []
    for src, slot in zip(sources, slots):
        width = src.shape[1]
        cuts = [(0, width)] if width <= LANES else halves(width)
        for half, (start, size) in enumerate(cuts):
            chunks.append(
                Gather(place, src, slot, pl.ds(start, size), half == 0, sems, local.at[len(chunks)])
            )
    for chunk in chunks:
        chunk.begin()
    steps = []
    for number, chunk in enumerate(chunks):
        for lag, step in enumerate((chunk.second, chunk.third, chunk.fourth, chunk.arrive)):
            steps.append((number // 2 + lag, lag, number, step))
    for _, _, _, step in sorted(steps, key=lambda entry: entry[:3]):
        step()
    for chunk in chunks:
        chunk.settle()


def gather_all(sources):
    count = len(sources)
    chunks = sum(1 if source.shape[1] <= LANES else 2 for source in sources)
    anywhere = pl.BlockSpec(memory_space=pl.ANY)
    shapes = [(Z_SIZE, 2, 2, 2) + source.shape for source in sources]
    return pl.pallas_call(
        partial(gather_kernel, count),
        out_shape=tuple(
            jax.ShapeDtypeStruct(shape, source.dtype) for shape, source in zip(shapes, sources)
        ),
        in_specs=[anywhere] * count,
        out_specs=(anywhere,) * count,
        scratch_shapes=[
            pltpu.SemaphoreType.DMA((GATHER_COPIES * chunks,)),
            pltpu.SemaphoreType.DMA((GATHER_COPIES * chunks,)),
            pltpu.SemaphoreType.DMA((chunks,)),
        ],
        compiler_params=pltpu.CompilerParams(collective_id=0, has_side_effects=True),
    )(*sources)


REDUCE_COPIES = 6


class Reduce:
    def __init__(self, place, grad, own, first, second, third, out, start, size, x_first, sems):
        self.place, self.grad, self.own, self.first = place, grad, own, first
        self.second, self.third, self.out = second, third, out
        self.start, self.size, self.x_first = start, size, x_first
        z, y, c, x = place.z, place.y, place.c, place.x
        every = slice(None)
        cols = pl.ds(start, size)
        self.cols = cols
        self.to_core = sems.copy(
            grad.at[:, :, 1 - c, :, :, cols], own.at[:, :, :, :, cols], place.sibling()
        )
        over_first, over_second = place.over_x(), place.over_y()
        if x_first:
            leaving, other = own.at[:, :, 1 - x, :, cols], 1 - y
        else:
            over_first, over_second = over_second, over_first
            leaving, other = own.at[:, 1 - y, :, :, cols], 1 - x
        self.kept = y if x_first else x
        self.over_first = sems.copy(leaving, first, over_first)
        self.over_second = sems.copy(first.at[:, other], second, over_second)
        self.along_z = []
        for step in range(1, Z_SIZE):
            target = place.z_of(step)
            self.along_z.append(
                sems.copy(second.at[target], third.at[step - 1], place.at(z=target))
            )

    def begin(self):
        self.to_core.start()

    def add_core(self):
        self.to_core.wait_recv()
        place = self.place

        def add(zy, carry):
            z, y = zy // 2, lax.rem(zy, 2)
            for x in range(2):
                mine = self.grad[z, y, place.c, x, :, self.cols].astype(F32)
                theirs = self.own[z, y, x, :, self.cols].astype(F32)
                self.own[z, y, x, :, self.cols] = (mine + theirs).astype(self.own.dtype)
            return carry

        lax.fori_loop(0, 2 * Z_SIZE, add, 0)
        self.over_first.start()

    def add_first(self):
        self.over_first.wait_recv()
        place = self.place

        def add(z, carry):
            for other in range(2):
                if self.x_first:
                    mine = self.own[z, other, place.x, :, self.cols].astype(F32)
                else:
                    mine = self.own[z, place.y, other, :, self.cols].astype(F32)
                theirs = self.first[z, other].astype(F32)
                self.first[z, other] = (mine + theirs).astype(self.first.dtype)
            return carry

        lax.fori_loop(0, Z_SIZE, add, 0)
        self.over_second.start()

    def add_second(self):
        self.over_second.wait_recv()

        def add(z, carry):
            mine = self.first[z, self.kept].astype(F32)
            theirs = self.second[z].astype(F32)
            self.second[z] = (mine + theirs).astype(self.second.dtype)
            return carry

        lax.fori_loop(0, Z_SIZE, add, 0)
        for copy in self.along_z:
            copy.start()

    def finish(self):
        total = self.second[self.place.z].astype(F32)
        for step, copy in enumerate(self.along_z):
            copy.wait_recv()
            total = total + self.third[step].astype(F32)
        self.out[:, self.cols] = total

    def settle(self):
        for copy in [self.to_core, self.over_first, self.over_second] + self.along_z:
            copy.wait_send()


def reduce_buffers(rows, width, dtype):
    cuts = [(0, width)] if width <= LANES else halves(width)
    shapes = [pltpu.VMEM((Z_SIZE, 2, 2, rows, width), dtype)]
    for _, size in cuts:
        shapes.append(pltpu.VMEM((Z_SIZE, 2, rows, size), dtype))
        shapes.append(pltpu.VMEM((Z_SIZE, rows, size), dtype))
        shapes.append(pltpu.VMEM((Z_SIZE - 1, rows, size), dtype))
    return shapes, cuts


def reduce_kernel(count, *refs):
    grads, outs, table = refs[:count], refs[count : 2 * count], refs[2 * count]
    refs = list(refs[2 * count + 1 :])
    send, recv, local = refs[-3:]
    place = Place()
    meet(place)
    sems = Sems(send, recv)
    chunks = []
    for grad, out in zip(grads, outs):
        rows, width = grad.shape[4:]
        _, cuts = reduce_buffers(rows, width, grad.dtype)
        own = refs.pop(0)
        for half, (start, size) in enumerate(cuts):
            first, second, third = refs.pop(0), refs.pop(0), refs.pop(0)
            chunks.append(
                Reduce(place, grad, own, first, second, third, out, start, size, half == 0, sems)
            )
    for chunk in chunks:
        chunk.begin()
    steps = []
    for number, chunk in enumerate(chunks):
        for lag, step in enumerate(
            (chunk.add_core, chunk.add_first, chunk.add_second, chunk.finish)
        ):
            steps.append((number // 2 + lag, -lag, number, step))
    for _, _, _, step in sorted(steps, key=lambda entry: entry[:3]):
        step()
    spread = Gather(
        place, outs[0].at[16:24], table, slice(None), True, sems, local.at[0]
    )
    for step in (spread.begin, spread.second, spread.third, spread.fourth, spread.arrive, spread.settle):
        step()
    for chunk in chunks:
        chunk.settle()


def reduce_all(grads):
    count = len(grads)
    vmem = pl.BlockSpec(memory_space=pltpu.VMEM)
    scratch, chunks = [], 0
    for grad in grads:
        shapes, cuts = reduce_buffers(grad.shape[4], grad.shape[5], grad.dtype)
        scratch += shapes
        chunks += len(cuts)
    copies = REDUCE_COPIES * chunks + GATHER_COPIES
    return pl.pallas_call(
        partial(reduce_kernel, count),
        out_shape=tuple(jax.ShapeDtypeStruct(grad.shape[4:], F32) for grad in grads)
        + (jax.ShapeDtypeStruct((Z_SIZE, 2, 2, 2, 8, LANES), F32),),
        in_specs=[vmem] * count,
        out_specs=(vmem,) * (count + 1),
        scratch_shapes=scratch
        + [
            pltpu.SemaphoreType.DMA((copies,)),
            pltpu.SemaphoreType.DMA((copies,)),
            pltpu.SemaphoreType.DMA((1,)),
        ],
        compiler_params=pltpu.CompilerParams(
            collective_id=1, has_side_effects=True, vmem_limit_bytes=60 << 20
        ),
    )(*grads)


def layer_norm(values, gain, shift):
    centred = values - jnp.mean(values, axis=-1, keepdims=True)
    inv_std = lax.rsqrt(jnp.mean(centred * centred, axis=-1, keepdims=True) + EPSILON)
    normed = centred * inv_std
    return (normed * gain + shift, normed, inv_std)


def norm_back(grad_out, normed, inv_std, gain):
    scaled = grad_out * gain
    return inv_std * (
        scaled
        - jnp.mean(scaled, axis=-1, keepdims=True)
        - normed * jnp.mean(scaled * normed, axis=-1, keepdims=True)
    )


def row_sum(values):
    return jnp.sum(values.astype(jnp.float32), axis=0)


def per_device_native(
    tokens,
    cotangent,
    counts,
    widths,
    norm1_gain,
    norm1_shift,
    w_qkv,
    q_bias,
    v_bias,
    w_proj,
    proj_bias,
    gamma1,
    norm2_gain,
    norm2_shift,
    w_fc1,
    fc1_bias,
    w_fc2,
    fc2_bias,
    gamma2,
    bias_table,
):
    fetched = (
        lax.all_gather(norm1_gain, ("img", "seq"), axis=0, tiled=True),
        lax.all_gather(norm1_shift, ("img", "seq"), axis=0, tiled=True),
        lax.all_gather(w_qkv, ("img", "seq"), axis=0, tiled=True),
        lax.all_gather(q_bias, ("img", "seq"), axis=0, tiled=True),
        lax.all_gather(v_bias, ("img", "seq"), axis=0, tiled=True),
        lax.all_gather(w_proj, ("img", "seq"), axis=0, tiled=True),
        lax.all_gather(proj_bias, ("img", "seq"), axis=0, tiled=True),
        lax.all_gather(gamma1, ("img", "seq"), axis=0, tiled=True),
        lax.all_gather(norm2_gain, ("img", "seq"), axis=0, tiled=True),
        lax.all_gather(norm2_shift, ("img", "seq"), axis=0, tiled=True),
        lax.all_gather(w_fc1, ("img", "seq"), axis=0, tiled=True),
        lax.all_gather(fc1_bias, ("img", "seq"), axis=0, tiled=True),
        lax.all_gather(w_fc2, ("img", "seq"), axis=0, tiled=True),
        lax.all_gather(fc2_bias, ("img", "seq"), axis=0, tiled=True),
        lax.all_gather(gamma2, ("img", "seq"), axis=0, tiled=True),
    )
    (
        gain_one,
        shift_one,
        qkv_weight,
        query_bias,
        value_bias,
        proj_weight,
        proj_shift,
        scale_one,
        gain_two,
        shift_two,
        fc1_weight,
        fc1_shift,
        fc2_weight,
        fc2_shift,
        scale_two,
    ) = fetched
    gain_one = gain_one.astype(jnp.float32)
    shift_one = shift_one.astype(jnp.float32)
    proj_shift = proj_shift.astype(jnp.float32)
    scale_one = scale_one.astype(jnp.float32)
    gain_two = gain_two.astype(jnp.float32)
    shift_two = shift_two.astype(jnp.float32)
    fc1_shift = fc1_shift.astype(jnp.float32)
    fc2_shift = fc2_shift.astype(jnp.float32)
    scale_two = scale_two.astype(jnp.float32)
    local_rows = tokens.shape[0]
    width_model = tokens.shape[1]
    seq_len = local_rows * lax.axis_size("seq")
    offset = lax.axis_index("seq") * local_rows
    row_span = (seq_len - 1) // (SIDE // 2) + 1
    table_rows = bias_table.shape[0]
    entries = -(-table_rows // (2 * LANES)) * 2 * LANES
    table_lines = jnp.pad(
        bias_table.T, ((0, HEAD_ROWS - HEADS), (0, entries - table_rows))
    )
    scalars = jnp.stack([widths[0], counts[0], offset.astype(jnp.int32)])
    smem = pl.BlockSpec(memory_space=pltpu.SMEM)
    vmem = pl.BlockSpec(memory_space=pltpu.VMEM)
    params = pltpu.CompilerParams(vmem_limit_bytes=40 << 20)

    inputs_f = tokens.astype(jnp.float32)
    normed_full, normed_one, inv_std_one = layer_norm(inputs_f, gain_one, shift_one)
    normed_low = normed_full.astype(jnp.bfloat16)
    qkv_shift = jnp.concatenate(
        [query_bias, jnp.zeros((width_model,), jnp.bfloat16), value_bias]
    ).astype(jnp.float32)
    projected = (
        jnp.dot(normed_low, qkv_weight, preferred_element_type=jnp.float32) + qkv_shift
    ).astype(jnp.bfloat16)
    queries = projected[:, :width_model]
    key_local = projected[:, width_model:]
    keys_all = lax.all_gather(key_local, "seq", axis=0, tiled=True)

    attn_low, probs = pl.pallas_call(
        partial(attend_kernel, row_span),
        out_shape=(
            jax.ShapeDtypeStruct((local_rows, width_model), BF16),
            jax.ShapeDtypeStruct((HEADS, local_rows, seq_len), F32),
        ),
        in_specs=[smem, vmem, vmem, vmem],
        out_specs=(vmem, vmem),
        scratch_shapes=[pltpu.VMEM((HEAD_ROWS, 2 * (local_rows + seq_len)), F32)],
        compiler_params=params,
    )(scalars, queries, keys_all, table_lines)
    branch_one = jnp.dot(attn_low, proj_weight, preferred_element_type=jnp.float32) + proj_shift
    residual_one = inputs_f + scale_one * branch_one
    normed_full_two, normed_two, inv_std_two = layer_norm(residual_one, gain_two, shift_two)
    normed_low_two = normed_full_two.astype(jnp.bfloat16)
    pre_act = jnp.dot(normed_low_two, fc1_weight, preferred_element_type=jnp.float32) + fc1_shift
    activated, gelu_pull = jax.vjp(partial(jax.nn.gelu, approximate=False), pre_act)
    hidden = activated.astype(jnp.bfloat16)
    branch_two = jnp.dot(hidden, fc2_weight, preferred_element_type=jnp.float32) + fc2_shift
    output = (residual_one + scale_two * branch_two).astype(jnp.bfloat16)
    grad_out = cotangent.astype(jnp.float32)
    grad_scale_two = jnp.sum(grad_out * branch_two, axis=0)
    grad_branch_two = (scale_two * grad_out).astype(jnp.bfloat16)
    grad_fc2_weight = jnp.einsum(
        "tf,td->fd", hidden, grad_branch_two, preferred_element_type=jnp.float32
    )
    grad_fc2_shift = row_sum(grad_branch_two)
    grad_hidden = jnp.einsum(
        "td,fd->tf", grad_branch_two, fc2_weight, preferred_element_type=jnp.float32
    )
    grad_pre = gelu_pull(grad_hidden)[0].astype(jnp.bfloat16)
    grad_fc1_weight = jnp.einsum(
        "td,tf->df", normed_low_two, grad_pre, preferred_element_type=jnp.float32
    )
    grad_fc1_shift = row_sum(grad_pre)
    grad_normed_two = jnp.einsum(
        "tf,df->td", grad_pre, fc1_weight, preferred_element_type=jnp.float32
    )
    grad_gain_two = jnp.sum(grad_normed_two * normed_two, axis=0)
    grad_shift_two = jnp.sum(grad_normed_two, axis=0)
    grad_resid = grad_out + norm_back(grad_normed_two, normed_two, inv_std_two, gain_two)
    grad_scale_one = jnp.sum(grad_resid * branch_one, axis=0)
    grad_branch_one = (scale_one * grad_resid).astype(jnp.bfloat16)
    grad_proj_weight = jnp.einsum(
        "td,te->de", attn_low, grad_branch_one, preferred_element_type=jnp.float32
    )
    grad_proj_shift = row_sum(grad_branch_one)
    grad_attn = jnp.einsum(
        "te,de->td", grad_branch_one, proj_weight, preferred_element_type=jnp.float32
    ).astype(jnp.bfloat16)
    grad_query, key_terms, table_grad = pl.pallas_call(
        partial(attend_back_kernel, row_span),
        out_shape=(
            jax.ShapeDtypeStruct((local_rows, width_model), BF16),
            jax.ShapeDtypeStruct((seq_len, 2 * width_model), BF16),
            jax.ShapeDtypeStruct((HEAD_ROWS, entries), F32),
        ),
        in_specs=[smem, vmem, vmem, vmem, vmem],
        out_specs=(vmem, vmem, vmem),
        scratch_shapes=[
            pltpu.VMEM(((local_rows + seq_len) // LANES, 2 * HEAD_ROWS * 8, LANES), F32)
        ],
        compiler_params=params,
    )(scalars, queries, keys_all, probs, grad_attn)
    own_terms = lax.psum_scatter(key_terms, "seq", scatter_dimension=0, tiled=True)
    grad_qkv = jnp.concatenate([grad_query, own_terms], axis=1)
    grad_qkv_weight = jnp.einsum(
        "td,te->de", normed_low, grad_qkv, preferred_element_type=jnp.float32
    )
    grad_query_bias = row_sum(grad_qkv[:, :width_model])
    grad_value_bias = row_sum(grad_qkv[:, 2 * width_model :])
    grad_normed_one = jnp.einsum(
        "te,de->td", grad_qkv, qkv_weight, preferred_element_type=jnp.float32
    )
    grad_gain_one = jnp.sum(grad_normed_one * normed_one, axis=0)
    grad_shift_one = jnp.sum(grad_normed_one, axis=0)
    grad_inputs = (
        grad_resid + norm_back(grad_normed_one, normed_one, inv_std_one, gain_one)
    ).astype(jnp.bfloat16)
    summed = (
        lax.psum_scatter(grad_gain_one, ("img", "seq"), scatter_dimension=0, tiled=True),
        lax.psum_scatter(grad_shift_one, ("img", "seq"), scatter_dimension=0, tiled=True),
        lax.psum_scatter(grad_qkv_weight, ("img", "seq"), scatter_dimension=0, tiled=True),
        lax.psum_scatter(grad_query_bias, ("img", "seq"), scatter_dimension=0, tiled=True),
        lax.psum_scatter(grad_value_bias, ("img", "seq"), scatter_dimension=0, tiled=True),
        lax.psum_scatter(grad_proj_weight, ("img", "seq"), scatter_dimension=0, tiled=True),
        lax.psum_scatter(grad_proj_shift, ("img", "seq"), scatter_dimension=0, tiled=True),
        lax.psum_scatter(grad_scale_one, ("img", "seq"), scatter_dimension=0, tiled=True),
        lax.psum_scatter(grad_gain_two, ("img", "seq"), scatter_dimension=0, tiled=True),
        lax.psum_scatter(grad_shift_two, ("img", "seq"), scatter_dimension=0, tiled=True),
        lax.psum_scatter(grad_fc1_weight, ("img", "seq"), scatter_dimension=0, tiled=True),
        lax.psum_scatter(grad_fc1_shift, ("img", "seq"), scatter_dimension=0, tiled=True),
        lax.psum_scatter(grad_fc2_weight, ("img", "seq"), scatter_dimension=0, tiled=True),
        lax.psum_scatter(grad_fc2_shift, ("img", "seq"), scatter_dimension=0, tiled=True),
        lax.psum_scatter(grad_scale_two, ("img", "seq"), scatter_dimension=0, tiled=True),
    )
    table_total = lax.psum(table_grad, ("img", "seq"))[:HEADS, :table_rows].T
    return (output, grad_inputs) + tuple(summed) + (table_total,)


def per_device_linked(
    tokens,
    cotangent,
    counts,
    widths,
    norm1_gain,
    norm1_shift,
    w_qkv,
    q_bias,
    v_bias,
    w_proj,
    proj_bias,
    gamma1,
    norm2_gain,
    norm2_shift,
    w_fc1,
    fc1_bias,
    w_fc2,
    fc2_bias,
    gamma2,
    bias_table,
):
    shard = norm1_gain.shape[0]
    vectors = [
        norm1_gain, norm1_shift, q_bias, v_bias, proj_bias, gamma1, norm2_gain, norm2_shift, fc2_bias, gamma2,
    ]
    lines = jnp.stack(vectors).astype(F32)
    hidden_lines = fc1_bias.astype(F32).reshape(1, -1)
    packed = jnp.concatenate(
        [
            jnp.pad(lines, ((0, 16 - len(vectors)), (0, LANES - shard))),
            jnp.pad(hidden_lines, ((0, 7), (0, LANES - hidden_lines.shape[1]))),
        ]
    )
    packed, qkv_weight, proj_weight, fc1_weight, fc2_weight = gather_all(
        [packed, w_qkv, w_proj, w_fc1, w_fc2]
    )
    packed = packed.reshape(-1, 24, LANES)
    (
        gain_one, shift_one, query_bias, value_bias, proj_shift, scale_one, gain_two, shift_two, fc2_shift, scale_two,
    ) = packed[:, : len(vectors), :shard].transpose(1, 0, 2).reshape(len(vectors), -1)
    fc1_shift = packed[:, 16, : fc1_bias.shape[0]].reshape(-1)
    qkv_weight, proj_weight, fc1_weight, fc2_weight = (
        weight.reshape(-1, weight.shape[-1])
        for weight in (qkv_weight, proj_weight, fc1_weight, fc2_weight)
    )
    gain_one = gain_one.astype(jnp.float32)
    shift_one = shift_one.astype(jnp.float32)
    proj_shift = proj_shift.astype(jnp.float32)
    scale_one = scale_one.astype(jnp.float32)
    gain_two = gain_two.astype(jnp.float32)
    shift_two = shift_two.astype(jnp.float32)
    fc1_shift = fc1_shift.astype(jnp.float32)
    fc2_shift = fc2_shift.astype(jnp.float32)
    scale_two = scale_two.astype(jnp.float32)
    local_rows = tokens.shape[0]
    width_model = tokens.shape[1]
    seq_len = local_rows * lax.axis_size("seq")
    offset = lax.axis_index("seq") * local_rows
    row_span = (seq_len - 1) // (SIDE // 2) + 1
    table_rows = bias_table.shape[0]
    entries = -(-table_rows // (2 * LANES)) * 2 * LANES
    table_lines = jnp.pad(
        bias_table.T, ((0, HEAD_ROWS - HEADS), (0, entries - table_rows))
    )
    scalars = jnp.stack([widths[0], counts[0], offset.astype(jnp.int32)])
    smem = pl.BlockSpec(memory_space=pltpu.SMEM)
    vmem = pl.BlockSpec(memory_space=pltpu.VMEM)
    params = pltpu.CompilerParams(vmem_limit_bytes=40 << 20)

    inputs_f = tokens.astype(jnp.float32)
    normed_full, normed_one, inv_std_one = layer_norm(inputs_f, gain_one, shift_one)
    normed_low = normed_full.astype(jnp.bfloat16)
    qkv_shift = jnp.concatenate(
        [query_bias, jnp.zeros((width_model,), F32), value_bias]
    ).astype(jnp.float32)
    projected = (
        jnp.dot(normed_low, qkv_weight, preferred_element_type=jnp.float32) + qkv_shift
    ).astype(jnp.bfloat16)
    queries = projected[:, :width_model]
    key_local = projected[:, width_model:]
    keys_all = lax.all_gather(key_local, "seq", axis=0, tiled=True)

    attn_low, probs = pl.pallas_call(
        partial(attend_kernel, row_span),
        out_shape=(
            jax.ShapeDtypeStruct((local_rows, width_model), BF16),
            jax.ShapeDtypeStruct((HEADS, local_rows, seq_len), F32),
        ),
        in_specs=[smem, vmem, vmem, vmem],
        out_specs=(vmem, vmem),
        scratch_shapes=[pltpu.VMEM((HEAD_ROWS, 2 * (local_rows + seq_len)), F32)],
        compiler_params=params,
    )(scalars, queries, keys_all, table_lines)
    branch_one = jnp.dot(attn_low, proj_weight, preferred_element_type=jnp.float32) + proj_shift
    residual_one = inputs_f + scale_one * branch_one
    normed_full_two, normed_two, inv_std_two = layer_norm(residual_one, gain_two, shift_two)
    normed_low_two = normed_full_two.astype(jnp.bfloat16)
    pre_act = jnp.dot(normed_low_two, fc1_weight, preferred_element_type=jnp.float32) + fc1_shift
    activated, gelu_pull = jax.vjp(partial(jax.nn.gelu, approximate=False), pre_act)
    hidden = activated.astype(jnp.bfloat16)
    branch_two = jnp.dot(hidden, fc2_weight, preferred_element_type=jnp.float32) + fc2_shift
    output = (residual_one + scale_two * branch_two).astype(jnp.bfloat16)
    grad_out = cotangent.astype(jnp.float32)
    grad_scale_two = jnp.sum(grad_out * branch_two, axis=0)
    grad_branch_two = (scale_two * grad_out).astype(jnp.bfloat16)
    grad_fc2_weight = jnp.einsum(
        "tf,td->fd", hidden, grad_branch_two, preferred_element_type=jnp.float32
    )
    grad_fc2_shift = row_sum(grad_branch_two)
    grad_hidden = jnp.einsum(
        "td,fd->tf", grad_branch_two, fc2_weight, preferred_element_type=jnp.float32
    )
    grad_pre = gelu_pull(grad_hidden)[0].astype(jnp.bfloat16)
    grad_fc1_weight = jnp.einsum(
        "td,tf->df", normed_low_two, grad_pre, preferred_element_type=jnp.float32
    )
    grad_fc1_shift = row_sum(grad_pre)
    grad_normed_two = jnp.einsum(
        "tf,df->td", grad_pre, fc1_weight, preferred_element_type=jnp.float32
    )
    grad_gain_two = jnp.sum(grad_normed_two * normed_two, axis=0)
    grad_shift_two = jnp.sum(grad_normed_two, axis=0)
    grad_resid = grad_out + norm_back(grad_normed_two, normed_two, inv_std_two, gain_two)
    grad_scale_one = jnp.sum(grad_resid * branch_one, axis=0)
    grad_branch_one = (scale_one * grad_resid).astype(jnp.bfloat16)
    grad_proj_weight = jnp.einsum(
        "td,te->de", attn_low, grad_branch_one, preferred_element_type=jnp.float32
    )
    grad_proj_shift = row_sum(grad_branch_one)
    grad_attn = jnp.einsum(
        "te,de->td", grad_branch_one, proj_weight, preferred_element_type=jnp.float32
    ).astype(jnp.bfloat16)
    grad_query, key_terms, table_grad = pl.pallas_call(
        partial(attend_back_kernel, row_span),
        out_shape=(
            jax.ShapeDtypeStruct((local_rows, width_model), BF16),
            jax.ShapeDtypeStruct((seq_len, 2 * width_model), BF16),
            jax.ShapeDtypeStruct((HEAD_ROWS, entries), F32),
        ),
        in_specs=[smem, vmem, vmem, vmem, vmem],
        out_specs=(vmem, vmem, vmem),
        scratch_shapes=[
            pltpu.VMEM(((local_rows + seq_len) // LANES, 2 * HEAD_ROWS * 8, LANES), F32)
        ],
        compiler_params=params,
    )(scalars, queries, keys_all, probs, grad_attn)
    own_terms = lax.psum_scatter(key_terms, "seq", scatter_dimension=0, tiled=True)
    grad_qkv = jnp.concatenate([grad_query, own_terms], axis=1)
    grad_qkv_weight = jnp.einsum(
        "td,te->de", normed_low, grad_qkv, preferred_element_type=jnp.float32
    )
    grad_query_bias = row_sum(grad_qkv[:, :width_model])
    grad_value_bias = row_sum(grad_qkv[:, 2 * width_model :])
    grad_normed_one = jnp.einsum(
        "te,de->td", grad_qkv, qkv_weight, preferred_element_type=jnp.float32
    )
    grad_gain_one = jnp.sum(grad_normed_one * normed_one, axis=0)
    grad_shift_one = jnp.sum(grad_normed_one, axis=0)
    grad_inputs = (
        grad_resid + norm_back(grad_normed_one, normed_one, inv_std_one, gain_one)
    ).astype(jnp.bfloat16)
    lines = jnp.stack(
        [
            grad_gain_one, grad_shift_one, grad_query_bias, grad_value_bias, grad_proj_shift,
            grad_scale_one, grad_gain_two, grad_shift_two, grad_fc2_shift, grad_scale_two,
        ]
    )
    devices = 8 * Z_SIZE
    lines = lines.reshape(len(vectors), devices, shard).transpose(1, 0, 2)
    hidden_lines = grad_fc1_shift.reshape(devices, 1, -1)
    table_blocks = table_grad.reshape(2, 8, devices // 2, LANES).transpose(2, 0, 1, 3)
    small = jnp.concatenate(
        [
            jnp.pad(lines, ((0, 0), (0, 0), (0, LANES - shard))),
            jnp.pad(hidden_lines, ((0, 0), (0, 5), (0, LANES - hidden_lines.shape[2]))),
            table_blocks.reshape(devices, 8, LANES),
        ],
        axis=1,
    )

    def slots(values):
        return values.reshape(Z_SIZE, 2, 2, 2, -1, values.shape[-1])

    small, sum_fc2, sum_fc1, sum_proj, sum_qkv, table_all = reduce_all(
        [slots(small)]
        + [
            slots(grad.astype(BF16))
            for grad in (grad_fc2_weight, grad_fc1_weight, grad_proj_weight, grad_qkv_weight)
        ]
    )
    (
        sum_gain_one, sum_shift_one, sum_query, sum_value, sum_proj_shift,
        sum_scale_one, sum_gain_two, sum_shift_two, sum_fc2_shift, sum_scale_two,
    ) = (small[line, :shard] for line in range(len(vectors)))
    summed = (
        sum_gain_one, sum_shift_one, sum_qkv, sum_query, sum_value, sum_proj, sum_proj_shift, sum_scale_one,
        sum_gain_two, sum_shift_two, sum_fc1, small[len(vectors), : fc1_bias.shape[0]], sum_fc2, sum_fc2_shift,
        sum_scale_two,
    )
    table_total = (
        table_all.reshape(devices // 2, 2, 8, LANES).transpose(1, 2, 0, 3).reshape(HEAD_ROWS, -1)
    )[:HEADS, :table_rows].T
    return (output, grad_inputs) + summed + (table_total,)


def per_device(*arrays):
    devices = lax.axis_size("img") * lax.axis_size("seq")
    linked = lax.axis_size("img") == 4 * Z_SIZE and lax.axis_size("seq") == 2
    linked = linked and arrays[6].shape[0] % 8 == 0 and devices * 64 >= arrays[19].shape[0]
    return per_device_linked(*arrays) if linked else per_device_native(*arrays)


def solution(mesh):
    return jax.shard_map(
        per_device,
        mesh=mesh,
        in_specs=(
            P(("img", "seq"), None),
            P(("img", "seq"), None),
            P("img"),
            P("img"),
            P(("img", "seq")),
            P(("img", "seq")),
            P(("img", "seq"), None),
            P(("img", "seq")),
            P(("img", "seq")),
            P(("img", "seq"), None),
            P(("img", "seq")),
            P(("img", "seq")),
            P(("img", "seq")),
            P(("img", "seq")),
            P(("img", "seq"), None),
            P(("img", "seq")),
            P(("img", "seq"), None),
            P(("img", "seq")),
            P(("img", "seq")),
            P(),
        ),
        out_specs=(
            P(("img", "seq"), None),
            P(("img", "seq"), None),
            P(("img", "seq")),
            P(("img", "seq")),
            P(("img", "seq"), None),
            P(("img", "seq")),
            P(("img", "seq")),
            P(("img", "seq"), None),
            P(("img", "seq")),
            P(("img", "seq")),
            P(("img", "seq")),
            P(("img", "seq")),
            P(("img", "seq"), None),
            P(("img", "seq")),
            P(("img", "seq"), None),
            P(("img", "seq")),
            P(("img", "seq")),
            P(),
        ),
        check_vma=False,
    )
```

```python
from functools import partial

import jax
import jax.numpy as jnp
from jax import lax
from jax.experimental import pallas as pl
from jax.experimental.pallas import tpu as pltpu
from jax.sharding import PartitionSpec as P

HEADS = 12
HEAD_DIM = 64
SIDE = 32
PAIR = 2 * HEAD_DIM
PAIRS = HEADS // 2
HEAD_ROWS = 16
LANES = 128
F32 = jnp.float32
BF16 = jnp.bfloat16
NT = (((1,), (1,)), ((), ()))
TN = (((0,), (0,)), ((), ()))


VMEM_LIMIT = 63 << 20
ROW_GROUP = 8
EPSILON = 1e-06
NEG_FILL = -1e30


def dot(left, right, dims=(((1,), (0,)), ((), ()))):
    return lax.dot_general(left, right, dims, preferred_element_type=F32)


def iota(shape, dim):
    return lax.broadcasted_iota(jnp.int32, shape, dim)


def floor_div(values, width):
    return jnp.floor((values.astype(F32) + 0.5) / width.astype(F32)).astype(jnp.int32)


def table_index(place, span, rows, row_span, width, offset):
    right = place >= span
    diagonal = offset + rows - 1 - jnp.where(right, place - span, place)
    row = floor_div(diagonal, width)
    col = diagonal - row * width
    row = jnp.where(right, row + 1, row)
    col = jnp.where(right, col - width, col)
    return (row + row_span - 1) * (2 * SIDE - 1) + col + SIDE - 1


def same_side(rows, keys, width, offset):
    query = iota((rows, keys), 0) + offset
    key = iota((rows, keys), 1)
    return (query - floor_div(query, width) * width) >= (key - floor_div(key, width) * width)


def fill_diagonals(table_ref, diag_ref, rows, keys, row_span, width, offset):
    span = rows + keys
    entries = table_ref.shape[1]
    step = 2 * LANES
    index = table_index(iota((step, 2 * span), 1), span, rows, row_span, width, offset)
    entry = iota((step, 2 * span), 0)
    diag_ref[...] = jnp.zeros_like(diag_ref)

    def add(chunk, carry):
        start = pl.multiple_of(chunk * step, step)
        chosen = jnp.where(entry + start == index, 1.0, 0.0).astype(BF16)
        diag_ref[...] += dot(table_ref[:, pl.ds(start, step)], chosen)
        return carry

    lax.fori_loop(0, entries // step, add, 0)


def half_mask(shape, half):
    lane = iota(shape, 1)
    return lane < HEAD_DIM if half == 0 else lane >= HEAD_DIM


def pick(values, half):
    return jnp.where(half_mask(values.shape, half), values, jnp.zeros_like(values))


def attend(query_ref, kv_ref, diag_ref, probs_ref, mixed_ref, width, count, offset, pairs=(0, PAIRS)):
    rows, model = query_ref.shape
    keys = kv_ref.shape[0]
    span = rows + keys
    same = same_side(rows, keys, width, offset)
    valid = iota((rows, keys), 1) < count

    def one_pair(pair, carry):
        cols = pl.ds(pl.multiple_of(pair * PAIR, PAIR), PAIR)
        value_cols = pl.ds(pl.multiple_of(model + pair * PAIR, PAIR), PAIR)
        query_pair = query_ref[:, cols]
        key_pair = kv_ref[:, cols]
        value_pair = kv_ref[:, value_cols]
        mixed = jnp.zeros((rows, PAIR), F32)
        for half in range(2):
            head = pair * 2 + half
            product = dot(pick(query_pair, half), key_pair, NT)
            shifted = []
            for side in range(2):
                line = diag_ref[pl.ds(head, 1), side * span : (side + 1) * span]
                line = jnp.broadcast_to(line, (rows, span))
                line = pltpu.roll(line, keys + 1, 1, stride=1, stride_axis=0)
                shifted.append(line[:, :keys])
            scores = product * HEAD_DIM**-0.5 + jnp.where(same, shifted[0], shifted[1])
            scores = jnp.where(valid, scores, NEG_FILL)
            terms = jnp.exp(scores - jnp.max(scores, axis=1, keepdims=True))
            terms = jnp.where(valid, terms, 0.0)
            probs = terms / jnp.sum(terms, axis=1, keepdims=True)
            probs_ref[head] = probs
            mixed = mixed + dot(probs.astype(BF16), pick(value_pair, half))
        mixed_ref[:, cols] = mixed.astype(BF16)
        return carry

    lax.fori_loop(*pairs, one_pair, 0)


def fold_rows(values):
    while values.shape[0] > 8:
        half = values.shape[0] // 2
        values = values[half:] + pltpu.roll(values[:half], half, 1)
    return values


def attend_back(
    query_ref, kv_ref, probs_ref, grad_ref, grad_query_ref, grad_kv_ref, fold_ref, width, offset, pairs=(0, PAIRS)
):
    rows, model = query_ref.shape
    keys = kv_ref.shape[0]
    same = same_side(rows, keys, width, offset)

    def one_pair(pair, carry):
        cols = pl.ds(pl.multiple_of(pair * PAIR, PAIR), PAIR)
        value_cols = pl.ds(pl.multiple_of(model + pair * PAIR, PAIR), PAIR)
        query_pair = query_ref[:, cols]
        key_pair = kv_ref[:, cols]
        value_pair = kv_ref[:, value_cols]
        grad_pair = grad_ref[:, cols]
        grad_query = jnp.zeros((rows, PAIR), F32)
        grad_key = jnp.zeros((keys, PAIR), F32)
        grad_value = jnp.zeros((keys, PAIR), F32)
        for half in range(2):
            head = pair * 2 + half
            probs = probs_ref[head]
            grad_half = pick(grad_pair, half)
            grad_probs = dot(grad_half, value_pair, NT)
            grad_scores = probs * (
                grad_probs - jnp.sum(probs * grad_probs, axis=1, keepdims=True)
            )
            blank = jnp.zeros((rows, rows), F32)
            left = jnp.where(same, grad_scores, 0.0)
            right = jnp.where(same, 0.0, grad_scores)
            for side, part in enumerate((left, right)):
                place = pl.multiple_of((side * HEAD_ROWS + head) * 8, 8)
                folded = fold_rows(jnp.concatenate([part, blank], axis=1))
                for block in range((rows + keys) // LANES):
                    fold_ref[block, pl.ds(place, 8), :] = folded[:, block * LANES : (block + 1) * LANES]
            grad_prod = (grad_scores * HEAD_DIM**-0.5).astype(BF16)
            grad_query = grad_query + dot(grad_prod, pick(key_pair, half))
            grad_key = grad_key + dot(grad_prod, pick(query_pair, half), TN)
            grad_value = grad_value + dot(probs.astype(BF16), grad_half, TN)
        grad_query_ref[:, cols] = grad_query.astype(BF16)
        grad_kv_ref[:, cols] = grad_key.astype(BF16)
        grad_kv_ref[:, value_cols] = grad_value.astype(BF16)
        return carry

    lax.fori_loop(*pairs, one_pair, 0)


def table_gradient(fold_ref, out_ref, rows, keys, row_span, width, offset):
    span = rows + keys
    lines = 2 * HEAD_ROWS
    total = jnp.zeros((lines, span), F32)
    for row in range(8):
        blocks = [fold_ref[block, pl.ds(row, lines, stride=8), :] for block in range(span // LANES)]
        moved = jnp.concatenate(blocks, axis=1)
        total = total + (pltpu.roll(moved, 7 - row, 1) if row < 7 else moved)
    parts = []
    for side in range(2):
        rest = total[side * HEAD_ROWS : (side + 1) * HEAD_ROWS]
        pieces = []
        for _ in range(3):
            piece = rest.astype(BF16)
            rest = rest - piece.astype(F32)
            pieces.append(piece)
        parts.append(jnp.concatenate(pieces, axis=0))
    place = iota((span, LANES), 0)
    index = [
        table_index(place + side * span, span, rows, row_span, width, offset) for side in range(2)
    ]
    entry = iota((span, LANES), 1)

    def put(chunk, carry):
        start = pl.multiple_of(chunk * LANES, LANES)
        sums = jnp.zeros((3 * HEAD_ROWS, LANES), F32)
        for side in range(2):
            chosen = jnp.where(entry + start == index[side], 1.0, 0.0).astype(BF16)
            sums = sums + dot(parts[side], chosen)
        out_ref[:, pl.ds(start, LANES)] = (
            sums[:HEAD_ROWS] + sums[HEAD_ROWS : 2 * HEAD_ROWS] + sums[2 * HEAD_ROWS :]
        )
        return carry

    lax.fori_loop(0, out_ref.shape[1] // LANES, put, 0)


def attend_kernel(row_span, scal_ref, query_ref, kv_ref, table_ref, mixed_ref, probs_ref, diag_ref):
    rows, keys = query_ref.shape[0], kv_ref.shape[0]
    width, count, offset = scal_ref[0], scal_ref[1], scal_ref[2]
    fill_diagonals(table_ref, diag_ref, rows, keys, row_span, width, offset)
    attend(query_ref, kv_ref, diag_ref, probs_ref, mixed_ref, width, count, offset)


def attend_back_kernel(
    row_span, scal_ref, query_ref, kv_ref, probs_ref, grad_ref, grad_query_ref, grad_kv_ref, table_ref, fold_ref
):
    rows, keys = query_ref.shape[0], kv_ref.shape[0]
    width, offset = scal_ref[0], scal_ref[2]
    fold_ref[...] = jnp.zeros_like(fold_ref)
    attend_back(
        query_ref, kv_ref, probs_ref, grad_ref, grad_query_ref, grad_kv_ref, fold_ref, width, offset
    )
    table_gradient(fold_ref, table_ref, rows, keys, row_span, width, offset)


MESH = pl.DeviceIdType.MESH
Z_SIZE = 4


class Place:
    def __init__(self):
        img = lax.axis_index("img")
        self.x = lax.axis_index("seq")
        self.c = lax.rem(img, 2)
        self.y = lax.rem(img // 2, 2)
        self.z = img // 4

    def at(self, z=None, y=None, c=None, x=None):
        z = self.z if z is None else z
        y = self.y if y is None else y
        c = self.c if c is None else c
        x = self.x if x is None else x
        return {"img": (z * 2 + y) * 2 + c, "seq": x}

    def sibling(self):
        return self.at(c=1 - self.c)

    def over_x(self):
        return self.at(x=1 - self.x)

    def over_y(self):
        return self.at(y=1 - self.y)

    def z_of(self, step):
        return lax.rem(self.z + step, Z_SIZE)

    def partners(self):
        return [self.sibling(), self.over_x(), self.over_y()] + [
            self.at(z=self.z_of(step)) for step in range(1, Z_SIZE)
        ]


def meet(place):
    barrier = pltpu.get_barrier_semaphore()
    partners = place.partners()
    for partner in partners:
        pl.semaphore_signal(barrier, inc=1, device_id=partner, device_id_type=MESH)
    pl.semaphore_wait(barrier, len(partners))


class Sems:
    def __init__(self, send, recv):
        self.send, self.recv, self.used = send, recv, 0

    def copy(self, src, dst, device):
        index = self.used
        self.used += 1
        return pltpu.make_async_remote_copy(
            src_ref=src,
            dst_ref=dst,
            send_sem=self.send.at[index],
            recv_sem=self.recv.at[index],
            device_id=device,
            device_id_type=MESH,
        )


GATHER_COPIES = 10


class Gather:
    def __init__(self, place, src, slots, cols, x_last, sems, local_sem):
        z, y, c, x = place.z, place.y, place.c, place.x
        groups = src.shape[0]
        every = slice(None)

        def part(a, b, e):
            return slots.at[a, b, c, pl.ds(e * groups, groups), :, cols]

        own = part(z, y, x)
        self.local = pltpu.make_async_copy(src.at[:, :, cols], own, local_sem)
        self.along_z = [
            sems.copy(src.at[:, :, cols], own, place.at(z=place.z_of(step)))
            for step in range(1, Z_SIZE)
        ]
        line = part(every, y, x)
        mid_line = part(every, 1 - y, x) if x_last else part(every, y, 1 - x)
        far_line = part(every, y, 1 - x) if x_last else part(every, 1 - y, x)
        cross_line = part(every, 1 - y, 1 - x)
        mid, last = place.over_y(), place.over_x()
        if not x_last:
            mid, last = last, mid
        sibling = place.sibling()
        self.line_mid = sems.copy(line, line, mid)
        self.line_last = sems.copy(line, line, last)
        self.line_core = sems.copy(line, line, sibling)
        self.mid_last = sems.copy(mid_line, mid_line, last)
        self.mid_core = sems.copy(mid_line, mid_line, sibling)
        self.far_core = sems.copy(far_line, far_line, sibling)
        self.cross_core = sems.copy(cross_line, cross_line, sibling)

    def begin(self):
        self.local.start()
        for copy in self.along_z:
            copy.start()

    def second(self):
        self.local.wait()
        for copy in self.along_z:
            copy.wait_recv()
        self.line_mid.start()
        self.line_last.start()
        self.line_core.start()

    def third(self):
        self.line_mid.wait_recv()
        self.mid_last.start()
        self.mid_core.start()

    def fourth(self):
        self.line_last.wait_recv()
        self.far_core.start()
        self.mid_last.wait_recv()
        self.cross_core.start()

    def arrive(self):
        for copy in (self.line_core, self.mid_core, self.far_core, self.cross_core):
            copy.wait_recv()

    def settle(self):
        for copy in self.along_z + [
            self.line_mid,
            self.line_last,
            self.line_core,
            self.mid_last,
            self.mid_core,
            self.far_core,
            self.cross_core,
        ]:
            copy.wait_send()


def halves(width):
    middle = width // 2 // LANES * LANES
    return [(0, middle), (middle, width - middle)]


REDUCE_COPIES = 6


class Reduce:
    def __init__(self, place, grad, own, first, second, third, out, start, size, x_first, sems, pieces=None):
        rows = out.shape[0]

        def flat(ref):
            return ref.reshape(ref.shape[:-3] + (rows, ref.shape[-1]))

        self.place, self.out = place, out
        self.grad, self.own, self.first = flat(grad), flat(own), flat(first)
        self.second, self.third = flat(second), flat(third)
        self.pieces = pieces or [(0, start, size)]
        self.x_first = x_first
        z, y, c, x = place.z, place.y, place.c, place.x
        every = slice(None)
        cols = pl.ds(start, size)
        self.cols = cols
        self.to_core = sems.copy(
            grad.at[:, :, 1 - c, :, :, :, cols], own.at[:, :, :, :, :, cols], place.sibling()
        )
        over_first, over_second = place.over_x(), place.over_y()
        if x_first:
            leaving, other = own.at[:, :, 1 - x, :, :, cols], 1 - y
        else:
            over_first, over_second = over_second, over_first
            leaving, other = own.at[:, 1 - y, :, :, :, cols], 1 - x
        self.kept = y if x_first else x
        self.over_first = sems.copy(leaving, first, over_first)
        self.over_second = sems.copy(first.at[:, other], second, over_second)
        self.along_z = []
        for step in range(1, Z_SIZE):
            target = place.z_of(step)
            self.along_z.append(
                sems.copy(second.at[target], third.at[step - 1], place.at(z=target))
            )

    def begin(self):
        self.to_core.start()

    def add_core(self):
        self.to_core.wait_recv()
        place = self.place

        def add(zy, carry):
            z, y = zy // 2, lax.rem(zy, 2)
            for x in range(2):
                mine = self.grad[z, y, place.c, x, :, self.cols].astype(F32)
                theirs = self.own[z, y, x, :, self.cols].astype(F32)
                self.own[z, y, x, :, self.cols] = (mine + theirs).astype(self.own.dtype)
            return carry

        lax.fori_loop(0, 2 * Z_SIZE, add, 0)
        self.over_first.start()

    def add_first(self):
        self.over_first.wait_recv()
        place = self.place

        def add(z, carry):
            for other in range(2):
                if self.x_first:
                    mine = self.own[z, other, place.x, :, self.cols].astype(F32)
                else:
                    mine = self.own[z, place.y, other, :, self.cols].astype(F32)
                theirs = self.first[z, other].astype(F32)
                self.first[z, other] = (mine + theirs).astype(self.first.dtype)
            return carry

        lax.fori_loop(0, Z_SIZE, add, 0)
        self.over_second.start()

    def add_second(self):
        self.over_second.wait_recv()

        def add(z, carry):
            mine = self.first[z, self.kept].astype(F32)
            theirs = self.second[z].astype(F32)
            self.second[z] = (mine + theirs).astype(self.second.dtype)
            return carry

        lax.fori_loop(0, Z_SIZE, add, 0)
        for copy in self.along_z:
            copy.start()

    def finish(self):
        total = self.second[self.place.z].astype(F32)
        for step, copy in enumerate(self.along_z):
            copy.wait_recv()
            total = total + self.third[step].astype(F32)
        for source, target, size in self.pieces:
            self.out[:, target : target + size] = total[:, source : source + size]

    def settle(self):
        for copy in [self.to_core, self.over_first, self.over_second] + self.along_z:
            copy.wait_send()


class Names:
    pass


def norm_rows(values):
    centred = values - jnp.mean(values, axis=1, keepdims=True)
    inv_std = lax.rsqrt(jnp.mean(centred * centred, axis=1, keepdims=True) + EPSILON)
    return centred * inv_std, inv_std


def norm_rows_back(grad_out, normed, inv_std, gain):
    scaled = grad_out * gain
    return inv_std * (
        scaled
        - jnp.mean(scaled, axis=1, keepdims=True)
        - normed * jnp.mean(scaled * normed, axis=1, keepdims=True)
    )


def sum_rows(values):
    return jnp.sum(values.astype(F32), axis=0, keepdims=True)


def div_const(values, divisor):
    return jnp.floor((values.astype(F32) + 0.5) * (1.0 / divisor)).astype(jnp.int32)


def tile(slots, start, size):
    rows = slots.shape[3] * ROW_GROUP
    view = slots.reshape(4 * Z_SIZE, rows, slots.shape[-1])
    return view[:, :, pl.ds(start, size)].reshape(-1, size)


def put_slots(slots, cols, values):
    devices = 8 * Z_SIZE
    view = slots.reshape(devices, slots.shape[4] * ROW_GROUP, slots.shape[-1])
    view[:, :, cols] = values.reshape(devices, -1, values.shape[1]).astype(slots.dtype)


def tiles(count, step):
    def wrap(body):
        def run(number, carry):
            body(number, pl.multiple_of(number * step, step))
            return carry

        lax.fori_loop(0, count, run, 0)

    return wrap


LINES = 16
SLOT_ROWS = 24
(
    GAIN_ONE, SHIFT_ONE, QUERY_BIAS, VALUE_BIAS, PROJ_SHIFT, SCALE_ONE, GAIN_TWO, SHIFT_TWO, FC2_SHIFT, SCALE_TWO,
) = range(10)
HIDDEN_LINE = 10


def unpack_lines(packed, shard, hidden_shard, vec_ref, hidden_ref):
    rows = packed.shape[0]
    devices = rows // SLOT_ROWS
    low = packed.astype(BF16)
    width = shard * devices
    lane = iota((LANES, width), 1)
    spread = jnp.where(lane - div_const(lane, shard) * shard == iota((LANES, width), 0), 1.0, 0.0)
    wide = dot(low, spread.astype(BF16))
    owner = div_const(iota((rows, width), 0), SLOT_ROWS)
    wide = jnp.where(owner == div_const(iota((rows, width), 1), shard), wide, 0.0).astype(BF16)
    row = iota((LINES, rows), 1)
    line = row - div_const(row, SLOT_ROWS) * SLOT_ROWS
    vec_ref[...] = dot(jnp.where(line == iota((LINES, rows), 0), 1.0, 0.0).astype(BF16), wide)
    row = iota((devices, rows), 1)
    chosen = jnp.where(row == iota((devices, rows), 0) * SLOT_ROWS + HIDDEN_LINE, 1.0, 0.0)
    hidden = dot(chosen.astype(BF16), low).astype(BF16)
    step = 8 * LANES
    for start in range(0, hidden_shard * devices, step):
        lane = iota((LANES, step), 1) + start
        owner = div_const(lane, hidden_shard)
        spread = jnp.where(lane - owner * hidden_shard == iota((LANES, step), 0), 1.0, 0.0)
        wide = dot(hidden, spread.astype(BF16))
        owner = div_const(iota((devices, step), 1) + start, hidden_shard)
        wide = jnp.where(owner == iota((devices, step), 0), wide, 0.0)
        hidden_ref[:, start : start + step] = jnp.broadcast_to(sum_rows(wide), (8, step))


def layer_kernel(names, row_span, *refs):
    s = Names()
    s.__dict__.update(zip(names, refs))
    buffers = list(refs[len(names) :])
    send, recv, local = buffers[-3:]
    place = Place()
    x = place.x
    width, count, offset = s.scal[0], s.scal[1], s.scal[2]
    rows, model = s.tokens.shape
    keys = 2 * rows
    hidden = s.w_fc1.shape[2]
    shard, hidden_shard = s.w_qkv.shape[0] * ROW_GROUP, s.w_fc2.shape[0] * ROW_GROUP
    half = model // 2
    own_rows = pl.ds(pl.multiple_of(x * rows, rows), rows)
    far_rows = pl.ds(pl.multiple_of((1 - x) * rows, rows), rows)
    sems = Sems(send, recv)
    locals_used = []

    def gather(src, slots, cuts):
        chunks = []
        for number, (start, size) in enumerate(cuts):
            sem = local.at[len(locals_used)]
            locals_used.append(0)
            chunks.append(Gather(place, src, slots, pl.ds(start, size), number == 0, sems, sem))
        return chunks

    def reduce(out, cuts, pieces):
        chunks = []
        grad, own = buffers.pop(0), buffers.pop(0)
        for number, (start, size) in enumerate(cuts):
            stages = [buffers.pop(0) for _ in range(3)]
            chunks.append(
                Reduce(
                    place, grad, own, *stages, out, start, size, number == 0, sems, pieces and pieces[number],
                )
            )
        return grad, chunks

    def each(chunks, *steps):
        for step in steps:
            for chunk in chunks:
                step(chunk)

    swap = sems.copy(s.tokens, s.far_tokens, place.over_x())
    give = sems.copy(s.give, s.take, place.over_x())
    get_pack = gather(s.pack, s.packs, [(0, LANES)])
    get_qkv = gather(s.w_qkv, s.wq, halves(3 * model))
    get_proj = gather(s.w_proj, s.wp, halves(model))
    get_fc1 = gather(s.w_fc1, s.w1, halves(hidden))
    get_fc2 = gather(s.w_fc2, s.w2, halves(model))
    third = 3 * half
    qkv_pieces = [
        [(part * half, part * model + group * half, half) for part in range(3)] for group in range(2)
    ]
    s.g_fc2, put_fc2 = reduce(s.o_fc2, halves(model), None)
    s.g_fc1, put_fc1 = reduce(s.o_fc1, halves(hidden), None)
    s.g_proj, put_proj = reduce(s.o_proj, halves(model), None)
    s.g_qkv, put_qkv = reduce(s.o_qkv, [(0, third), (third, third)], qkv_pieces)
    s.g_table, put_table = reduce(s.o_table, [(0, LANES)], None)
    s.g_small, put_small = reduce(s.o_small, [(0, LANES)], None)
    get_table = gather(s.o_table.reshape(1, 8, LANES), s.table_all, [(0, LANES)])

    meet(place)
    swap.start()
    for chunks in (get_pack, get_qkv, get_proj, get_fc1, get_fc2):
        each(chunks, Gather.begin)

    fill_diagonals(s.table_lines, s.diag, rows, keys, row_span, width, offset)
    inputs = s.tokens[...].astype(F32)
    normed, inv_std = norm_rows(inputs)
    s.n1[...] = normed
    s.r1[...] = jnp.broadcast_to(inv_std, s.r1.shape)
    s.fold[...] = jnp.zeros_like(s.fold)
    s.lines[...] = jnp.zeros_like(s.lines)

    each(get_pack, Gather.second, Gather.third)
    each(get_qkv, Gather.second)
    each(get_pack, Gather.fourth, Gather.arrive)
    unpack_lines(tile(s.packs, 0, LANES), shard, hidden_shard, s.vec, s.b1)

    def line(number):
        return s.vec[number : number + 1, :]

    def set_line(number, values):
        s.lines[number : number + 1, :] = values

    s.h1[own_rows, :] = (s.n1[...] * line(GAIN_ONE) + line(SHIFT_ONE)).astype(BF16)
    swap.wait_recv()
    far = norm_rows(s.far_tokens[...].astype(F32))[0]
    s.h1[far_rows, :] = (far * line(GAIN_ONE) + line(SHIFT_ONE)).astype(BF16)
    each(get_proj, Gather.second)
    s.h1t[...] = s.h1[...].T
    s.dm[...] = (line(SCALE_TWO) * s.cot[...].astype(F32)).astype(BF16)
    set_line(FC2_SHIFT, sum_rows(s.dm[...]))
    each(get_qkv, Gather.third)
    each(get_fc1, Gather.second)
    each(get_qkv, Gather.fourth)
    each(get_proj, Gather.third)
    each(get_qkv, Gather.arrive)

    step = 2 * LANES

    @tiles(model // step, step)
    def _(number, start):
        s.kv[:, pl.ds(start, step)] = dot(s.h1[...], tile(s.wq, model + start, step)).astype(BF16)
        sums = dot(s.h1[...], tile(s.wq, 2 * model + start, step))
        sums = sums + s.vec[VALUE_BIAS : VALUE_BIAS + 1, pl.ds(start, step)]
        s.kv[:, pl.ds(model + start, step)] = sums.astype(BF16)

    @tiles(model // step, step)
    def _(number, start):
        cols = pl.ds(start, step)
        sums = dot(s.h1[own_rows, :], tile(s.wq, start, step))
        s.q[:, cols] = (sums + s.vec[QUERY_BIAS : QUERY_BIAS + 1, cols]).astype(BF16)

    each(get_fc1, Gather.third)
    attend(s.q, s.kv, s.diag, s.probs, s.mixed, width, count, offset, (0, PAIRS // 2))
    each(get_fc2, Gather.second)
    each(get_proj, Gather.fourth)
    attend(s.q, s.kv, s.diag, s.probs, s.mixed, width, count, offset, (PAIRS // 2, PAIRS))
    s.mixedt[...] = s.mixed[...].T
    each(get_fc1, Gather.fourth)
    each(get_proj, Gather.arrive)

    @tiles(model // step, step)
    def _(number, start):
        cols = pl.ds(start, step)
        branch = dot(s.mixed[...], tile(s.wp, start, step)) + s.vec[PROJ_SHIFT : PROJ_SHIFT + 1, cols]
        s.z[:, cols] = branch
        s.x1[:, cols] = s.tokens[:, cols].astype(F32) + s.vec[SCALE_ONE : SCALE_ONE + 1, cols] * branch

    normed, inv_std = norm_rows(s.x1[...])
    s.n2[...] = normed
    s.r2[...] = jnp.broadcast_to(inv_std, s.r2.shape)
    s.h2[...] = (normed * line(GAIN_TWO) + line(SHIFT_TWO)).astype(BF16)
    s.h2t[...] = s.h2[...].T
    each(get_fc2, Gather.third)
    each(get_fc1, Gather.arrive)

    @tiles(hidden // step, step)
    def _(number, start):
        cols = pl.ds(start, step)
        act = dot(s.h2[...], tile(s.w1, start, step)) + s.b1[0:1, cols]
        gate = 0.5 * (1.0 + lax.erf(act * 0.5**0.5))
        low = (act * gate).astype(BF16)
        s.u[:, cols] = low
        s.ut[cols, :] = low.T
        s.slope[:, cols] = gate + act * jnp.exp(act * act * -0.5) * 0.3989422804014327

    each(get_fc2, Gather.fourth)
    deep = 8 * hidden_shard
    for group in range(2):

        @tiles(Z_SIZE, deep)
        def _(number, start):
            cols = pl.ds(group * half, half)
            sums = dot(s.ut[pl.ds(start, deep), :], s.dm[:, cols])
            view = s.g_fc2.reshape(Z_SIZE, 8, hidden_shard, model)
            view[number, :, :, cols] = sums.reshape(8, hidden_shard, half).astype(BF16)

        put_fc2[group].begin()
    each(get_fc2, Gather.arrive)

    @tiles(Z_SIZE, deep)
    def _(number, start):
        cols = pl.ds(start, deep)
        weight = s.w2.reshape(Z_SIZE, deep, model)[number]
        grad_hidden = dot(s.dm[...], weight, NT)
        s.da[:, cols] = (grad_hidden * s.slope[:, cols]).astype(BF16)

    each(put_fc2, Reduce.add_core)
    for group in range(2):

        @tiles(hidden // 2 // step, step)
        def _(number, start):
            cols = pl.ds(start + group * (hidden // 2), step)
            sums = dot(s.h2t[...], s.da[:, cols])
            put_slots(s.g_fc1, cols, sums)

        put_fc1[group].begin()

    @tiles(model // step, step)
    def _(number, start):
        cols = pl.ds(start, step)
        branch = dot(s.u[...], tile(s.w2, start, step)) + s.vec[FC2_SHIFT : FC2_SHIFT + 1, cols]
        s.out[:, cols] = (s.x1[:, cols] + s.vec[SCALE_TWO : SCALE_TWO + 1, cols] * branch).astype(BF16)
        s.lines[SCALE_TWO : SCALE_TWO + 1, cols] = sum_rows(s.cot[:, cols].astype(F32) * branch)

    s.hidden_lines[...] = jnp.broadcast_to(sum_rows(s.da[...]), s.hidden_lines.shape)
    grad = jnp.zeros((rows, model), F32)
    for start in range(0, hidden, model):
        grad = grad + dot(s.da[:, start : start + model], tile(s.w1, start, model), NT)
    set_line(GAIN_TWO, sum_rows(grad * s.n2[...]))
    set_line(SHIFT_TWO, sum_rows(grad))
    dx1 = s.cot[...].astype(F32) + norm_rows_back(grad, s.n2[...], s.r2[:, 0:1], line(GAIN_TWO))
    s.dx1[...] = dx1
    set_line(SCALE_ONE, sum_rows(dx1 * s.z[...]))
    s.dz[...] = (line(SCALE_ONE) * dx1).astype(BF16)
    set_line(PROJ_SHIFT, sum_rows(s.dz[...]))
    for group in range(2):
        cols = pl.ds(group * half, half)
        sums = dot(s.mixedt[...], s.dz[:, cols])
        put_slots(s.g_proj, cols, sums)
        put_proj[group].begin()
    s.dmixed[...] = dot(s.dz[...], tile(s.wp, 0, model), NT).astype(BF16)
    each(put_fc1, Reduce.add_core)
    each(put_fc2, Reduce.add_first)

    def qkv_grad(group):
        cols = pl.ds(group * half, half)
        value_cols = pl.ds(model + group * half, half)
        own_lines = s.h1t[:, own_rows]
        all_lines = s.h1t[...]
        for part, sums in enumerate(
            (
                dot(own_lines, s.dq[:, cols]),
                dot(all_lines, s.dkv[:, cols]),
                dot(all_lines, s.dkv[:, value_cols]),
            )
        ):
            target = pl.ds(group * third + part * half, half)
            put_slots(s.g_qkv, target, sums)
        put_qkv[group].begin()

    attend_back(
        s.q, s.kv, s.probs, s.dmixed, s.dq, s.dkv, s.fold, width, offset, (0, PAIRS // 2)
    )
    qkv_grad(0)
    each(put_proj, Reduce.add_core)
    each(put_fc1, Reduce.add_first)
    each(put_fc2, Reduce.add_second)
    attend_back(
        s.q, s.kv, s.probs, s.dmixed, s.dq, s.dkv, s.fold, width, offset, (PAIRS // 2, PAIRS)
    )
    qkv_grad(1)
    grad_key = dot(s.dkv[:, :model], tile(s.wq, model, model), NT)
    s.dh1[...] = grad_key + dot(s.dkv[:, model:], tile(s.wq, 2 * model, model), NT)
    s.give[...] = s.dh1[far_rows, :].astype(BF16)
    give.start()
    table_gradient(s.fold, s.table_sums, rows, keys, row_span, width, offset)

    @tiles(4 * Z_SIZE, LANES)
    def _(number, start):
        zz, yy, cc = number // 4, lax.rem(number // 2, 2), lax.rem(number, 2)
        for xx in range(2):
            s.g_table[zz, yy, cc, xx, 0] = s.table_sums[8 * xx : 8 * xx + 8, pl.ds(start, LANES)]

    each(put_table, Reduce.begin)
    each(put_qkv, Reduce.add_core)
    each(put_proj, Reduce.add_first)
    each(put_table, Reduce.add_core)
    each(put_fc1, Reduce.add_second)
    each(put_fc2, Reduce.finish)
    set_line(QUERY_BIAS, sum_rows(s.dq[...]))
    set_line(VALUE_BIAS, sum_rows(s.dkv[:, model:]))
    grad = s.dh1[own_rows, :] + dot(s.dq[...], tile(s.wq, 0, model), NT)
    give.wait_recv()
    grad = grad + s.take[...].astype(F32)
    set_line(GAIN_ONE, sum_rows(grad * s.n1[...]))
    set_line(SHIFT_ONE, sum_rows(grad))
    dx = s.dx1[...] + norm_rows_back(grad, s.n1[...], s.r1[:, 0:1], line(GAIN_ONE))
    s.grad_tokens[...] = dx.astype(BF16)

    @tiles(8 * Z_SIZE, 1)
    def _(number, start):
        zz, yy, cc, xx = number // 8, lax.rem(number // 4, 2), lax.rem(number // 2, 2), lax.rem(number, 2)
        moved = pltpu.roll(s.lines[...], model - number * shard, 1)
        for group in range(LINES // ROW_GROUP):
            s.g_small[zz, yy, cc, xx, group] = moved[group * ROW_GROUP : (group + 1) * ROW_GROUP, :LANES]
        moved = pltpu.roll(s.hidden_lines[...], hidden - number * hidden_shard, 1)
        s.g_small[zz, yy, cc, xx, LINES // ROW_GROUP] = moved[:, :LANES]

    each(put_small, Reduce.begin)
    each(put_table, Reduce.add_first)
    each(put_small, Reduce.add_core)
    each(put_qkv, Reduce.add_first)
    each(put_proj, Reduce.add_second)
    each(put_table, Reduce.add_second)
    each(put_small, Reduce.add_first)
    each(put_fc1, Reduce.finish)
    each(put_table, Reduce.finish)
    each(get_table, Gather.begin)
    each(put_small, Reduce.add_second)
    each(put_qkv, Reduce.add_second)
    each(get_table, Gather.second, Gather.third)
    each(put_proj, Reduce.finish)
    each(put_small, Reduce.finish)
    each(get_table, Gather.fourth, Gather.arrive)
    each(put_qkv, Reduce.finish)
    swap.wait_send()
    give.wait_send()
    for chunks in (get_pack, get_qkv, get_proj, get_fc1, get_fc2, get_table):
        each(chunks, Gather.settle)
    for chunks in (put_fc2, put_fc1, put_proj, put_qkv, put_table, put_small):
        each(chunks, Reduce.settle)


def grouped(array):
    return array.reshape(-1, ROW_GROUP, array.shape[-1])


def run_layer(row_span, scalars, tokens, cotangent, packed, w_qkv, w_proj, w_fc1, w_fc2, table_lines):
    rows, model = tokens.shape
    keys = 2 * rows
    shard, hidden, hidden_shard = w_qkv.shape[0], w_fc1.shape[1], w_fc2.shape[0]
    smem = pl.BlockSpec(memory_space=pltpu.SMEM)
    vmem = pl.BlockSpec(memory_space=pltpu.VMEM)
    anywhere = pl.BlockSpec(memory_space=pl.ANY)
    inputs = dict(
        scal=(scalars, smem),
        tokens=(tokens, vmem),
        cot=(cotangent, vmem),
        pack=(grouped(packed), vmem),
        w_qkv=(grouped(w_qkv), anywhere),
        w_proj=(grouped(w_proj), anywhere),
        w_fc1=(grouped(w_fc1), anywhere),
        w_fc2=(grouped(w_fc2), anywhere),
        table_lines=(table_lines, vmem),
    )
    outputs = dict(
        out=((rows, model), BF16),
        grad_tokens=((rows, model), BF16),
        o_small=((SLOT_ROWS, LANES), F32),
        o_qkv=((shard, 3 * model), F32),
        o_proj=((shard, model), F32),
        o_fc1=((shard, hidden), F32),
        o_fc2=((hidden_shard, model), F32),
        table_all=((Z_SIZE, 2, 2, 2, 8, LANES), F32),
    )
    scratch = dict(
        o_table=((8, LANES), F32),
        far_tokens=((rows, model), BF16),
        give=((rows, model), BF16),
        take=((rows, model), BF16),
        packs=((Z_SIZE, 2, 2, 2 * SLOT_ROWS // ROW_GROUP, ROW_GROUP, LANES), F32),
        wq=((Z_SIZE, 2, 2, 2 * shard // ROW_GROUP, ROW_GROUP, 3 * model), BF16),
        wp=((Z_SIZE, 2, 2, 2 * shard // ROW_GROUP, ROW_GROUP, model), BF16),
        w1=((Z_SIZE, 2, 2, 2 * shard // ROW_GROUP, ROW_GROUP, hidden), BF16),
        w2=((Z_SIZE, 2, 2, 2 * hidden_shard // ROW_GROUP, ROW_GROUP, model), BF16),
        vec=((LINES, model), F32),
        b1=((8, hidden), F32),
        diag=((HEAD_ROWS, 2 * (rows + keys)), F32),
        h1=((keys, model), BF16),
        h1t=((model, keys), BF16),
        n1=((rows, model), F32),
        r1=((rows, LANES), F32),
        q=((rows, model), BF16),
        kv=((keys, 2 * model), BF16),
        probs=((HEADS, rows, keys), F32),
        mixed=((rows, model), BF16),
        mixedt=((model, rows), BF16),
        z=((rows, model), F32),
        x1=((rows, model), F32),
        n2=((rows, model), F32),
        r2=((rows, LANES), F32),
        h2=((rows, model), BF16),
        h2t=((model, rows), BF16),
        u=((rows, hidden), BF16),
        ut=((hidden, rows), BF16),
        slope=((rows, hidden), F32),
        dm=((rows, model), BF16),
        da=((rows, hidden), BF16),
        dx1=((rows, model), F32),
        dz=((rows, model), BF16),
        dmixed=((rows, model), BF16),
        dq=((rows, model), BF16),
        dkv=((keys, 2 * model), BF16),
        dh1=((keys, model), F32),
        fold=(((rows + keys) // LANES, 2 * HEAD_ROWS * 8, LANES), F32),
        table_sums=((HEAD_ROWS, table_lines.shape[1]), F32),
        lines=((LINES, model), F32),
        hidden_lines=((8, hidden), F32),
    )
    stages = []
    chunks = 0
    for slot_rows, slot_width, dtype, cuts in (
        (hidden_shard, model, BF16, None),
        (shard, hidden, BF16, None),
        (shard, model, BF16, None),
        (shard, 3 * model, BF16, [(0, 3 * model // 2)] * 2),
        (8, LANES, F32, None),
        (SLOT_ROWS, LANES, F32, None),
    ):
        cuts = cuts or ([(0, slot_width)] if slot_width <= LANES else halves(slot_width))
        groups = slot_rows // ROW_GROUP
        stages.append(((Z_SIZE, 2, 2, 2, groups, ROW_GROUP, slot_width), dtype))
        stages.append(((Z_SIZE, 2, 2, groups, ROW_GROUP, slot_width), dtype))
        for _, size in cuts:
            for lead in ((Z_SIZE, 2), (Z_SIZE,), (Z_SIZE - 1,)):
                stages.append((lead + (groups, ROW_GROUP, size), dtype))
            chunks += 1
    copies = 2 + GATHER_COPIES * 10 + REDUCE_COPIES * chunks
    names = list(inputs) + list(outputs) + list(scratch)
    return pl.pallas_call(
        partial(layer_kernel, names, row_span),
        out_shape=tuple(jax.ShapeDtypeStruct(shape, dtype) for shape, dtype in outputs.values()),
        in_specs=[spec for _, spec in inputs.values()],
        out_specs=(vmem,) * len(outputs),
        scratch_shapes=[pltpu.VMEM(shape, dtype) for shape, dtype in list(scratch.values()) + stages]
        + [
            pltpu.SemaphoreType.DMA((copies,)),
            pltpu.SemaphoreType.DMA((copies,)),
            pltpu.SemaphoreType.DMA((10,)),
        ],
        compiler_params=pltpu.CompilerParams(
            collective_id=0, has_side_effects=True, vmem_limit_bytes=VMEM_LIMIT
        ),
    )(*[array for array, _ in inputs.values()])


def layer_norm(values, gain, shift):
    centred = values - jnp.mean(values, axis=-1, keepdims=True)
    inv_std = lax.rsqrt(jnp.mean(centred * centred, axis=-1, keepdims=True) + EPSILON)
    normed = centred * inv_std
    return (normed * gain + shift, normed, inv_std)


def norm_back(grad_out, normed, inv_std, gain):
    scaled = grad_out * gain
    return inv_std * (
        scaled
        - jnp.mean(scaled, axis=-1, keepdims=True)
        - normed * jnp.mean(scaled * normed, axis=-1, keepdims=True)
    )


def row_sum(values):
    return jnp.sum(values.astype(jnp.float32), axis=0)


def per_device_native(
    tokens,
    cotangent,
    counts,
    widths,
    norm1_gain,
    norm1_shift,
    w_qkv,
    q_bias,
    v_bias,
    w_proj,
    proj_bias,
    gamma1,
    norm2_gain,
    norm2_shift,
    w_fc1,
    fc1_bias,
    w_fc2,
    fc2_bias,
    gamma2,
    bias_table,
):
    fetched = (
        lax.all_gather(norm1_gain, ("img", "seq"), axis=0, tiled=True),
        lax.all_gather(norm1_shift, ("img", "seq"), axis=0, tiled=True),
        lax.all_gather(w_qkv, ("img", "seq"), axis=0, tiled=True),
        lax.all_gather(q_bias, ("img", "seq"), axis=0, tiled=True),
        lax.all_gather(v_bias, ("img", "seq"), axis=0, tiled=True),
        lax.all_gather(w_proj, ("img", "seq"), axis=0, tiled=True),
        lax.all_gather(proj_bias, ("img", "seq"), axis=0, tiled=True),
        lax.all_gather(gamma1, ("img", "seq"), axis=0, tiled=True),
        lax.all_gather(norm2_gain, ("img", "seq"), axis=0, tiled=True),
        lax.all_gather(norm2_shift, ("img", "seq"), axis=0, tiled=True),
        lax.all_gather(w_fc1, ("img", "seq"), axis=0, tiled=True),
        lax.all_gather(fc1_bias, ("img", "seq"), axis=0, tiled=True),
        lax.all_gather(w_fc2, ("img", "seq"), axis=0, tiled=True),
        lax.all_gather(fc2_bias, ("img", "seq"), axis=0, tiled=True),
        lax.all_gather(gamma2, ("img", "seq"), axis=0, tiled=True),
    )
    (
        gain_one,
        shift_one,
        qkv_weight,
        query_bias,
        value_bias,
        proj_weight,
        proj_shift,
        scale_one,
        gain_two,
        shift_two,
        fc1_weight,
        fc1_shift,
        fc2_weight,
        fc2_shift,
        scale_two,
    ) = fetched
    gain_one = gain_one.astype(jnp.float32)
    shift_one = shift_one.astype(jnp.float32)
    proj_shift = proj_shift.astype(jnp.float32)
    scale_one = scale_one.astype(jnp.float32)
    gain_two = gain_two.astype(jnp.float32)
    shift_two = shift_two.astype(jnp.float32)
    fc1_shift = fc1_shift.astype(jnp.float32)
    fc2_shift = fc2_shift.astype(jnp.float32)
    scale_two = scale_two.astype(jnp.float32)
    local_rows = tokens.shape[0]
    width_model = tokens.shape[1]
    seq_len = local_rows * lax.axis_size("seq")
    offset = lax.axis_index("seq") * local_rows
    row_span = (seq_len - 1) // (SIDE // 2) + 1
    table_rows = bias_table.shape[0]
    entries = -(-table_rows // (2 * LANES)) * 2 * LANES
    table_lines = jnp.pad(
        bias_table.T, ((0, HEAD_ROWS - HEADS), (0, entries - table_rows))
    )
    scalars = jnp.stack([widths[0], counts[0], offset.astype(jnp.int32)])
    smem = pl.BlockSpec(memory_space=pltpu.SMEM)
    vmem = pl.BlockSpec(memory_space=pltpu.VMEM)
    params = pltpu.CompilerParams(vmem_limit_bytes=40 << 20)

    inputs_f = tokens.astype(jnp.float32)
    normed_full, normed_one, inv_std_one = layer_norm(inputs_f, gain_one, shift_one)
    normed_low = normed_full.astype(jnp.bfloat16)
    qkv_shift = jnp.concatenate(
        [query_bias, jnp.zeros((width_model,), jnp.bfloat16), value_bias]
    ).astype(jnp.float32)
    projected = (
        jnp.dot(normed_low, qkv_weight, preferred_element_type=jnp.float32) + qkv_shift
    ).astype(jnp.bfloat16)
    queries = projected[:, :width_model]
    key_local = projected[:, width_model:]
    keys_all = lax.all_gather(key_local, "seq", axis=0, tiled=True)

    attn_low, probs = pl.pallas_call(
        partial(attend_kernel, row_span),
        out_shape=(
            jax.ShapeDtypeStruct((local_rows, width_model), BF16),
            jax.ShapeDtypeStruct((HEADS, local_rows, seq_len), F32),
        ),
        in_specs=[smem, vmem, vmem, vmem],
        out_specs=(vmem, vmem),
        scratch_shapes=[pltpu.VMEM((HEAD_ROWS, 2 * (local_rows + seq_len)), F32)],
        compiler_params=params,
    )(scalars, queries, keys_all, table_lines)
    branch_one = jnp.dot(attn_low, proj_weight, preferred_element_type=jnp.float32) + proj_shift
    residual_one = inputs_f + scale_one * branch_one
    normed_full_two, normed_two, inv_std_two = layer_norm(residual_one, gain_two, shift_two)
    normed_low_two = normed_full_two.astype(jnp.bfloat16)
    pre_act = jnp.dot(normed_low_two, fc1_weight, preferred_element_type=jnp.float32) + fc1_shift
    activated, gelu_pull = jax.vjp(partial(jax.nn.gelu, approximate=False), pre_act)
    hidden = activated.astype(jnp.bfloat16)
    branch_two = jnp.dot(hidden, fc2_weight, preferred_element_type=jnp.float32) + fc2_shift
    output = (residual_one + scale_two * branch_two).astype(jnp.bfloat16)
    grad_out = cotangent.astype(jnp.float32)
    grad_scale_two = jnp.sum(grad_out * branch_two, axis=0)
    grad_branch_two = (scale_two * grad_out).astype(jnp.bfloat16)
    grad_fc2_weight = jnp.einsum(
        "tf,td->fd", hidden, grad_branch_two, preferred_element_type=jnp.float32
    )
    grad_fc2_shift = row_sum(grad_branch_two)
    grad_hidden = jnp.einsum(
        "td,fd->tf", grad_branch_two, fc2_weight, preferred_element_type=jnp.float32
    )
    grad_pre = gelu_pull(grad_hidden)[0].astype(jnp.bfloat16)
    grad_fc1_weight = jnp.einsum(
        "td,tf->df", normed_low_two, grad_pre, preferred_element_type=jnp.float32
    )
    grad_fc1_shift = row_sum(grad_pre)
    grad_normed_two = jnp.einsum(
        "tf,df->td", grad_pre, fc1_weight, preferred_element_type=jnp.float32
    )
    grad_gain_two = jnp.sum(grad_normed_two * normed_two, axis=0)
    grad_shift_two = jnp.sum(grad_normed_two, axis=0)
    grad_resid = grad_out + norm_back(grad_normed_two, normed_two, inv_std_two, gain_two)
    grad_scale_one = jnp.sum(grad_resid * branch_one, axis=0)
    grad_branch_one = (scale_one * grad_resid).astype(jnp.bfloat16)
    grad_proj_weight = jnp.einsum(
        "td,te->de", attn_low, grad_branch_one, preferred_element_type=jnp.float32
    )
    grad_proj_shift = row_sum(grad_branch_one)
    grad_attn = jnp.einsum(
        "te,de->td", grad_branch_one, proj_weight, preferred_element_type=jnp.float32
    ).astype(jnp.bfloat16)
    grad_query, key_terms, table_grad = pl.pallas_call(
        partial(attend_back_kernel, row_span),
        out_shape=(
            jax.ShapeDtypeStruct((local_rows, width_model), BF16),
            jax.ShapeDtypeStruct((seq_len, 2 * width_model), BF16),
            jax.ShapeDtypeStruct((HEAD_ROWS, entries), F32),
        ),
        in_specs=[smem, vmem, vmem, vmem, vmem],
        out_specs=(vmem, vmem, vmem),
        scratch_shapes=[
            pltpu.VMEM(((local_rows + seq_len) // LANES, 2 * HEAD_ROWS * 8, LANES), F32)
        ],
        compiler_params=params,
    )(scalars, queries, keys_all, probs, grad_attn)
    own_terms = lax.psum_scatter(key_terms, "seq", scatter_dimension=0, tiled=True)
    grad_qkv = jnp.concatenate([grad_query, own_terms], axis=1)
    grad_qkv_weight = jnp.einsum(
        "td,te->de", normed_low, grad_qkv, preferred_element_type=jnp.float32
    )
    grad_query_bias = row_sum(grad_qkv[:, :width_model])
    grad_value_bias = row_sum(grad_qkv[:, 2 * width_model :])
    grad_normed_one = jnp.einsum(
        "te,de->td", grad_qkv, qkv_weight, preferred_element_type=jnp.float32
    )
    grad_gain_one = jnp.sum(grad_normed_one * normed_one, axis=0)
    grad_shift_one = jnp.sum(grad_normed_one, axis=0)
    grad_inputs = (
        grad_resid + norm_back(grad_normed_one, normed_one, inv_std_one, gain_one)
    ).astype(jnp.bfloat16)
    summed = (
        lax.psum_scatter(grad_gain_one, ("img", "seq"), scatter_dimension=0, tiled=True),
        lax.psum_scatter(grad_shift_one, ("img", "seq"), scatter_dimension=0, tiled=True),
        lax.psum_scatter(grad_qkv_weight, ("img", "seq"), scatter_dimension=0, tiled=True),
        lax.psum_scatter(grad_query_bias, ("img", "seq"), scatter_dimension=0, tiled=True),
        lax.psum_scatter(grad_value_bias, ("img", "seq"), scatter_dimension=0, tiled=True),
        lax.psum_scatter(grad_proj_weight, ("img", "seq"), scatter_dimension=0, tiled=True),
        lax.psum_scatter(grad_proj_shift, ("img", "seq"), scatter_dimension=0, tiled=True),
        lax.psum_scatter(grad_scale_one, ("img", "seq"), scatter_dimension=0, tiled=True),
        lax.psum_scatter(grad_gain_two, ("img", "seq"), scatter_dimension=0, tiled=True),
        lax.psum_scatter(grad_shift_two, ("img", "seq"), scatter_dimension=0, tiled=True),
        lax.psum_scatter(grad_fc1_weight, ("img", "seq"), scatter_dimension=0, tiled=True),
        lax.psum_scatter(grad_fc1_shift, ("img", "seq"), scatter_dimension=0, tiled=True),
        lax.psum_scatter(grad_fc2_weight, ("img", "seq"), scatter_dimension=0, tiled=True),
        lax.psum_scatter(grad_fc2_shift, ("img", "seq"), scatter_dimension=0, tiled=True),
        lax.psum_scatter(grad_scale_two, ("img", "seq"), scatter_dimension=0, tiled=True),
    )
    table_total = lax.psum(table_grad, ("img", "seq"))[:HEADS, :table_rows].T
    return (output, grad_inputs) + tuple(summed) + (table_total,)


def per_device_linked(
    tokens,
    cotangent,
    counts,
    widths,
    norm1_gain,
    norm1_shift,
    w_qkv,
    q_bias,
    v_bias,
    w_proj,
    proj_bias,
    gamma1,
    norm2_gain,
    norm2_shift,
    w_fc1,
    fc1_bias,
    w_fc2,
    fc2_bias,
    gamma2,
    bias_table,
):
    local_rows = tokens.shape[0]
    seq_len = local_rows * lax.axis_size("seq")
    offset = lax.axis_index("seq") * local_rows
    row_span = (seq_len - 1) // (SIDE // 2) + 1
    table_rows = bias_table.shape[0]
    entries = -(-table_rows // (2 * LANES)) * 2 * LANES
    table_lines = jnp.pad(bias_table.T, ((0, HEAD_ROWS - HEADS), (0, entries - table_rows)))
    scalars = jnp.stack([widths[0], counts[0], offset.astype(jnp.int32)])
    shard = norm1_gain.shape[0]
    hidden_shard = fc1_bias.shape[0]
    vectors = [
        norm1_gain, norm1_shift, q_bias, v_bias, proj_bias, gamma1, norm2_gain, norm2_shift, fc2_bias, gamma2,
    ]
    packed = jnp.concatenate(
        [
            jnp.pad(jnp.stack(vectors), ((0, 0), (0, LANES - shard))),
            jnp.pad(fc1_bias.reshape(1, -1), ((0, SLOT_ROWS - len(vectors) - 1), (0, LANES - hidden_shard))),
        ]
    ).astype(F32)
    output, grad_tokens, small, sum_qkv, sum_proj, sum_fc1, sum_fc2, table_all = run_layer(
        row_span, scalars, tokens, cotangent, packed, w_qkv, w_proj, w_fc1, w_fc2, table_lines
    )
    sums = [small[number, :shard] for number in range(len(vectors))]
    table_total = (
        table_all.reshape(entries // LANES, 2, 8, LANES).transpose(1, 2, 0, 3).reshape(HEAD_ROWS, -1)
    )[:HEADS, :table_rows].T
    return (
        output, grad_tokens, sums[GAIN_ONE], sums[SHIFT_ONE], sum_qkv, sums[QUERY_BIAS], sums[VALUE_BIAS],
        sum_proj, sums[PROJ_SHIFT], sums[SCALE_ONE], sums[GAIN_TWO], sums[SHIFT_TWO], sum_fc1,
        small[LINES, :hidden_shard], sum_fc2, sums[FC2_SHIFT], sums[SCALE_TWO], table_total,
    )


def per_device(*arrays):
    tokens, bias_table = arrays[0], arrays[19]
    linked = lax.axis_size("img") == 4 * Z_SIZE and lax.axis_size("seq") == 2
    linked = linked and arrays[6].shape[0] % 8 == 0 and tokens.shape[0] == LANES
    linked = linked and 15 * LANES < bias_table.shape[0] <= 4 * Z_SIZE * LANES
    return per_device_linked(*arrays) if linked else per_device_native(*arrays)


def solution(mesh):
    return jax.shard_map(
        per_device,
        mesh=mesh,
        in_specs=(
            P(("img", "seq"), None),
            P(("img", "seq"), None),
            P("img"),
            P("img"),
            P(("img", "seq")),
            P(("img", "seq")),
            P(("img", "seq"), None),
            P(("img", "seq")),
            P(("img", "seq")),
            P(("img", "seq"), None),
            P(("img", "seq")),
            P(("img", "seq")),
            P(("img", "seq")),
            P(("img", "seq")),
            P(("img", "seq"), None),
            P(("img", "seq")),
            P(("img", "seq"), None),
            P(("img", "seq")),
            P(("img", "seq")),
            P(),
        ),
        out_specs=(
            P(("img", "seq"), None),
            P(("img", "seq"), None),
            P(("img", "seq")),
            P(("img", "seq")),
            P(("img", "seq"), None),
            P(("img", "seq")),
            P(("img", "seq")),
            P(("img", "seq"), None),
            P(("img", "seq")),
            P(("img", "seq")),
            P(("img", "seq")),
            P(("img", "seq")),
            P(("img", "seq"), None),
            P(("img", "seq")),
            P(("img", "seq"), None),
            P(("img", "seq")),
            P(("img", "seq")),
            P(),
        ),
        check_vma=False,
    )
```

```python
from functools import partial

import jax
import jax.numpy as jnp
from jax import lax
from jax.experimental import pallas as pl
from jax.experimental.pallas import tpu as pltpu
from jax.sharding import PartitionSpec as P

HEADS = 12
HEAD_DIM = 64
SIDE = 32
PAIR = 2 * HEAD_DIM
PAIRS = HEADS // 2
HEAD_ROWS = 16
LANES = 128
F32 = jnp.float32
BF16 = jnp.bfloat16
NT = (((1,), (1,)), ((), ()))
TN = (((0,), (0,)), ((), ()))


VMEM_LIMIT = 63 << 20
ROW_GROUP = 8
EPSILON = 1e-06
NEG_FILL = -1e30


def dot(left, right, dims=(((1,), (0,)), ((), ()))):
    return lax.dot_general(left, right, dims, preferred_element_type=F32)


def iota(shape, dim):
    return lax.broadcasted_iota(jnp.int32, shape, dim)


def floor_div(values, width):
    return jnp.floor((values.astype(F32) + 0.5) / width.astype(F32)).astype(jnp.int32)


def table_index(place, span, rows, row_span, width, offset):
    right = place >= span
    diagonal = offset + rows - 1 - jnp.where(right, place - span, place)
    row = floor_div(diagonal, width)
    col = diagonal - row * width
    row = jnp.where(right, row + 1, row)
    col = jnp.where(right, col - width, col)
    return (row + row_span - 1) * (2 * SIDE - 1) + col + SIDE - 1


def same_side(rows, keys, width, offset):
    query = iota((rows, keys), 0) + offset
    key = iota((rows, keys), 1)
    return (query - floor_div(query, width) * width) >= (key - floor_div(key, width) * width)


def fill_diagonals(table_ref, diag_ref, rows, keys, row_span, width, offset):
    span = rows + keys
    entries = table_ref.shape[1]
    step = 2 * LANES
    index = table_index(iota((step, 2 * span), 1), span, rows, row_span, width, offset)
    entry = iota((step, 2 * span), 0)
    diag_ref[...] = jnp.zeros_like(diag_ref)

    def add(chunk, carry):
        start = pl.multiple_of(chunk * step, step)
        chosen = jnp.where(entry + start == index, 1.0, 0.0).astype(BF16)
        diag_ref[...] += dot(table_ref[:, pl.ds(start, step)], chosen)
        return carry

    lax.fori_loop(0, entries // step, add, 0)


def half_mask(shape, half):
    lane = iota(shape, 1)
    return lane < HEAD_DIM if half == 0 else lane >= HEAD_DIM


def pick(values, half):
    return jnp.where(half_mask(values.shape, half), values, jnp.zeros_like(values))


def attend(query_ref, kv_ref, diag_ref, probs_ref, mixed_ref, width, count, offset, pairs=(0, PAIRS)):
    rows, model = query_ref.shape
    keys = kv_ref.shape[0]
    span = rows + keys
    same = same_side(rows, keys, width, offset)
    valid = iota((rows, keys), 1) < count

    def one_pair(pair, carry):
        cols = pl.ds(pl.multiple_of(pair * PAIR, PAIR), PAIR)
        value_cols = pl.ds(pl.multiple_of(model + pair * PAIR, PAIR), PAIR)
        query_pair = query_ref[:, cols]
        key_pair = kv_ref[:, cols]
        value_pair = kv_ref[:, value_cols]
        mixed = jnp.zeros((rows, PAIR), F32)
        for half in range(2):
            head = pair * 2 + half
            product = dot(pick(query_pair, half), key_pair, NT)
            shifted = []
            for side in range(2):
                line = diag_ref[pl.ds(head, 1), side * span : (side + 1) * span]
                line = jnp.broadcast_to(line, (rows, span))
                line = pltpu.roll(line, keys + 1, 1, stride=1, stride_axis=0)
                shifted.append(line[:, :keys])
            scores = product * HEAD_DIM**-0.5 + jnp.where(same, shifted[0], shifted[1])
            scores = jnp.where(valid, scores, NEG_FILL)
            terms = jnp.exp(scores - jnp.max(scores, axis=1, keepdims=True))
            terms = jnp.where(valid, terms, 0.0)
            probs = terms / jnp.sum(terms, axis=1, keepdims=True)
            probs_ref[head] = probs
            mixed = mixed + dot(probs.astype(BF16), pick(value_pair, half))
        mixed_ref[:, cols] = mixed.astype(BF16)
        return carry

    lax.fori_loop(*pairs, one_pair, 0)


def fold_rows(values):
    while values.shape[0] > 8:
        half = values.shape[0] // 2
        values = values[half:] + pltpu.roll(values[:half], half, 1)
    return values


def attend_back(
    query_ref, kv_ref, probs_ref, grad_ref, grad_query_ref, grad_kv_ref, fold_ref, width, offset, pairs=(0, PAIRS)
):
    rows, model = query_ref.shape
    keys = kv_ref.shape[0]
    same = same_side(rows, keys, width, offset)

    def one_pair(pair, carry):
        cols = pl.ds(pl.multiple_of(pair * PAIR, PAIR), PAIR)
        value_cols = pl.ds(pl.multiple_of(model + pair * PAIR, PAIR), PAIR)
        query_pair = query_ref[:, cols]
        key_pair = kv_ref[:, cols]
        value_pair = kv_ref[:, value_cols]
        grad_pair = grad_ref[:, cols]
        grad_query = jnp.zeros((rows, PAIR), F32)
        grad_key = jnp.zeros((keys, PAIR), F32)
        grad_value = jnp.zeros((keys, PAIR), F32)
        for half in range(2):
            head = pair * 2 + half
            probs = probs_ref[head]
            grad_half = pick(grad_pair, half)
            grad_probs = dot(grad_half, value_pair, NT)
            grad_scores = probs * (
                grad_probs - jnp.sum(probs * grad_probs, axis=1, keepdims=True)
            )
            blank = jnp.zeros((rows, rows), F32)
            left = jnp.where(same, grad_scores, 0.0)
            right = jnp.where(same, 0.0, grad_scores)
            for side, part in enumerate((left, right)):
                place = pl.multiple_of((side * HEAD_ROWS + head) * 8, 8)
                folded = fold_rows(jnp.concatenate([part, blank], axis=1))
                for block in range((rows + keys) // LANES):
                    fold_ref[block, pl.ds(place, 8), :] = folded[:, block * LANES : (block + 1) * LANES]
            grad_prod = (grad_scores * HEAD_DIM**-0.5).astype(BF16)
            grad_query = grad_query + dot(grad_prod, pick(key_pair, half))
            grad_key = grad_key + dot(grad_prod, pick(query_pair, half), TN)
            grad_value = grad_value + dot(probs.astype(BF16), grad_half, TN)
        grad_query_ref[:, cols] = grad_query.astype(BF16)
        grad_kv_ref[:, cols] = grad_key.astype(BF16)
        grad_kv_ref[:, value_cols] = grad_value.astype(BF16)
        return carry

    lax.fori_loop(*pairs, one_pair, 0)


def table_gradient(fold_ref, out_ref, rows, keys, row_span, width, offset):
    span = rows + keys
    lines = 2 * HEAD_ROWS
    total = jnp.zeros((lines, span), F32)
    for row in range(8):
        blocks = [fold_ref[block, pl.ds(row, lines, stride=8), :] for block in range(span // LANES)]
        moved = jnp.concatenate(blocks, axis=1)
        total = total + (pltpu.roll(moved, 7 - row, 1) if row < 7 else moved)
    parts = []
    for side in range(2):
        rest = total[side * HEAD_ROWS : (side + 1) * HEAD_ROWS]
        pieces = []
        for _ in range(3):
            piece = rest.astype(BF16)
            rest = rest - piece.astype(F32)
            pieces.append(piece)
        parts.append(jnp.concatenate(pieces, axis=0))
    place = iota((span, LANES), 0)
    index = [
        table_index(place + side * span, span, rows, row_span, width, offset) for side in range(2)
    ]
    entry = iota((span, LANES), 1)

    def put(chunk, carry):
        start = pl.multiple_of(chunk * LANES, LANES)
        sums = jnp.zeros((3 * HEAD_ROWS, LANES), F32)
        for side in range(2):
            chosen = jnp.where(entry + start == index[side], 1.0, 0.0).astype(BF16)
            sums = sums + dot(parts[side], chosen)
        out_ref[:, pl.ds(start, LANES)] = (
            sums[:HEAD_ROWS] + sums[HEAD_ROWS : 2 * HEAD_ROWS] + sums[2 * HEAD_ROWS :]
        )
        return carry

    lax.fori_loop(0, out_ref.shape[1] // LANES, put, 0)


def attend_kernel(row_span, scal_ref, query_ref, kv_ref, table_ref, mixed_ref, probs_ref, diag_ref):
    rows, keys = query_ref.shape[0], kv_ref.shape[0]
    width, count, offset = scal_ref[0], scal_ref[1], scal_ref[2]
    fill_diagonals(table_ref, diag_ref, rows, keys, row_span, width, offset)
    attend(query_ref, kv_ref, diag_ref, probs_ref, mixed_ref, width, count, offset)


def attend_back_kernel(
    row_span, scal_ref, query_ref, kv_ref, probs_ref, grad_ref, grad_query_ref, grad_kv_ref, table_ref, fold_ref
):
    rows, keys = query_ref.shape[0], kv_ref.shape[0]
    width, offset = scal_ref[0], scal_ref[2]
    fold_ref[...] = jnp.zeros_like(fold_ref)
    attend_back(
        query_ref, kv_ref, probs_ref, grad_ref, grad_query_ref, grad_kv_ref, fold_ref, width, offset
    )
    table_gradient(fold_ref, table_ref, rows, keys, row_span, width, offset)


MESH = pl.DeviceIdType.MESH
Z_SIZE = 4


class Place:
    def __init__(self):
        img = lax.axis_index("img")
        self.x = lax.axis_index("seq")
        self.c = lax.rem(img, 2)
        self.y = lax.rem(img // 2, 2)
        self.z = img // 4

    def at(self, z=None, y=None, c=None, x=None):
        z = self.z if z is None else z
        y = self.y if y is None else y
        c = self.c if c is None else c
        x = self.x if x is None else x
        return {"img": (z * 2 + y) * 2 + c, "seq": x}

    def sibling(self):
        return self.at(c=1 - self.c)

    def over_x(self):
        return self.at(x=1 - self.x)

    def over_y(self):
        return self.at(y=1 - self.y)

    def z_of(self, step):
        return lax.rem(self.z + step, Z_SIZE)

    def partners(self):
        return [self.sibling(), self.over_x(), self.over_y()] + [
            self.at(z=self.z_of(step)) for step in range(1, Z_SIZE)
        ]


def meet(place):
    barrier = pltpu.get_barrier_semaphore()
    partners = place.partners()
    for partner in partners:
        pl.semaphore_signal(barrier, inc=1, device_id=partner, device_id_type=MESH)
    pl.semaphore_wait(barrier, len(partners))


class Sems:
    def __init__(self, send, recv):
        self.send, self.recv, self.used = send, recv, 0

    def copy(self, src, dst, device):
        index = self.used
        self.used += 1
        return pltpu.make_async_remote_copy(
            src_ref=src,
            dst_ref=dst,
            send_sem=self.send.at[index],
            recv_sem=self.recv.at[index],
            device_id=device,
            device_id_type=MESH,
        )


GATHER_COPIES = 16


class Gather:
    def __init__(self, place, src, slots, cols, x_last, sems, local_sem):
        z, y, c, x = place.z, place.y, place.c, place.x
        groups = src.shape[0]
        every = slice(None)

        def part(a, b, e):
            return slots.at[a, b, c, pl.ds(e * groups, groups), :, cols]

        mine = src.at[:, :, cols]
        own = part(z, y, x)
        self.local = pltpu.make_async_copy(mine, own, local_sem)
        steps = range(1, Z_SIZE)
        self.along_z = [sems.copy(mine, own, place.at(z=place.z_of(step))) for step in steps]
        line = part(every, y, x)
        mid_line = part(every, 1 - y, x) if x_last else part(every, y, 1 - x)
        far_line = part(every, y, 1 - x) if x_last else part(every, 1 - y, x)
        cross_line = part(every, 1 - y, 1 - x)
        mid, last = place.over_y(), place.over_x()
        if not x_last:
            mid, last = last, mid
        sibling = place.sibling()
        self.own_mid = sems.copy(mine, own, mid)
        self.own_last = sems.copy(mine, own, last)
        came = [part(place.z_of(Z_SIZE - step), y, x) for step in steps]
        self.line_mid = [sems.copy(piece, piece, mid) for piece in came]
        self.line_last = [sems.copy(piece, piece, last) for piece in came]
        self.line_core = sems.copy(line, line, sibling)
        self.mid_last = sems.copy(mid_line, mid_line, last)
        self.mid_core = sems.copy(mid_line, mid_line, sibling)
        self.far_core = sems.copy(far_line, far_line, sibling)
        self.cross_core = sems.copy(cross_line, cross_line, sibling)

    def begin_own(self):
        self.local.start()
        self.own_mid.start()
        self.own_last.start()

    def begin_z(self):
        for copy in self.along_z:
            copy.start()

    def second(self):
        for copy, onward, beyond in zip(self.along_z, self.line_mid, self.line_last):
            copy.wait_recv()
            onward.start()
            beyond.start()
        self.local.wait()
        self.line_core.start()

    def third(self):
        for copy in [self.own_mid] + self.line_mid:
            copy.wait_recv()
        self.mid_last.start()
        self.mid_core.start()

    def fourth(self):
        for copy in [self.own_last] + self.line_last:
            copy.wait_recv()
        self.far_core.start()
        self.mid_last.wait_recv()
        self.cross_core.start()

    def arrive(self):
        for copy in (self.line_core, self.mid_core, self.far_core, self.cross_core):
            copy.wait_recv()

    def settle(self):
        for copy in (
            self.along_z
            + [self.own_mid, self.own_last]
            + self.line_mid
            + self.line_last
            + [self.line_core, self.mid_last, self.mid_core, self.far_core, self.cross_core]
        ):
            copy.wait_send()


def halves(width):
    middle = width // 2 // LANES * LANES
    return [(0, middle), (middle, width - middle)]


REDUCE_COPIES = 6


class Reduce:
    def __init__(self, place, grad, own, first, second, third, out, start, size, x_first, sems, pieces=None):
        rows = out.shape[0]

        def flat(ref):
            return ref.reshape(ref.shape[:-3] + (rows, ref.shape[-1]))

        self.place, self.out = place, out
        self.grad, self.own, self.first = flat(grad), flat(own), flat(first)
        self.second, self.third = flat(second), flat(third)
        self.pieces = pieces or [(0, start, size)]
        self.x_first = x_first
        z, y, c, x = place.z, place.y, place.c, place.x
        every = slice(None)
        cols = pl.ds(start, size)
        self.cols = cols
        self.to_core = sems.copy(
            grad.at[:, :, 1 - c, :, :, :, cols], own.at[:, :, :, :, :, cols], place.sibling()
        )
        over_first, over_second = place.over_x(), place.over_y()
        if x_first:
            leaving, other = own.at[:, :, 1 - x, :, :, cols], 1 - y
        else:
            over_first, over_second = over_second, over_first
            leaving, other = own.at[:, 1 - y, :, :, :, cols], 1 - x
        self.kept = y if x_first else x
        self.over_first = sems.copy(leaving, first, over_first)
        self.over_second = sems.copy(first.at[:, other], second, over_second)
        self.along_z = []
        for step in range(1, Z_SIZE):
            target = place.z_of(step)
            self.along_z.append(
                sems.copy(second.at[target], third.at[step - 1], place.at(z=target))
            )

    def begin(self):
        self.to_core.start()

    def add_core(self):
        self.to_core.wait_recv()
        place = self.place

        def add(zy, carry):
            z, y = zy // 2, lax.rem(zy, 2)
            for x in range(2):
                mine = self.grad[z, y, place.c, x, :, self.cols].astype(F32)
                theirs = self.own[z, y, x, :, self.cols].astype(F32)
                self.own[z, y, x, :, self.cols] = (mine + theirs).astype(self.own.dtype)
            return carry

        lax.fori_loop(0, 2 * Z_SIZE, add, 0)
        self.over_first.start()

    def add_first(self):
        self.over_first.wait_recv()
        place = self.place

        def add(z, carry):
            for other in range(2):
                if self.x_first:
                    mine = self.own[z, other, place.x, :, self.cols].astype(F32)
                else:
                    mine = self.own[z, place.y, other, :, self.cols].astype(F32)
                theirs = self.first[z, other].astype(F32)
                self.first[z, other] = (mine + theirs).astype(self.first.dtype)
            return carry

        lax.fori_loop(0, Z_SIZE, add, 0)
        self.over_second.start()

    def add_second(self):
        self.over_second.wait_recv()

        def add(z, carry):
            mine = self.first[z, self.kept].astype(F32)
            theirs = self.second[z].astype(F32)
            self.second[z] = (mine + theirs).astype(self.second.dtype)
            return carry

        lax.fori_loop(0, Z_SIZE, add, 0)
        for copy in self.along_z:
            copy.start()

    def finish(self):
        total = self.second[self.place.z].astype(F32)
        for step, copy in enumerate(self.along_z):
            copy.wait_recv()
            total = total + self.third[step].astype(F32)
        for source, target, size in self.pieces:
            self.out[:, target : target + size] = total[:, source : source + size]

    def settle(self):
        for copy in [self.to_core, self.over_first, self.over_second] + self.along_z:
            copy.wait_send()


class Names:
    pass


def norm_rows(values):
    centred = values - jnp.mean(values, axis=1, keepdims=True)
    inv_std = lax.rsqrt(jnp.mean(centred * centred, axis=1, keepdims=True) + EPSILON)
    return centred * inv_std, inv_std


def norm_rows_back(grad_out, normed, inv_std, gain):
    scaled = grad_out * gain
    return inv_std * (
        scaled
        - jnp.mean(scaled, axis=1, keepdims=True)
        - normed * jnp.mean(scaled * normed, axis=1, keepdims=True)
    )


def sum_rows(values):
    return jnp.sum(values.astype(F32), axis=0, keepdims=True)


def div_const(values, divisor):
    return jnp.floor((values.astype(F32) + 0.5) * (1.0 / divisor)).astype(jnp.int32)


def tile(slots, start, size):
    rows = slots.shape[3] * ROW_GROUP
    view = slots.reshape(4 * Z_SIZE, rows, slots.shape[-1])
    return view[:, :, pl.ds(start, size)].reshape(-1, size)


def put_slots(slots, cols, values):
    devices = 8 * Z_SIZE
    view = slots.reshape(devices, slots.shape[4] * ROW_GROUP, slots.shape[-1])
    view[:, :, cols] = values.reshape(devices, -1, values.shape[1]).astype(slots.dtype)


def tiles(count, step):
    def wrap(body):
        def run(number, carry):
            body(number, pl.multiple_of(number * step, step))
            return carry

        lax.fori_loop(0, count, run, 0)

    return wrap


LINES = 16
SLOT_ROWS = 24
QKV_COLS = 256


def qkv_cuts(model):
    size = 3 * QKV_COLS // 2
    return [(start, size) for start in range(0, 3 * model, size)]


(
    GAIN_ONE, SHIFT_ONE, QUERY_BIAS, VALUE_BIAS, PROJ_SHIFT, SCALE_ONE, GAIN_TWO, SHIFT_TWO, FC2_SHIFT, SCALE_TWO,
) = range(10)
HIDDEN_LINE = 10
LINE_NAMES = ["line" + str(number) for number in range(HIDDEN_LINE + 1)]


def unpack_lines(packed, shard, hidden_shard, vec_ref, hidden_ref):
    rows = packed.shape[0]
    devices = rows // SLOT_ROWS
    low = packed.astype(BF16)
    width = shard * devices
    lane = iota((LANES, width), 1)
    spread = jnp.where(lane - div_const(lane, shard) * shard == iota((LANES, width), 0), 1.0, 0.0)
    wide = dot(low, spread.astype(BF16))
    owner = div_const(iota((rows, width), 0), SLOT_ROWS)
    wide = jnp.where(owner == div_const(iota((rows, width), 1), shard), wide, 0.0).astype(BF16)
    row = iota((LINES, rows), 1)
    line = row - div_const(row, SLOT_ROWS) * SLOT_ROWS
    vec_ref[...] = dot(jnp.where(line == iota((LINES, rows), 0), 1.0, 0.0).astype(BF16), wide)
    row = iota((devices, rows), 1)
    chosen = jnp.where(row == iota((devices, rows), 0) * SLOT_ROWS + HIDDEN_LINE, 1.0, 0.0)
    hidden = dot(chosen.astype(BF16), low).astype(BF16)
    step = 8 * LANES
    for start in range(0, hidden_shard * devices, step):
        lane = iota((LANES, step), 1) + start
        owner = div_const(lane, hidden_shard)
        spread = jnp.where(lane - owner * hidden_shard == iota((LANES, step), 0), 1.0, 0.0)
        wide = dot(hidden, spread.astype(BF16))
        owner = div_const(iota((devices, step), 1) + start, hidden_shard)
        wide = jnp.where(owner == iota((devices, step), 0), wide, 0.0)
        hidden_ref[:, start : start + step] = jnp.broadcast_to(sum_rows(wide), (8, step))


def layer_kernel(names, row_span, *refs):
    s = Names()
    s.__dict__.update(zip(names, refs))
    buffers = list(refs[len(names) :])
    send, recv, local = buffers[-3:]
    place = Place()
    x = place.x
    rows, model = s.tokens.shape
    width, count, offset = s.widths[0], s.counts[0], x * rows
    keys = 2 * rows
    hidden = s.w_fc1.shape[2]
    shard, hidden_shard = s.w_qkv.shape[0] * ROW_GROUP, s.w_fc2.shape[0] * ROW_GROUP
    half = model // 2
    own_rows = pl.ds(pl.multiple_of(x * rows, rows), rows)
    far_rows = pl.ds(pl.multiple_of((1 - x) * rows, rows), rows)
    sems = Sems(send, recv)
    locals_used = []
    outgoing = []

    def move(src, dst):
        locals_used.append(0)
        copy = pltpu.make_async_copy(src, dst, local.at[len(locals_used) - 1])
        copy.start()
        return copy

    def gather(src, slots, cuts):
        chunks = []
        for number, (start, size) in enumerate(cuts):
            locals_used.append(0)
            sem = local.at[len(locals_used) - 1]
            chunks.append(Gather(place, src, slots, pl.ds(start, size), number == 0, sems, sem))
        return chunks

    def reduce(out, cuts, pieces):
        chunks = []
        grad, own = buffers.pop(0), buffers.pop(0)
        for number, (start, size) in enumerate(cuts):
            stages = [buffers.pop(0) for _ in range(3)]
            chunks.append(
                Reduce(
                    place, grad, own, *stages, out, start, size, number % 2 == 0, sems, pieces and pieces[number],
                )
            )
        return grad, chunks

    def each(chunks, *steps):
        for step in steps:
            for chunk in chunks:
                step(chunk)

    line_copies = [
        move(getattr(s, LINE_NAMES[number]), s.raw_hidden if number == HIDDEN_LINE else s.raw.at[number])
        for number in range(HIDDEN_LINE + 1)
    ]
    table_copy = move(s.table, s.table_in)
    tokens_copy = move(s.tokens, s.tokens_in)
    cot_copy = move(s.cot, s.cot_in)
    swap = sems.copy(s.tokens, s.far_tokens, place.over_x())
    give = sems.copy(s.give, s.take, place.over_x())
    get_pack = gather(s.pack, s.packs, [(0, LANES)])
    get_qkv = gather(s.w_qkv, s.wq, halves(3 * model))
    get_proj = gather(s.w_proj, s.wp, halves(model))
    get_fc1 = gather(s.w_fc1, s.w1, halves(hidden))
    get_fc2 = gather(s.w_fc2, s.w2, halves(model))
    s.g_fc2, put_fc2 = reduce(s.o_fc2, halves(model), None)
    s.g_fc1, put_fc1 = reduce(s.o_fc1, halves(hidden), None)
    s.g_proj, put_proj = reduce(s.o_proj, halves(model), None)
    wide = QKV_COLS
    qkv_pieces = []
    for group in range(model // wide):
        start = group * wide
        qkv_pieces.append([(0, start, wide), (wide, model + start, wide // 2)])
        qkv_pieces.append(
            [(0, model + start + wide // 2, wide // 2), (wide // 2, 2 * model + start, wide)]
        )
    s.g_qkv, put_qkv = reduce(s.o_qkv, qkv_cuts(model), qkv_pieces)
    s.g_table, put_table = reduce(s.o_table, [(0, LANES)], None)
    s.g_small, put_small = reduce(s.o_small, [(0, LANES)], None)
    get_table = gather(s.o_table.reshape(1, 8, LANES), s.table_all, [(0, LANES)])

    meet(place)
    for copy in line_copies:
        copy.wait()
    s.pack[...] = jnp.zeros_like(s.pack)
    for number in range(HIDDEN_LINE + 1):
        source = s.raw_hidden if number == HIDDEN_LINE else s.raw.at[number]
        s.pack[number // 8, number % 8 : number % 8 + 1, 0 : source.shape[1]] = source[...].astype(F32)
    each(get_pack, Gather.begin_own, Gather.begin_z)
    each(get_qkv, Gather.begin_z, Gather.begin_own)
    swap.start()
    each(get_proj, Gather.begin_own)
    table_copy.wait()
    s.table_lines[...] = jnp.zeros_like(s.table_lines)
    s.table_lines[0:HEADS, 0 : s.table.shape[1]] = s.table_in[...]
    fill_diagonals(s.table_lines, s.diag, rows, keys, row_span, width, offset)
    each(get_pack, Gather.second)
    tokens_copy.wait()
    normed, inv_std = norm_rows(s.tokens_in[...].astype(F32))
    s.n1[...] = normed
    s.r1[...] = jnp.broadcast_to(inv_std, s.r1.shape)
    each(get_pack, Gather.third)
    each(get_fc1, Gather.begin_own)
    s.fold[...] = jnp.zeros_like(s.fold)
    s.lines[...] = jnp.zeros_like(s.lines)
    each(get_pack, Gather.fourth)
    each(get_fc2, Gather.begin_own)
    each(get_qkv, Gather.second)
    each(get_proj, Gather.begin_z)
    each(get_fc1, Gather.begin_z)
    each(get_pack, Gather.arrive)
    unpack_lines(tile(s.packs, 0, LANES), shard, hidden_shard, s.vec, s.b1)

    def line(number):
        return s.vec[number : number + 1, :]

    def set_line(number, values):
        s.lines[number : number + 1, :] = values

    s.h1[own_rows, :] = (s.n1[...] * line(GAIN_ONE) + line(SHIFT_ONE)).astype(BF16)
    swap.wait_recv()
    far = norm_rows(s.far_tokens[...].astype(F32))[0]
    s.h1[far_rows, :] = (far * line(GAIN_ONE) + line(SHIFT_ONE)).astype(BF16)
    each(get_proj, Gather.second)
    s.h1t[...] = s.h1[...].T
    cot_copy.wait()
    s.dm[...] = (line(SCALE_TWO) * s.cot_in[...].astype(F32)).astype(BF16)
    set_line(FC2_SHIFT, sum_rows(s.dm[...]))
    each(get_qkv, Gather.third)
    each(get_proj, Gather.third)
    each(get_qkv, Gather.fourth)
    each(get_fc1, Gather.second)
    each(get_fc2, Gather.begin_z)
    each(get_qkv, Gather.arrive)

    step = 2 * LANES

    @tiles(model // step, step)
    def _(number, start):
        s.kv[:, pl.ds(start, step)] = dot(s.h1[...], tile(s.wq, model + start, step)).astype(BF16)
        sums = dot(s.h1[...], tile(s.wq, 2 * model + start, step))
        sums = sums + s.vec[VALUE_BIAS : VALUE_BIAS + 1, pl.ds(start, step)]
        s.kv[:, pl.ds(model + start, step)] = sums.astype(BF16)

    @tiles(model // step, step)
    def _(number, start):
        cols = pl.ds(start, step)
        sums = dot(s.h1[own_rows, :], tile(s.wq, start, step))
        s.q[:, cols] = (sums + s.vec[QUERY_BIAS : QUERY_BIAS + 1, cols]).astype(BF16)

    def look(first, last):
        attend(s.q, s.kv, s.diag, s.probs, s.mixed, width, count, offset, (first, last))

    each(get_proj, Gather.fourth)
    look(0, 2)
    look(2, 4)
    each(get_fc1, Gather.third)
    look(4, PAIRS)
    s.mixedt[...] = s.mixed[...].T
    each(get_fc2, Gather.second)
    each(get_proj, Gather.arrive)

    @tiles(model // step, step)
    def _(number, start):
        cols = pl.ds(start, step)
        branch = dot(s.mixed[...], tile(s.wp, start, step)) + s.vec[PROJ_SHIFT : PROJ_SHIFT + 1, cols]
        s.z[:, cols] = branch
        s.x1[:, cols] = s.tokens_in[:, cols].astype(F32) + s.vec[SCALE_ONE : SCALE_ONE + 1, cols] * branch

    normed, inv_std = norm_rows(s.x1[...])
    s.n2[...] = normed
    s.r2[...] = jnp.broadcast_to(inv_std, s.r2.shape)
    s.h2[...] = (normed * line(GAIN_TWO) + line(SHIFT_TWO)).astype(BF16)
    s.h2t[...] = s.h2[...].T
    each(get_fc1, Gather.fourth, Gather.arrive)

    @tiles(hidden // step, step)
    def _(number, start):
        cols = pl.ds(start, step)
        act = dot(s.h2[...], tile(s.w1, start, step)) + s.b1[0:1, cols]
        gate = 0.5 * (1.0 + lax.erf(act * 0.5**0.5))
        low = (act * gate).astype(BF16)
        s.u[:, cols] = low
        s.ut[cols, :] = low.T
        s.slope[:, cols] = gate + act * jnp.exp(act * act * -0.5) * 0.3989422804014327

    each(get_fc2, Gather.third)
    deep = 8 * hidden_shard
    for group in range(2):

        @tiles(Z_SIZE, deep)
        def _(number, start):
            cols = pl.ds(group * half, half)
            sums = dot(s.ut[pl.ds(start, deep), :], s.dm[:, cols])
            view = s.g_fc2.reshape(Z_SIZE, 8, hidden_shard, model)
            view[number, :, :, cols] = sums.reshape(8, hidden_shard, half).astype(BF16)

        put_fc2[group].begin()
    each(get_fc2, Gather.fourth)
    each(put_fc2, Reduce.add_core)
    each(get_fc2, Gather.arrive)

    @tiles(Z_SIZE, deep)
    def _(number, start):
        cols = pl.ds(start, deep)
        weight = s.w2.reshape(Z_SIZE, deep, model)[number]
        grad_hidden = dot(s.dm[...], weight, NT)
        s.da[:, cols] = (grad_hidden * s.slope[:, cols]).astype(BF16)

    for group in range(2):

        @tiles(hidden // 2 // step, step)
        def _(number, start):
            cols = pl.ds(start + group * (hidden // 2), step)
            sums = dot(s.h2t[...], s.da[:, cols])
            put_slots(s.g_fc1, cols, sums)

        put_fc1[group].begin()

    grad = jnp.zeros((rows, model), F32)
    for start in range(0, hidden, model):
        grad = grad + dot(s.da[:, start : start + model], tile(s.w1, start, model), NT)
    set_line(GAIN_TWO, sum_rows(grad * s.n2[...]))
    set_line(SHIFT_TWO, sum_rows(grad))
    dx1 = s.cot_in[...].astype(F32) + norm_rows_back(grad, s.n2[...], s.r2[:, 0:1], line(GAIN_TWO))
    s.dx1[...] = dx1
    set_line(SCALE_ONE, sum_rows(dx1 * s.z[...]))
    s.dz[...] = (line(SCALE_ONE) * dx1).astype(BF16)
    set_line(PROJ_SHIFT, sum_rows(s.dz[...]))
    each(put_fc1, Reduce.add_core)
    for group in range(2):
        cols = pl.ds(group * half, half)
        put_slots(s.g_proj, cols, dot(s.mixedt[...], s.dz[:, cols]))
        put_proj[group].begin()
    s.dmixed[...] = dot(s.dz[...], tile(s.wp, 0, model), NT).astype(BF16)
    each(put_fc2, Reduce.add_first)

    def look_back(group):
        pairs = (group * wide // PAIR, (group + 1) * wide // PAIR)
        attend_back(s.q, s.kv, s.probs, s.dmixed, s.dq, s.dkv, s.fold, width, offset, pairs)
        cols = pl.ds(group * wide, wide)
        value_cols = pl.ds(model + group * wide, wide)
        own_lines = s.h1t[:, own_rows]
        all_lines = s.h1t[...]
        for part, sums in enumerate(
            (
                dot(own_lines, s.dq[:, cols]),
                dot(all_lines, s.dkv[:, cols]),
                dot(all_lines, s.dkv[:, value_cols]),
            )
        ):
            put_slots(s.g_qkv, pl.ds((3 * group + part) * wide, wide), sums)
        each(put_qkv[2 * group : 2 * group + 2], Reduce.begin)

    look_back(0)
    each(put_proj, Reduce.add_core)
    look_back(1)
    each(put_qkv[:2], Reduce.add_core)
    each(put_fc1, Reduce.add_first)
    each(put_fc2, Reduce.add_second)
    look_back(2)
    grad_key = dot(s.dkv[:, :model], tile(s.wq, model, model), NT)
    s.dh1[...] = grad_key + dot(s.dkv[:, model:], tile(s.wq, 2 * model, model), NT)
    s.give[...] = s.dh1[far_rows, :].astype(BF16)
    give.start()
    each(put_qkv[2:4], Reduce.add_core)
    each(put_proj, Reduce.add_first)
    table_gradient(s.fold, s.table_sums, rows, keys, row_span, width, offset)

    @tiles(4 * Z_SIZE, LANES)
    def _(number, start):
        zz, yy, cc = number // 4, lax.rem(number // 2, 2), lax.rem(number, 2)
        for xx in range(2):
            s.g_table[zz, yy, cc, xx, 0] = s.table_sums[8 * xx : 8 * xx + 8, pl.ds(start, LANES)]

    each(put_table, Reduce.begin)
    each(put_qkv[4:], Reduce.add_core)
    each(put_qkv[:2], Reduce.add_first)

    @tiles(model // step, step)
    def _(number, start):
        cols = pl.ds(start, step)
        branch = dot(s.u[...], tile(s.w2, start, step)) + s.vec[FC2_SHIFT : FC2_SHIFT + 1, cols]
        s.out_low[:, cols] = (s.x1[:, cols] + s.vec[SCALE_TWO : SCALE_TWO + 1, cols] * branch).astype(BF16)
        s.lines[SCALE_TWO : SCALE_TWO + 1, cols] = sum_rows(s.cot_in[:, cols].astype(F32) * branch)

    outgoing.append(move(s.out_low, s.out))
    s.hidden_lines[...] = jnp.broadcast_to(sum_rows(s.da[...]), s.hidden_lines.shape)
    set_line(QUERY_BIAS, sum_rows(s.dq[...]))
    set_line(VALUE_BIAS, sum_rows(s.dkv[:, model:]))
    each(put_table, Reduce.add_core)
    each(put_fc1, Reduce.add_second)
    each(put_fc2, Reduce.finish)
    outgoing.append(move(s.o_fc2, s.sum_fc2))
    grad = s.dh1[own_rows, :] + dot(s.dq[...], tile(s.wq, 0, model), NT)
    give.wait_recv()
    grad = grad + s.take[...].astype(F32)
    set_line(GAIN_ONE, sum_rows(grad * s.n1[...]))
    set_line(SHIFT_ONE, sum_rows(grad))
    dx = s.dx1[...] + norm_rows_back(grad, s.n1[...], s.r1[:, 0:1], line(GAIN_ONE))
    s.dx_low[...] = dx.astype(BF16)
    outgoing.append(move(s.dx_low, s.grad_tokens))

    @tiles(8 * Z_SIZE, 1)
    def _(number, start):
        zz, yy, cc, xx = number // 8, lax.rem(number // 4, 2), lax.rem(number // 2, 2), lax.rem(number, 2)
        moved = pltpu.roll(s.lines[...], model - number * shard, 1)
        for group in range(LINES // ROW_GROUP):
            s.g_small[zz, yy, cc, xx, group] = moved[group * ROW_GROUP : (group + 1) * ROW_GROUP, :LANES]
        moved = pltpu.roll(s.hidden_lines[...], hidden - number * hidden_shard, 1)
        s.g_small[zz, yy, cc, xx, LINES // ROW_GROUP] = moved[:, :LANES]

    each(put_small, Reduce.begin)
    each(put_table, Reduce.add_first)
    each(put_qkv[2:4], Reduce.add_first)
    each(put_small, Reduce.add_core)
    each(put_proj, Reduce.add_second)
    each(put_table, Reduce.add_second)
    each(put_qkv[:2], Reduce.add_second)
    each(put_small, Reduce.add_first)
    each(put_fc1, Reduce.finish)
    outgoing.append(move(s.o_fc1, s.sum_fc1))
    each(put_table, Reduce.finish)
    each(get_table, Gather.begin_own, Gather.begin_z)
    each(put_qkv[4:], Reduce.add_first)
    each(put_proj, Reduce.finish)
    outgoing.append(move(s.o_proj, s.sum_proj))
    each(put_small, Reduce.add_second)
    each(get_table, Gather.second)
    each(put_qkv[2:4], Reduce.add_second)
    each(get_table, Gather.third)
    each(put_qkv[:2], Reduce.finish)
    each(put_qkv[4:], Reduce.add_second)
    each(put_small, Reduce.finish)
    outgoing.append(move(s.o_small, s.sum_small))
    each(get_table, Gather.fourth)
    each(put_qkv[2:4], Reduce.finish)
    each(get_table, Gather.arrive)
    for block in range(4 * Z_SIZE):
        slots = s.table_all.at[block // 4, block // 2 % 2, block % 2]
        start = block * LANES
        size = min(LANES, s.o_sums.shape[1] - start)
        s.o_sums[0:8, start : start + size] = slots[0, :, 0:size]
        s.o_sums[8:HEADS, start : start + size] = slots[1, 0 : HEADS - 8, 0:size]
    outgoing.append(move(s.o_sums, s.sum_table))
    each(put_qkv[4:], Reduce.finish)
    outgoing.append(move(s.o_qkv, s.sum_qkv))
    swap.wait_send()
    give.wait_send()
    for chunks in (get_pack, get_qkv, get_proj, get_fc1, get_fc2, get_table):
        each(chunks, Gather.settle)
    for chunks in (put_fc2, put_fc1, put_proj, put_qkv, put_table, put_small):
        each(chunks, Reduce.settle)
    for copy in outgoing:
        copy.wait()


def hand_kernel(count, *refs):
    small, arrays = refs[0], refs[1 : 1 + count]
    outs, lines = refs[1 + count : 1 + 2 * count], refs[1 + 2 * count :]
    for array, out in zip(arrays, outs):
        out[...] = array[...]
    for number, out in enumerate(lines):
        row = number if number < HIDDEN_LINE else LINES
        out[...] = small[row : row + 1, 0 : out.shape[1]]


def hand_out(small, arrays, sizes):
    vmem = pl.BlockSpec(memory_space=pltpu.VMEM)
    count = len(arrays)
    return pl.pallas_call(
        partial(hand_kernel, count),
        out_shape=tuple(jax.ShapeDtypeStruct(array.shape, array.dtype) for array in arrays)
        + tuple(jax.ShapeDtypeStruct((1, size), F32) for size in sizes),
        in_specs=[vmem] * (1 + count),
        out_specs=(vmem,) * (count + len(sizes)),
    )(small, *arrays)


def grouped(array):
    return array.reshape(-1, ROW_GROUP, array.shape[-1])


def run_layer(row_span, widths, counts, tokens, cotangent, vectors, w_qkv, w_proj, w_fc1, w_fc2, table):
    rows, model = tokens.shape
    keys = 2 * rows
    shard, hidden, hidden_shard = w_qkv.shape[0], w_fc1.shape[1], w_fc2.shape[0]
    smem = pl.BlockSpec(memory_space=pltpu.SMEM)
    vmem = pl.BlockSpec(memory_space=pltpu.VMEM)
    anywhere = pl.BlockSpec(memory_space=pl.ANY)
    inputs = dict(
        widths=(widths, smem),
        counts=(counts, smem),
        tokens=(tokens, anywhere),
        cot=(cotangent, anywhere),
        w_qkv=(grouped(w_qkv), anywhere),
        w_proj=(grouped(w_proj), anywhere),
        w_fc1=(grouped(w_fc1), anywhere),
        w_fc2=(grouped(w_fc2), anywhere),
        table=(table, anywhere),
    )
    for name, vector in zip(LINE_NAMES, vectors):
        inputs[name] = (vector.reshape(1, -1), anywhere)
    outputs = dict(
        out=((rows, model), BF16),
        grad_tokens=((rows, model), BF16),
        sum_small=((SLOT_ROWS, LANES), F32),
        sum_qkv=((shard, 3 * model), F32),
        sum_proj=((shard, model), F32),
        sum_fc1=((shard, hidden), F32),
        sum_fc2=((hidden_shard, model), F32),
        sum_table=((HEADS, table.shape[1]), F32),
    )
    entries = -(-table.shape[1] // (2 * LANES)) * 2 * LANES
    scratch = dict(
        raw=((HIDDEN_LINE, 1, shard), BF16),
        raw_hidden=((1, hidden_shard), BF16),
        table_in=(table.shape, BF16),
        tokens_in=((rows, model), BF16),
        cot_in=((rows, model), BF16),
        out_low=((rows, model), BF16),
        dx_low=((rows, model), BF16),
        o_small=((SLOT_ROWS, LANES), F32),
        o_qkv=((shard, 3 * model), F32),
        o_proj=((shard, model), F32),
        o_fc1=((shard, hidden), F32),
        o_fc2=((hidden_shard, model), F32),
        o_sums=((HEADS, table.shape[1]), F32),
        pack=((SLOT_ROWS // ROW_GROUP, ROW_GROUP, LANES), F32),
        table_lines=((HEAD_ROWS, entries), BF16),
        table_all=((Z_SIZE, 2, 2, 2, 8, LANES), F32),
        o_table=((8, LANES), F32),
        far_tokens=((rows, model), BF16),
        give=((rows, model), BF16),
        take=((rows, model), BF16),
        packs=((Z_SIZE, 2, 2, 2 * SLOT_ROWS // ROW_GROUP, ROW_GROUP, LANES), F32),
        wq=((Z_SIZE, 2, 2, 2 * shard // ROW_GROUP, ROW_GROUP, 3 * model), BF16),
        wp=((Z_SIZE, 2, 2, 2 * shard // ROW_GROUP, ROW_GROUP, model), BF16),
        w1=((Z_SIZE, 2, 2, 2 * shard // ROW_GROUP, ROW_GROUP, hidden), BF16),
        w2=((Z_SIZE, 2, 2, 2 * hidden_shard // ROW_GROUP, ROW_GROUP, model), BF16),
        vec=((LINES, model), F32),
        b1=((8, hidden), F32),
        diag=((HEAD_ROWS, 2 * (rows + keys)), F32),
        h1=((keys, model), BF16),
        h1t=((model, keys), BF16),
        n1=((rows, model), F32),
        r1=((rows, LANES), F32),
        q=((rows, model), BF16),
        kv=((keys, 2 * model), BF16),
        probs=((HEADS, rows, keys), F32),
        mixed=((rows, model), BF16),
        mixedt=((model, rows), BF16),
        z=((rows, model), F32),
        x1=((rows, model), F32),
        n2=((rows, model), F32),
        r2=((rows, LANES), F32),
        h2=((rows, model), BF16),
        h2t=((model, rows), BF16),
        u=((rows, hidden), BF16),
        ut=((hidden, rows), BF16),
        slope=((rows, hidden), F32),
        dm=((rows, model), BF16),
        da=((rows, hidden), BF16),
        dx1=((rows, model), F32),
        dz=((rows, model), BF16),
        dmixed=((rows, model), BF16),
        dq=((rows, model), BF16),
        dkv=((keys, 2 * model), BF16),
        dh1=((keys, model), F32),
        fold=(((rows + keys) // LANES, 2 * HEAD_ROWS * 8, LANES), F32),
        table_sums=((HEAD_ROWS, entries), F32),
        lines=((LINES, model), F32),
        hidden_lines=((8, hidden), F32),
    )
    stages = []
    chunks = 0
    for slot_rows, slot_width, dtype, cuts in (
        (hidden_shard, model, BF16, None),
        (shard, hidden, BF16, None),
        (shard, model, BF16, None),
        (shard, 3 * model, BF16, qkv_cuts(model)),
        (8, LANES, F32, None),
        (SLOT_ROWS, LANES, F32, None),
    ):
        cuts = cuts or ([(0, slot_width)] if slot_width <= LANES else halves(slot_width))
        groups = slot_rows // ROW_GROUP
        stages.append(((Z_SIZE, 2, 2, 2, groups, ROW_GROUP, slot_width), dtype))
        stages.append(((Z_SIZE, 2, 2, groups, ROW_GROUP, slot_width), dtype))
        for _, size in cuts:
            for lead in ((Z_SIZE, 2), (Z_SIZE,), (Z_SIZE - 1,)):
                stages.append((lead + (groups, ROW_GROUP, size), dtype))
            chunks += 1
    copies = 2 + GATHER_COPIES * 10 + REDUCE_COPIES * chunks
    names = list(inputs) + list(outputs) + list(scratch)
    return pl.pallas_call(
        partial(layer_kernel, names, row_span),
        out_shape=tuple(jax.ShapeDtypeStruct(shape, dtype) for shape, dtype in outputs.values()),
        in_specs=[spec for _, spec in inputs.values()],
        out_specs=(anywhere,) * len(outputs),
        scratch_shapes=[pltpu.VMEM(shape, dtype) for shape, dtype in list(scratch.values()) + stages]
        + [
            pltpu.SemaphoreType.DMA((copies,)),
            pltpu.SemaphoreType.DMA((copies,)),
            pltpu.SemaphoreType.DMA((40,)),
        ],
        compiler_params=pltpu.CompilerParams(
            collective_id=0, has_side_effects=True, vmem_limit_bytes=VMEM_LIMIT
        ),
    )(*[array for array, _ in inputs.values()])


def layer_norm(values, gain, shift):
    centred = values - jnp.mean(values, axis=-1, keepdims=True)
    inv_std = lax.rsqrt(jnp.mean(centred * centred, axis=-1, keepdims=True) + EPSILON)
    normed = centred * inv_std
    return (normed * gain + shift, normed, inv_std)


def norm_back(grad_out, normed, inv_std, gain):
    scaled = grad_out * gain
    return inv_std * (
        scaled
        - jnp.mean(scaled, axis=-1, keepdims=True)
        - normed * jnp.mean(scaled * normed, axis=-1, keepdims=True)
    )


def row_sum(values):
    return jnp.sum(values.astype(jnp.float32), axis=0)


def per_device_native(
    tokens,
    cotangent,
    counts,
    widths,
    norm1_gain,
    norm1_shift,
    w_qkv,
    q_bias,
    v_bias,
    w_proj,
    proj_bias,
    gamma1,
    norm2_gain,
    norm2_shift,
    w_fc1,
    fc1_bias,
    w_fc2,
    fc2_bias,
    gamma2,
    bias_table,
):
    fetched = (
        lax.all_gather(norm1_gain, ("img", "seq"), axis=0, tiled=True),
        lax.all_gather(norm1_shift, ("img", "seq"), axis=0, tiled=True),
        lax.all_gather(w_qkv, ("img", "seq"), axis=0, tiled=True),
        lax.all_gather(q_bias, ("img", "seq"), axis=0, tiled=True),
        lax.all_gather(v_bias, ("img", "seq"), axis=0, tiled=True),
        lax.all_gather(w_proj, ("img", "seq"), axis=0, tiled=True),
        lax.all_gather(proj_bias, ("img", "seq"), axis=0, tiled=True),
        lax.all_gather(gamma1, ("img", "seq"), axis=0, tiled=True),
        lax.all_gather(norm2_gain, ("img", "seq"), axis=0, tiled=True),
        lax.all_gather(norm2_shift, ("img", "seq"), axis=0, tiled=True),
        lax.all_gather(w_fc1, ("img", "seq"), axis=0, tiled=True),
        lax.all_gather(fc1_bias, ("img", "seq"), axis=0, tiled=True),
        lax.all_gather(w_fc2, ("img", "seq"), axis=0, tiled=True),
        lax.all_gather(fc2_bias, ("img", "seq"), axis=0, tiled=True),
        lax.all_gather(gamma2, ("img", "seq"), axis=0, tiled=True),
    )
    (
        gain_one,
        shift_one,
        qkv_weight,
        query_bias,
        value_bias,
        proj_weight,
        proj_shift,
        scale_one,
        gain_two,
        shift_two,
        fc1_weight,
        fc1_shift,
        fc2_weight,
        fc2_shift,
        scale_two,
    ) = fetched
    gain_one = gain_one.astype(jnp.float32)
    shift_one = shift_one.astype(jnp.float32)
    proj_shift = proj_shift.astype(jnp.float32)
    scale_one = scale_one.astype(jnp.float32)
    gain_two = gain_two.astype(jnp.float32)
    shift_two = shift_two.astype(jnp.float32)
    fc1_shift = fc1_shift.astype(jnp.float32)
    fc2_shift = fc2_shift.astype(jnp.float32)
    scale_two = scale_two.astype(jnp.float32)
    local_rows = tokens.shape[0]
    width_model = tokens.shape[1]
    seq_len = local_rows * lax.axis_size("seq")
    offset = lax.axis_index("seq") * local_rows
    row_span = (seq_len - 1) // (SIDE // 2) + 1
    table_rows = bias_table.shape[0]
    entries = -(-table_rows // (2 * LANES)) * 2 * LANES
    table_lines = jnp.pad(
        bias_table.T, ((0, HEAD_ROWS - HEADS), (0, entries - table_rows))
    )
    scalars = jnp.stack([widths[0], counts[0], offset.astype(jnp.int32)])
    smem = pl.BlockSpec(memory_space=pltpu.SMEM)
    vmem = pl.BlockSpec(memory_space=pltpu.VMEM)
    params = pltpu.CompilerParams(vmem_limit_bytes=40 << 20)

    inputs_f = tokens.astype(jnp.float32)
    normed_full, normed_one, inv_std_one = layer_norm(inputs_f, gain_one, shift_one)
    normed_low = normed_full.astype(jnp.bfloat16)
    qkv_shift = jnp.concatenate(
        [query_bias, jnp.zeros((width_model,), jnp.bfloat16), value_bias]
    ).astype(jnp.float32)
    projected = (
        jnp.dot(normed_low, qkv_weight, preferred_element_type=jnp.float32) + qkv_shift
    ).astype(jnp.bfloat16)
    queries = projected[:, :width_model]
    key_local = projected[:, width_model:]
    keys_all = lax.all_gather(key_local, "seq", axis=0, tiled=True)

    attn_low, probs = pl.pallas_call(
        partial(attend_kernel, row_span),
        out_shape=(
            jax.ShapeDtypeStruct((local_rows, width_model), BF16),
            jax.ShapeDtypeStruct((HEADS, local_rows, seq_len), F32),
        ),
        in_specs=[smem, vmem, vmem, vmem],
        out_specs=(vmem, vmem),
        scratch_shapes=[pltpu.VMEM((HEAD_ROWS, 2 * (local_rows + seq_len)), F32)],
        compiler_params=params,
    )(scalars, queries, keys_all, table_lines)
    branch_one = jnp.dot(attn_low, proj_weight, preferred_element_type=jnp.float32) + proj_shift
    residual_one = inputs_f + scale_one * branch_one
    normed_full_two, normed_two, inv_std_two = layer_norm(residual_one, gain_two, shift_two)
    normed_low_two = normed_full_two.astype(jnp.bfloat16)
    pre_act = jnp.dot(normed_low_two, fc1_weight, preferred_element_type=jnp.float32) + fc1_shift
    activated, gelu_pull = jax.vjp(partial(jax.nn.gelu, approximate=False), pre_act)
    hidden = activated.astype(jnp.bfloat16)
    branch_two = jnp.dot(hidden, fc2_weight, preferred_element_type=jnp.float32) + fc2_shift
    output = (residual_one + scale_two * branch_two).astype(jnp.bfloat16)
    grad_out = cotangent.astype(jnp.float32)
    grad_scale_two = jnp.sum(grad_out * branch_two, axis=0)
    grad_branch_two = (scale_two * grad_out).astype(jnp.bfloat16)
    grad_fc2_weight = jnp.einsum(
        "tf,td->fd", hidden, grad_branch_two, preferred_element_type=jnp.float32
    )
    grad_fc2_shift = row_sum(grad_branch_two)
    grad_hidden = jnp.einsum(
        "td,fd->tf", grad_branch_two, fc2_weight, preferred_element_type=jnp.float32
    )
    grad_pre = gelu_pull(grad_hidden)[0].astype(jnp.bfloat16)
    grad_fc1_weight = jnp.einsum(
        "td,tf->df", normed_low_two, grad_pre, preferred_element_type=jnp.float32
    )
    grad_fc1_shift = row_sum(grad_pre)
    grad_normed_two = jnp.einsum(
        "tf,df->td", grad_pre, fc1_weight, preferred_element_type=jnp.float32
    )
    grad_gain_two = jnp.sum(grad_normed_two * normed_two, axis=0)
    grad_shift_two = jnp.sum(grad_normed_two, axis=0)
    grad_resid = grad_out + norm_back(grad_normed_two, normed_two, inv_std_two, gain_two)
    grad_scale_one = jnp.sum(grad_resid * branch_one, axis=0)
    grad_branch_one = (scale_one * grad_resid).astype(jnp.bfloat16)
    grad_proj_weight = jnp.einsum(
        "td,te->de", attn_low, grad_branch_one, preferred_element_type=jnp.float32
    )
    grad_proj_shift = row_sum(grad_branch_one)
    grad_attn = jnp.einsum(
        "te,de->td", grad_branch_one, proj_weight, preferred_element_type=jnp.float32
    ).astype(jnp.bfloat16)
    grad_query, key_terms, table_grad = pl.pallas_call(
        partial(attend_back_kernel, row_span),
        out_shape=(
            jax.ShapeDtypeStruct((local_rows, width_model), BF16),
            jax.ShapeDtypeStruct((seq_len, 2 * width_model), BF16),
            jax.ShapeDtypeStruct((HEAD_ROWS, entries), F32),
        ),
        in_specs=[smem, vmem, vmem, vmem, vmem],
        out_specs=(vmem, vmem, vmem),
        scratch_shapes=[
            pltpu.VMEM(((local_rows + seq_len) // LANES, 2 * HEAD_ROWS * 8, LANES), F32)
        ],
        compiler_params=params,
    )(scalars, queries, keys_all, probs, grad_attn)
    own_terms = lax.psum_scatter(key_terms, "seq", scatter_dimension=0, tiled=True)
    grad_qkv = jnp.concatenate([grad_query, own_terms], axis=1)
    grad_qkv_weight = jnp.einsum(
        "td,te->de", normed_low, grad_qkv, preferred_element_type=jnp.float32
    )
    grad_query_bias = row_sum(grad_qkv[:, :width_model])
    grad_value_bias = row_sum(grad_qkv[:, 2 * width_model :])
    grad_normed_one = jnp.einsum(
        "te,de->td", grad_qkv, qkv_weight, preferred_element_type=jnp.float32
    )
    grad_gain_one = jnp.sum(grad_normed_one * normed_one, axis=0)
    grad_shift_one = jnp.sum(grad_normed_one, axis=0)
    grad_inputs = (
        grad_resid + norm_back(grad_normed_one, normed_one, inv_std_one, gain_one)
    ).astype(jnp.bfloat16)
    summed = (
        lax.psum_scatter(grad_gain_one, ("img", "seq"), scatter_dimension=0, tiled=True),
        lax.psum_scatter(grad_shift_one, ("img", "seq"), scatter_dimension=0, tiled=True),
        lax.psum_scatter(grad_qkv_weight, ("img", "seq"), scatter_dimension=0, tiled=True),
        lax.psum_scatter(grad_query_bias, ("img", "seq"), scatter_dimension=0, tiled=True),
        lax.psum_scatter(grad_value_bias, ("img", "seq"), scatter_dimension=0, tiled=True),
        lax.psum_scatter(grad_proj_weight, ("img", "seq"), scatter_dimension=0, tiled=True),
        lax.psum_scatter(grad_proj_shift, ("img", "seq"), scatter_dimension=0, tiled=True),
        lax.psum_scatter(grad_scale_one, ("img", "seq"), scatter_dimension=0, tiled=True),
        lax.psum_scatter(grad_gain_two, ("img", "seq"), scatter_dimension=0, tiled=True),
        lax.psum_scatter(grad_shift_two, ("img", "seq"), scatter_dimension=0, tiled=True),
        lax.psum_scatter(grad_fc1_weight, ("img", "seq"), scatter_dimension=0, tiled=True),
        lax.psum_scatter(grad_fc1_shift, ("img", "seq"), scatter_dimension=0, tiled=True),
        lax.psum_scatter(grad_fc2_weight, ("img", "seq"), scatter_dimension=0, tiled=True),
        lax.psum_scatter(grad_fc2_shift, ("img", "seq"), scatter_dimension=0, tiled=True),
        lax.psum_scatter(grad_scale_two, ("img", "seq"), scatter_dimension=0, tiled=True),
    )
    table_total = lax.psum(table_grad, ("img", "seq"))[:HEADS, :table_rows].T
    return (output, grad_inputs) + tuple(summed) + (table_total,)


def per_device_linked(
    tokens,
    cotangent,
    counts,
    widths,
    norm1_gain,
    norm1_shift,
    w_qkv,
    q_bias,
    v_bias,
    w_proj,
    proj_bias,
    gamma1,
    norm2_gain,
    norm2_shift,
    w_fc1,
    fc1_bias,
    w_fc2,
    fc2_bias,
    gamma2,
    bias_table,
):
    seq_len = tokens.shape[0] * lax.axis_size("seq")
    row_span = (seq_len - 1) // (SIDE // 2) + 1
    vectors = [
        norm1_gain, norm1_shift, q_bias, v_bias, proj_bias, gamma1, norm2_gain, norm2_shift, fc2_bias, gamma2, fc1_bias,
    ]
    output, grad_tokens, small, *sums = run_layer(
        row_span, widths, counts, tokens, cotangent, vectors, w_qkv, w_proj, w_fc1, w_fc2, bias_table.T
    )
    sizes = [vector.shape[0] for vector in vectors]
    output, grad_tokens, sum_qkv, sum_proj, sum_fc1, sum_fc2, table_total, *lines = hand_out(
        small, [output, grad_tokens, *sums], sizes
    )
    lines = [line.reshape(-1) for line in lines]
    return (
        output, grad_tokens, lines[GAIN_ONE], lines[SHIFT_ONE], sum_qkv, lines[QUERY_BIAS], lines[VALUE_BIAS],
        sum_proj, lines[PROJ_SHIFT], lines[SCALE_ONE], lines[GAIN_TWO], lines[SHIFT_TWO], sum_fc1,
        lines[HIDDEN_LINE], sum_fc2, lines[FC2_SHIFT], lines[SCALE_TWO], table_total.T,
    )


def per_device(*arrays):
    tokens, bias_table = arrays[0], arrays[19]
    linked = lax.axis_size("img") == 4 * Z_SIZE and lax.axis_size("seq") == 2
    linked = linked and arrays[6].shape[0] % 8 == 0 and tokens.shape[0] == LANES
    linked = linked and 15 * LANES < bias_table.shape[0] <= 4 * Z_SIZE * LANES
    return per_device_linked(*arrays) if linked else per_device_native(*arrays)


def solution(mesh):
    return jax.shard_map(
        per_device,
        mesh=mesh,
        in_specs=(
            P(("img", "seq"), None),
            P(("img", "seq"), None),
            P("img"),
            P("img"),
            P(("img", "seq")),
            P(("img", "seq")),
            P(("img", "seq"), None),
            P(("img", "seq")),
            P(("img", "seq")),
            P(("img", "seq"), None),
            P(("img", "seq")),
            P(("img", "seq")),
            P(("img", "seq")),
            P(("img", "seq")),
            P(("img", "seq"), None),
            P(("img", "seq")),
            P(("img", "seq"), None),
            P(("img", "seq")),
            P(("img", "seq")),
            P(),
        ),
        out_specs=(
            P(("img", "seq"), None),
            P(("img", "seq"), None),
            P(("img", "seq")),
            P(("img", "seq")),
            P(("img", "seq"), None),
            P(("img", "seq")),
            P(("img", "seq")),
            P(("img", "seq"), None),
            P(("img", "seq")),
            P(("img", "seq")),
            P(("img", "seq")),
            P(("img", "seq")),
            P(("img", "seq"), None),
            P(("img", "seq")),
            P(("img", "seq"), None),
            P(("img", "seq")),
            P(("img", "seq")),
            P(),
        ),
        check_vma=False,
    )
```

```python
from functools import partial

import jax
import jax.numpy as jnp
from jax import lax
from jax.experimental import pallas as pl
from jax.experimental.pallas import tpu as pltpu
from jax.sharding import PartitionSpec as P

HEADS = 12
HEAD_DIM = 64
SIDE = 32
PAIR = 2 * HEAD_DIM
PAIRS = HEADS // 2
HEAD_ROWS = 16
LANES = 128
F32 = jnp.float32
BF16 = jnp.bfloat16
NT = (((1,), (1,)), ((), ()))
TN = (((0,), (0,)), ((), ()))


VMEM_LIMIT = 63 << 20
ROW_GROUP = 8
EPSILON = 1e-06
NEG_FILL = -1e30


def dot(left, right, dims=(((1,), (0,)), ((), ()))):
    return lax.dot_general(left, right, dims, preferred_element_type=F32)


def iota(shape, dim):
    return lax.broadcasted_iota(jnp.int32, shape, dim)


def floor_div(values, width):
    return jnp.floor((values.astype(F32) + 0.5) / width.astype(F32)).astype(jnp.int32)


def table_index(place, span, rows, row_span, width, offset):
    right = place >= span
    diagonal = offset + rows - 1 - jnp.where(right, place - span, place)
    row = floor_div(diagonal, width)
    col = diagonal - row * width
    row = jnp.where(right, row + 1, row)
    col = jnp.where(right, col - width, col)
    return (row + row_span - 1) * (2 * SIDE - 1) + col + SIDE - 1


def same_side(rows, keys, width, offset):
    query = iota((rows, keys), 0) + offset
    key = iota((rows, keys), 1)
    return (query - floor_div(query, width) * width) >= (key - floor_div(key, width) * width)


def fill_diagonals(table_ref, diag_ref, rows, keys, row_span, width, offset):
    span = rows + keys
    entries = table_ref.shape[1]
    step = 2 * LANES
    index = table_index(iota((step, 2 * span), 1), span, rows, row_span, width, offset)
    entry = iota((step, 2 * span), 0)
    diag_ref[...] = jnp.zeros_like(diag_ref)

    def add(chunk, carry):
        start = pl.multiple_of(chunk * step, step)
        chosen = jnp.where(entry + start == index, 1.0, 0.0).astype(BF16)
        diag_ref[...] += dot(table_ref[:, pl.ds(start, step)], chosen)
        return carry

    lax.fori_loop(0, entries // step, add, 0)


def half_mask(shape, half):
    lane = iota(shape, 1)
    return lane < HEAD_DIM if half == 0 else lane >= HEAD_DIM


def pick(values, half):
    return jnp.where(half_mask(values.shape, half), values, jnp.zeros_like(values))


def attend(query_ref, kv_ref, diag_ref, probs_ref, mixed_ref, width, count, offset, pairs=(0, PAIRS)):
    rows, model = query_ref.shape
    keys = kv_ref.shape[0]
    span = rows + keys
    same = same_side(rows, keys, width, offset)
    valid = iota((rows, keys), 1) < count

    def one_pair(pair, carry):
        cols = pl.ds(pl.multiple_of(pair * PAIR, PAIR), PAIR)
        value_cols = pl.ds(pl.multiple_of(model + pair * PAIR, PAIR), PAIR)
        query_pair = query_ref[:, cols]
        key_pair = kv_ref[:, cols]
        value_pair = kv_ref[:, value_cols]
        mixed = jnp.zeros((rows, PAIR), F32)
        for half in range(2):
            head = pair * 2 + half
            product = dot(pick(query_pair, half), key_pair, NT)
            shifted = []
            for side in range(2):
                line = diag_ref[pl.ds(head, 1), side * span : (side + 1) * span]
                line = jnp.broadcast_to(line, (rows, span))
                line = pltpu.roll(line, keys + 1, 1, stride=1, stride_axis=0)
                shifted.append(line[:, :keys])
            scores = product * HEAD_DIM**-0.5 + jnp.where(same, shifted[0], shifted[1])
            scores = jnp.where(valid, scores, NEG_FILL)
            terms = jnp.exp(scores - jnp.max(scores, axis=1, keepdims=True))
            terms = jnp.where(valid, terms, 0.0)
            probs = terms / jnp.sum(terms, axis=1, keepdims=True)
            probs_ref[head] = probs
            mixed = mixed + dot(probs.astype(BF16), pick(value_pair, half))
        mixed_ref[:, cols] = mixed.astype(BF16)
        return carry

    lax.fori_loop(*pairs, one_pair, 0)


def fold_rows(values):
    while values.shape[0] > 8:
        half = values.shape[0] // 2
        values = values[half:] + pltpu.roll(values[:half], half, 1)
    return values


def attend_back(
    query_ref, kv_ref, probs_ref, grad_ref, grad_query_ref, grad_kv_ref, fold_ref, width, offset, pairs=(0, PAIRS)
):
    rows, model = query_ref.shape
    keys = kv_ref.shape[0]
    same = same_side(rows, keys, width, offset)

    def one_pair(pair, carry):
        cols = pl.ds(pl.multiple_of(pair * PAIR, PAIR), PAIR)
        value_cols = pl.ds(pl.multiple_of(model + pair * PAIR, PAIR), PAIR)
        query_pair = query_ref[:, cols]
        key_pair = kv_ref[:, cols]
        value_pair = kv_ref[:, value_cols]
        grad_pair = grad_ref[:, cols]
        grad_query = jnp.zeros((rows, PAIR), F32)
        grad_key = jnp.zeros((keys, PAIR), F32)
        grad_value = jnp.zeros((keys, PAIR), F32)
        for half in range(2):
            head = pair * 2 + half
            probs = probs_ref[head]
            grad_half = pick(grad_pair, half)
            grad_probs = dot(grad_half, value_pair, NT)
            grad_scores = probs * (
                grad_probs - jnp.sum(probs * grad_probs, axis=1, keepdims=True)
            )
            blank = jnp.zeros((rows, rows), F32)
            left = jnp.where(same, grad_scores, 0.0)
            right = jnp.where(same, 0.0, grad_scores)
            for side, part in enumerate((left, right)):
                place = pl.multiple_of((side * HEAD_ROWS + head) * 8, 8)
                folded = fold_rows(jnp.concatenate([part, blank], axis=1))
                for block in range((rows + keys) // LANES):
                    fold_ref[block, pl.ds(place, 8), :] = folded[:, block * LANES : (block + 1) * LANES]
            grad_prod = (grad_scores * HEAD_DIM**-0.5).astype(BF16)
            grad_query = grad_query + dot(grad_prod, pick(key_pair, half))
            grad_key = grad_key + dot(grad_prod, pick(query_pair, half), TN)
            grad_value = grad_value + dot(probs.astype(BF16), grad_half, TN)
        grad_query_ref[:, cols] = grad_query.astype(BF16)
        grad_kv_ref[:, cols] = grad_key.astype(BF16)
        grad_kv_ref[:, value_cols] = grad_value.astype(BF16)
        return carry

    lax.fori_loop(*pairs, one_pair, 0)


def table_gradient(fold_ref, out_ref, rows, keys, row_span, width, offset):
    span = rows + keys
    lines = 2 * HEAD_ROWS
    total = jnp.zeros((lines, span), F32)
    for row in range(8):
        blocks = [fold_ref[block, pl.ds(row, lines, stride=8), :] for block in range(span // LANES)]
        moved = jnp.concatenate(blocks, axis=1)
        total = total + (pltpu.roll(moved, 7 - row, 1) if row < 7 else moved)
    parts = []
    for side in range(2):
        rest = total[side * HEAD_ROWS : (side + 1) * HEAD_ROWS]
        pieces = []
        for _ in range(3):
            piece = rest.astype(BF16)
            rest = rest - piece.astype(F32)
            pieces.append(piece)
        parts.append(jnp.concatenate(pieces, axis=0))
    place = iota((span, LANES), 0)
    index = [
        table_index(place + side * span, span, rows, row_span, width, offset) for side in range(2)
    ]
    entry = iota((span, LANES), 1)

    def put(chunk, carry):
        start = pl.multiple_of(chunk * LANES, LANES)
        sums = jnp.zeros((3 * HEAD_ROWS, LANES), F32)
        for side in range(2):
            chosen = jnp.where(entry + start == index[side], 1.0, 0.0).astype(BF16)
            sums = sums + dot(parts[side], chosen)
        out_ref[:, pl.ds(start, LANES)] = (
            sums[:HEAD_ROWS] + sums[HEAD_ROWS : 2 * HEAD_ROWS] + sums[2 * HEAD_ROWS :]
        )
        return carry

    lax.fori_loop(0, out_ref.shape[1] // LANES, put, 0)


def attend_kernel(row_span, scal_ref, query_ref, kv_ref, table_ref, mixed_ref, probs_ref, diag_ref):
    rows, keys = query_ref.shape[0], kv_ref.shape[0]
    width, count, offset = scal_ref[0], scal_ref[1], scal_ref[2]
    fill_diagonals(table_ref, diag_ref, rows, keys, row_span, width, offset)
    attend(query_ref, kv_ref, diag_ref, probs_ref, mixed_ref, width, count, offset)


def attend_back_kernel(
    row_span, scal_ref, query_ref, kv_ref, probs_ref, grad_ref, grad_query_ref, grad_kv_ref, table_ref, fold_ref
):
    rows, keys = query_ref.shape[0], kv_ref.shape[0]
    width, offset = scal_ref[0], scal_ref[2]
    fold_ref[...] = jnp.zeros_like(fold_ref)
    attend_back(
        query_ref, kv_ref, probs_ref, grad_ref, grad_query_ref, grad_kv_ref, fold_ref, width, offset
    )
    table_gradient(fold_ref, table_ref, rows, keys, row_span, width, offset)


MESH = pl.DeviceIdType.MESH
Z_SIZE = 4


class Place:
    def __init__(self):
        img = lax.axis_index("img")
        self.x = lax.axis_index("seq")
        self.c = lax.rem(img, 2)
        self.y = lax.rem(img // 2, 2)
        self.z = img // 4

    def at(self, z=None, y=None, c=None, x=None):
        z = self.z if z is None else z
        y = self.y if y is None else y
        c = self.c if c is None else c
        x = self.x if x is None else x
        return {"img": (z * 2 + y) * 2 + c, "seq": x}

    def sibling(self):
        return self.at(c=1 - self.c)

    def over_x(self):
        return self.at(x=1 - self.x)

    def over_y(self):
        return self.at(y=1 - self.y)

    def z_of(self, step):
        return lax.rem(self.z + step, Z_SIZE)

    def partners(self):
        return [self.sibling(), self.over_x(), self.over_y()] + [
            self.at(z=self.z_of(step)) for step in range(1, Z_SIZE)
        ]


def meet(place):
    barrier = pltpu.get_barrier_semaphore()
    partners = place.partners()
    for partner in partners:
        pl.semaphore_signal(barrier, inc=1, device_id=partner, device_id_type=MESH)
    pl.semaphore_wait(barrier, len(partners))


class Sems:
    def __init__(self, send, recv, place):
        self.send, self.recv, self.place = send, recv, place
        self.sends = self.recvs = 0

    def take_send(self):
        self.sends += 1
        return self.send.at[self.sends - 1]

    def take_recv(self):
        self.recvs += 1
        return self.recv.at[self.recvs - 1]

    def copy(self, src, dst, device, sent=None, came=None):
        return pltpu.make_async_remote_copy(
            src_ref=src,
            dst_ref=dst,
            send_sem=self.take_send() if sent is None else sent,
            recv_sem=self.take_recv() if came is None else came,
            device_id=device,
            device_id_type=MESH,
        )

    def total(self, ref, sem):
        return pltpu.make_async_remote_copy(
            src_ref=ref,
            dst_ref=ref,
            send_sem=sem,
            recv_sem=sem,
            device_id=self.place.sibling(),
            device_id_type=MESH,
        )


class Gather:
    def __init__(self, place, src, slots, cols, x_last, sems, local_sem):
        z, y, c, x = place.z, place.y, place.c, place.x
        groups = src.shape[0]
        every = slice(None)

        def part(a, b, e):
            return slots.at[a, b, c, pl.ds(e * groups, groups), :, cols]

        mine = src.at[:, :, cols]
        own = part(z, y, x)
        self.z = z
        self.local = pltpu.make_async_copy(mine, own, local_sem)
        sent = sems.take_send()
        came = [sems.take_recv() for _ in range(1, Z_SIZE)]
        self.along_z = [
            sems.copy(mine, own, place.at(z=place.z_of(step)), sent, came[step - 1])
            for step in range(1, Z_SIZE)
        ]
        last_z = Z_SIZE - 1
        self.relay_up = sems.copy(part(0, y, x), part(0, y, x), place.at(z=last_z), sent, came[last_z - 1])
        self.relay_down = sems.copy(part(last_z, y, x), part(last_z, y, x), place.at(z=0), sent, came[0])
        line = part(every, y, x)
        mid_line = part(every, 1 - y, x) if x_last else part(every, y, 1 - x)
        far_line = part(every, y, 1 - x) if x_last else part(every, 1 - y, x)
        cross_line = part(every, 1 - y, 1 - x)
        mid, last = place.over_y(), place.over_x()
        if not x_last:
            mid, last = last, mid
        sibling = place.sibling()
        mid_came, last_came, core_came = sems.take_recv(), sems.take_recv(), sems.take_recv()
        self.own_mid = sems.copy(mine, own, mid, sent, mid_came)
        self.own_last = sems.copy(mine, own, last, sent, last_came)
        pieces = [part(place.z_of(Z_SIZE - step), y, x) for step in range(1, Z_SIZE)]
        self.line_mid = [sems.copy(piece, piece, mid, sent, mid_came) for piece in pieces]
        self.line_last = [sems.copy(piece, piece, last, sent, last_came) for piece in pieces]
        self.line_core = sems.copy(line, line, sibling, sent, core_came)
        self.mid_last = sems.copy(mid_line, mid_line, last, sent)
        self.mid_core = sems.copy(mid_line, mid_line, sibling, sent, core_came)
        self.far_core = sems.copy(far_line, far_line, sibling, sent, core_came)
        self.cross_core = sems.copy(cross_line, cross_line, sibling, sent, core_came)
        self.all_mid = sems.total(mid_line, mid_came)
        self.all_last = sems.total(far_line, last_came)
        self.all_core = sems.total(slots.at[:, :, 1 - c, :, :, cols], core_came)
        flat = slots.reshape((8 * Z_SIZE * groups,) + slots.shape[4:])
        self.outer_sent = sems.total(flat.at[pl.ds(0, (8 * Z_SIZE - 2) * groups), :, cols], sent)
        self.inner_sent = sems.total(flat.at[:, :, cols], sent)

    def begin_own(self):
        self.local.start()
        self.own_mid.start()
        self.own_last.start()

    def begin_z(self):
        up, across, down = self.along_z

        @pl.when(self.z != Z_SIZE - 1)
        def _():
            up.start()

        @pl.when(self.z != 0)
        def _():
            down.start()

        across.start()

    def pass_on(self, number):
        self.line_mid[number].start()
        self.line_last[number].start()

    def second(self):
        up, across, down = self.along_z
        across.wait_recv()

        @pl.when(self.z == Z_SIZE - 2)
        def _():
            self.relay_up.start()

        @pl.when(self.z == 1)
        def _():
            self.relay_down.start()

        self.pass_on(1)

        @pl.when(self.z >= Z_SIZE // 2)
        def _():
            up.wait_recv()
            self.pass_on(0)
            down.wait_recv()
            self.pass_on(2)

        @pl.when(self.z < Z_SIZE // 2)
        def _():
            down.wait_recv()
            self.pass_on(2)
            up.wait_recv()
            self.pass_on(0)

        self.local.wait()
        self.line_core.start()

    def third(self):
        self.all_mid.wait_recv()
        self.mid_last.start()
        self.mid_core.start()

    def fourth(self):
        self.all_last.wait_recv()
        self.far_core.start()
        self.mid_last.wait_recv()
        self.cross_core.start()

    def arrive(self):
        self.all_core.wait_recv()

    def settle(self):
        inner = (self.z - 1) * (Z_SIZE - 2 - self.z) >= 0

        @pl.when(inner)
        def _():
            self.inner_sent.wait_send()

        @pl.when(jnp.logical_not(inner))
        def _():
            self.outer_sent.wait_send()


class GatherLate(Gather):
    def __init__(self, place, src, slots, cols, x_last, sems, local_sem):
        z, y, c, x = place.z, place.y, place.c, place.x
        groups = src.shape[0]
        sibling = place.sibling()

        def plane(a):
            return slots.at[a, :, c, :, :, cols]

        def part(b, e):
            return slots.at[z, b, c, pl.ds(e * groups, groups), :, cols]

        mine = src.at[:, :, cols]
        own = part(y, x)
        self.local = pltpu.make_async_copy(mine, own, local_sem)
        sent = sems.take_send()
        near, last = place.over_x(), place.over_y()
        piece = part(y, 1 - x)
        if not x_last:
            near, last = last, near
            piece = part(1 - y, x)
        self.own_near = sems.copy(mine, own, near, sent)
        self.own_last = sems.copy(mine, own, last, sent)
        self.near_last = sems.copy(piece, piece, last, sent)
        self.along_z = [
            sems.copy(plane(z), plane(z), place.at(z=place.z_of(step)), sent) for step in range(1, Z_SIZE)
        ]
        core_came = sems.take_recv()
        self.line_core = sems.copy(plane(z), plane(z), sibling, sent, core_came)
        self.far_core = []
        for step in range(1, Z_SIZE):
            far = plane(place.z_of(Z_SIZE - step))
            self.far_core.append(sems.copy(far, far, sibling, sent, core_came))
        self.all_core = sems.total(slots.at[:, :, 1 - c, :, :, cols], core_came)
        flat = slots.reshape((8 * Z_SIZE * groups,) + slots.shape[4:])
        self.all_sent = sems.total(flat.at[pl.ds(0, (8 * Z_SIZE - 1) * groups), :, cols], sent)

    def begin_own(self):
        self.local.start()
        self.own_near.start()
        self.own_last.start()

    def begin_z(self):
        self.own_near.wait_recv()
        self.near_last.start()

    def second(self):
        self.own_last.wait_recv()
        self.near_last.wait_recv()
        self.local.wait()
        for copy in self.along_z:
            copy.start()
        self.line_core.start()

    def third(self):
        pass

    def fourth(self):
        for copy, onward in zip(self.along_z, self.far_core):
            copy.wait_recv()
            onward.start()

    def settle(self):
        self.all_sent.wait_send()


class Reduce:
    def __init__(self, place, grad, own, first, second, third, out, start, size, x_first, sems, pieces=None):
        rows = out.shape[0]

        def flat(ref):
            return ref.reshape(ref.shape[:-3] + (rows, ref.shape[-1]))

        self.place, self.out = place, out
        self.grad, self.own, self.first = flat(grad), flat(own), flat(first)
        self.second, self.third = flat(second), flat(third)
        self.pieces = pieces or [(0, start, size)]
        self.x_first = x_first
        z, y, c, x = place.z, place.y, place.c, place.x
        every = slice(None)
        cols = pl.ds(start, size)
        self.cols = cols
        sent = sems.take_send()
        self.to_core = sems.copy(
            grad.at[:, :, 1 - c, :, :, :, cols], own.at[:, :, :, :, :, cols], place.sibling(), sent
        )
        over_first, over_second = place.over_x(), place.over_y()
        if x_first:
            leaving, other = own.at[:, :, 1 - x, :, :, cols], 1 - y
        else:
            over_first, over_second = over_second, over_first
            leaving, other = own.at[:, 1 - y, :, :, :, cols], 1 - x
        self.kept = y if x_first else x
        self.over_first = sems.copy(leaving, first, over_first, sent)
        self.over_second = sems.copy(first.at[:, other], second, over_second, sent)
        came = sems.take_recv()
        self.along_z = []
        for step in range(1, Z_SIZE):
            target = place.z_of(step)
            self.along_z.append(
                sems.copy(second.at[target], third.at[step - 1], place.at(z=target), sent, came)
            )
        self.all_z = sems.total(third, came)
        slots = grad.reshape((8 * Z_SIZE,) + grad.shape[4:])
        self.all_sent = sems.total(slots.at[pl.ds(0, 8 * Z_SIZE - 1), :, :, cols], sent)

    def begin(self):
        self.to_core.start()

    def add_core(self):
        self.to_core.wait_recv()
        place = self.place

        def add(zy, carry):
            z, y = zy // 2, lax.rem(zy, 2)
            for x in range(2):
                mine = self.grad[z, y, place.c, x, :, self.cols].astype(F32)
                theirs = self.own[z, y, x, :, self.cols].astype(F32)
                self.own[z, y, x, :, self.cols] = (mine + theirs).astype(self.own.dtype)
            return carry

        lax.fori_loop(0, 2 * Z_SIZE, add, 0)
        self.send_core()

    def send_core(self):
        self.over_first.start()

    def add_first(self):
        self.over_first.wait_recv()
        place = self.place

        def add(z, carry):
            for other in range(2):
                if self.x_first:
                    mine = self.own[z, other, place.x, :, self.cols].astype(F32)
                else:
                    mine = self.own[z, place.y, other, :, self.cols].astype(F32)
                theirs = self.first[z, other].astype(F32)
                self.first[z, other] = (mine + theirs).astype(self.first.dtype)
            return carry

        lax.fori_loop(0, Z_SIZE, add, 0)
        self.over_second.start()

    def add_second(self):
        self.over_second.wait_recv()

        def add(z, carry):
            mine = self.first[z, self.kept].astype(F32)
            theirs = self.second[z].astype(F32)
            self.second[z] = (mine + theirs).astype(self.second.dtype)
            return carry

        lax.fori_loop(0, Z_SIZE, add, 0)
        for copy in self.along_z:
            copy.start()

    def finish(self):
        total = self.second[self.place.z].astype(F32)
        self.all_z.wait_recv()
        for step in range(Z_SIZE - 1):
            total = total + self.third[step].astype(F32)
        for source, target, size in self.pieces:
            self.out[:, target : target + size] = total[:, source : source + size]

    def settle(self):
        self.all_sent.wait_send()


class ReduceEarly(Reduce):
    def __init__(self, place, grad, own, by_z, plane, first, second, out, start, size, x_first, sems, pieces=None):
        self.pieces = pieces or [(0, start, size)]
        self.x_first = x_first
        rows = out.shape[0]

        def flat(ref):
            return ref.reshape(ref.shape[:-3] + (rows, ref.shape[-1]))

        self.place, self.out = place, out
        self.grad, self.own, self.by_z = flat(grad), flat(own), flat(by_z)
        self.plane, self.first, self.second = flat(plane), flat(first), flat(second)
        c, x, y = place.c, place.x, place.y
        cols = pl.ds(start, size)
        self.cols = cols
        sent = sems.take_send()
        self.to_core = sems.copy(
            grad.at[:, :, 1 - c, :, :, :, cols], own.at[:, :, :, :, :, cols], place.sibling(), sent
        )
        came = sems.take_recv()
        self.along_z = []
        for step in range(1, Z_SIZE):
            target = place.z_of(step)
            self.along_z.append(
                sems.copy(
                    own.at[target, :, :, :, :, cols], by_z.at[step - 1], place.at(z=target), sent, came
                )
            )
        self.all_z = sems.total(by_z, came)
        over_first, over_second = place.over_x(), place.over_y()
        if x_first:
            leaving, other = plane.at[:, 1 - x], 1 - y
        else:
            over_first, over_second = over_second, over_first
            leaving, other = plane.at[1 - y], 1 - x
        self.kept = y if x_first else x
        self.over_first = sems.copy(leaving, first, over_first, sent)
        self.over_second = sems.copy(first.at[other], second, over_second, sent)
        slots = grad.reshape((8 * Z_SIZE,) + grad.shape[4:])
        self.all_sent = sems.total(slots.at[pl.ds(0, 8 * Z_SIZE - 1), :, :, cols], sent)

    def send_core(self):
        for copy in self.along_z:
            copy.start()

    def add_first(self):
        self.all_z.wait_recv()
        z = self.place.z
        for y in range(2):
            for x in range(2):
                total = self.own[z, y, x, :, self.cols].astype(F32)
                for step in range(Z_SIZE - 1):
                    total = total + self.by_z[step, y, x].astype(F32)
                self.plane[y, x] = total.astype(self.plane.dtype)
        self.over_first.start()

    def add_second(self):
        self.over_first.wait_recv()
        for other in range(2):
            if self.x_first:
                mine = self.plane[other, self.place.x].astype(F32)
            else:
                mine = self.plane[self.place.y, other].astype(F32)
            self.first[other] = (mine + self.first[other].astype(F32)).astype(self.first.dtype)
        self.over_second.start()

    def finish(self):
        self.over_second.wait_recv()
        total = self.first[self.kept].astype(F32) + self.second[...].astype(F32)
        for source, target, size in self.pieces:
            self.out[:, target : target + size] = total[:, source : source + size]


class Names:
    pass


def norm_rows(values):
    centred = values - jnp.mean(values, axis=1, keepdims=True)
    inv_std = lax.rsqrt(jnp.mean(centred * centred, axis=1, keepdims=True) + EPSILON)
    return centred * inv_std, inv_std


def norm_rows_back(grad_out, normed, inv_std, gain):
    scaled = grad_out * gain
    return inv_std * (
        scaled
        - jnp.mean(scaled, axis=1, keepdims=True)
        - normed * jnp.mean(scaled * normed, axis=1, keepdims=True)
    )


def sum_rows(values):
    return jnp.sum(values.astype(F32), axis=0, keepdims=True)


def div_const(values, divisor):
    return jnp.floor((values.astype(F32) + 0.5) * (1.0 / divisor)).astype(jnp.int32)


def tile(slots, start, size):
    rows = slots.shape[3] * ROW_GROUP
    view = slots.reshape(4 * Z_SIZE, rows, slots.shape[-1])
    return view[:, :, pl.ds(start, size)].reshape(-1, size)


def put_slots(slots, cols, values):
    devices = 8 * Z_SIZE
    view = slots.reshape(devices, slots.shape[4] * ROW_GROUP, slots.shape[-1])
    view[:, :, cols] = values.reshape(devices, -1, values.shape[1]).astype(slots.dtype)


def tiles(count, step):
    def wrap(body):
        def run(number, carry):
            body(number, pl.multiple_of(number * step, step))
            return carry

        lax.fori_loop(0, count, run, 0)

    return wrap


LINES = 16
SLOT_ROWS = 24
QKV_COLS = 256


def quarters(width):
    large = -(-width // 4 // LANES) * LANES
    small = width // 2 - large
    cuts = [(0, large), (large, large), (2 * large, small), (2 * large + small, small)]
    return [(start, size, False) for start, size in cuts]


def halves(width, turned):
    middle = width // 2 // LANES * LANES
    return [(0, middle, turned), (middle, width - middle, turned)]


def fc2_cuts(width):
    part = width // 3
    return [(0, part, False), (part, part, False), (2 * part, width - 2 * part, True)]


def qkv_cuts(model):
    size = 3 * QKV_COLS // 2
    return [(start, size, False) for start in range(0, 3 * model, size)]


(
    GAIN_ONE, SHIFT_ONE, QUERY_BIAS, VALUE_BIAS, PROJ_SHIFT, SCALE_ONE, GAIN_TWO, SHIFT_TWO, FC2_SHIFT, SCALE_TWO,
) = range(10)
HIDDEN_LINE = 10
LINE_NAMES = ["line" + str(number) for number in range(HIDDEN_LINE + 1)]


def unpack_lines(packed, shard, hidden_shard, vec_ref, hidden_ref):
    rows = packed.shape[0]
    devices = rows // SLOT_ROWS
    low = packed.astype(BF16)
    width = shard * devices
    lane = iota((LANES, width), 1)
    spread = jnp.where(lane - div_const(lane, shard) * shard == iota((LANES, width), 0), 1.0, 0.0)
    wide = dot(low, spread.astype(BF16))
    owner = div_const(iota((rows, width), 0), SLOT_ROWS)
    wide = jnp.where(owner == div_const(iota((rows, width), 1), shard), wide, 0.0).astype(BF16)
    row = iota((LINES, rows), 1)
    line = row - div_const(row, SLOT_ROWS) * SLOT_ROWS
    vec_ref[...] = dot(jnp.where(line == iota((LINES, rows), 0), 1.0, 0.0).astype(BF16), wide)
    row = iota((devices, rows), 1)
    chosen = jnp.where(row == iota((devices, rows), 0) * SLOT_ROWS + HIDDEN_LINE, 1.0, 0.0)
    hidden = dot(chosen.astype(BF16), low).astype(BF16)
    step = 8 * LANES
    for start in range(0, hidden_shard * devices, step):
        lane = iota((LANES, step), 1) + start
        owner = div_const(lane, hidden_shard)
        spread = jnp.where(lane - owner * hidden_shard == iota((LANES, step), 0), 1.0, 0.0)
        wide = dot(hidden, spread.astype(BF16))
        owner = div_const(iota((devices, step), 1) + start, hidden_shard)
        wide = jnp.where(owner == iota((devices, step), 0), wide, 0.0)
        hidden_ref[:, start : start + step] = jnp.broadcast_to(sum_rows(wide), (8, step))


def layer_kernel(names, row_span, *refs):
    s = Names()
    s.__dict__.update(zip(names, refs))
    buffers = list(refs[len(names) :])
    send, recv, local = buffers[-3:]
    place = Place()
    x = place.x
    rows, model = s.tokens.shape
    width, count, offset = s.widths[0], s.counts[0], x * rows
    keys = 2 * rows
    hidden = s.w_fc1.shape[2]
    shard, hidden_shard = s.w_qkv.shape[0] * ROW_GROUP, s.w_fc2.shape[0] * ROW_GROUP
    half = model // 2
    own_rows = pl.ds(pl.multiple_of(x * rows, rows), rows)
    far_rows = pl.ds(pl.multiple_of((1 - x) * rows, rows), rows)
    sems = Sems(send, recv, place)
    locals_used = []
    outgoing = []

    def move(src, dst):
        locals_used.append(0)
        copy = pltpu.make_async_copy(src, dst, local.at[len(locals_used) - 1])
        copy.start()
        return copy

    def hand(src, dst):
        copy = pltpu.make_async_copy(src, dst, local.at[len(outgoing)])
        copy.start()
        outgoing.append(copy)

    def gather(src, slots, cuts):
        chunks = []
        for number, (start, size, late) in enumerate(cuts):
            locals_used.append(0)
            sem = local.at[len(locals_used) - 1]
            kind = GatherLate if late else Gather
            chunks.append(kind(place, src, slots, pl.ds(start, size), number % 2 == 0, sems, sem))
        return chunks

    def reduce(out, cuts, pieces):
        chunks = []
        grad, own = buffers.pop(0), buffers.pop(0)
        for number, (start, size, early) in enumerate(cuts):
            stages = [buffers.pop(0) for _ in range(4 if early else 3)]
            kind = ReduceEarly if early else Reduce
            chunks.append(
                kind(
                    place, grad, own, *stages, out, start, size, number % 2 == 0, sems, pieces and pieces[number],
                )
            )
        return grad, chunks

    def each(chunks, *steps):
        for step in steps:
            for chunk in chunks:
                getattr(chunk, step.__name__)()

    line_copies = [
        move(getattr(s, LINE_NAMES[number]), s.raw_hidden if number == HIDDEN_LINE else s.raw.at[number])
        for number in range(HIDDEN_LINE + 1)
    ]
    table_copy = move(s.table, s.table_in)
    tokens_copy = move(s.tokens, s.tokens_in)
    cot_copy = move(s.cot, s.cot_in)
    swap = sems.copy(s.tokens, s.far_tokens, place.over_x())
    give = sems.copy(s.give, s.take, place.over_x())
    get_pack = gather(s.pack, s.packs, [(0, LANES, False)])
    get_qkv = gather(s.w_qkv, s.wq, halves(3 * model, False))
    get_proj = gather(s.w_proj, s.wp, halves(model, False))
    get_fc1 = gather(s.w_fc1, s.w1, quarters(hidden))
    get_fc2 = gather(s.w_fc2, s.w2, fc2_cuts(model))
    s.g_fc2, put_fc2 = reduce(s.o_fc2, fc2_cuts(model), None)
    s.g_fc1, put_fc1 = reduce(s.o_fc1, quarters(hidden), None)
    s.g_proj, put_proj = reduce(s.o_proj, halves(model, False), None)
    wide = QKV_COLS
    qkv_pieces = []
    for group in range(model // wide):
        start = group * wide
        qkv_pieces.append([(0, start, wide), (wide, model + start, wide // 2)])
        qkv_pieces.append(
            [(0, model + start + wide // 2, wide // 2), (wide // 2, 2 * model + start, wide)]
        )
    s.g_qkv, put_qkv = reduce(s.o_qkv, qkv_cuts(model), qkv_pieces)
    s.g_table, put_table = reduce(s.o_table, [(0, LANES, False)], None)
    s.g_small, put_small = reduce(s.o_small, [(0, LANES, False)], None)
    get_table = gather(s.o_table.reshape(1, 8, LANES), s.table_all, [(0, LANES, False)])

    meet(place)
    for copy in line_copies:
        copy.wait()
    s.pack[...] = jnp.zeros_like(s.pack)
    for number in range(HIDDEN_LINE + 1):
        source = s.raw_hidden if number == HIDDEN_LINE else s.raw.at[number]
        s.pack[number // 8, number % 8 : number % 8 + 1, 0 : source.shape[1]] = source[...].astype(F32)
    each(get_pack, Gather.begin_own, Gather.begin_z)
    each(get_qkv, Gather.begin_z, Gather.begin_own)
    swap.start()
    each(get_proj, Gather.begin_own)
    table_copy.wait()
    s.table_lines[...] = jnp.zeros_like(s.table_lines)
    s.table_lines[0:HEADS, 0 : s.table.shape[1]] = s.table_in[...]
    fill_diagonals(s.table_lines, s.diag, rows, keys, row_span, width, offset)
    each(get_pack, Gather.second)
    tokens_copy.wait()
    normed, inv_std = norm_rows(s.tokens_in[...].astype(F32))
    s.n1[...] = normed
    s.r1[...] = jnp.broadcast_to(inv_std, s.r1.shape)
    each(get_pack, Gather.third)
    each(get_proj, Gather.begin_z)
    each(get_fc1[:2], Gather.begin_z)
    each(get_fc1, Gather.begin_own)
    s.fold[...] = jnp.zeros_like(s.fold)
    s.lines[...] = jnp.zeros_like(s.lines)
    each(get_pack, Gather.fourth)
    each(get_fc2, Gather.begin_own)
    each(get_qkv, Gather.second)
    each(get_fc1[2:], Gather.begin_z)
    each(get_pack, Gather.arrive)
    unpack_lines(tile(s.packs, 0, LANES), shard, hidden_shard, s.vec, s.b1)

    def line(number):
        return s.vec[number : number + 1, :]

    def set_line(number, values):
        s.lines[number : number + 1, :] = values

    s.h1[own_rows, :] = (s.n1[...] * line(GAIN_ONE) + line(SHIFT_ONE)).astype(BF16)
    swap.wait_recv()
    far = norm_rows(s.far_tokens[...].astype(F32))[0]
    s.h1[far_rows, :] = (far * line(GAIN_ONE) + line(SHIFT_ONE)).astype(BF16)
    each(get_proj, Gather.second)
    s.h1t[...] = s.h1[...].T
    cot_copy.wait()
    s.dm[...] = (line(SCALE_TWO) * s.cot_in[...].astype(F32)).astype(BF16)
    set_line(FC2_SHIFT, sum_rows(s.dm[...]))
    each(get_fc1[:2], Gather.second)
    each(get_fc2, Gather.begin_z)
    each(get_fc2[2:], Gather.second)
    each(get_qkv, Gather.third)
    each(get_proj, Gather.third)
    each(get_fc1[2:], Gather.second)
    each(get_qkv, Gather.fourth)
    each(get_fc1[:2], Gather.third)
    each(get_fc2[:2], Gather.second)
    each(get_qkv, Gather.arrive)

    step = 2 * LANES

    @tiles(model // step, step)
    def _(number, start):
        s.kv[:, pl.ds(start, step)] = dot(s.h1[...], tile(s.wq, model + start, step)).astype(BF16)
        sums = dot(s.h1[...], tile(s.wq, 2 * model + start, step))
        sums = sums + s.vec[VALUE_BIAS : VALUE_BIAS + 1, pl.ds(start, step)]
        s.kv[:, pl.ds(model + start, step)] = sums.astype(BF16)

    @tiles(model // step, step)
    def _(number, start):
        cols = pl.ds(start, step)
        sums = dot(s.h1[own_rows, :], tile(s.wq, start, step))
        s.q[:, cols] = (sums + s.vec[QUERY_BIAS : QUERY_BIAS + 1, cols]).astype(BF16)

    def look(first, last):
        attend(s.q, s.kv, s.diag, s.probs, s.mixed, width, count, offset, (first, last))

    each(get_proj, Gather.fourth)
    look(0, 2)
    each(get_fc1[2:], Gather.third)
    look(2, 4)
    each(get_fc1[:2], Gather.fourth)
    look(4, PAIRS)
    each(get_fc2[:2], Gather.third)
    s.mixedt[...] = s.mixed[...].T
    each(get_proj, Gather.arrive)

    @tiles(model // step, step)
    def _(number, start):
        cols = pl.ds(start, step)
        branch = dot(s.mixed[...], tile(s.wp, start, step)) + s.vec[PROJ_SHIFT : PROJ_SHIFT + 1, cols]
        s.z[:, cols] = branch
        s.x1[:, cols] = s.tokens_in[:, cols].astype(F32) + s.vec[SCALE_ONE : SCALE_ONE + 1, cols] * branch

    normed, inv_std = norm_rows(s.x1[...])
    s.n2[...] = normed
    s.r2[...] = jnp.broadcast_to(inv_std, s.r2.shape)
    s.h2[...] = (normed * line(GAIN_TWO) + line(SHIFT_TWO)).astype(BF16)
    s.h2t[...] = s.h2[...].T
    each(get_fc1[2:], Gather.fourth)
    each(get_fc1, Gather.arrive)

    @tiles(hidden // step, step)
    def _(number, start):
        cols = pl.ds(start, step)
        act = dot(s.h2[...], tile(s.w1, start, step)) + s.b1[0:1, cols]
        gate = 0.5 * (1.0 + lax.erf(act * 0.5**0.5))
        low = (act * gate).astype(BF16)
        s.u[:, cols] = low
        s.ut[cols, :] = low.T
        s.slope[:, cols] = gate + act * jnp.exp(act * act * -0.5) * 0.3989422804014327

    deep = 8 * hidden_shard
    for chunk, (first, size, _) in zip(put_fc2, fc2_cuts(model)):

        @tiles(Z_SIZE, deep)
        def _(number, start):
            cols = pl.ds(first, size)
            sums = dot(s.ut[pl.ds(start, deep), :], s.dm[:, cols])
            view = s.g_fc2.reshape(Z_SIZE, 8, hidden_shard, model)
            view[number, :, :, cols] = sums.reshape(8, hidden_shard, size).astype(BF16)

        chunk.begin()
    each(get_fc2, Gather.fourth)
    each(put_fc2, Reduce.add_core)
    each(get_fc2, Gather.arrive)

    @tiles(Z_SIZE, deep)
    def _(number, start):
        cols = pl.ds(start, deep)
        weight = s.w2.reshape(Z_SIZE, deep, model)[number]
        grad_hidden = dot(s.dm[...], weight, NT)
        s.da[:, cols] = (grad_hidden * s.slope[:, cols]).astype(BF16)

    for chunk, (first, size, _) in zip(put_fc1, quarters(hidden)):

        @tiles(size // step, step)
        def _(number, start):
            cols = pl.ds(start + first, step)
            put_slots(s.g_fc1, cols, dot(s.h2t[...], s.da[:, cols]))

        chunk.begin()

    grad = jnp.zeros((rows, model), F32)
    for start in range(0, hidden, model):
        grad = grad + dot(s.da[:, start : start + model], tile(s.w1, start, model), NT)
    s.dh2[...] = grad
    each(put_fc2[:2], Reduce.add_first)
    each(put_fc1, Reduce.add_core)
    grad = s.dh2[...]
    set_line(GAIN_TWO, sum_rows(grad * s.n2[...]))
    set_line(SHIFT_TWO, sum_rows(grad))
    dx1 = s.cot_in[...].astype(F32) + norm_rows_back(grad, s.n2[...], s.r2[:, 0:1], line(GAIN_TWO))
    s.dx1[...] = dx1
    set_line(SCALE_ONE, sum_rows(dx1 * s.z[...]))
    s.dz[...] = (line(SCALE_ONE) * dx1).astype(BF16)
    set_line(PROJ_SHIFT, sum_rows(s.dz[...]))
    for group in range(2):
        cols = pl.ds(group * half, half)
        put_slots(s.g_proj, cols, dot(s.mixedt[...], s.dz[:, cols]))
        put_proj[group].begin()
    s.dmixed[...] = dot(s.dz[...], tile(s.wp, 0, model), NT).astype(BF16)

    def look_back(group):
        pairs = (group * wide // PAIR, (group + 1) * wide // PAIR)
        attend_back(s.q, s.kv, s.probs, s.dmixed, s.dq, s.dkv, s.fold, width, offset, pairs)
        cols = pl.ds(group * wide, wide)
        value_cols = pl.ds(model + group * wide, wide)
        own_lines = s.h1t[:, own_rows]
        all_lines = s.h1t[...]
        for part, sums in enumerate(
            (
                dot(own_lines, s.dq[:, cols]),
                dot(all_lines, s.dkv[:, cols]),
                dot(all_lines, s.dkv[:, value_cols]),
            )
        ):
            put_slots(s.g_qkv, pl.ds((3 * group + part) * wide, wide), sums)
        each(put_qkv[2 * group : 2 * group + 2], Reduce.begin)

    look_back(0)
    each(put_proj, Reduce.add_core)
    look_back(1)
    each(put_fc2[:2], Reduce.add_second)
    look_back(2)
    grad_key = dot(s.dkv[:, :model], tile(s.wq, model, model), NT)
    s.dh1[...] = grad_key + dot(s.dkv[:, model:], tile(s.wq, 2 * model, model), NT)
    s.give[...] = s.dh1[far_rows, :].astype(BF16)
    give.start()
    table_gradient(s.fold, s.table_sums, rows, keys, row_span, width, offset)

    @tiles(4 * Z_SIZE, LANES)
    def _(number, start):
        zz, yy, cc = number // 4, lax.rem(number // 2, 2), lax.rem(number, 2)
        for xx in range(2):
            s.g_table[zz, yy, cc, xx, 0] = s.table_sums[8 * xx : 8 * xx + 8, pl.ds(start, LANES)]

    each(put_table, Reduce.begin)
    each(put_fc2[2:], Reduce.add_first)
    each(put_fc1[:2], Reduce.add_first)
    each(put_table, Reduce.add_core)
    each(put_fc1[2:], Reduce.add_first)
    each(put_qkv, Reduce.add_core)
    @tiles(model // step, step)
    def _(number, start):
        cols = pl.ds(start, step)
        branch = dot(s.u[...], tile(s.w2, start, step)) + s.vec[FC2_SHIFT : FC2_SHIFT + 1, cols]
        s.out_low[:, cols] = (s.x1[:, cols] + s.vec[SCALE_TWO : SCALE_TWO + 1, cols] * branch).astype(BF16)
        s.lines[SCALE_TWO : SCALE_TWO + 1, cols] = sum_rows(s.cot_in[:, cols].astype(F32) * branch)

    hand(s.out_low, s.out)
    s.hidden_lines[...] = jnp.broadcast_to(sum_rows(s.da[...]), s.hidden_lines.shape)
    set_line(QUERY_BIAS, sum_rows(s.dq[...]))
    set_line(VALUE_BIAS, sum_rows(s.dkv[:, model:]))
    grad = s.dh1[own_rows, :] + dot(s.dq[...], tile(s.wq, 0, model), NT)
    give.wait_recv()
    grad = grad + s.take[...].astype(F32)
    set_line(GAIN_ONE, sum_rows(grad * s.n1[...]))
    set_line(SHIFT_ONE, sum_rows(grad))
    dx = s.dx1[...] + norm_rows_back(grad, s.n1[...], s.r1[:, 0:1], line(GAIN_ONE))
    s.dx_low[...] = dx.astype(BF16)
    hand(s.dx_low, s.grad_tokens)

    @tiles(8 * Z_SIZE, 1)
    def _(number, start):
        zz, yy, cc, xx = number // 8, lax.rem(number // 4, 2), lax.rem(number // 2, 2), lax.rem(number, 2)
        moved = pltpu.roll(s.lines[...], model - number * shard, 1)
        for group in range(LINES // ROW_GROUP):
            s.g_small[zz, yy, cc, xx, group] = moved[group * ROW_GROUP : (group + 1) * ROW_GROUP, :LANES]
        moved = pltpu.roll(s.hidden_lines[...], hidden - number * hidden_shard, 1)
        s.g_small[zz, yy, cc, xx, LINES // ROW_GROUP] = moved[:, :LANES]

    each(put_small, Reduce.begin)
    each(put_fc1[:2], Reduce.add_second)
    each(put_table, Reduce.add_first)
    each(put_fc1[2:], Reduce.add_second)
    each(put_small, Reduce.add_core)
    each(put_proj, Reduce.add_first)
    each(put_fc2[2:], Reduce.add_second)
    each(put_table, Reduce.add_second)
    each(put_qkv[:2], Reduce.add_first)
    each(put_qkv[2:4], Reduce.add_first)
    each(put_small, Reduce.add_first)
    each(put_qkv[4:], Reduce.add_first)
    each(put_proj, Reduce.add_second)
    each(put_table, Reduce.finish)
    each(get_table, Gather.begin_own, Gather.begin_z)
    each(put_qkv[:2], Reduce.add_second)
    each(put_small, Reduce.add_second)
    each(put_qkv[2:4], Reduce.add_second)
    each(put_fc2, Reduce.finish)
    hand(s.o_fc2, s.sum_fc2)
    each(put_qkv[4:], Reduce.add_second)
    each(get_table, Gather.second)
    each(put_fc1, Reduce.finish)
    hand(s.o_fc1, s.sum_fc1)
    each(get_table, Gather.third)
    each(put_proj, Reduce.finish)
    hand(s.o_proj, s.sum_proj)
    each(get_table, Gather.fourth)
    each(put_small, Reduce.finish)
    hand(s.o_small, s.sum_small)
    each(put_qkv[:4], Reduce.finish)
    each(get_table, Gather.arrive)
    for block in range(4 * Z_SIZE):
        slots = s.table_all.at[block // 4, block // 2 % 2, block % 2]
        start = block * LANES
        size = min(LANES, s.o_sums.shape[1] - start)
        s.o_sums[0:8, start : start + size] = slots[0, :, 0:size]
        s.o_sums[8:HEADS, start : start + size] = slots[1, 0 : HEADS - 8, 0:size]
    hand(s.o_sums, s.sum_table)
    each(put_qkv[4:], Reduce.finish)
    hand(s.o_qkv, s.sum_qkv)
    swap.wait_send()
    give.wait_send()
    for chunks in (get_pack, get_qkv, get_proj, get_fc1, get_fc2, get_table):
        each(chunks, Gather.settle)
    for chunks in (put_fc2, put_fc1, put_proj, put_qkv, put_table, put_small):
        each(chunks, Reduce.settle)
    for copy in outgoing:
        copy.wait()


def hand_kernel(count, *refs):
    small, arrays = refs[0], refs[1 : 1 + count]
    outs, lines = refs[1 + count : 1 + 2 * count], refs[1 + 2 * count :]
    for array, out in zip(arrays, outs):
        out[...] = array[...]
    for number, out in enumerate(lines):
        row = number if number < HIDDEN_LINE else LINES
        out[...] = small[row : row + 1, 0 : out.shape[1]]


def hand_out(small, arrays, sizes):
    vmem = pl.BlockSpec(memory_space=pltpu.VMEM)
    count = len(arrays)
    return pl.pallas_call(
        partial(hand_kernel, count),
        out_shape=tuple(jax.ShapeDtypeStruct(array.shape, array.dtype) for array in arrays)
        + tuple(jax.ShapeDtypeStruct((1, size), F32) for size in sizes),
        in_specs=[vmem] * (1 + count),
        out_specs=(vmem,) * (count + len(sizes)),
    )(small, *arrays)


def grouped(array):
    return array.reshape(-1, ROW_GROUP, array.shape[-1])


def run_layer(row_span, widths, counts, tokens, cotangent, vectors, w_qkv, w_proj, w_fc1, w_fc2, table):
    rows, model = tokens.shape
    keys = 2 * rows
    shard, hidden, hidden_shard = w_qkv.shape[0], w_fc1.shape[1], w_fc2.shape[0]
    smem = pl.BlockSpec(memory_space=pltpu.SMEM)
    vmem = pl.BlockSpec(memory_space=pltpu.VMEM)
    anywhere = pl.BlockSpec(memory_space=pl.ANY)
    inputs = dict(
        widths=(widths, smem),
        counts=(counts, smem),
        tokens=(tokens, anywhere),
        cot=(cotangent, anywhere),
        w_qkv=(grouped(w_qkv), anywhere),
        w_proj=(grouped(w_proj), anywhere),
        w_fc1=(grouped(w_fc1), anywhere),
        w_fc2=(grouped(w_fc2), anywhere),
        table=(table, anywhere),
    )
    for name, vector in zip(LINE_NAMES, vectors):
        inputs[name] = (vector.reshape(1, -1), anywhere)
    outputs = dict(
        out=((rows, model), BF16),
        grad_tokens=((rows, model), BF16),
        sum_small=((SLOT_ROWS, LANES), F32),
        sum_qkv=((shard, 3 * model), F32),
        sum_proj=((shard, model), F32),
        sum_fc1=((shard, hidden), F32),
        sum_fc2=((hidden_shard, model), F32),
        sum_table=((HEADS, table.shape[1]), F32),
    )
    entries = -(-table.shape[1] // (2 * LANES)) * 2 * LANES
    scratch = dict(
        raw=((HIDDEN_LINE, 1, shard), BF16),
        raw_hidden=((1, hidden_shard), BF16),
        table_in=(table.shape, BF16),
        tokens_in=((rows, model), BF16),
        cot_in=((rows, model), BF16),
        out_low=((rows, model), BF16),
        dx_low=((rows, model), BF16),
        o_small=((SLOT_ROWS, LANES), F32),
        o_qkv=((shard, 3 * model), F32),
        o_proj=((shard, model), F32),
        o_fc1=((shard, hidden), F32),
        o_fc2=((hidden_shard, model), F32),
        o_sums=((HEADS, table.shape[1]), F32),
        pack=((SLOT_ROWS // ROW_GROUP, ROW_GROUP, LANES), F32),
        table_lines=((HEAD_ROWS, entries), BF16),
        table_all=((Z_SIZE, 2, 2, 2, 8, LANES), F32),
        o_table=((8, LANES), F32),
        far_tokens=((rows, model), BF16),
        give=((rows, model), BF16),
        take=((rows, model), BF16),
        packs=((Z_SIZE, 2, 2, 2 * SLOT_ROWS // ROW_GROUP, ROW_GROUP, LANES), F32),
        wq=((Z_SIZE, 2, 2, 2 * shard // ROW_GROUP, ROW_GROUP, 3 * model), BF16),
        wp=((Z_SIZE, 2, 2, 2 * shard // ROW_GROUP, ROW_GROUP, model), BF16),
        w1=((Z_SIZE, 2, 2, 2 * shard // ROW_GROUP, ROW_GROUP, hidden), BF16),
        w2=((Z_SIZE, 2, 2, 2 * hidden_shard // ROW_GROUP, ROW_GROUP, model), BF16),
        vec=((LINES, model), F32),
        b1=((8, hidden), F32),
        diag=((HEAD_ROWS, 2 * (rows + keys)), F32),
        h1=((keys, model), BF16),
        h1t=((model, keys), BF16),
        n1=((rows, model), F32),
        r1=((rows, LANES), F32),
        q=((rows, model), BF16),
        kv=((keys, 2 * model), BF16),
        probs=((HEADS, rows, keys), F32),
        mixed=((rows, model), BF16),
        mixedt=((model, rows), BF16),
        z=((rows, model), F32),
        x1=((rows, model), F32),
        n2=((rows, model), F32),
        r2=((rows, LANES), F32),
        h2=((rows, model), BF16),
        h2t=((model, rows), BF16),
        u=((rows, hidden), BF16),
        ut=((hidden, rows), BF16),
        slope=((rows, hidden), F32),
        dm=((rows, model), BF16),
        da=((rows, hidden), BF16),
        dx1=((rows, model), F32),
        dz=((rows, model), BF16),
        dmixed=((rows, model), BF16),
        dq=((rows, model), BF16),
        dkv=((keys, 2 * model), BF16),
        dh1=((keys, model), F32),
        dh2=((rows, model), F32),
        fold=(((rows + keys) // LANES, 2 * HEAD_ROWS * 8, LANES), F32),
        table_sums=((HEAD_ROWS, entries), F32),
        lines=((LINES, model), F32),
        hidden_lines=((8, hidden), F32),
    )
    stages = []
    chunks = 0
    for slot_rows, slot_width, dtype, cuts in (
        (hidden_shard, model, BF16, fc2_cuts(model)),
        (shard, hidden, BF16, quarters(hidden)),
        (shard, model, BF16, halves(model, False)),
        (shard, 3 * model, BF16, qkv_cuts(model)),
        (8, LANES, F32, [(0, LANES, False)]),
        (SLOT_ROWS, LANES, F32, [(0, LANES, False)]),
    ):
        groups = slot_rows // ROW_GROUP
        stages.append(((Z_SIZE, 2, 2, 2, groups, ROW_GROUP, slot_width), dtype))
        stages.append(((Z_SIZE, 2, 2, groups, ROW_GROUP, slot_width), dtype))
        for _, size, early in cuts:
            leads = ((Z_SIZE, 2), (Z_SIZE,), (Z_SIZE - 1,))
            if early:
                leads = ((Z_SIZE - 1, 2, 2), (2, 2), (2,), ())
            for lead in leads:
                stages.append((lead + (groups, ROW_GROUP, size), dtype))
            chunks += 1
    gathers = 13
    sends, recvs = 2 + gathers + chunks, 2 + 7 * gathers + 4 * chunks
    names = list(inputs) + list(outputs) + list(scratch)
    return pl.pallas_call(
        partial(layer_kernel, names, row_span),
        out_shape=tuple(jax.ShapeDtypeStruct(shape, dtype) for shape, dtype in outputs.values()),
        in_specs=[spec for _, spec in inputs.values()],
        out_specs=(anywhere,) * len(outputs),
        scratch_shapes=[pltpu.VMEM(shape, dtype) for shape, dtype in list(scratch.values()) + stages]
        + [
            pltpu.SemaphoreType.DMA((sends,)),
            pltpu.SemaphoreType.DMA((recvs,)),
            pltpu.SemaphoreType.DMA((HIDDEN_LINE + 4 + gathers,)),
        ],
        compiler_params=pltpu.CompilerParams(
            collective_id=0, has_side_effects=True, vmem_limit_bytes=VMEM_LIMIT
        ),
    )(*[array for array, _ in inputs.values()])


def layer_norm(values, gain, shift):
    centred = values - jnp.mean(values, axis=-1, keepdims=True)
    inv_std = lax.rsqrt(jnp.mean(centred * centred, axis=-1, keepdims=True) + EPSILON)
    normed = centred * inv_std
    return (normed * gain + shift, normed, inv_std)


def norm_back(grad_out, normed, inv_std, gain):
    scaled = grad_out * gain
    return inv_std * (
        scaled
        - jnp.mean(scaled, axis=-1, keepdims=True)
        - normed * jnp.mean(scaled * normed, axis=-1, keepdims=True)
    )


def row_sum(values):
    return jnp.sum(values.astype(jnp.float32), axis=0)


def per_device_native(
    tokens,
    cotangent,
    counts,
    widths,
    norm1_gain,
    norm1_shift,
    w_qkv,
    q_bias,
    v_bias,
    w_proj,
    proj_bias,
    gamma1,
    norm2_gain,
    norm2_shift,
    w_fc1,
    fc1_bias,
    w_fc2,
    fc2_bias,
    gamma2,
    bias_table,
):
    fetched = (
        lax.all_gather(norm1_gain, ("img", "seq"), axis=0, tiled=True),
        lax.all_gather(norm1_shift, ("img", "seq"), axis=0, tiled=True),
        lax.all_gather(w_qkv, ("img", "seq"), axis=0, tiled=True),
        lax.all_gather(q_bias, ("img", "seq"), axis=0, tiled=True),
        lax.all_gather(v_bias, ("img", "seq"), axis=0, tiled=True),
        lax.all_gather(w_proj, ("img", "seq"), axis=0, tiled=True),
        lax.all_gather(proj_bias, ("img", "seq"), axis=0, tiled=True),
        lax.all_gather(gamma1, ("img", "seq"), axis=0, tiled=True),
        lax.all_gather(norm2_gain, ("img", "seq"), axis=0, tiled=True),
        lax.all_gather(norm2_shift, ("img", "seq"), axis=0, tiled=True),
        lax.all_gather(w_fc1, ("img", "seq"), axis=0, tiled=True),
        lax.all_gather(fc1_bias, ("img", "seq"), axis=0, tiled=True),
        lax.all_gather(w_fc2, ("img", "seq"), axis=0, tiled=True),
        lax.all_gather(fc2_bias, ("img", "seq"), axis=0, tiled=True),
        lax.all_gather(gamma2, ("img", "seq"), axis=0, tiled=True),
    )
    (
        gain_one,
        shift_one,
        qkv_weight,
        query_bias,
        value_bias,
        proj_weight,
        proj_shift,
        scale_one,
        gain_two,
        shift_two,
        fc1_weight,
        fc1_shift,
        fc2_weight,
        fc2_shift,
        scale_two,
    ) = fetched
    gain_one = gain_one.astype(jnp.float32)
    shift_one = shift_one.astype(jnp.float32)
    proj_shift = proj_shift.astype(jnp.float32)
    scale_one = scale_one.astype(jnp.float32)
    gain_two = gain_two.astype(jnp.float32)
    shift_two = shift_two.astype(jnp.float32)
    fc1_shift = fc1_shift.astype(jnp.float32)
    fc2_shift = fc2_shift.astype(jnp.float32)
    scale_two = scale_two.astype(jnp.float32)
    local_rows = tokens.shape[0]
    width_model = tokens.shape[1]
    seq_len = local_rows * lax.axis_size("seq")
    offset = lax.axis_index("seq") * local_rows
    row_span = (seq_len - 1) // (SIDE // 2) + 1
    table_rows = bias_table.shape[0]
    entries = -(-table_rows // (2 * LANES)) * 2 * LANES
    table_lines = jnp.pad(
        bias_table.T, ((0, HEAD_ROWS - HEADS), (0, entries - table_rows))
    )
    scalars = jnp.stack([widths[0], counts[0], offset.astype(jnp.int32)])
    smem = pl.BlockSpec(memory_space=pltpu.SMEM)
    vmem = pl.BlockSpec(memory_space=pltpu.VMEM)
    params = pltpu.CompilerParams(vmem_limit_bytes=40 << 20)

    inputs_f = tokens.astype(jnp.float32)
    normed_full, normed_one, inv_std_one = layer_norm(inputs_f, gain_one, shift_one)
    normed_low = normed_full.astype(jnp.bfloat16)
    qkv_shift = jnp.concatenate(
        [query_bias, jnp.zeros((width_model,), jnp.bfloat16), value_bias]
    ).astype(jnp.float32)
    projected = (
        jnp.dot(normed_low, qkv_weight, preferred_element_type=jnp.float32) + qkv_shift
    ).astype(jnp.bfloat16)
    queries = projected[:, :width_model]
    key_local = projected[:, width_model:]
    keys_all = lax.all_gather(key_local, "seq", axis=0, tiled=True)

    attn_low, probs = pl.pallas_call(
        partial(attend_kernel, row_span),
        out_shape=(
            jax.ShapeDtypeStruct((local_rows, width_model), BF16),
            jax.ShapeDtypeStruct((HEADS, local_rows, seq_len), F32),
        ),
        in_specs=[smem, vmem, vmem, vmem],
        out_specs=(vmem, vmem),
        scratch_shapes=[pltpu.VMEM((HEAD_ROWS, 2 * (local_rows + seq_len)), F32)],
        compiler_params=params,
    )(scalars, queries, keys_all, table_lines)
    branch_one = jnp.dot(attn_low, proj_weight, preferred_element_type=jnp.float32) + proj_shift
    residual_one = inputs_f + scale_one * branch_one
    normed_full_two, normed_two, inv_std_two = layer_norm(residual_one, gain_two, shift_two)
    normed_low_two = normed_full_two.astype(jnp.bfloat16)
    pre_act = jnp.dot(normed_low_two, fc1_weight, preferred_element_type=jnp.float32) + fc1_shift
    activated, gelu_pull = jax.vjp(partial(jax.nn.gelu, approximate=False), pre_act)
    hidden = activated.astype(jnp.bfloat16)
    branch_two = jnp.dot(hidden, fc2_weight, preferred_element_type=jnp.float32) + fc2_shift
    output = (residual_one + scale_two * branch_two).astype(jnp.bfloat16)
    grad_out = cotangent.astype(jnp.float32)
    grad_scale_two = jnp.sum(grad_out * branch_two, axis=0)
    grad_branch_two = (scale_two * grad_out).astype(jnp.bfloat16)
    grad_fc2_weight = jnp.einsum(
        "tf,td->fd", hidden, grad_branch_two, preferred_element_type=jnp.float32
    )
    grad_fc2_shift = row_sum(grad_branch_two)
    grad_hidden = jnp.einsum(
        "td,fd->tf", grad_branch_two, fc2_weight, preferred_element_type=jnp.float32
    )
    grad_pre = gelu_pull(grad_hidden)[0].astype(jnp.bfloat16)
    grad_fc1_weight = jnp.einsum(
        "td,tf->df", normed_low_two, grad_pre, preferred_element_type=jnp.float32
    )
    grad_fc1_shift = row_sum(grad_pre)
    grad_normed_two = jnp.einsum(
        "tf,df->td", grad_pre, fc1_weight, preferred_element_type=jnp.float32
    )
    grad_gain_two = jnp.sum(grad_normed_two * normed_two, axis=0)
    grad_shift_two = jnp.sum(grad_normed_two, axis=0)
    grad_resid = grad_out + norm_back(grad_normed_two, normed_two, inv_std_two, gain_two)
    grad_scale_one = jnp.sum(grad_resid * branch_one, axis=0)
    grad_branch_one = (scale_one * grad_resid).astype(jnp.bfloat16)
    grad_proj_weight = jnp.einsum(
        "td,te->de", attn_low, grad_branch_one, preferred_element_type=jnp.float32
    )
    grad_proj_shift = row_sum(grad_branch_one)
    grad_attn = jnp.einsum(
        "te,de->td", grad_branch_one, proj_weight, preferred_element_type=jnp.float32
    ).astype(jnp.bfloat16)
    grad_query, key_terms, table_grad = pl.pallas_call(
        partial(attend_back_kernel, row_span),
        out_shape=(
            jax.ShapeDtypeStruct((local_rows, width_model), BF16),
            jax.ShapeDtypeStruct((seq_len, 2 * width_model), BF16),
            jax.ShapeDtypeStruct((HEAD_ROWS, entries), F32),
        ),
        in_specs=[smem, vmem, vmem, vmem, vmem],
        out_specs=(vmem, vmem, vmem),
        scratch_shapes=[
            pltpu.VMEM(((local_rows + seq_len) // LANES, 2 * HEAD_ROWS * 8, LANES), F32)
        ],
        compiler_params=params,
    )(scalars, queries, keys_all, probs, grad_attn)
    own_terms = lax.psum_scatter(key_terms, "seq", scatter_dimension=0, tiled=True)
    grad_qkv = jnp.concatenate([grad_query, own_terms], axis=1)
    grad_qkv_weight = jnp.einsum(
        "td,te->de", normed_low, grad_qkv, preferred_element_type=jnp.float32
    )
    grad_query_bias = row_sum(grad_qkv[:, :width_model])
    grad_value_bias = row_sum(grad_qkv[:, 2 * width_model :])
    grad_normed_one = jnp.einsum(
        "te,de->td", grad_qkv, qkv_weight, preferred_element_type=jnp.float32
    )
    grad_gain_one = jnp.sum(grad_normed_one * normed_one, axis=0)
    grad_shift_one = jnp.sum(grad_normed_one, axis=0)
    grad_inputs = (
        grad_resid + norm_back(grad_normed_one, normed_one, inv_std_one, gain_one)
    ).astype(jnp.bfloat16)
    summed = (
        lax.psum_scatter(grad_gain_one, ("img", "seq"), scatter_dimension=0, tiled=True),
        lax.psum_scatter(grad_shift_one, ("img", "seq"), scatter_dimension=0, tiled=True),
        lax.psum_scatter(grad_qkv_weight, ("img", "seq"), scatter_dimension=0, tiled=True),
        lax.psum_scatter(grad_query_bias, ("img", "seq"), scatter_dimension=0, tiled=True),
        lax.psum_scatter(grad_value_bias, ("img", "seq"), scatter_dimension=0, tiled=True),
        lax.psum_scatter(grad_proj_weight, ("img", "seq"), scatter_dimension=0, tiled=True),
        lax.psum_scatter(grad_proj_shift, ("img", "seq"), scatter_dimension=0, tiled=True),
        lax.psum_scatter(grad_scale_one, ("img", "seq"), scatter_dimension=0, tiled=True),
        lax.psum_scatter(grad_gain_two, ("img", "seq"), scatter_dimension=0, tiled=True),
        lax.psum_scatter(grad_shift_two, ("img", "seq"), scatter_dimension=0, tiled=True),
        lax.psum_scatter(grad_fc1_weight, ("img", "seq"), scatter_dimension=0, tiled=True),
        lax.psum_scatter(grad_fc1_shift, ("img", "seq"), scatter_dimension=0, tiled=True),
        lax.psum_scatter(grad_fc2_weight, ("img", "seq"), scatter_dimension=0, tiled=True),
        lax.psum_scatter(grad_fc2_shift, ("img", "seq"), scatter_dimension=0, tiled=True),
        lax.psum_scatter(grad_scale_two, ("img", "seq"), scatter_dimension=0, tiled=True),
    )
    table_total = lax.psum(table_grad, ("img", "seq"))[:HEADS, :table_rows].T
    return (output, grad_inputs) + tuple(summed) + (table_total,)


def per_device_linked(
    tokens,
    cotangent,
    counts,
    widths,
    norm1_gain,
    norm1_shift,
    w_qkv,
    q_bias,
    v_bias,
    w_proj,
    proj_bias,
    gamma1,
    norm2_gain,
    norm2_shift,
    w_fc1,
    fc1_bias,
    w_fc2,
    fc2_bias,
    gamma2,
    bias_table,
):
    seq_len = tokens.shape[0] * lax.axis_size("seq")
    row_span = (seq_len - 1) // (SIDE // 2) + 1
    vectors = [
        norm1_gain, norm1_shift, q_bias, v_bias, proj_bias, gamma1, norm2_gain, norm2_shift, fc2_bias, gamma2, fc1_bias,
    ]
    output, grad_tokens, small, *sums = run_layer(
        row_span, widths, counts, tokens, cotangent, vectors, w_qkv, w_proj, w_fc1, w_fc2, bias_table.T
    )
    sizes = [vector.shape[0] for vector in vectors]
    output, grad_tokens, sum_qkv, sum_proj, sum_fc1, sum_fc2, table_total, *lines = hand_out(
        small, [output, grad_tokens, *sums], sizes
    )
    lines = [line.reshape(-1) for line in lines]
    return (
        output, grad_tokens, lines[GAIN_ONE], lines[SHIFT_ONE], sum_qkv, lines[QUERY_BIAS], lines[VALUE_BIAS],
        sum_proj, lines[PROJ_SHIFT], lines[SCALE_ONE], lines[GAIN_TWO], lines[SHIFT_TWO], sum_fc1,
        lines[HIDDEN_LINE], sum_fc2, lines[FC2_SHIFT], lines[SCALE_TWO], table_total.T,
    )


def per_device(*arrays):
    tokens, bias_table = arrays[0], arrays[19]
    linked = lax.axis_size("img") == 4 * Z_SIZE and lax.axis_size("seq") == 2
    linked = linked and arrays[6].shape[0] % 8 == 0 and tokens.shape[0] == LANES
    linked = linked and 15 * LANES < bias_table.shape[0] <= 4 * Z_SIZE * LANES
    return per_device_linked(*arrays) if linked else per_device_native(*arrays)


def solution(mesh):
    return jax.shard_map(
        per_device,
        mesh=mesh,
        in_specs=(
            P(("img", "seq"), None),
            P(("img", "seq"), None),
            P("img"),
            P("img"),
            P(("img", "seq")),
            P(("img", "seq")),
            P(("img", "seq"), None),
            P(("img", "seq")),
            P(("img", "seq")),
            P(("img", "seq"), None),
            P(("img", "seq")),
            P(("img", "seq")),
            P(("img", "seq")),
            P(("img", "seq")),
            P(("img", "seq"), None),
            P(("img", "seq")),
            P(("img", "seq"), None),
            P(("img", "seq")),
            P(("img", "seq")),
            P(),
        ),
        out_specs=(
            P(("img", "seq"), None),
            P(("img", "seq"), None),
            P(("img", "seq")),
            P(("img", "seq")),
            P(("img", "seq"), None),
            P(("img", "seq")),
            P(("img", "seq")),
            P(("img", "seq"), None),
            P(("img", "seq")),
            P(("img", "seq")),
            P(("img", "seq")),
            P(("img", "seq")),
            P(("img", "seq"), None),
            P(("img", "seq")),
            P(("img", "seq"), None),
            P(("img", "seq")),
            P(("img", "seq")),
            P(),
        ),
        check_vma=False,
    )
```

```python
from functools import partial

import jax
import jax.numpy as jnp
from jax import lax
from jax.experimental import pallas as pl
from jax.experimental.pallas import tpu as pltpu
from jax.sharding import PartitionSpec as P

HEADS = 12
HEAD_DIM = 64
SIDE = 32
PAIR = 2 * HEAD_DIM
PAIRS = HEADS // 2
HEAD_ROWS = 16
LANES = 128
F32 = jnp.float32
BF16 = jnp.bfloat16
NT = (((1,), (1,)), ((), ()))
TN = (((0,), (0,)), ((), ()))


VMEM_LIMIT = 63 << 20
ROW_GROUP = 8
EPSILON = 1e-06
NEG_FILL = -1e30


def dot(left, right, dims=(((1,), (0,)), ((), ()))):
    return lax.dot_general(left, right, dims, preferred_element_type=F32)


def iota(shape, dim):
    return lax.broadcasted_iota(jnp.int32, shape, dim)


def floor_div(values, width):
    return jnp.floor((values.astype(F32) + 0.5) / width.astype(F32)).astype(jnp.int32)


def table_index(place, span, rows, row_span, width, offset):
    right = place >= span
    diagonal = offset + rows - 1 - jnp.where(right, place - span, place)
    row = floor_div(diagonal, width)
    col = diagonal - row * width
    row = jnp.where(right, row + 1, row)
    col = jnp.where(right, col - width, col)
    return (row + row_span - 1) * (2 * SIDE - 1) + col + SIDE - 1


def same_side(rows, keys, width, offset):
    query = iota((rows, keys), 0) + offset
    key = iota((rows, keys), 1)
    return (query - floor_div(query, width) * width) >= (key - floor_div(key, width) * width)


def fill_diagonals(table_ref, diag_ref, rows, keys, row_span, width, offset):
    span = rows + keys
    entries = table_ref.shape[1]
    step = 2 * LANES
    index = table_index(iota((step, 2 * span), 1), span, rows, row_span, width, offset)
    entry = iota((step, 2 * span), 0)
    diag_ref[...] = jnp.zeros_like(diag_ref)

    def add(chunk, carry):
        start = pl.multiple_of(chunk * step, step)
        chosen = jnp.where(entry + start == index, 1.0, 0.0).astype(BF16)
        diag_ref[...] += dot(table_ref[:, pl.ds(start, step)], chosen)
        return carry

    lax.fori_loop(0, entries // step, add, 0)


def half_mask(shape, half):
    lane = iota(shape, 1)
    return lane < HEAD_DIM if half == 0 else lane >= HEAD_DIM


def pick(values, half):
    return jnp.where(half_mask(values.shape, half), values, jnp.zeros_like(values))


def attend(query_ref, kv_ref, diag_ref, probs_ref, mixed_ref, width, count, offset, pairs=(0, PAIRS)):
    rows, model = query_ref.shape
    keys = kv_ref.shape[0]
    span = rows + keys
    same = same_side(rows, keys, width, offset)
    valid = iota((rows, keys), 1) < count

    def one_pair(pair, carry):
        cols = pl.ds(pl.multiple_of(pair * PAIR, PAIR), PAIR)
        value_cols = pl.ds(pl.multiple_of(model + pair * PAIR, PAIR), PAIR)
        query_pair = query_ref[:, cols]
        key_pair = kv_ref[:, cols]
        value_pair = kv_ref[:, value_cols]
        mixed = jnp.zeros((rows, PAIR), F32)
        for half in range(2):
            head = pair * 2 + half
            product = dot(pick(query_pair, half), key_pair, NT)
            shifted = []
            for side in range(2):
                line = diag_ref[pl.ds(head, 1), side * span : (side + 1) * span]
                line = jnp.broadcast_to(line, (rows, span))
                line = pltpu.roll(line, keys + 1, 1, stride=1, stride_axis=0)
                shifted.append(line[:, :keys])
            scores = product * HEAD_DIM**-0.5 + jnp.where(same, shifted[0], shifted[1])
            scores = jnp.where(valid, scores, NEG_FILL)
            terms = jnp.exp(scores - jnp.max(scores, axis=1, keepdims=True))
            terms = jnp.where(valid, terms, 0.0)
            probs = terms / jnp.sum(terms, axis=1, keepdims=True)
            probs_ref[head] = probs
            mixed = mixed + dot(probs.astype(BF16), pick(value_pair, half))
        mixed_ref[:, cols] = mixed.astype(BF16)
        return carry

    lax.fori_loop(*pairs, one_pair, 0)


def fold_rows(values):
    while values.shape[0] > 8:
        half = values.shape[0] // 2
        values = values[half:] + pltpu.roll(values[:half], half, 1)
    return values


def attend_back(
    query_ref, kv_ref, probs_ref, grad_ref, grad_query_ref, grad_kv_ref, fold_ref, width, offset, pairs=(0, PAIRS)
):
    rows, model = query_ref.shape
    keys = kv_ref.shape[0]
    same = same_side(rows, keys, width, offset)

    def one_pair(pair, carry):
        cols = pl.ds(pl.multiple_of(pair * PAIR, PAIR), PAIR)
        value_cols = pl.ds(pl.multiple_of(model + pair * PAIR, PAIR), PAIR)
        query_pair = query_ref[:, cols]
        key_pair = kv_ref[:, cols]
        value_pair = kv_ref[:, value_cols]
        grad_pair = grad_ref[:, cols]
        grad_query = jnp.zeros((rows, PAIR), F32)
        grad_key = jnp.zeros((keys, PAIR), F32)
        grad_value = jnp.zeros((keys, PAIR), F32)
        for half in range(2):
            head = pair * 2 + half
            probs = probs_ref[head]
            grad_half = pick(grad_pair, half)
            grad_probs = dot(grad_half, value_pair, NT)
            grad_scores = probs * (
                grad_probs - jnp.sum(probs * grad_probs, axis=1, keepdims=True)
            )
            blank = jnp.zeros((rows, rows), F32)
            left = jnp.where(same, grad_scores, 0.0)
            right = jnp.where(same, 0.0, grad_scores)
            for side, part in enumerate((left, right)):
                place = pl.multiple_of((side * HEAD_ROWS + head) * 8, 8)
                folded = fold_rows(jnp.concatenate([part, blank], axis=1))
                for block in range((rows + keys) // LANES):
                    fold_ref[block, pl.ds(place, 8), :] = folded[:, block * LANES : (block + 1) * LANES]
            grad_prod = (grad_scores * HEAD_DIM**-0.5).astype(BF16)
            grad_query = grad_query + dot(grad_prod, pick(key_pair, half))
            grad_key = grad_key + dot(grad_prod, pick(query_pair, half), TN)
            grad_value = grad_value + dot(probs.astype(BF16), grad_half, TN)
        grad_query_ref[:, cols] = grad_query.astype(BF16)
        grad_kv_ref[:, cols] = grad_key.astype(BF16)
        grad_kv_ref[:, value_cols] = grad_value.astype(BF16)
        return carry

    lax.fori_loop(*pairs, one_pair, 0)


def table_gradient(fold_ref, out_ref, rows, keys, row_span, width, offset):
    span = rows + keys
    lines = 2 * HEAD_ROWS
    total = jnp.zeros((lines, span), F32)
    for row in range(8):
        blocks = [fold_ref[block, pl.ds(row, lines, stride=8), :] for block in range(span // LANES)]
        moved = jnp.concatenate(blocks, axis=1)
        total = total + (pltpu.roll(moved, 7 - row, 1) if row < 7 else moved)
    parts = []
    for side in range(2):
        rest = total[side * HEAD_ROWS : (side + 1) * HEAD_ROWS]
        pieces = []
        for _ in range(3):
            piece = rest.astype(BF16)
            rest = rest - piece.astype(F32)
            pieces.append(piece)
        parts.append(jnp.concatenate(pieces, axis=0))
    place = iota((span, LANES), 0)
    index = [
        table_index(place + side * span, span, rows, row_span, width, offset) for side in range(2)
    ]
    entry = iota((span, LANES), 1)

    def put(chunk, carry):
        start = pl.multiple_of(chunk * LANES, LANES)
        sums = jnp.zeros((3 * HEAD_ROWS, LANES), F32)
        for side in range(2):
            chosen = jnp.where(entry + start == index[side], 1.0, 0.0).astype(BF16)
            sums = sums + dot(parts[side], chosen)
        out_ref[:, pl.ds(start, LANES)] = (
            sums[:HEAD_ROWS] + sums[HEAD_ROWS : 2 * HEAD_ROWS] + sums[2 * HEAD_ROWS :]
        )
        return carry

    lax.fori_loop(0, out_ref.shape[1] // LANES, put, 0)


def attend_kernel(row_span, scal_ref, query_ref, kv_ref, table_ref, mixed_ref, probs_ref, diag_ref):
    rows, keys = query_ref.shape[0], kv_ref.shape[0]
    width, count, offset = scal_ref[0], scal_ref[1], scal_ref[2]
    fill_diagonals(table_ref, diag_ref, rows, keys, row_span, width, offset)
    attend(query_ref, kv_ref, diag_ref, probs_ref, mixed_ref, width, count, offset)


def attend_back_kernel(
    row_span, scal_ref, query_ref, kv_ref, probs_ref, grad_ref, grad_query_ref, grad_kv_ref, table_ref, fold_ref
):
    rows, keys = query_ref.shape[0], kv_ref.shape[0]
    width, offset = scal_ref[0], scal_ref[2]
    fold_ref[...] = jnp.zeros_like(fold_ref)
    attend_back(
        query_ref, kv_ref, probs_ref, grad_ref, grad_query_ref, grad_kv_ref, fold_ref, width, offset
    )
    table_gradient(fold_ref, table_ref, rows, keys, row_span, width, offset)


MESH = pl.DeviceIdType.MESH
Z_SIZE = 4


class Place:
    def __init__(self):
        img = lax.axis_index("img")
        self.x = lax.axis_index("seq")
        self.c = lax.rem(img, 2)
        self.y = lax.rem(img // 2, 2)
        self.z = img // 4

    def at(self, z=None, y=None, c=None, x=None):
        z = self.z if z is None else z
        y = self.y if y is None else y
        c = self.c if c is None else c
        x = self.x if x is None else x
        return {"img": (z * 2 + y) * 2 + c, "seq": x}

    def sibling(self):
        return self.at(c=1 - self.c)

    def over_x(self):
        return self.at(x=1 - self.x)

    def over_y(self):
        return self.at(y=1 - self.y)

    def z_of(self, step):
        return lax.rem(self.z + step, Z_SIZE)

    def partners(self):
        return [self.sibling(), self.over_x(), self.over_y()] + [
            self.at(z=self.z_of(step)) for step in range(1, Z_SIZE)
        ]


def meet(place):
    barrier = pltpu.get_barrier_semaphore()
    partners = place.partners()
    for partner in partners:
        pl.semaphore_signal(barrier, inc=1, device_id=partner, device_id_type=MESH)
    pl.semaphore_wait(barrier, len(partners))


class Sems:
    def __init__(self, send, recv, place):
        self.send, self.recv, self.place = send, recv, place
        self.sends = self.recvs = 0

    def take_send(self):
        self.sends += 1
        return self.send.at[self.sends - 1]

    def take_recv(self):
        self.recvs += 1
        return self.recv.at[self.recvs - 1]

    def copy(self, src, dst, device, sent=None, came=None):
        return pltpu.make_async_remote_copy(
            src_ref=src,
            dst_ref=dst,
            send_sem=self.take_send() if sent is None else sent,
            recv_sem=self.take_recv() if came is None else came,
            device_id=device,
            device_id_type=MESH,
        )

    def total(self, ref, sem):
        return pltpu.make_async_remote_copy(
            src_ref=ref,
            dst_ref=ref,
            send_sem=sem,
            recv_sem=sem,
            device_id=self.place.sibling(),
            device_id_type=MESH,
        )


class Gather:
    def __init__(self, place, src, slots, cols, x_last, sems, local_sem):
        z, y, c, x = place.z, place.y, place.c, place.x
        groups = src.shape[0]
        every = slice(None)

        def part(a, b, e):
            return slots.at[a, b, c, pl.ds(e * groups, groups), :, cols]

        mine = src.at[:, :, cols]
        own = part(z, y, x)
        self.z = z
        self.local = pltpu.make_async_copy(mine, own, local_sem)
        sent = sems.take_send()
        came = [sems.take_recv() for _ in range(1, Z_SIZE)]
        self.along_z = [
            sems.copy(mine, own, place.at(z=place.z_of(step)), sent, came[step - 1])
            for step in range(1, Z_SIZE)
        ]
        line = part(every, y, x)
        mid_line = part(every, 1 - y, x) if x_last else part(every, y, 1 - x)
        far_line = part(every, y, 1 - x) if x_last else part(every, 1 - y, x)
        cross_line = part(every, 1 - y, 1 - x)
        mid, last = place.over_y(), place.over_x()
        if not x_last:
            mid, last = last, mid
        sibling = place.sibling()
        mid_came, last_came, core_came = sems.take_recv(), sems.take_recv(), sems.take_recv()
        self.own_mid = sems.copy(mine, own, mid, sent, mid_came)
        self.own_last = sems.copy(mine, own, last, sent, last_came)
        pieces = [part(place.z_of(Z_SIZE - step), y, x) for step in range(1, Z_SIZE)]
        self.line_mid = [sems.copy(piece, piece, mid, sent, mid_came) for piece in pieces]
        self.line_last = [sems.copy(piece, piece, last, sent, last_came) for piece in pieces]
        self.line_core = sems.copy(line, line, sibling, sent, core_came)
        self.mid_last = sems.copy(mid_line, mid_line, last, sent)
        self.mid_core = sems.copy(mid_line, mid_line, sibling, sent, core_came)
        self.far_core = sems.copy(far_line, far_line, sibling, sent, core_came)
        self.cross_core = sems.copy(cross_line, cross_line, sibling, sent, core_came)
        self.all_mid = sems.total(mid_line, mid_came)
        self.all_last = sems.total(far_line, last_came)
        self.all_core = sems.total(slots.at[:, :, 1 - c, :, :, cols], core_came)
        flat = slots.reshape((8 * Z_SIZE * groups,) + slots.shape[4:])
        self.all_sent = sems.total(flat.at[pl.ds(0, (8 * Z_SIZE - 1) * groups), :, cols], sent)

    def begin_own(self):
        self.local.start()
        self.own_mid.start()
        self.own_last.start()

    def begin_z(self):
        for copy in self.along_z:
            copy.start()

    def pass_on(self, number):
        self.line_mid[number].start()
        self.line_last[number].start()

    def second(self):

        def take(number):
            self.along_z[number].wait_recv()
            self.pass_on(number)

        @pl.when(self.z >= Z_SIZE // 2)
        def _():
            for number in range(Z_SIZE - 1):
                take(number)

        @pl.when(self.z < Z_SIZE // 2)
        def _():
            for number in reversed(range(Z_SIZE - 1)):
                take(number)

        self.local.wait()
        self.line_core.start()

    def third(self):
        self.all_mid.wait_recv()
        self.mid_last.start()
        self.mid_core.start()

    def fourth(self):
        self.all_last.wait_recv()
        self.far_core.start()
        self.mid_last.wait_recv()
        self.cross_core.start()

    def arrive(self):
        self.all_core.wait_recv()

    def settle(self):
        self.all_sent.wait_send()


class GatherLate(Gather):
    def __init__(self, place, src, slots, cols, x_last, sems, local_sem):
        z, y, c, x = place.z, place.y, place.c, place.x
        groups = src.shape[0]
        sibling = place.sibling()

        def plane(a):
            return slots.at[a, :, c, :, :, cols]

        def part(b, e):
            return slots.at[z, b, c, pl.ds(e * groups, groups), :, cols]

        mine = src.at[:, :, cols]
        own = part(y, x)
        self.local = pltpu.make_async_copy(mine, own, local_sem)
        sent = sems.take_send()
        near, last = place.over_x(), place.over_y()
        piece = part(y, 1 - x)
        if not x_last:
            near, last = last, near
            piece = part(1 - y, x)
        self.own_near = sems.copy(mine, own, near, sent)
        self.own_last = sems.copy(mine, own, last, sent)
        self.near_last = sems.copy(piece, piece, last, sent)
        self.along_z = [
            sems.copy(plane(z), plane(z), place.at(z=place.z_of(step)), sent) for step in range(1, Z_SIZE)
        ]
        core_came = sems.take_recv()
        self.line_core = sems.copy(plane(z), plane(z), sibling, sent, core_came)
        self.far_core = []
        for step in range(1, Z_SIZE):
            far = plane(place.z_of(Z_SIZE - step))
            self.far_core.append(sems.copy(far, far, sibling, sent, core_came))
        self.all_core = sems.total(slots.at[:, :, 1 - c, :, :, cols], core_came)
        flat = slots.reshape((8 * Z_SIZE * groups,) + slots.shape[4:])
        self.all_sent = sems.total(flat.at[pl.ds(0, (8 * Z_SIZE - 1) * groups), :, cols], sent)

    def begin_own(self):
        self.local.start()
        self.own_near.start()
        self.own_last.start()

    def begin_z(self):
        self.own_near.wait_recv()
        self.near_last.start()

    def second(self):
        self.own_last.wait_recv()
        self.near_last.wait_recv()
        self.local.wait()
        for copy in self.along_z:
            copy.start()
        self.line_core.start()

    def third(self):
        pass

    def fourth(self):
        for copy, onward in zip(self.along_z, self.far_core):
            copy.wait_recv()
            onward.start()

    def settle(self):
        self.all_sent.wait_send()


class Reduce:
    def __init__(self, place, grad, own, first, second, third, out, start, size, x_first, sems, pieces=None):
        rows = out.shape[0]

        def flat(ref):
            return ref.reshape(ref.shape[:-3] + (rows, ref.shape[-1]))

        self.place, self.out = place, out
        self.grad, self.own, self.first = flat(grad), flat(own), flat(first)
        self.second, self.third = flat(second), flat(third)
        self.pieces = pieces or [(0, start, size)]
        self.x_first = x_first
        z, y, c, x = place.z, place.y, place.c, place.x
        every = slice(None)
        cols = pl.ds(start, size)
        self.cols = cols
        sent = sems.take_send()
        self.to_core = sems.copy(
            grad.at[:, :, 1 - c, :, :, :, cols], own.at[:, :, :, :, :, cols], place.sibling(), sent
        )
        over_first, over_second = place.over_x(), place.over_y()
        if x_first:
            leaving, other = own.at[:, :, 1 - x, :, :, cols], 1 - y
        else:
            over_first, over_second = over_second, over_first
            leaving, other = own.at[:, 1 - y, :, :, :, cols], 1 - x
        self.kept = y if x_first else x
        self.over_first = sems.copy(leaving, first, over_first, sent)
        self.over_second = sems.copy(first.at[:, other], second, over_second, sent)
        came = sems.take_recv()
        self.along_z = []
        for step in range(1, Z_SIZE):
            target = place.z_of(step)
            self.along_z.append(
                sems.copy(second.at[target], third.at[step - 1], place.at(z=target), sent, came)
            )
        self.all_z = sems.total(third, came)
        slots = grad.reshape((8 * Z_SIZE,) + grad.shape[4:])
        self.all_sent = sems.total(slots.at[pl.ds(0, 8 * Z_SIZE - 1), :, :, cols], sent)

    def begin(self):
        self.to_core.start()

    def add_core(self):
        self.to_core.wait_recv()
        place = self.place

        def add(zy, carry):
            z, y = zy // 2, lax.rem(zy, 2)
            for x in range(2):
                mine = self.grad[z, y, place.c, x, :, self.cols].astype(F32)
                theirs = self.own[z, y, x, :, self.cols].astype(F32)
                self.own[z, y, x, :, self.cols] = (mine + theirs).astype(self.own.dtype)
            return carry

        lax.fori_loop(0, 2 * Z_SIZE, add, 0)
        self.send_core()

    def send_core(self):
        self.over_first.start()

    def add_first(self):
        self.over_first.wait_recv()
        place = self.place

        def add(z, carry):
            for other in range(2):
                if self.x_first:
                    mine = self.own[z, other, place.x, :, self.cols].astype(F32)
                else:
                    mine = self.own[z, place.y, other, :, self.cols].astype(F32)
                theirs = self.first[z, other].astype(F32)
                self.first[z, other] = (mine + theirs).astype(self.first.dtype)
            return carry

        lax.fori_loop(0, Z_SIZE, add, 0)
        self.over_second.start()

    def add_second(self):
        self.over_second.wait_recv()

        def add(z, carry):
            mine = self.first[z, self.kept].astype(F32)
            theirs = self.second[z].astype(F32)
            self.second[z] = (mine + theirs).astype(self.second.dtype)
            return carry

        lax.fori_loop(0, Z_SIZE, add, 0)
        for copy in self.along_z:
            copy.start()

    def finish(self):
        total = self.second[self.place.z].astype(F32)
        self.all_z.wait_recv()
        for step in range(Z_SIZE - 1):
            total = total + self.third[step].astype(F32)
        for source, target, size in self.pieces:
            self.out[:, target : target + size] = total[:, source : source + size]

    def settle(self):
        self.all_sent.wait_send()


class ReduceEarly(Reduce):
    def __init__(self, place, grad, own, by_z, plane, first, second, out, start, size, x_first, sems, pieces=None):
        self.pieces = pieces or [(0, start, size)]
        self.x_first = x_first
        rows = out.shape[0]

        def flat(ref):
            return ref.reshape(ref.shape[:-3] + (rows, ref.shape[-1]))

        self.place, self.out = place, out
        self.grad, self.own, self.by_z = flat(grad), flat(own), flat(by_z)
        self.plane, self.first, self.second = flat(plane), flat(first), flat(second)
        c, x, y = place.c, place.x, place.y
        cols = pl.ds(start, size)
        self.cols = cols
        sent = sems.take_send()
        self.to_core = sems.copy(
            grad.at[:, :, 1 - c, :, :, :, cols], own.at[:, :, :, :, :, cols], place.sibling(), sent
        )
        came = sems.take_recv()
        self.along_z = []
        for step in range(1, Z_SIZE):
            target = place.z_of(step)
            self.along_z.append(
                sems.copy(
                    own.at[target, :, :, :, :, cols], by_z.at[step - 1], place.at(z=target), sent, came
                )
            )
        self.all_z = sems.total(by_z, came)
        over_first, over_second = place.over_x(), place.over_y()
        if x_first:
            leaving, other = plane.at[:, 1 - x], 1 - y
        else:
            over_first, over_second = over_second, over_first
            leaving, other = plane.at[1 - y], 1 - x
        self.kept = y if x_first else x
        self.over_first = sems.copy(leaving, first, over_first, sent)
        self.over_second = sems.copy(first.at[other], second, over_second, sent)
        slots = grad.reshape((8 * Z_SIZE,) + grad.shape[4:])
        self.all_sent = sems.total(slots.at[pl.ds(0, 8 * Z_SIZE - 1), :, :, cols], sent)

    def send_core(self):
        for copy in self.along_z:
            copy.start()

    def add_first(self):
        self.all_z.wait_recv()
        z = self.place.z
        for y in range(2):
            for x in range(2):
                total = self.own[z, y, x, :, self.cols].astype(F32)
                for step in range(Z_SIZE - 1):
                    total = total + self.by_z[step, y, x].astype(F32)
                self.plane[y, x] = total.astype(self.plane.dtype)
        self.over_first.start()

    def add_second(self):
        self.over_first.wait_recv()
        for other in range(2):
            if self.x_first:
                mine = self.plane[other, self.place.x].astype(F32)
            else:
                mine = self.plane[self.place.y, other].astype(F32)
            self.first[other] = (mine + self.first[other].astype(F32)).astype(self.first.dtype)
        self.over_second.start()

    def finish(self):
        self.over_second.wait_recv()
        total = self.first[self.kept].astype(F32) + self.second[...].astype(F32)
        for source, target, size in self.pieces:
            self.out[:, target : target + size] = total[:, source : source + size]


class Names:
    pass


def norm_rows(values):
    centred = values - jnp.mean(values, axis=1, keepdims=True)
    inv_std = lax.rsqrt(jnp.mean(centred * centred, axis=1, keepdims=True) + EPSILON)
    return centred * inv_std, inv_std


def norm_rows_back(grad_out, normed, inv_std, gain):
    scaled = grad_out * gain
    return inv_std * (
        scaled
        - jnp.mean(scaled, axis=1, keepdims=True)
        - normed * jnp.mean(scaled * normed, axis=1, keepdims=True)
    )


def sum_rows(values):
    return jnp.sum(values.astype(F32), axis=0, keepdims=True)


def div_const(values, divisor):
    return jnp.floor((values.astype(F32) + 0.5) * (1.0 / divisor)).astype(jnp.int32)


def tile(slots, start, size):
    rows = slots.shape[3] * ROW_GROUP
    view = slots.reshape(4 * Z_SIZE, rows, slots.shape[-1])
    return view[:, :, pl.ds(start, size)].reshape(-1, size)


def put_slots(slots, cols, values):
    devices = 8 * Z_SIZE
    view = slots.reshape(devices, slots.shape[4] * ROW_GROUP, slots.shape[-1])
    view[:, :, cols] = values.reshape(devices, -1, values.shape[1]).astype(slots.dtype)


def tiles(count, step):
    def wrap(body):
        def run(number, carry):
            body(number, pl.multiple_of(number * step, step))
            return carry

        lax.fori_loop(0, count, run, 0)

    return wrap


LINES = 16
SLOT_ROWS = 24
QKV_COLS = 256


def quarters(width):
    large = -(-width // 4 // LANES) * LANES
    small = width // 2 - large
    cuts = [(0, large), (large, large), (2 * large, small), (2 * large + small, small)]
    return [(start, size, False) for start, size in cuts]


def halves(width, turned):
    middle = width // 2 // LANES * LANES
    return [(0, middle, turned), (middle, width - middle, turned)]


def fc2_cuts(width):
    part = width // 3
    return [(0, part, False), (part, part, False), (2 * part, width - 2 * part, True)]


def qkv_cuts(model):
    size = 3 * QKV_COLS // 2
    return [(start, size, False) for start in range(0, 3 * model, size)]


(
    GAIN_ONE, SHIFT_ONE, QUERY_BIAS, VALUE_BIAS, PROJ_SHIFT, SCALE_ONE, GAIN_TWO, SHIFT_TWO, FC2_SHIFT, SCALE_TWO,
) = range(10)
HIDDEN_LINE = 10
LINE_NAMES = ["line" + str(number) for number in range(HIDDEN_LINE + 1)]


def unpack_lines(packed, shard, hidden_shard, vec_ref, hidden_ref):
    rows = packed.shape[0]
    devices = rows // SLOT_ROWS
    low = packed.astype(BF16)
    width = shard * devices
    lane = iota((LANES, width), 1)
    spread = jnp.where(lane - div_const(lane, shard) * shard == iota((LANES, width), 0), 1.0, 0.0)
    wide = dot(low, spread.astype(BF16))
    owner = div_const(iota((rows, width), 0), SLOT_ROWS)
    wide = jnp.where(owner == div_const(iota((rows, width), 1), shard), wide, 0.0).astype(BF16)
    row = iota((LINES, rows), 1)
    line = row - div_const(row, SLOT_ROWS) * SLOT_ROWS
    vec_ref[...] = dot(jnp.where(line == iota((LINES, rows), 0), 1.0, 0.0).astype(BF16), wide)
    row = iota((devices, rows), 1)
    chosen = jnp.where(row == iota((devices, rows), 0) * SLOT_ROWS + HIDDEN_LINE, 1.0, 0.0)
    hidden = dot(chosen.astype(BF16), low).astype(BF16)
    step = 8 * LANES
    for start in range(0, hidden_shard * devices, step):
        lane = iota((LANES, step), 1) + start
        owner = div_const(lane, hidden_shard)
        spread = jnp.where(lane - owner * hidden_shard == iota((LANES, step), 0), 1.0, 0.0)
        wide = dot(hidden, spread.astype(BF16))
        owner = div_const(iota((devices, step), 1) + start, hidden_shard)
        wide = jnp.where(owner == iota((devices, step), 0), wide, 0.0)
        hidden_ref[:, start : start + step] = jnp.broadcast_to(sum_rows(wide), (8, step))


def layer_kernel(names, row_span, *refs):
    s = Names()
    s.__dict__.update(zip(names, refs))
    buffers = list(refs[len(names) :])
    send, recv, local = buffers[-3:]
    place = Place()
    x = place.x
    rows, model = s.tokens.shape
    width, count, offset = s.widths[0], s.counts[0], x * rows
    keys = 2 * rows
    hidden = s.w_fc1.shape[2]
    shard, hidden_shard = s.w_qkv.shape[0] * ROW_GROUP, s.w_fc2.shape[0] * ROW_GROUP
    half = model // 2
    own_rows = pl.ds(pl.multiple_of(x * rows, rows), rows)
    far_rows = pl.ds(pl.multiple_of((1 - x) * rows, rows), rows)
    sems = Sems(send, recv, place)
    locals_used = []
    outgoing = []

    def move(src, dst):
        locals_used.append(0)
        copy = pltpu.make_async_copy(src, dst, local.at[len(locals_used) - 1])
        copy.start()
        return copy

    def hand(src, dst):
        copy = pltpu.make_async_copy(src, dst, local.at[len(outgoing)])
        copy.start()
        outgoing.append(copy)

    def gather(src, slots, cuts):
        chunks = []
        for number, (start, size, late) in enumerate(cuts):
            locals_used.append(0)
            sem = local.at[len(locals_used) - 1]
            kind = GatherLate if late else Gather
            chunks.append(kind(place, src, slots, pl.ds(start, size), number % 2 == 0, sems, sem))
        return chunks

    def reduce(out, cuts, pieces):
        chunks = []
        grad, own = buffers.pop(0), buffers.pop(0)
        for number, (start, size, early) in enumerate(cuts):
            stages = [buffers.pop(0) for _ in range(4 if early else 3)]
            kind = ReduceEarly if early else Reduce
            chunks.append(
                kind(
                    place, grad, own, *stages, out, start, size, number % 2 == 0, sems, pieces and pieces[number],
                )
            )
        return grad, chunks

    def each(chunks, *steps):
        for step in steps:
            for chunk in chunks:
                getattr(chunk, step.__name__)()

    line_copies = [
        move(getattr(s, LINE_NAMES[number]), s.raw_hidden if number == HIDDEN_LINE else s.raw.at[number])
        for number in range(HIDDEN_LINE + 1)
    ]
    table_copy = move(s.table, s.table_in)
    tokens_copy = move(s.tokens, s.tokens_in)
    cot_copy = move(s.cot, s.cot_in)
    swap = sems.copy(s.tokens, s.far_tokens, place.over_x())
    give = sems.copy(s.give, s.take, place.over_x())
    get_pack = gather(s.pack, s.packs, [(0, LANES, False)])
    get_qkv = gather(s.w_qkv, s.wq, halves(3 * model, False))
    get_proj = gather(s.w_proj, s.wp, halves(model, False))
    get_fc1 = gather(s.w_fc1, s.w1, quarters(hidden))
    get_fc2 = gather(s.w_fc2, s.w2, fc2_cuts(model))
    s.g_fc2, put_fc2 = reduce(s.o_fc2, fc2_cuts(model), None)
    s.g_fc1, put_fc1 = reduce(s.o_fc1, quarters(hidden), None)
    s.g_proj, put_proj = reduce(s.o_proj, halves(model, False), None)
    wide = QKV_COLS
    qkv_pieces = []
    for group in range(model // wide):
        start = group * wide
        qkv_pieces.append([(0, start, wide), (wide, model + start, wide // 2)])
        qkv_pieces.append(
            [(0, model + start + wide // 2, wide // 2), (wide // 2, 2 * model + start, wide)]
        )
    s.g_qkv, put_qkv = reduce(s.o_qkv, qkv_cuts(model), qkv_pieces)
    s.g_table, put_table = reduce(s.o_table, [(0, LANES, False)], None)
    s.g_small, put_small = reduce(s.o_small, [(0, LANES, False)], None)
    get_table = gather(s.o_table.reshape(1, 8, LANES), s.table_all, [(0, LANES, False)])

    meet(place)
    for copy in line_copies:
        copy.wait()
    s.pack[...] = jnp.zeros_like(s.pack)
    for number in range(HIDDEN_LINE + 1):
        source = s.raw_hidden if number == HIDDEN_LINE else s.raw.at[number]
        s.pack[number // 8, number % 8 : number % 8 + 1, 0 : source.shape[1]] = source[...].astype(F32)
    each(get_pack, Gather.begin_own, Gather.begin_z)
    each(get_qkv, Gather.begin_z, Gather.begin_own)
    swap.start()
    each(get_proj, Gather.begin_own)
    table_copy.wait()
    s.table_lines[...] = jnp.zeros_like(s.table_lines)
    s.table_lines[0:HEADS, 0 : s.table.shape[1]] = s.table_in[...]
    fill_diagonals(s.table_lines, s.diag, rows, keys, row_span, width, offset)
    each(get_pack, Gather.second)
    tokens_copy.wait()
    normed, inv_std = norm_rows(s.tokens_in[...].astype(F32))
    s.n1[...] = normed
    s.r1[...] = jnp.broadcast_to(inv_std, s.r1.shape)
    each(get_pack, Gather.third)
    each(get_proj, Gather.begin_z)
    each(get_fc1[:2], Gather.begin_z)
    each(get_fc1, Gather.begin_own)
    s.fold[...] = jnp.zeros_like(s.fold)
    s.lines[...] = jnp.zeros_like(s.lines)
    each(get_pack, Gather.fourth)
    each(get_fc2, Gather.begin_own)
    each(get_qkv, Gather.second)
    each(get_fc1[2:], Gather.begin_z)
    each(get_pack, Gather.arrive)
    unpack_lines(tile(s.packs, 0, LANES), shard, hidden_shard, s.vec, s.b1)

    def line(number):
        return s.vec[number : number + 1, :]

    def set_line(number, values):
        s.lines[number : number + 1, :] = values

    s.h1[own_rows, :] = (s.n1[...] * line(GAIN_ONE) + line(SHIFT_ONE)).astype(BF16)
    swap.wait_recv()
    far = norm_rows(s.far_tokens[...].astype(F32))[0]
    s.h1[far_rows, :] = (far * line(GAIN_ONE) + line(SHIFT_ONE)).astype(BF16)
    each(get_proj, Gather.second)
    s.h1t[...] = s.h1[...].T
    cot_copy.wait()
    s.dm[...] = (line(SCALE_TWO) * s.cot_in[...].astype(F32)).astype(BF16)
    set_line(FC2_SHIFT, sum_rows(s.dm[...]))
    each(get_fc1[:2], Gather.second)
    each(get_fc2, Gather.begin_z)
    each(get_fc2[2:], Gather.second)
    each(get_qkv, Gather.third)
    each(get_proj, Gather.third)
    each(get_fc1[2:], Gather.second)
    each(get_qkv, Gather.fourth)
    each(get_fc1[:2], Gather.third)
    each(get_qkv, Gather.arrive)

    step = 2 * LANES

    @tiles(model // step, step)
    def _(number, start):
        s.kv[:, pl.ds(start, step)] = dot(s.h1[...], tile(s.wq, model + start, step)).astype(BF16)
        sums = dot(s.h1[...], tile(s.wq, 2 * model + start, step))
        sums = sums + s.vec[VALUE_BIAS : VALUE_BIAS + 1, pl.ds(start, step)]
        s.kv[:, pl.ds(model + start, step)] = sums.astype(BF16)

    @tiles(model // step, step)
    def _(number, start):
        cols = pl.ds(start, step)
        sums = dot(s.h1[own_rows, :], tile(s.wq, start, step))
        s.q[:, cols] = (sums + s.vec[QUERY_BIAS : QUERY_BIAS + 1, cols]).astype(BF16)

    def look(first, last):
        attend(s.q, s.kv, s.diag, s.probs, s.mixed, width, count, offset, (first, last))

    each(get_fc1[2:], Gather.third)
    each(get_fc2[:2], Gather.second)
    each(get_proj, Gather.fourth)
    look(0, 2)
    look(2, 4)
    each(get_fc1[:2], Gather.fourth)
    look(4, PAIRS)
    s.mixedt[...] = s.mixed[...].T
    each(get_proj, Gather.arrive)

    @tiles(model // step, step)
    def _(number, start):
        cols = pl.ds(start, step)
        branch = dot(s.mixed[...], tile(s.wp, start, step)) + s.vec[PROJ_SHIFT : PROJ_SHIFT + 1, cols]
        s.z[:, cols] = branch
        s.x1[:, cols] = s.tokens_in[:, cols].astype(F32) + s.vec[SCALE_ONE : SCALE_ONE + 1, cols] * branch

    normed, inv_std = norm_rows(s.x1[...])
    s.n2[...] = normed
    s.r2[...] = jnp.broadcast_to(inv_std, s.r2.shape)
    s.h2[...] = (normed * line(GAIN_TWO) + line(SHIFT_TWO)).astype(BF16)
    s.h2t[...] = s.h2[...].T
    each(get_fc2[:2], Gather.third)
    each(get_fc1[2:], Gather.fourth)
    each(get_fc1, Gather.arrive)

    @tiles(hidden // step, step)
    def _(number, start):
        cols = pl.ds(start, step)
        act = dot(s.h2[...], tile(s.w1, start, step)) + s.b1[0:1, cols]
        gate = 0.5 * (1.0 + lax.erf(act * 0.5**0.5))
        low = (act * gate).astype(BF16)
        s.u[:, cols] = low
        s.ut[cols, :] = low.T
        s.slope[:, cols] = gate + act * jnp.exp(act * act * -0.5) * 0.3989422804014327

    each(get_fc2, Gather.fourth)
    deep = 8 * hidden_shard
    for chunk, (first, size, _) in zip(put_fc2, fc2_cuts(model)):

        @tiles(Z_SIZE, deep)
        def _(number, start):
            cols = pl.ds(first, size)
            sums = dot(s.ut[pl.ds(start, deep), :], s.dm[:, cols])
            view = s.g_fc2.reshape(Z_SIZE, 8, hidden_shard, model)
            view[number, :, :, cols] = sums.reshape(8, hidden_shard, size).astype(BF16)

        chunk.begin()
    each(put_fc2, Reduce.add_core)
    each(get_fc2, Gather.arrive)

    @tiles(Z_SIZE, deep)
    def _(number, start):
        cols = pl.ds(start, deep)
        weight = s.w2.reshape(Z_SIZE, deep, model)[number]
        grad_hidden = dot(s.dm[...], weight, NT)
        s.da[:, cols] = (grad_hidden * s.slope[:, cols]).astype(BF16)

    for chunk, (first, size, _) in zip(put_fc1, quarters(hidden)):

        @tiles(size // step, step)
        def _(number, start):
            cols = pl.ds(start + first, step)
            put_slots(s.g_fc1, cols, dot(s.h2t[...], s.da[:, cols]))

        chunk.begin()

    grad = jnp.zeros((rows, model), F32)
    for start in range(0, hidden, model):
        grad = grad + dot(s.da[:, start : start + model], tile(s.w1, start, model), NT)
    s.dh2[...] = grad
    each(put_fc2[:2], Reduce.add_first)
    each(put_fc1, Reduce.add_core)
    grad = s.dh2[...]
    set_line(GAIN_TWO, sum_rows(grad * s.n2[...]))
    set_line(SHIFT_TWO, sum_rows(grad))
    dx1 = s.cot_in[...].astype(F32) + norm_rows_back(grad, s.n2[...], s.r2[:, 0:1], line(GAIN_TWO))
    s.dx1[...] = dx1
    set_line(SCALE_ONE, sum_rows(dx1 * s.z[...]))
    s.dz[...] = (line(SCALE_ONE) * dx1).astype(BF16)
    set_line(PROJ_SHIFT, sum_rows(s.dz[...]))
    for group in range(2):
        cols = pl.ds(group * half, half)
        put_slots(s.g_proj, cols, dot(s.mixedt[...], s.dz[:, cols]))
        put_proj[group].begin()
    s.dmixed[...] = dot(s.dz[...], tile(s.wp, 0, model), NT).astype(BF16)

    def look_back(group):
        pairs = (group * wide // PAIR, (group + 1) * wide // PAIR)
        attend_back(s.q, s.kv, s.probs, s.dmixed, s.dq, s.dkv, s.fold, width, offset, pairs)
        cols = pl.ds(group * wide, wide)
        value_cols = pl.ds(model + group * wide, wide)
        own_lines = s.h1t[:, own_rows]
        all_lines = s.h1t[...]
        for part, sums in enumerate(
            (
                dot(own_lines, s.dq[:, cols]),
                dot(all_lines, s.dkv[:, cols]),
                dot(all_lines, s.dkv[:, value_cols]),
            )
        ):
            put_slots(s.g_qkv, pl.ds((3 * group + part) * wide, wide), sums)
        each(put_qkv[2 * group : 2 * group + 2], Reduce.begin)

    look_back(0)
    each(put_proj, Reduce.add_core)
    look_back(1)
    each(put_fc2[:2], Reduce.add_second)
    look_back(2)
    grad_key = dot(s.dkv[:, :model], tile(s.wq, model, model), NT)
    s.dh1[...] = grad_key + dot(s.dkv[:, model:], tile(s.wq, 2 * model, model), NT)
    s.give[...] = s.dh1[far_rows, :].astype(BF16)
    give.start()
    table_gradient(s.fold, s.table_sums, rows, keys, row_span, width, offset)

    @tiles(4 * Z_SIZE, LANES)
    def _(number, start):
        zz, yy, cc = number // 4, lax.rem(number // 2, 2), lax.rem(number, 2)
        for xx in range(2):
            s.g_table[zz, yy, cc, xx, 0] = s.table_sums[8 * xx : 8 * xx + 8, pl.ds(start, LANES)]

    each(put_table, Reduce.begin)
    each(put_fc2[2:], Reduce.add_first)
    each(put_fc1[:2], Reduce.add_first)
    each(put_table, Reduce.add_core)
    each(put_fc1[2:], Reduce.add_first)
    each(put_qkv, Reduce.add_core)
    @tiles(model // step, step)
    def _(number, start):
        cols = pl.ds(start, step)
        branch = dot(s.u[...], tile(s.w2, start, step)) + s.vec[FC2_SHIFT : FC2_SHIFT + 1, cols]
        s.out_low[:, cols] = (s.x1[:, cols] + s.vec[SCALE_TWO : SCALE_TWO + 1, cols] * branch).astype(BF16)
        s.lines[SCALE_TWO : SCALE_TWO + 1, cols] = sum_rows(s.cot_in[:, cols].astype(F32) * branch)

    hand(s.out_low, s.out)
    s.hidden_lines[...] = jnp.broadcast_to(sum_rows(s.da[...]), s.hidden_lines.shape)
    set_line(QUERY_BIAS, sum_rows(s.dq[...]))
    set_line(VALUE_BIAS, sum_rows(s.dkv[:, model:]))
    grad = s.dh1[own_rows, :] + dot(s.dq[...], tile(s.wq, 0, model), NT)
    give.wait_recv()
    grad = grad + s.take[...].astype(F32)
    set_line(GAIN_ONE, sum_rows(grad * s.n1[...]))
    set_line(SHIFT_ONE, sum_rows(grad))
    dx = s.dx1[...] + norm_rows_back(grad, s.n1[...], s.r1[:, 0:1], line(GAIN_ONE))
    s.dx_low[...] = dx.astype(BF16)
    hand(s.dx_low, s.grad_tokens)

    @tiles(8 * Z_SIZE, 1)
    def _(number, start):
        zz, yy, cc, xx = number // 8, lax.rem(number // 4, 2), lax.rem(number // 2, 2), lax.rem(number, 2)
        moved = pltpu.roll(s.lines[...], model - number * shard, 1)
        for group in range(LINES // ROW_GROUP):
            s.g_small[zz, yy, cc, xx, group] = moved[group * ROW_GROUP : (group + 1) * ROW_GROUP, :LANES]
        moved = pltpu.roll(s.hidden_lines[...], hidden - number * hidden_shard, 1)
        s.g_small[zz, yy, cc, xx, LINES // ROW_GROUP] = moved[:, :LANES]

    each(put_small, Reduce.begin)
    each(put_fc1[:2], Reduce.add_second)
    each(put_table, Reduce.add_first)
    each(put_fc1[2:], Reduce.add_second)
    each(put_small, Reduce.add_core)
    each(put_proj, Reduce.add_first)
    each(put_fc2[2:], Reduce.add_second)
    each(put_table, Reduce.add_second)
    each(put_qkv[:2], Reduce.add_first)
    each(put_qkv[2:4], Reduce.add_first)
    each(put_small, Reduce.add_first)
    each(put_qkv[4:], Reduce.add_first)
    each(put_proj, Reduce.add_second)
    each(put_table, Reduce.finish)
    each(get_table, Gather.begin_own, Gather.begin_z)
    each(put_qkv[:2], Reduce.add_second)
    each(put_small, Reduce.add_second)
    each(put_qkv[2:4], Reduce.add_second)
    each(put_fc2, Reduce.finish)
    hand(s.o_fc2, s.sum_fc2)
    each(put_qkv[4:], Reduce.add_second)
    each(get_table, Gather.second)
    each(put_fc1, Reduce.finish)
    hand(s.o_fc1, s.sum_fc1)
    each(get_table, Gather.third)
    each(put_proj, Reduce.finish)
    hand(s.o_proj, s.sum_proj)
    each(get_table, Gather.fourth)
    each(put_small, Reduce.finish)
    hand(s.o_small, s.sum_small)
    each(put_qkv[:4], Reduce.finish)
    each(get_table, Gather.arrive)
    for block in range(4 * Z_SIZE):
        slots = s.table_all.at[block // 4, block // 2 % 2, block % 2]
        start = block * LANES
        size = min(LANES, s.o_sums.shape[1] - start)
        s.o_sums[0:8, start : start + size] = slots[0, :, 0:size]
        s.o_sums[8:HEADS, start : start + size] = slots[1, 0 : HEADS - 8, 0:size]
    hand(s.o_sums, s.sum_table)
    each(put_qkv[4:], Reduce.finish)
    hand(s.o_qkv, s.sum_qkv)
    swap.wait_send()
    give.wait_send()
    for chunks in (get_pack, get_qkv, get_proj, get_fc1, get_fc2, get_table):
        each(chunks, Gather.settle)
    for chunks in (put_fc2, put_fc1, put_proj, put_qkv, put_table, put_small):
        each(chunks, Reduce.settle)
    for copy in outgoing:
        copy.wait()


def hand_kernel(count, *refs):
    small, arrays = refs[0], refs[1 : 1 + count]
    outs, lines = refs[1 + count : 1 + 2 * count], refs[1 + 2 * count :]
    for array, out in zip(arrays, outs):
        out[...] = array[...]
    for number, out in enumerate(lines):
        row = number if number < HIDDEN_LINE else LINES
        out[...] = small[row : row + 1, 0 : out.shape[1]]


def hand_out(small, arrays, sizes):
    vmem = pl.BlockSpec(memory_space=pltpu.VMEM)
    count = len(arrays)
    return pl.pallas_call(
        partial(hand_kernel, count),
        out_shape=tuple(jax.ShapeDtypeStruct(array.shape, array.dtype) for array in arrays)
        + tuple(jax.ShapeDtypeStruct((1, size), F32) for size in sizes),
        in_specs=[vmem] * (1 + count),
        out_specs=(vmem,) * (count + len(sizes)),
    )(small, *arrays)


def grouped(array):
    return array.reshape(-1, ROW_GROUP, array.shape[-1])


def run_layer(row_span, widths, counts, tokens, cotangent, vectors, w_qkv, w_proj, w_fc1, w_fc2, table):
    rows, model = tokens.shape
    keys = 2 * rows
    shard, hidden, hidden_shard = w_qkv.shape[0], w_fc1.shape[1], w_fc2.shape[0]
    smem = pl.BlockSpec(memory_space=pltpu.SMEM)
    vmem = pl.BlockSpec(memory_space=pltpu.VMEM)
    anywhere = pl.BlockSpec(memory_space=pl.ANY)
    inputs = dict(
        widths=(widths, smem),
        counts=(counts, smem),
        tokens=(tokens, anywhere),
        cot=(cotangent, anywhere),
        w_qkv=(grouped(w_qkv), anywhere),
        w_proj=(grouped(w_proj), anywhere),
        w_fc1=(grouped(w_fc1), anywhere),
        w_fc2=(grouped(w_fc2), anywhere),
        table=(table, anywhere),
    )
    for name, vector in zip(LINE_NAMES, vectors):
        inputs[name] = (vector.reshape(1, -1), anywhere)
    outputs = dict(
        out=((rows, model), BF16),
        grad_tokens=((rows, model), BF16),
        sum_small=((SLOT_ROWS, LANES), F32),
        sum_qkv=((shard, 3 * model), F32),
        sum_proj=((shard, model), F32),
        sum_fc1=((shard, hidden), F32),
        sum_fc2=((hidden_shard, model), F32),
        sum_table=((HEADS, table.shape[1]), F32),
    )
    entries = -(-table.shape[1] // (2 * LANES)) * 2 * LANES
    scratch = dict(
        raw=((HIDDEN_LINE, 1, shard), BF16),
        raw_hidden=((1, hidden_shard), BF16),
        table_in=(table.shape, BF16),
        tokens_in=((rows, model), BF16),
        cot_in=((rows, model), BF16),
        out_low=((rows, model), BF16),
        dx_low=((rows, model), BF16),
        o_small=((SLOT_ROWS, LANES), F32),
        o_qkv=((shard, 3 * model), F32),
        o_proj=((shard, model), F32),
        o_fc1=((shard, hidden), F32),
        o_fc2=((hidden_shard, model), F32),
        o_sums=((HEADS, table.shape[1]), F32),
        pack=((SLOT_ROWS // ROW_GROUP, ROW_GROUP, LANES), F32),
        table_lines=((HEAD_ROWS, entries), BF16),
        table_all=((Z_SIZE, 2, 2, 2, 8, LANES), F32),
        o_table=((8, LANES), F32),
        far_tokens=((rows, model), BF16),
        give=((rows, model), BF16),
        take=((rows, model), BF16),
        packs=((Z_SIZE, 2, 2, 2 * SLOT_ROWS // ROW_GROUP, ROW_GROUP, LANES), F32),
        wq=((Z_SIZE, 2, 2, 2 * shard // ROW_GROUP, ROW_GROUP, 3 * model), BF16),
        wp=((Z_SIZE, 2, 2, 2 * shard // ROW_GROUP, ROW_GROUP, model), BF16),
        w1=((Z_SIZE, 2, 2, 2 * shard // ROW_GROUP, ROW_GROUP, hidden), BF16),
        w2=((Z_SIZE, 2, 2, 2 * hidden_shard // ROW_GROUP, ROW_GROUP, model), BF16),
        vec=((LINES, model), F32),
        b1=((8, hidden), F32),
        diag=((HEAD_ROWS, 2 * (rows + keys)), F32),
        h1=((keys, model), BF16),
        h1t=((model, keys), BF16),
        n1=((rows, model), F32),
        r1=((rows, LANES), F32),
        q=((rows, model), BF16),
        kv=((keys, 2 * model), BF16),
        probs=((HEADS, rows, keys), F32),
        mixed=((rows, model), BF16),
        mixedt=((model, rows), BF16),
        z=((rows, model), F32),
        x1=((rows, model), F32),
        n2=((rows, model), F32),
        r2=((rows, LANES), F32),
        h2=((rows, model), BF16),
        h2t=((model, rows), BF16),
        u=((rows, hidden), BF16),
        ut=((hidden, rows), BF16),
        slope=((rows, hidden), F32),
        dm=((rows, model), BF16),
        da=((rows, hidden), BF16),
        dx1=((rows, model), F32),
        dz=((rows, model), BF16),
        dmixed=((rows, model), BF16),
        dq=((rows, model), BF16),
        dkv=((keys, 2 * model), BF16),
        dh1=((keys, model), F32),
        dh2=((rows, model), F32),
        fold=(((rows + keys) // LANES, 2 * HEAD_ROWS * 8, LANES), F32),
        table_sums=((HEAD_ROWS, entries), F32),
        lines=((LINES, model), F32),
        hidden_lines=((8, hidden), F32),
    )
    stages = []
    chunks = 0
    for slot_rows, slot_width, dtype, cuts in (
        (hidden_shard, model, BF16, fc2_cuts(model)),
        (shard, hidden, BF16, quarters(hidden)),
        (shard, model, BF16, halves(model, False)),
        (shard, 3 * model, BF16, qkv_cuts(model)),
        (8, LANES, F32, [(0, LANES, False)]),
        (SLOT_ROWS, LANES, F32, [(0, LANES, False)]),
    ):
        groups = slot_rows // ROW_GROUP
        stages.append(((Z_SIZE, 2, 2, 2, groups, ROW_GROUP, slot_width), dtype))
        stages.append(((Z_SIZE, 2, 2, groups, ROW_GROUP, slot_width), dtype))
        for _, size, early in cuts:
            leads = ((Z_SIZE, 2), (Z_SIZE,), (Z_SIZE - 1,))
            if early:
                leads = ((Z_SIZE - 1, 2, 2), (2, 2), (2,), ())
            for lead in leads:
                stages.append((lead + (groups, ROW_GROUP, size), dtype))
            chunks += 1
    gathers = 13
    sends, recvs = 2 + gathers + chunks, 2 + 7 * gathers + 4 * chunks
    names = list(inputs) + list(outputs) + list(scratch)
    return pl.pallas_call(
        partial(layer_kernel, names, row_span),
        out_shape=tuple(jax.ShapeDtypeStruct(shape, dtype) for shape, dtype in outputs.values()),
        in_specs=[spec for _, spec in inputs.values()],
        out_specs=(anywhere,) * len(outputs),
        scratch_shapes=[pltpu.VMEM(shape, dtype) for shape, dtype in list(scratch.values()) + stages]
        + [
            pltpu.SemaphoreType.DMA((sends,)),
            pltpu.SemaphoreType.DMA((recvs,)),
            pltpu.SemaphoreType.DMA((HIDDEN_LINE + 4 + gathers,)),
        ],
        compiler_params=pltpu.CompilerParams(
            collective_id=0, has_side_effects=True, vmem_limit_bytes=VMEM_LIMIT
        ),
    )(*[array for array, _ in inputs.values()])


def layer_norm(values, gain, shift):
    centred = values - jnp.mean(values, axis=-1, keepdims=True)
    inv_std = lax.rsqrt(jnp.mean(centred * centred, axis=-1, keepdims=True) + EPSILON)
    normed = centred * inv_std
    return (normed * gain + shift, normed, inv_std)


def norm_back(grad_out, normed, inv_std, gain):
    scaled = grad_out * gain
    return inv_std * (
        scaled
        - jnp.mean(scaled, axis=-1, keepdims=True)
        - normed * jnp.mean(scaled * normed, axis=-1, keepdims=True)
    )


def row_sum(values):
    return jnp.sum(values.astype(jnp.float32), axis=0)


def per_device_native(
    tokens,
    cotangent,
    counts,
    widths,
    norm1_gain,
    norm1_shift,
    w_qkv,
    q_bias,
    v_bias,
    w_proj,
    proj_bias,
    gamma1,
    norm2_gain,
    norm2_shift,
    w_fc1,
    fc1_bias,
    w_fc2,
    fc2_bias,
    gamma2,
    bias_table,
):
    fetched = (
        lax.all_gather(norm1_gain, ("img", "seq"), axis=0, tiled=True),
        lax.all_gather(norm1_shift, ("img", "seq"), axis=0, tiled=True),
        lax.all_gather(w_qkv, ("img", "seq"), axis=0, tiled=True),
        lax.all_gather(q_bias, ("img", "seq"), axis=0, tiled=True),
        lax.all_gather(v_bias, ("img", "seq"), axis=0, tiled=True),
        lax.all_gather(w_proj, ("img", "seq"), axis=0, tiled=True),
        lax.all_gather(proj_bias, ("img", "seq"), axis=0, tiled=True),
        lax.all_gather(gamma1, ("img", "seq"), axis=0, tiled=True),
        lax.all_gather(norm2_gain, ("img", "seq"), axis=0, tiled=True),
        lax.all_gather(norm2_shift, ("img", "seq"), axis=0, tiled=True),
        lax.all_gather(w_fc1, ("img", "seq"), axis=0, tiled=True),
        lax.all_gather(fc1_bias, ("img", "seq"), axis=0, tiled=True),
        lax.all_gather(w_fc2, ("img", "seq"), axis=0, tiled=True),
        lax.all_gather(fc2_bias, ("img", "seq"), axis=0, tiled=True),
        lax.all_gather(gamma2, ("img", "seq"), axis=0, tiled=True),
    )
    (
        gain_one,
        shift_one,
        qkv_weight,
        query_bias,
        value_bias,
        proj_weight,
        proj_shift,
        scale_one,
        gain_two,
        shift_two,
        fc1_weight,
        fc1_shift,
        fc2_weight,
        fc2_shift,
        scale_two,
    ) = fetched
    gain_one = gain_one.astype(jnp.float32)
    shift_one = shift_one.astype(jnp.float32)
    proj_shift = proj_shift.astype(jnp.float32)
    scale_one = scale_one.astype(jnp.float32)
    gain_two = gain_two.astype(jnp.float32)
    shift_two = shift_two.astype(jnp.float32)
    fc1_shift = fc1_shift.astype(jnp.float32)
    fc2_shift = fc2_shift.astype(jnp.float32)
    scale_two = scale_two.astype(jnp.float32)
    local_rows = tokens.shape[0]
    width_model = tokens.shape[1]
    seq_len = local_rows * lax.axis_size("seq")
    offset = lax.axis_index("seq") * local_rows
    row_span = (seq_len - 1) // (SIDE // 2) + 1
    table_rows = bias_table.shape[0]
    entries = -(-table_rows // (2 * LANES)) * 2 * LANES
    table_lines = jnp.pad(
        bias_table.T, ((0, HEAD_ROWS - HEADS), (0, entries - table_rows))
    )
    scalars = jnp.stack([widths[0], counts[0], offset.astype(jnp.int32)])
    smem = pl.BlockSpec(memory_space=pltpu.SMEM)
    vmem = pl.BlockSpec(memory_space=pltpu.VMEM)
    params = pltpu.CompilerParams(vmem_limit_bytes=40 << 20)

    inputs_f = tokens.astype(jnp.float32)
    normed_full, normed_one, inv_std_one = layer_norm(inputs_f, gain_one, shift_one)
    normed_low = normed_full.astype(jnp.bfloat16)
    qkv_shift = jnp.concatenate(
        [query_bias, jnp.zeros((width_model,), jnp.bfloat16), value_bias]
    ).astype(jnp.float32)
    projected = (
        jnp.dot(normed_low, qkv_weight, preferred_element_type=jnp.float32) + qkv_shift
    ).astype(jnp.bfloat16)
    queries = projected[:, :width_model]
    key_local = projected[:, width_model:]
    keys_all = lax.all_gather(key_local, "seq", axis=0, tiled=True)

    attn_low, probs = pl.pallas_call(
        partial(attend_kernel, row_span),
        out_shape=(
            jax.ShapeDtypeStruct((local_rows, width_model), BF16),
            jax.ShapeDtypeStruct((HEADS, local_rows, seq_len), F32),
        ),
        in_specs=[smem, vmem, vmem, vmem],
        out_specs=(vmem, vmem),
        scratch_shapes=[pltpu.VMEM((HEAD_ROWS, 2 * (local_rows + seq_len)), F32)],
        compiler_params=params,
    )(scalars, queries, keys_all, table_lines)
    branch_one = jnp.dot(attn_low, proj_weight, preferred_element_type=jnp.float32) + proj_shift
    residual_one = inputs_f + scale_one * branch_one
    normed_full_two, normed_two, inv_std_two = layer_norm(residual_one, gain_two, shift_two)
    normed_low_two = normed_full_two.astype(jnp.bfloat16)
    pre_act = jnp.dot(normed_low_two, fc1_weight, preferred_element_type=jnp.float32) + fc1_shift
    activated, gelu_pull = jax.vjp(partial(jax.nn.gelu, approximate=False), pre_act)
    hidden = activated.astype(jnp.bfloat16)
    branch_two = jnp.dot(hidden, fc2_weight, preferred_element_type=jnp.float32) + fc2_shift
    output = (residual_one + scale_two * branch_two).astype(jnp.bfloat16)
    grad_out = cotangent.astype(jnp.float32)
    grad_scale_two = jnp.sum(grad_out * branch_two, axis=0)
    grad_branch_two = (scale_two * grad_out).astype(jnp.bfloat16)
    grad_fc2_weight = jnp.einsum(
        "tf,td->fd", hidden, grad_branch_two, preferred_element_type=jnp.float32
    )
    grad_fc2_shift = row_sum(grad_branch_two)
    grad_hidden = jnp.einsum(
        "td,fd->tf", grad_branch_two, fc2_weight, preferred_element_type=jnp.float32
    )
    grad_pre = gelu_pull(grad_hidden)[0].astype(jnp.bfloat16)
    grad_fc1_weight = jnp.einsum(
        "td,tf->df", normed_low_two, grad_pre, preferred_element_type=jnp.float32
    )
    grad_fc1_shift = row_sum(grad_pre)
    grad_normed_two = jnp.einsum(
        "tf,df->td", grad_pre, fc1_weight, preferred_element_type=jnp.float32
    )
    grad_gain_two = jnp.sum(grad_normed_two * normed_two, axis=0)
    grad_shift_two = jnp.sum(grad_normed_two, axis=0)
    grad_resid = grad_out + norm_back(grad_normed_two, normed_two, inv_std_two, gain_two)
    grad_scale_one = jnp.sum(grad_resid * branch_one, axis=0)
    grad_branch_one = (scale_one * grad_resid).astype(jnp.bfloat16)
    grad_proj_weight = jnp.einsum(
        "td,te->de", attn_low, grad_branch_one, preferred_element_type=jnp.float32
    )
    grad_proj_shift = row_sum(grad_branch_one)
    grad_attn = jnp.einsum(
        "te,de->td", grad_branch_one, proj_weight, preferred_element_type=jnp.float32
    ).astype(jnp.bfloat16)
    grad_query, key_terms, table_grad = pl.pallas_call(
        partial(attend_back_kernel, row_span),
        out_shape=(
            jax.ShapeDtypeStruct((local_rows, width_model), BF16),
            jax.ShapeDtypeStruct((seq_len, 2 * width_model), BF16),
            jax.ShapeDtypeStruct((HEAD_ROWS, entries), F32),
        ),
        in_specs=[smem, vmem, vmem, vmem, vmem],
        out_specs=(vmem, vmem, vmem),
        scratch_shapes=[
            pltpu.VMEM(((local_rows + seq_len) // LANES, 2 * HEAD_ROWS * 8, LANES), F32)
        ],
        compiler_params=params,
    )(scalars, queries, keys_all, probs, grad_attn)
    own_terms = lax.psum_scatter(key_terms, "seq", scatter_dimension=0, tiled=True)
    grad_qkv = jnp.concatenate([grad_query, own_terms], axis=1)
    grad_qkv_weight = jnp.einsum(
        "td,te->de", normed_low, grad_qkv, preferred_element_type=jnp.float32
    )
    grad_query_bias = row_sum(grad_qkv[:, :width_model])
    grad_value_bias = row_sum(grad_qkv[:, 2 * width_model :])
    grad_normed_one = jnp.einsum(
        "te,de->td", grad_qkv, qkv_weight, preferred_element_type=jnp.float32
    )
    grad_gain_one = jnp.sum(grad_normed_one * normed_one, axis=0)
    grad_shift_one = jnp.sum(grad_normed_one, axis=0)
    grad_inputs = (
        grad_resid + norm_back(grad_normed_one, normed_one, inv_std_one, gain_one)
    ).astype(jnp.bfloat16)
    summed = (
        lax.psum_scatter(grad_gain_one, ("img", "seq"), scatter_dimension=0, tiled=True),
        lax.psum_scatter(grad_shift_one, ("img", "seq"), scatter_dimension=0, tiled=True),
        lax.psum_scatter(grad_qkv_weight, ("img", "seq"), scatter_dimension=0, tiled=True),
        lax.psum_scatter(grad_query_bias, ("img", "seq"), scatter_dimension=0, tiled=True),
        lax.psum_scatter(grad_value_bias, ("img", "seq"), scatter_dimension=0, tiled=True),
        lax.psum_scatter(grad_proj_weight, ("img", "seq"), scatter_dimension=0, tiled=True),
        lax.psum_scatter(grad_proj_shift, ("img", "seq"), scatter_dimension=0, tiled=True),
        lax.psum_scatter(grad_scale_one, ("img", "seq"), scatter_dimension=0, tiled=True),
        lax.psum_scatter(grad_gain_two, ("img", "seq"), scatter_dimension=0, tiled=True),
        lax.psum_scatter(grad_shift_two, ("img", "seq"), scatter_dimension=0, tiled=True),
        lax.psum_scatter(grad_fc1_weight, ("img", "seq"), scatter_dimension=0, tiled=True),
        lax.psum_scatter(grad_fc1_shift, ("img", "seq"), scatter_dimension=0, tiled=True),
        lax.psum_scatter(grad_fc2_weight, ("img", "seq"), scatter_dimension=0, tiled=True),
        lax.psum_scatter(grad_fc2_shift, ("img", "seq"), scatter_dimension=0, tiled=True),
        lax.psum_scatter(grad_scale_two, ("img", "seq"), scatter_dimension=0, tiled=True),
    )
    table_total = lax.psum(table_grad, ("img", "seq"))[:HEADS, :table_rows].T
    return (output, grad_inputs) + tuple(summed) + (table_total,)


def per_device_linked(
    tokens,
    cotangent,
    counts,
    widths,
    norm1_gain,
    norm1_shift,
    w_qkv,
    q_bias,
    v_bias,
    w_proj,
    proj_bias,
    gamma1,
    norm2_gain,
    norm2_shift,
    w_fc1,
    fc1_bias,
    w_fc2,
    fc2_bias,
    gamma2,
    bias_table,
):
    seq_len = tokens.shape[0] * lax.axis_size("seq")
    row_span = (seq_len - 1) // (SIDE // 2) + 1
    vectors = [
        norm1_gain, norm1_shift, q_bias, v_bias, proj_bias, gamma1, norm2_gain, norm2_shift, fc2_bias, gamma2, fc1_bias,
    ]
    output, grad_tokens, small, *sums = run_layer(
        row_span, widths, counts, tokens, cotangent, vectors, w_qkv, w_proj, w_fc1, w_fc2, bias_table.T
    )
    sizes = [vector.shape[0] for vector in vectors]
    output, grad_tokens, sum_qkv, sum_proj, sum_fc1, sum_fc2, table_total, *lines = hand_out(
        small, [output, grad_tokens, *sums], sizes
    )
    lines = [line.reshape(-1) for line in lines]
    return (
        output, grad_tokens, lines[GAIN_ONE], lines[SHIFT_ONE], sum_qkv, lines[QUERY_BIAS], lines[VALUE_BIAS],
        sum_proj, lines[PROJ_SHIFT], lines[SCALE_ONE], lines[GAIN_TWO], lines[SHIFT_TWO], sum_fc1,
        lines[HIDDEN_LINE], sum_fc2, lines[FC2_SHIFT], lines[SCALE_TWO], table_total.T,
    )


def per_device(*arrays):
    tokens, bias_table = arrays[0], arrays[19]
    linked = lax.axis_size("img") == 4 * Z_SIZE and lax.axis_size("seq") == 2
    linked = linked and arrays[6].shape[0] % 8 == 0 and tokens.shape[0] == LANES
    linked = linked and 15 * LANES < bias_table.shape[0] <= 4 * Z_SIZE * LANES
    return per_device_linked(*arrays) if linked else per_device_native(*arrays)


def solution(mesh):
    return jax.shard_map(
        per_device,
        mesh=mesh,
        in_specs=(
            P(("img", "seq"), None),
            P(("img", "seq"), None),
            P("img"),
            P("img"),
            P(("img", "seq")),
            P(("img", "seq")),
            P(("img", "seq"), None),
            P(("img", "seq")),
            P(("img", "seq")),
            P(("img", "seq"), None),
            P(("img", "seq")),
            P(("img", "seq")),
            P(("img", "seq")),
            P(("img", "seq")),
            P(("img", "seq"), None),
            P(("img", "seq")),
            P(("img", "seq"), None),
            P(("img", "seq")),
            P(("img", "seq")),
            P(),
        ),
        out_specs=(
            P(("img", "seq"), None),
            P(("img", "seq"), None),
            P(("img", "seq")),
            P(("img", "seq")),
            P(("img", "seq"), None),
            P(("img", "seq")),
            P(("img", "seq")),
            P(("img", "seq"), None),
            P(("img", "seq")),
            P(("img", "seq")),
            P(("img", "seq")),
            P(("img", "seq")),
            P(("img", "seq"), None),
            P(("img", "seq")),
            P(("img", "seq"), None),
            P(("img", "seq")),
            P(("img", "seq")),
            P(),
        ),
        check_vma=False,
    )
```

```python
from functools import partial

import jax
import jax.numpy as jnp
from jax import lax
from jax.experimental import pallas as pl
from jax.experimental.pallas import tpu as pltpu
from jax.sharding import PartitionSpec as P

HEADS = 12
HEAD_DIM = 64
SIDE = 32
PAIR = 2 * HEAD_DIM
PAIRS = HEADS // 2
HEAD_ROWS = 16
LANES = 128
F32 = jnp.float32
BF16 = jnp.bfloat16
NT = (((1,), (1,)), ((), ()))
TN = (((0,), (0,)), ((), ()))


VMEM_LIMIT = 63 << 20
ROW_GROUP = 8
EPSILON = 1e-06
NEG_FILL = -1e30


def dot(left, right, dims=(((1,), (0,)), ((), ()))):
    return lax.dot_general(left, right, dims, preferred_element_type=F32)


def iota(shape, dim):
    return lax.broadcasted_iota(jnp.int32, shape, dim)


def floor_div(values, width):
    return jnp.floor((values.astype(F32) + 0.5) / width.astype(F32)).astype(jnp.int32)


def table_index(place, span, rows, row_span, width, offset):
    right = place >= span
    diagonal = offset + rows - 1 - jnp.where(right, place - span, place)
    row = floor_div(diagonal, width)
    col = diagonal - row * width
    row = jnp.where(right, row + 1, row)
    col = jnp.where(right, col - width, col)
    return (row + row_span - 1) * (2 * SIDE - 1) + col + SIDE - 1


def same_side(rows, keys, width, offset):
    query = iota((rows, keys), 0) + offset
    key = iota((rows, keys), 1)
    return (query - floor_div(query, width) * width) >= (key - floor_div(key, width) * width)


def fill_diagonals(table_ref, diag_ref, rows, keys, row_span, width, offset):
    span = rows + keys
    entries = table_ref.shape[1]
    step = 2 * LANES
    index = table_index(iota((step, 2 * span), 1), span, rows, row_span, width, offset)
    entry = iota((step, 2 * span), 0)
    diag_ref[...] = jnp.zeros_like(diag_ref)

    def add(chunk, carry):
        start = pl.multiple_of(chunk * step, step)
        chosen = jnp.where(entry + start == index, 1.0, 0.0).astype(BF16)
        diag_ref[...] += dot(table_ref[:, pl.ds(start, step)], chosen)
        return carry

    lax.fori_loop(0, entries // step, add, 0)


def half_mask(shape, half):
    lane = iota(shape, 1)
    return lane < HEAD_DIM if half == 0 else lane >= HEAD_DIM


def pick(values, half):
    return jnp.where(half_mask(values.shape, half), values, jnp.zeros_like(values))


def attend(query_ref, kv_ref, diag_ref, probs_ref, mixed_ref, width, count, offset, pairs=(0, PAIRS)):
    rows, model = query_ref.shape
    keys = kv_ref.shape[0]
    span = rows + keys
    same = same_side(rows, keys, width, offset)
    valid = iota((rows, keys), 1) < count

    def one_pair(pair, carry):
        cols = pl.ds(pl.multiple_of(pair * PAIR, PAIR), PAIR)
        value_cols = pl.ds(pl.multiple_of(model + pair * PAIR, PAIR), PAIR)
        query_pair = query_ref[:, cols]
        key_pair = kv_ref[:, cols]
        value_pair = kv_ref[:, value_cols]
        mixed = jnp.zeros((rows, PAIR), F32)
        for half in range(2):
            head = pair * 2 + half
            product = dot(pick(query_pair, half), key_pair, NT)
            shifted = []
            for side in range(2):
                line = diag_ref[pl.ds(head, 1), side * span : (side + 1) * span]
                line = jnp.broadcast_to(line, (rows, span))
                line = pltpu.roll(line, keys + 1, 1, stride=1, stride_axis=0)
                shifted.append(line[:, :keys])
            scores = product * HEAD_DIM**-0.5 + jnp.where(same, shifted[0], shifted[1])
            scores = jnp.where(valid, scores, NEG_FILL)
            terms = jnp.exp(scores - jnp.max(scores, axis=1, keepdims=True))
            terms = jnp.where(valid, terms, 0.0)
            probs = terms / jnp.sum(terms, axis=1, keepdims=True)
            probs_ref[head] = probs
            mixed = mixed + dot(probs.astype(BF16), pick(value_pair, half))
        mixed_ref[:, cols] = mixed.astype(BF16)
        return carry

    lax.fori_loop(*pairs, one_pair, 0)


def fold_rows(values):
    while values.shape[0] > 8:
        half = values.shape[0] // 2
        values = values[half:] + pltpu.roll(values[:half], half, 1)
    return values


def attend_back(
    query_ref, kv_ref, probs_ref, grad_ref, grad_query_ref, grad_kv_ref, fold_ref, width, offset, pairs=(0, PAIRS)
):
    rows, model = query_ref.shape
    keys = kv_ref.shape[0]
    same = same_side(rows, keys, width, offset)

    def one_pair(pair, carry):
        cols = pl.ds(pl.multiple_of(pair * PAIR, PAIR), PAIR)
        value_cols = pl.ds(pl.multiple_of(model + pair * PAIR, PAIR), PAIR)
        query_pair = query_ref[:, cols]
        key_pair = kv_ref[:, cols]
        value_pair = kv_ref[:, value_cols]
        grad_pair = grad_ref[:, cols]
        grad_query = jnp.zeros((rows, PAIR), F32)
        grad_key = jnp.zeros((keys, PAIR), F32)
        grad_value = jnp.zeros((keys, PAIR), F32)
        for half in range(2):
            head = pair * 2 + half
            probs = probs_ref[head]
            grad_half = pick(grad_pair, half)
            grad_probs = dot(grad_half, value_pair, NT)
            grad_scores = probs * (
                grad_probs - jnp.sum(probs * grad_probs, axis=1, keepdims=True)
            )
            blank = jnp.zeros((rows, rows), F32)
            left = jnp.where(same, grad_scores, 0.0)
            right = jnp.where(same, 0.0, grad_scores)
            for side, part in enumerate((left, right)):
                place = pl.multiple_of((side * HEAD_ROWS + head) * 8, 8)
                folded = fold_rows(jnp.concatenate([part, blank], axis=1))
                for block in range((rows + keys) // LANES):
                    fold_ref[block, pl.ds(place, 8), :] = folded[:, block * LANES : (block + 1) * LANES]
            grad_prod = (grad_scores * HEAD_DIM**-0.5).astype(BF16)
            grad_query = grad_query + dot(grad_prod, pick(key_pair, half))
            grad_key = grad_key + dot(grad_prod, pick(query_pair, half), TN)
            grad_value = grad_value + dot(probs.astype(BF16), grad_half, TN)
        grad_query_ref[:, cols] = grad_query.astype(BF16)
        grad_kv_ref[:, cols] = grad_key.astype(BF16)
        grad_kv_ref[:, value_cols] = grad_value.astype(BF16)
        return carry

    lax.fori_loop(*pairs, one_pair, 0)


def table_gradient(fold_ref, out_ref, rows, keys, row_span, width, offset):
    span = rows + keys
    lines = 2 * HEAD_ROWS
    total = jnp.zeros((lines, span), F32)
    for row in range(8):
        blocks = [fold_ref[block, pl.ds(row, lines, stride=8), :] for block in range(span // LANES)]
        moved = jnp.concatenate(blocks, axis=1)
        total = total + (pltpu.roll(moved, 7 - row, 1) if row < 7 else moved)
    parts = []
    for side in range(2):
        rest = total[side * HEAD_ROWS : (side + 1) * HEAD_ROWS]
        pieces = []
        for _ in range(3):
            piece = rest.astype(BF16)
            rest = rest - piece.astype(F32)
            pieces.append(piece)
        parts.append(jnp.concatenate(pieces, axis=0))
    place = iota((span, LANES), 0)
    index = [
        table_index(place + side * span, span, rows, row_span, width, offset) for side in range(2)
    ]
    entry = iota((span, LANES), 1)

    def put(chunk, carry):
        start = pl.multiple_of(chunk * LANES, LANES)
        sums = jnp.zeros((3 * HEAD_ROWS, LANES), F32)
        for side in range(2):
            chosen = jnp.where(entry + start == index[side], 1.0, 0.0).astype(BF16)
            sums = sums + dot(parts[side], chosen)
        out_ref[:, pl.ds(start, LANES)] = (
            sums[:HEAD_ROWS] + sums[HEAD_ROWS : 2 * HEAD_ROWS] + sums[2 * HEAD_ROWS :]
        )
        return carry

    lax.fori_loop(0, out_ref.shape[1] // LANES, put, 0)


def attend_kernel(row_span, scal_ref, query_ref, kv_ref, table_ref, mixed_ref, probs_ref, diag_ref):
    rows, keys = query_ref.shape[0], kv_ref.shape[0]
    width, count, offset = scal_ref[0], scal_ref[1], scal_ref[2]
    fill_diagonals(table_ref, diag_ref, rows, keys, row_span, width, offset)
    attend(query_ref, kv_ref, diag_ref, probs_ref, mixed_ref, width, count, offset)


def attend_back_kernel(
    row_span, scal_ref, query_ref, kv_ref, probs_ref, grad_ref, grad_query_ref, grad_kv_ref, table_ref, fold_ref
):
    rows, keys = query_ref.shape[0], kv_ref.shape[0]
    width, offset = scal_ref[0], scal_ref[2]
    fold_ref[...] = jnp.zeros_like(fold_ref)
    attend_back(
        query_ref, kv_ref, probs_ref, grad_ref, grad_query_ref, grad_kv_ref, fold_ref, width, offset
    )
    table_gradient(fold_ref, table_ref, rows, keys, row_span, width, offset)


MESH = pl.DeviceIdType.MESH
Z_SIZE = 4


class Place:
    def __init__(self):
        img = lax.axis_index("img")
        self.x = lax.axis_index("seq")
        self.c = lax.rem(img, 2)
        self.y = lax.rem(img // 2, 2)
        self.z = img // 4

    def at(self, z=None, y=None, c=None, x=None):
        z = self.z if z is None else z
        y = self.y if y is None else y
        c = self.c if c is None else c
        x = self.x if x is None else x
        return {"img": (z * 2 + y) * 2 + c, "seq": x}

    def sibling(self):
        return self.at(c=1 - self.c)

    def over_x(self):
        return self.at(x=1 - self.x)

    def over_y(self):
        return self.at(y=1 - self.y)

    def z_of(self, step):
        return lax.rem(self.z + step, Z_SIZE)

    def partners(self):
        return [self.sibling(), self.over_x(), self.over_y()] + [
            self.at(z=self.z_of(step)) for step in range(1, Z_SIZE)
        ]


def meet(place):
    barrier = pltpu.get_barrier_semaphore()
    partners = place.partners()
    for partner in partners:
        pl.semaphore_signal(barrier, inc=1, device_id=partner, device_id_type=MESH)
    pl.semaphore_wait(barrier, len(partners))


class Sems:
    def __init__(self, send, recv, place):
        self.send, self.recv, self.place = send, recv, place
        self.sends = self.recvs = 0

    def take_send(self):
        self.sends += 1
        return self.send.at[self.sends - 1]

    def take_recv(self):
        self.recvs += 1
        return self.recv.at[self.recvs - 1]

    def copy(self, src, dst, device, sent=None, came=None):
        return pltpu.make_async_remote_copy(
            src_ref=src,
            dst_ref=dst,
            send_sem=self.take_send() if sent is None else sent,
            recv_sem=self.take_recv() if came is None else came,
            device_id=device,
            device_id_type=MESH,
        )

    def total(self, ref, sem):
        return pltpu.make_async_remote_copy(
            src_ref=ref,
            dst_ref=ref,
            send_sem=sem,
            recv_sem=sem,
            device_id=self.place.sibling(),
            device_id_type=MESH,
        )


class Gather:
    def __init__(self, place, src, slots, cols, x_last, sems, local_sem):
        z, y, c, x = place.z, place.y, place.c, place.x
        groups = src.shape[0]
        every = slice(None)

        def part(a, b, e):
            return slots.at[a, b, c, pl.ds(e * groups, groups), :, cols]

        mine = src.at[:, :, cols]
        own = part(z, y, x)
        self.z = z
        self.local = pltpu.make_async_copy(mine, own, local_sem)
        sent = sems.take_send()
        came = [sems.take_recv() for _ in range(1, Z_SIZE)]
        self.along_z = [
            sems.copy(mine, own, place.at(z=place.z_of(step)), sent, came[step - 1])
            for step in range(1, Z_SIZE)
        ]
        line = part(every, y, x)
        mid_line = part(every, 1 - y, x) if x_last else part(every, y, 1 - x)
        far_line = part(every, y, 1 - x) if x_last else part(every, 1 - y, x)
        cross_line = part(every, 1 - y, 1 - x)
        mid, last = place.over_y(), place.over_x()
        if not x_last:
            mid, last = last, mid
        sibling = place.sibling()
        mid_came, last_came, core_came = sems.take_recv(), sems.take_recv(), sems.take_recv()
        self.own_mid = sems.copy(mine, own, mid, sent, mid_came)
        self.own_last = sems.copy(mine, own, last, sent, last_came)
        pieces = [part(place.z_of(Z_SIZE - step), y, x) for step in range(1, Z_SIZE)]
        self.line_mid = [sems.copy(piece, piece, mid, sent, mid_came) for piece in pieces]
        self.line_last = [sems.copy(piece, piece, last, sent, last_came) for piece in pieces]
        self.line_core = sems.copy(line, line, sibling, sent, core_came)
        self.mid_last = sems.copy(mid_line, mid_line, last, sent)
        self.mid_core = sems.copy(mid_line, mid_line, sibling, sent, core_came)
        self.far_core = sems.copy(far_line, far_line, sibling, sent, core_came)
        self.cross_core = sems.copy(cross_line, cross_line, sibling, sent, core_came)
        self.all_mid = sems.total(mid_line, mid_came)
        self.all_last = sems.total(far_line, last_came)
        self.all_core = sems.total(slots.at[:, :, 1 - c, :, :, cols], core_came)
        flat = slots.reshape((8 * Z_SIZE * groups,) + slots.shape[4:])
        self.all_sent = sems.total(flat.at[pl.ds(0, (8 * Z_SIZE - 1) * groups), :, cols], sent)

    def begin_own(self):
        self.local.start()
        self.own_mid.start()
        self.own_last.start()

    def begin_z(self):
        for copy in self.along_z:
            copy.start()

    def pass_on(self, number):
        self.line_mid[number].start()
        self.line_last[number].start()

    def second(self):

        def take(number):
            self.along_z[number].wait_recv()
            self.pass_on(number)

        @pl.when(self.z >= Z_SIZE // 2)
        def _():
            for number in range(Z_SIZE - 1):
                take(number)

        @pl.when(self.z < Z_SIZE // 2)
        def _():
            for number in reversed(range(Z_SIZE - 1)):
                take(number)

        self.local.wait()
        self.line_core.start()

    def third(self):
        self.all_mid.wait_recv()
        self.mid_last.start()
        self.mid_core.start()

    def fourth(self):
        self.all_last.wait_recv()
        self.far_core.start()
        self.mid_last.wait_recv()
        self.cross_core.start()

    def arrive(self):
        self.all_core.wait_recv()

    def settle(self):
        self.all_sent.wait_send()


class GatherLate(Gather):
    def __init__(self, place, src, slots, cols, x_last, sems, local_sem):
        z, y, c, x = place.z, place.y, place.c, place.x
        groups = src.shape[0]
        sibling = place.sibling()

        def plane(a):
            return slots.at[a, :, c, :, :, cols]

        def part(b, e):
            return slots.at[z, b, c, pl.ds(e * groups, groups), :, cols]

        mine = src.at[:, :, cols]
        own = part(y, x)
        self.local = pltpu.make_async_copy(mine, own, local_sem)
        sent = sems.take_send()
        near, last = place.over_x(), place.over_y()
        piece = part(y, 1 - x)
        if not x_last:
            near, last = last, near
            piece = part(1 - y, x)
        self.own_near = sems.copy(mine, own, near, sent)
        self.own_last = sems.copy(mine, own, last, sent)
        self.near_last = sems.copy(piece, piece, last, sent)
        self.along_z = [
            sems.copy(plane(z), plane(z), place.at(z=place.z_of(step)), sent) for step in range(1, Z_SIZE)
        ]
        core_came = sems.take_recv()
        self.line_core = sems.copy(plane(z), plane(z), sibling, sent, core_came)
        self.far_core = []
        for step in range(1, Z_SIZE):
            far = plane(place.z_of(Z_SIZE - step))
            self.far_core.append(sems.copy(far, far, sibling, sent, core_came))
        self.all_core = sems.total(slots.at[:, :, 1 - c, :, :, cols], core_came)
        flat = slots.reshape((8 * Z_SIZE * groups,) + slots.shape[4:])
        self.all_sent = sems.total(flat.at[pl.ds(0, (8 * Z_SIZE - 1) * groups), :, cols], sent)

    def begin_own(self):
        self.local.start()
        self.own_near.start()
        self.own_last.start()

    def begin_z(self):
        self.own_near.wait_recv()
        self.near_last.start()

    def second(self):
        self.own_last.wait_recv()
        self.near_last.wait_recv()
        self.local.wait()
        for copy in self.along_z:
            copy.start()
        self.line_core.start()

    def third(self):
        pass

    def fourth(self):
        for copy, onward in zip(self.along_z, self.far_core):
            copy.wait_recv()
            onward.start()

    def settle(self):
        self.all_sent.wait_send()


class Reduce:
    def __init__(self, place, grad, own, first, second, third, out, start, size, x_first, sems, pieces=None):
        rows = out.shape[0]

        def flat(ref):
            return ref.reshape(ref.shape[:-3] + (rows, ref.shape[-1]))

        self.place, self.out = place, out
        self.grad, self.own, self.first = flat(grad), flat(own), flat(first)
        self.second, self.third = flat(second), flat(third)
        self.pieces = pieces or [(0, start, size)]
        self.x_first = x_first
        z, y, c, x = place.z, place.y, place.c, place.x
        every = slice(None)
        cols = pl.ds(start, size)
        self.cols = cols
        sent = sems.take_send()
        self.to_core = sems.copy(
            grad.at[:, :, 1 - c, :, :, :, cols], own.at[:, :, :, :, :, cols], place.sibling(), sent
        )
        over_first, over_second = place.over_x(), place.over_y()
        if x_first:
            leaving, other = own.at[:, :, 1 - x, :, :, cols], 1 - y
        else:
            over_first, over_second = over_second, over_first
            leaving, other = own.at[:, 1 - y, :, :, :, cols], 1 - x
        self.kept = y if x_first else x
        self.over_first = sems.copy(leaving, first, over_first, sent)
        self.over_second = sems.copy(first.at[:, other], second, over_second, sent)
        came = sems.take_recv()
        self.along_z = []
        for step in range(1, Z_SIZE):
            target = place.z_of(step)
            self.along_z.append(
                sems.copy(second.at[target], third.at[step - 1], place.at(z=target), sent, came)
            )
        self.all_z = sems.total(third, came)
        slots = grad.reshape((8 * Z_SIZE,) + grad.shape[4:])
        self.all_sent = sems.total(slots.at[pl.ds(0, 8 * Z_SIZE - 1), :, :, cols], sent)

    def begin(self):
        self.to_core.start()

    def add_core(self):
        self.to_core.wait_recv()
        place = self.place

        def add(zy, carry):
            z, y = zy // 2, lax.rem(zy, 2)
            for x in range(2):
                mine = self.grad[z, y, place.c, x, :, self.cols].astype(F32)
                theirs = self.own[z, y, x, :, self.cols].astype(F32)
                self.own[z, y, x, :, self.cols] = (mine + theirs).astype(self.own.dtype)
            return carry

        lax.fori_loop(0, 2 * Z_SIZE, add, 0)
        self.send_core()

    def send_core(self):
        self.over_first.start()

    def add_first(self):
        self.over_first.wait_recv()
        place = self.place

        def add(z, carry):
            for other in range(2):
                if self.x_first:
                    mine = self.own[z, other, place.x, :, self.cols].astype(F32)
                else:
                    mine = self.own[z, place.y, other, :, self.cols].astype(F32)
                theirs = self.first[z, other].astype(F32)
                self.first[z, other] = (mine + theirs).astype(self.first.dtype)
            return carry

        lax.fori_loop(0, Z_SIZE, add, 0)
        self.over_second.start()

    def add_second(self):
        self.over_second.wait_recv()

        def add(z, carry):
            mine = self.first[z, self.kept].astype(F32)
            theirs = self.second[z].astype(F32)
            self.second[z] = (mine + theirs).astype(self.second.dtype)
            return carry

        lax.fori_loop(0, Z_SIZE, add, 0)
        for copy in self.along_z:
            copy.start()

    def finish(self):
        total = self.second[self.place.z].astype(F32)
        self.all_z.wait_recv()
        for step in range(Z_SIZE - 1):
            total = total + self.third[step].astype(F32)
        for source, target, size in self.pieces:
            self.out[:, target : target + size] = total[:, source : source + size]

    def settle(self):
        self.all_sent.wait_send()


class ReduceEarly(Reduce):
    def __init__(self, place, grad, own, by_z, plane, first, second, out, start, size, x_first, sems, pieces=None):
        self.pieces = pieces or [(0, start, size)]
        self.x_first = x_first
        rows = out.shape[0]

        def flat(ref):
            return ref.reshape(ref.shape[:-3] + (rows, ref.shape[-1]))

        self.place, self.out = place, out
        self.grad, self.own, self.by_z = flat(grad), flat(own), flat(by_z)
        self.plane, self.first, self.second = flat(plane), flat(first), flat(second)
        c, x, y = place.c, place.x, place.y
        cols = pl.ds(start, size)
        self.cols = cols
        sent = sems.take_send()
        self.to_core = sems.copy(
            grad.at[:, :, 1 - c, :, :, :, cols], own.at[:, :, :, :, :, cols], place.sibling(), sent
        )
        came = sems.take_recv()
        self.along_z = []
        for step in range(1, Z_SIZE):
            target = place.z_of(step)
            self.along_z.append(
                sems.copy(
                    own.at[target, :, :, :, :, cols], by_z.at[step - 1], place.at(z=target), sent, came
                )
            )
        self.all_z = sems.total(by_z, came)
        over_first, over_second = place.over_x(), place.over_y()
        if x_first:
            leaving, other = plane.at[:, 1 - x], 1 - y
        else:
            over_first, over_second = over_second, over_first
            leaving, other = plane.at[1 - y], 1 - x
        self.kept = y if x_first else x
        self.over_first = sems.copy(leaving, first, over_first, sent)
        self.over_second = sems.copy(first.at[other], second, over_second, sent)
        slots = grad.reshape((8 * Z_SIZE,) + grad.shape[4:])
        self.all_sent = sems.total(slots.at[pl.ds(0, 8 * Z_SIZE - 1), :, :, cols], sent)

    def send_core(self):
        for copy in self.along_z:
            copy.start()

    def add_first(self):
        self.all_z.wait_recv()
        z = self.place.z
        for y in range(2):
            for x in range(2):
                total = self.own[z, y, x, :, self.cols].astype(F32)
                for step in range(Z_SIZE - 1):
                    total = total + self.by_z[step, y, x].astype(F32)
                self.plane[y, x] = total.astype(self.plane.dtype)
        self.over_first.start()

    def add_second(self):
        self.over_first.wait_recv()
        for other in range(2):
            if self.x_first:
                mine = self.plane[other, self.place.x].astype(F32)
            else:
                mine = self.plane[self.place.y, other].astype(F32)
            self.first[other] = (mine + self.first[other].astype(F32)).astype(self.first.dtype)
        self.over_second.start()

    def finish(self):
        self.over_second.wait_recv()
        total = self.first[self.kept].astype(F32) + self.second[...].astype(F32)
        for source, target, size in self.pieces:
            self.out[:, target : target + size] = total[:, source : source + size]


class Names:
    pass


def norm_rows(values):
    centred = values - jnp.mean(values, axis=1, keepdims=True)
    inv_std = lax.rsqrt(jnp.mean(centred * centred, axis=1, keepdims=True) + EPSILON)
    return centred * inv_std, inv_std


def norm_rows_back(grad_out, normed, inv_std, gain):
    scaled = grad_out * gain
    return inv_std * (
        scaled
        - jnp.mean(scaled, axis=1, keepdims=True)
        - normed * jnp.mean(scaled * normed, axis=1, keepdims=True)
    )


def sum_rows(values):
    return jnp.sum(values.astype(F32), axis=0, keepdims=True)


def div_const(values, divisor):
    return jnp.floor((values.astype(F32) + 0.5) * (1.0 / divisor)).astype(jnp.int32)


def tile(slots, start, size):
    rows = slots.shape[3] * ROW_GROUP
    view = slots.reshape(4 * Z_SIZE, rows, slots.shape[-1])
    return view[:, :, pl.ds(start, size)].reshape(-1, size)


def put_slots(slots, cols, values):
    devices = 8 * Z_SIZE
    view = slots.reshape(devices, slots.shape[4] * ROW_GROUP, slots.shape[-1])
    view[:, :, cols] = values.reshape(devices, -1, values.shape[1]).astype(slots.dtype)


def tiles(count, step):
    def wrap(body):
        def run(number, carry):
            body(number, pl.multiple_of(number * step, step))
            return carry

        lax.fori_loop(0, count, run, 0)

    return wrap


LINES = 16
SLOT_ROWS = 24
QKV_COLS = 256


def quarters(width):
    large = -(-width // 4 // LANES) * LANES
    small = width // 2 - large
    cuts = [(0, large), (large, large), (2 * large, small), (2 * large + small, small)]
    return [(start, size, False) for start, size in cuts]


def halves(width, turned):
    middle = width // 2 // LANES * LANES
    return [(0, middle, turned), (middle, width - middle, turned)]


def fc1_sum_cuts(width):
    large, small = width // 4, width // 6
    cuts = [(0, large), (large, large), (2 * large, small), (2 * large + small, small)]
    cuts = [(start, size, False) for start, size in cuts]
    return cuts + [(2 * large + 2 * small, width - 2 * large - 2 * small, True)]


def fc2_cuts(width):
    part = width // 3
    return [(0, part, False), (part, part, False), (2 * part, width - 2 * part, True)]


def qkv_cuts(model):
    size = 3 * QKV_COLS // 2
    return [(start, size, False) for start in range(0, 3 * model, size)]


(
    GAIN_ONE, SHIFT_ONE, QUERY_BIAS, VALUE_BIAS, PROJ_SHIFT, SCALE_ONE, GAIN_TWO, SHIFT_TWO, FC2_SHIFT, SCALE_TWO,
) = range(10)
HIDDEN_LINE = 10
LINE_NAMES = ["line" + str(number) for number in range(HIDDEN_LINE + 1)]


def unpack_lines(packed, shard, hidden_shard, vec_ref, hidden_ref):
    rows = packed.shape[0]
    devices = rows // SLOT_ROWS
    low = packed.astype(BF16)
    width = shard * devices
    lane = iota((LANES, width), 1)
    spread = jnp.where(lane - div_const(lane, shard) * shard == iota((LANES, width), 0), 1.0, 0.0)
    wide = dot(low, spread.astype(BF16))
    owner = div_const(iota((rows, width), 0), SLOT_ROWS)
    wide = jnp.where(owner == div_const(iota((rows, width), 1), shard), wide, 0.0).astype(BF16)
    row = iota((LINES, rows), 1)
    line = row - div_const(row, SLOT_ROWS) * SLOT_ROWS
    vec_ref[...] = dot(jnp.where(line == iota((LINES, rows), 0), 1.0, 0.0).astype(BF16), wide)
    row = iota((devices, rows), 1)
    chosen = jnp.where(row == iota((devices, rows), 0) * SLOT_ROWS + HIDDEN_LINE, 1.0, 0.0)
    hidden = dot(chosen.astype(BF16), low).astype(BF16)
    step = 8 * LANES
    for start in range(0, hidden_shard * devices, step):
        lane = iota((LANES, step), 1) + start
        owner = div_const(lane, hidden_shard)
        spread = jnp.where(lane - owner * hidden_shard == iota((LANES, step), 0), 1.0, 0.0)
        wide = dot(hidden, spread.astype(BF16))
        owner = div_const(iota((devices, step), 1) + start, hidden_shard)
        wide = jnp.where(owner == iota((devices, step), 0), wide, 0.0)
        hidden_ref[:, start : start + step] = jnp.broadcast_to(sum_rows(wide), (8, step))


def layer_kernel(names, row_span, *refs):
    s = Names()
    s.__dict__.update(zip(names, refs))
    buffers = list(refs[len(names) :])
    send, recv, local = buffers[-3:]
    place = Place()
    x = place.x
    rows, model = s.tokens.shape
    width, count, offset = s.widths[0], s.counts[0], x * rows
    keys = 2 * rows
    hidden = s.w_fc1.shape[2]
    shard, hidden_shard = s.w_qkv.shape[0] * ROW_GROUP, s.w_fc2.shape[0] * ROW_GROUP
    half = model // 2
    own_rows = pl.ds(pl.multiple_of(x * rows, rows), rows)
    far_rows = pl.ds(pl.multiple_of((1 - x) * rows, rows), rows)
    sems = Sems(send, recv, place)
    locals_used = []
    outgoing = []

    def move(src, dst):
        locals_used.append(0)
        copy = pltpu.make_async_copy(src, dst, local.at[len(locals_used) - 1])
        copy.start()
        return copy

    def hand(src, dst):
        copy = pltpu.make_async_copy(src, dst, local.at[len(outgoing)])
        copy.start()
        outgoing.append(copy)

    def gather(src, slots, cuts):
        chunks = []
        for number, (start, size, late) in enumerate(cuts):
            locals_used.append(0)
            sem = local.at[len(locals_used) - 1]
            kind = GatherLate if late else Gather
            chunks.append(kind(place, src, slots, pl.ds(start, size), number % 2 == 0, sems, sem))
        return chunks

    def reduce(out, cuts, pieces):
        chunks = []
        grad, own = buffers.pop(0), buffers.pop(0)
        for number, (start, size, early) in enumerate(cuts):
            stages = [buffers.pop(0) for _ in range(4 if early else 3)]
            kind = ReduceEarly if early else Reduce
            chunks.append(
                kind(
                    place, grad, own, *stages, out, start, size, number % 2 == 0, sems, pieces and pieces[number],
                )
            )
        return grad, chunks

    def each(chunks, *steps):
        for step in steps:
            for chunk in chunks:
                getattr(chunk, step.__name__)()

    line_copies = [
        move(getattr(s, LINE_NAMES[number]), s.raw_hidden if number == HIDDEN_LINE else s.raw.at[number])
        for number in range(HIDDEN_LINE + 1)
    ]
    table_copy = move(s.table, s.table_in)
    tokens_copy = move(s.tokens, s.tokens_in)
    cot_copy = move(s.cot, s.cot_in)
    swap = sems.copy(s.tokens, s.far_tokens, place.over_x())
    give = sems.copy(s.give, s.take, place.over_x())
    get_pack = gather(s.pack, s.packs, [(0, LANES, False)])
    get_qkv = gather(s.w_qkv, s.wq, halves(3 * model, False))
    get_proj = gather(s.w_proj, s.wp, halves(model, False))
    get_fc1 = gather(s.w_fc1, s.w1, quarters(hidden))
    get_fc2 = gather(s.w_fc2, s.w2, [(0, LANES, False), (LANES, 2 * LANES, False), (3 * LANES, model - 3 * LANES, True)])
    s.g_fc2, put_fc2 = reduce(s.o_fc2, fc2_cuts(model), None)
    s.g_fc1, put_fc1 = reduce(s.o_fc1, fc1_sum_cuts(hidden), None)
    s.g_proj, put_proj = reduce(s.o_proj, halves(model, False), None)
    wide = QKV_COLS
    qkv_pieces = []
    for group in range(model // wide):
        start = group * wide
        qkv_pieces.append([(0, start, wide), (wide, model + start, wide // 2)])
        qkv_pieces.append(
            [(0, model + start + wide // 2, wide // 2), (wide // 2, 2 * model + start, wide)]
        )
    s.g_qkv, put_qkv = reduce(s.o_qkv, qkv_cuts(model), qkv_pieces)
    s.g_table, put_table = reduce(s.o_table, [(0, LANES, False)], None)
    s.g_small, put_small = reduce(s.o_small, [(0, LANES, False)], None)
    get_table = gather(s.o_table.reshape(1, 8, LANES), s.table_all, [(0, LANES, False)])

    meet(place)
    for copy in line_copies:
        copy.wait()
    s.pack[...] = jnp.zeros_like(s.pack)
    for number in range(HIDDEN_LINE + 1):
        source = s.raw_hidden if number == HIDDEN_LINE else s.raw.at[number]
        s.pack[number // 8, number % 8 : number % 8 + 1, 0 : source.shape[1]] = source[...].astype(F32)
    each(get_pack, Gather.begin_own, Gather.begin_z)
    each(get_qkv, Gather.begin_z, Gather.begin_own)
    swap.start()
    each(get_proj, Gather.begin_own)
    table_copy.wait()
    s.table_lines[...] = jnp.zeros_like(s.table_lines)
    s.table_lines[0:HEADS, 0 : s.table.shape[1]] = s.table_in[...]
    fill_diagonals(s.table_lines, s.diag, rows, keys, row_span, width, offset)
    each(get_pack, Gather.second)
    tokens_copy.wait()
    normed, inv_std = norm_rows(s.tokens_in[...].astype(F32))
    s.n1[...] = normed
    s.r1[...] = jnp.broadcast_to(inv_std, s.r1.shape)
    each(get_pack, Gather.third)
    each(get_proj, Gather.begin_z)
    each(get_fc1[:2], Gather.begin_z)
    each(get_fc1, Gather.begin_own)
    s.fold[...] = jnp.zeros_like(s.fold)
    s.lines[...] = jnp.zeros_like(s.lines)
    each(get_pack, Gather.fourth)
    each(get_fc2, Gather.begin_own)
    each(get_qkv, Gather.second)
    each(get_fc1[2:], Gather.begin_z)
    each(get_pack, Gather.arrive)
    unpack_lines(tile(s.packs, 0, LANES), shard, hidden_shard, s.vec, s.b1)

    def line(number):
        return s.vec[number : number + 1, :]

    def set_line(number, values):
        s.lines[number : number + 1, :] = values

    s.h1[own_rows, :] = (s.n1[...] * line(GAIN_ONE) + line(SHIFT_ONE)).astype(BF16)
    swap.wait_recv()
    far = norm_rows(s.far_tokens[...].astype(F32))[0]
    s.h1[far_rows, :] = (far * line(GAIN_ONE) + line(SHIFT_ONE)).astype(BF16)
    each(get_proj, Gather.second)
    s.h1t[...] = s.h1[...].T
    cot_copy.wait()
    s.dm[...] = (line(SCALE_TWO) * s.cot_in[...].astype(F32)).astype(BF16)
    set_line(FC2_SHIFT, sum_rows(s.dm[...]))
    each(get_fc1[:2], Gather.second)
    each(get_fc2, Gather.begin_z)
    each(get_fc2[2:], Gather.second)
    each(get_qkv, Gather.third)
    each(get_proj, Gather.third)
    each(get_fc1[2:], Gather.second)
    each(get_qkv, Gather.fourth)
    each(get_fc1[:2], Gather.third)
    each(get_qkv, Gather.arrive)

    step = 2 * LANES

    @tiles(model // step, step)
    def _(number, start):
        s.kv[:, pl.ds(start, step)] = dot(s.h1[...], tile(s.wq, model + start, step)).astype(BF16)
        sums = dot(s.h1[...], tile(s.wq, 2 * model + start, step))
        sums = sums + s.vec[VALUE_BIAS : VALUE_BIAS + 1, pl.ds(start, step)]
        s.kv[:, pl.ds(model + start, step)] = sums.astype(BF16)

    @tiles(model // step, step)
    def _(number, start):
        cols = pl.ds(start, step)
        sums = dot(s.h1[own_rows, :], tile(s.wq, start, step))
        s.q[:, cols] = (sums + s.vec[QUERY_BIAS : QUERY_BIAS + 1, cols]).astype(BF16)

    def look(first, last):
        attend(s.q, s.kv, s.diag, s.probs, s.mixed, width, count, offset, (first, last))

    each(get_fc1[2:], Gather.third)
    each(get_fc2[:2], Gather.second)
    each(get_proj, Gather.fourth)
    look(0, 2)
    look(2, 4)
    each(get_fc1[:2], Gather.fourth)
    look(4, PAIRS)
    s.mixedt[...] = s.mixed[...].T
    each(get_proj, Gather.arrive)

    @tiles(model // step, step)
    def _(number, start):
        cols = pl.ds(start, step)
        branch = dot(s.mixed[...], tile(s.wp, start, step)) + s.vec[PROJ_SHIFT : PROJ_SHIFT + 1, cols]
        s.z[:, cols] = branch
        s.x1[:, cols] = s.tokens_in[:, cols].astype(F32) + s.vec[SCALE_ONE : SCALE_ONE + 1, cols] * branch

    normed, inv_std = norm_rows(s.x1[...])
    s.n2[...] = normed
    s.r2[...] = jnp.broadcast_to(inv_std, s.r2.shape)
    s.h2[...] = (normed * line(GAIN_TWO) + line(SHIFT_TWO)).astype(BF16)
    s.h2t[...] = s.h2[...].T
    each(get_fc2[:2], Gather.third)
    each(get_fc1[2:], Gather.fourth)
    each(get_fc1, Gather.arrive)

    @tiles(hidden // step, step)
    def _(number, start):
        cols = pl.ds(start, step)
        act = dot(s.h2[...], tile(s.w1, start, step)) + s.b1[0:1, cols]
        gate = 0.5 * (1.0 + lax.erf(act * 0.5**0.5))
        low = (act * gate).astype(BF16)
        s.u[:, cols] = low
        s.ut[cols, :] = low.T
        s.slope[:, cols] = gate + act * jnp.exp(act * act * -0.5) * 0.3989422804014327

    each(get_fc2, Gather.fourth)
    deep = 8 * hidden_shard
    for chunk, (first, size, _) in zip(put_fc2, fc2_cuts(model)):

        @tiles(Z_SIZE, deep)
        def _(number, start):
            cols = pl.ds(first, size)
            sums = dot(s.ut[pl.ds(start, deep), :], s.dm[:, cols])
            view = s.g_fc2.reshape(Z_SIZE, 8, hidden_shard, model)
            view[number, :, :, cols] = sums.reshape(8, hidden_shard, size).astype(BF16)

        chunk.begin()
    each(put_fc2, Reduce.add_core)
    each(get_fc2, Gather.arrive)

    @tiles(Z_SIZE, deep)
    def _(number, start):
        cols = pl.ds(start, deep)
        weight = s.w2.reshape(Z_SIZE, deep, model)[number]
        grad_hidden = dot(s.dm[...], weight, NT)
        s.da[:, cols] = (grad_hidden * s.slope[:, cols]).astype(BF16)

    for chunk, (first, size, _) in zip(put_fc1, fc1_sum_cuts(hidden)):

        @tiles(size // step, step)
        def _(number, start):
            cols = pl.ds(start + first, step)
            put_slots(s.g_fc1, cols, dot(s.h2t[...], s.da[:, cols]))

        chunk.begin()

    grad = jnp.zeros((rows, model), F32)
    for start in range(0, hidden, model):
        grad = grad + dot(s.da[:, start : start + model], tile(s.w1, start, model), NT)
    s.dh2[...] = grad
    each(put_fc2[:2], Reduce.add_first)
    each(put_fc1, Reduce.add_core)
    grad = s.dh2[...]
    set_line(GAIN_TWO, sum_rows(grad * s.n2[...]))
    set_line(SHIFT_TWO, sum_rows(grad))
    dx1 = s.cot_in[...].astype(F32) + norm_rows_back(grad, s.n2[...], s.r2[:, 0:1], line(GAIN_TWO))
    s.dx1[...] = dx1
    set_line(SCALE_ONE, sum_rows(dx1 * s.z[...]))
    s.dz[...] = (line(SCALE_ONE) * dx1).astype(BF16)
    set_line(PROJ_SHIFT, sum_rows(s.dz[...]))
    for group in range(2):
        cols = pl.ds(group * half, half)
        put_slots(s.g_proj, cols, dot(s.mixedt[...], s.dz[:, cols]))
        put_proj[group].begin()
    s.dmixed[...] = dot(s.dz[...], tile(s.wp, 0, model), NT).astype(BF16)

    def look_back(group):
        pairs = (group * wide // PAIR, (group + 1) * wide // PAIR)
        attend_back(s.q, s.kv, s.probs, s.dmixed, s.dq, s.dkv, s.fold, width, offset, pairs)
        cols = pl.ds(group * wide, wide)
        value_cols = pl.ds(model + group * wide, wide)
        own_lines = s.h1t[:, own_rows]
        all_lines = s.h1t[...]
        for part, sums in enumerate(
            (
                dot(own_lines, s.dq[:, cols]),
                dot(all_lines, s.dkv[:, cols]),
                dot(all_lines, s.dkv[:, value_cols]),
            )
        ):
            put_slots(s.g_qkv, pl.ds((3 * group + part) * wide, wide), sums)
        each(put_qkv[2 * group : 2 * group + 2], Reduce.begin)

    look_back(0)
    each(put_proj, Reduce.add_core)
    look_back(1)
    each(put_fc2[:2], Reduce.add_second)
    look_back(2)
    grad_key = dot(s.dkv[:, :model], tile(s.wq, model, model), NT)
    s.dh1[...] = grad_key + dot(s.dkv[:, model:], tile(s.wq, 2 * model, model), NT)
    s.give[...] = s.dh1[far_rows, :].astype(BF16)
    give.start()
    table_gradient(s.fold, s.table_sums, rows, keys, row_span, width, offset)

    @tiles(4 * Z_SIZE, LANES)
    def _(number, start):
        zz, yy, cc = number // 4, lax.rem(number // 2, 2), lax.rem(number, 2)
        for xx in range(2):
            s.g_table[zz, yy, cc, xx, 0] = s.table_sums[8 * xx : 8 * xx + 8, pl.ds(start, LANES)]

    each(put_table, Reduce.begin)
    each(put_fc2[2:], Reduce.add_first)
    each(put_fc1[:2], Reduce.add_first)
    each(put_table, Reduce.add_core)
    each(put_fc1[2:], Reduce.add_first)
    each(put_qkv, Reduce.add_core)
    @tiles(model // step, step)
    def _(number, start):
        cols = pl.ds(start, step)
        branch = dot(s.u[...], tile(s.w2, start, step)) + s.vec[FC2_SHIFT : FC2_SHIFT + 1, cols]
        s.out_low[:, cols] = (s.x1[:, cols] + s.vec[SCALE_TWO : SCALE_TWO + 1, cols] * branch).astype(BF16)
        s.lines[SCALE_TWO : SCALE_TWO + 1, cols] = sum_rows(s.cot_in[:, cols].astype(F32) * branch)

    hand(s.out_low, s.out)
    s.hidden_lines[...] = jnp.broadcast_to(sum_rows(s.da[...]), s.hidden_lines.shape)
    set_line(QUERY_BIAS, sum_rows(s.dq[...]))
    set_line(VALUE_BIAS, sum_rows(s.dkv[:, model:]))
    grad = s.dh1[own_rows, :] + dot(s.dq[...], tile(s.wq, 0, model), NT)
    give.wait_recv()
    grad = grad + s.take[...].astype(F32)
    set_line(GAIN_ONE, sum_rows(grad * s.n1[...]))
    set_line(SHIFT_ONE, sum_rows(grad))
    dx = s.dx1[...] + norm_rows_back(grad, s.n1[...], s.r1[:, 0:1], line(GAIN_ONE))
    s.dx_low[...] = dx.astype(BF16)
    hand(s.dx_low, s.grad_tokens)

    @tiles(8 * Z_SIZE, 1)
    def _(number, start):
        zz, yy, cc, xx = number // 8, lax.rem(number // 4, 2), lax.rem(number // 2, 2), lax.rem(number, 2)
        moved = pltpu.roll(s.lines[...], model - number * shard, 1)
        for group in range(LINES // ROW_GROUP):
            s.g_small[zz, yy, cc, xx, group] = moved[group * ROW_GROUP : (group + 1) * ROW_GROUP, :LANES]
        moved = pltpu.roll(s.hidden_lines[...], hidden - number * hidden_shard, 1)
        s.g_small[zz, yy, cc, xx, LINES // ROW_GROUP] = moved[:, :LANES]

    each(put_small, Reduce.begin)
    each(put_fc1[:2], Reduce.add_second)
    each(put_table, Reduce.add_first)
    each(put_fc1[2:], Reduce.add_second)
    each(put_small, Reduce.add_core)
    each(put_proj, Reduce.add_first)
    each(put_fc2[2:], Reduce.add_second)
    each(put_table, Reduce.add_second)
    each(put_qkv[:2], Reduce.add_first)
    each(put_qkv[2:4], Reduce.add_first)
    each(put_small, Reduce.add_first)
    each(put_qkv[4:], Reduce.add_first)
    each(put_proj, Reduce.add_second)
    each(put_table, Reduce.finish)
    each(get_table, Gather.begin_own, Gather.begin_z)
    each(put_qkv[:2], Reduce.add_second)
    each(put_small, Reduce.add_second)
    each(put_qkv[2:4], Reduce.add_second)
    each(put_fc2, Reduce.finish)
    hand(s.o_fc2, s.sum_fc2)
    each(put_qkv[4:], Reduce.add_second)
    each(get_table, Gather.second)
    each(put_fc1, Reduce.finish)
    hand(s.o_fc1, s.sum_fc1)
    each(get_table, Gather.third)
    each(put_proj, Reduce.finish)
    hand(s.o_proj, s.sum_proj)
    each(get_table, Gather.fourth)
    each(put_small, Reduce.finish)
    hand(s.o_small, s.sum_small)
    each(put_qkv[:4], Reduce.finish)
    each(get_table, Gather.arrive)
    for block in range(4 * Z_SIZE):
        slots = s.table_all.at[block // 4, block // 2 % 2, block % 2]
        start = block * LANES
        size = min(LANES, s.o_sums.shape[1] - start)
        s.o_sums[0:8, start : start + size] = slots[0, :, 0:size]
        s.o_sums[8:HEADS, start : start + size] = slots[1, 0 : HEADS - 8, 0:size]
    hand(s.o_sums, s.sum_table)
    each(put_qkv[4:], Reduce.finish)
    hand(s.o_qkv, s.sum_qkv)
    swap.wait_send()
    give.wait_send()
    for chunks in (get_pack, get_qkv, get_proj, get_fc1, get_fc2, get_table):
        each(chunks, Gather.settle)
    for chunks in (put_fc2, put_fc1, put_proj, put_qkv, put_table, put_small):
        each(chunks, Reduce.settle)
    for copy in outgoing:
        copy.wait()


def hand_kernel(count, *refs):
    small, arrays = refs[0], refs[1 : 1 + count]
    outs, lines = refs[1 + count : 1 + 2 * count], refs[1 + 2 * count :]
    for array, out in zip(arrays, outs):
        out[...] = array[...]
    for number, out in enumerate(lines):
        row = number if number < HIDDEN_LINE else LINES
        out[...] = small[row : row + 1, 0 : out.shape[1]]


def hand_out(small, arrays, sizes):
    vmem = pl.BlockSpec(memory_space=pltpu.VMEM)
    count = len(arrays)
    return pl.pallas_call(
        partial(hand_kernel, count),
        out_shape=tuple(jax.ShapeDtypeStruct(array.shape, array.dtype) for array in arrays)
        + tuple(jax.ShapeDtypeStruct((1, size), F32) for size in sizes),
        in_specs=[vmem] * (1 + count),
        out_specs=(vmem,) * (count + len(sizes)),
    )(small, *arrays)


def grouped(array):
    return array.reshape(-1, ROW_GROUP, array.shape[-1])


def run_layer(row_span, widths, counts, tokens, cotangent, vectors, w_qkv, w_proj, w_fc1, w_fc2, table):
    rows, model = tokens.shape
    keys = 2 * rows
    shard, hidden, hidden_shard = w_qkv.shape[0], w_fc1.shape[1], w_fc2.shape[0]
    smem = pl.BlockSpec(memory_space=pltpu.SMEM)
    vmem = pl.BlockSpec(memory_space=pltpu.VMEM)
    anywhere = pl.BlockSpec(memory_space=pl.ANY)
    inputs = dict(
        widths=(widths, smem),
        counts=(counts, smem),
        tokens=(tokens, anywhere),
        cot=(cotangent, anywhere),
        w_qkv=(grouped(w_qkv), anywhere),
        w_proj=(grouped(w_proj), anywhere),
        w_fc1=(grouped(w_fc1), anywhere),
        w_fc2=(grouped(w_fc2), anywhere),
        table=(table, anywhere),
    )
    for name, vector in zip(LINE_NAMES, vectors):
        inputs[name] = (vector.reshape(1, -1), anywhere)
    outputs = dict(
        out=((rows, model), BF16),
        grad_tokens=((rows, model), BF16),
        sum_small=((SLOT_ROWS, LANES), F32),
        sum_qkv=((shard, 3 * model), F32),
        sum_proj=((shard, model), F32),
        sum_fc1=((shard, hidden), F32),
        sum_fc2=((hidden_shard, model), F32),
        sum_table=((HEADS, table.shape[1]), F32),
    )
    entries = -(-table.shape[1] // (2 * LANES)) * 2 * LANES
    scratch = dict(
        raw=((HIDDEN_LINE, 1, shard), BF16),
        raw_hidden=((1, hidden_shard), BF16),
        table_in=(table.shape, BF16),
        tokens_in=((rows, model), BF16),
        cot_in=((rows, model), BF16),
        out_low=((rows, model), BF16),
        dx_low=((rows, model), BF16),
        o_small=((SLOT_ROWS, LANES), F32),
        o_qkv=((shard, 3 * model), F32),
        o_proj=((shard, model), F32),
        o_fc1=((shard, hidden), F32),
        o_fc2=((hidden_shard, model), F32),
        o_sums=((HEADS, table.shape[1]), F32),
        pack=((SLOT_ROWS // ROW_GROUP, ROW_GROUP, LANES), F32),
        table_lines=((HEAD_ROWS, entries), BF16),
        table_all=((Z_SIZE, 2, 2, 2, 8, LANES), F32),
        o_table=((8, LANES), F32),
        far_tokens=((rows, model), BF16),
        give=((rows, model), BF16),
        take=((rows, model), BF16),
        packs=((Z_SIZE, 2, 2, 2 * SLOT_ROWS // ROW_GROUP, ROW_GROUP, LANES), F32),
        wq=((Z_SIZE, 2, 2, 2 * shard // ROW_GROUP, ROW_GROUP, 3 * model), BF16),
        wp=((Z_SIZE, 2, 2, 2 * shard // ROW_GROUP, ROW_GROUP, model), BF16),
        w1=((Z_SIZE, 2, 2, 2 * shard // ROW_GROUP, ROW_GROUP, hidden), BF16),
        w2=((Z_SIZE, 2, 2, 2 * hidden_shard // ROW_GROUP, ROW_GROUP, model), BF16),
        vec=((LINES, model), F32),
        b1=((8, hidden), F32),
        diag=((HEAD_ROWS, 2 * (rows + keys)), F32),
        h1=((keys, model), BF16),
        h1t=((model, keys), BF16),
        n1=((rows, model), F32),
        r1=((rows, LANES), F32),
        q=((rows, model), BF16),
        kv=((keys, 2 * model), BF16),
        probs=((HEADS, rows, keys), F32),
        mixed=((rows, model), BF16),
        mixedt=((model, rows), BF16),
        z=((rows, model), F32),
        x1=((rows, model), F32),
        n2=((rows, model), F32),
        r2=((rows, LANES), F32),
        h2=((rows, model), BF16),
        h2t=((model, rows), BF16),
        u=((rows, hidden), BF16),
        ut=((hidden, rows), BF16),
        slope=((rows, hidden), F32),
        dm=((rows, model), BF16),
        da=((rows, hidden), BF16),
        dx1=((rows, model), F32),
        dz=((rows, model), BF16),
        dmixed=((rows, model), BF16),
        dq=((rows, model), BF16),
        dkv=((keys, 2 * model), BF16),
        dh1=((keys, model), F32),
        dh2=((rows, model), F32),
        fold=(((rows + keys) // LANES, 2 * HEAD_ROWS * 8, LANES), F32),
        table_sums=((HEAD_ROWS, entries), F32),
        lines=((LINES, model), F32),
        hidden_lines=((8, hidden), F32),
    )
    stages = []
    chunks = 0
    for slot_rows, slot_width, dtype, cuts in (
        (hidden_shard, model, BF16, fc2_cuts(model)),
        (shard, hidden, BF16, fc1_sum_cuts(hidden)),
        (shard, model, BF16, halves(model, False)),
        (shard, 3 * model, BF16, qkv_cuts(model)),
        (8, LANES, F32, [(0, LANES, False)]),
        (SLOT_ROWS, LANES, F32, [(0, LANES, False)]),
    ):
        groups = slot_rows // ROW_GROUP
        stages.append(((Z_SIZE, 2, 2, 2, groups, ROW_GROUP, slot_width), dtype))
        stages.append(((Z_SIZE, 2, 2, groups, ROW_GROUP, slot_width), dtype))
        for _, size, early in cuts:
            leads = ((Z_SIZE, 2), (Z_SIZE,), (Z_SIZE - 1,))
            if early:
                leads = ((Z_SIZE - 1, 2, 2), (2, 2), (2,), ())
            for lead in leads:
                stages.append((lead + (groups, ROW_GROUP, size), dtype))
            chunks += 1
    gathers = 13
    sends, recvs = 2 + gathers + chunks, 2 + 7 * gathers + 4 * chunks
    names = list(inputs) + list(outputs) + list(scratch)
    return pl.pallas_call(
        partial(layer_kernel, names, row_span),
        out_shape=tuple(jax.ShapeDtypeStruct(shape, dtype) for shape, dtype in outputs.values()),
        in_specs=[spec for _, spec in inputs.values()],
        out_specs=(anywhere,) * len(outputs),
        scratch_shapes=[pltpu.VMEM(shape, dtype) for shape, dtype in list(scratch.values()) + stages]
        + [
            pltpu.SemaphoreType.DMA((sends,)),
            pltpu.SemaphoreType.DMA((recvs,)),
            pltpu.SemaphoreType.DMA((HIDDEN_LINE + 4 + gathers,)),
        ],
        compiler_params=pltpu.CompilerParams(
            collective_id=0, has_side_effects=True, vmem_limit_bytes=VMEM_LIMIT
        ),
    )(*[array for array, _ in inputs.values()])


def layer_norm(values, gain, shift):
    centred = values - jnp.mean(values, axis=-1, keepdims=True)
    inv_std = lax.rsqrt(jnp.mean(centred * centred, axis=-1, keepdims=True) + EPSILON)
    normed = centred * inv_std
    return (normed * gain + shift, normed, inv_std)


def norm_back(grad_out, normed, inv_std, gain):
    scaled = grad_out * gain
    return inv_std * (
        scaled
        - jnp.mean(scaled, axis=-1, keepdims=True)
        - normed * jnp.mean(scaled * normed, axis=-1, keepdims=True)
    )


def row_sum(values):
    return jnp.sum(values.astype(jnp.float32), axis=0)


def per_device_native(
    tokens,
    cotangent,
    counts,
    widths,
    norm1_gain,
    norm1_shift,
    w_qkv,
    q_bias,
    v_bias,
    w_proj,
    proj_bias,
    gamma1,
    norm2_gain,
    norm2_shift,
    w_fc1,
    fc1_bias,
    w_fc2,
    fc2_bias,
    gamma2,
    bias_table,
):
    fetched = (
        lax.all_gather(norm1_gain, ("img", "seq"), axis=0, tiled=True),
        lax.all_gather(norm1_shift, ("img", "seq"), axis=0, tiled=True),
        lax.all_gather(w_qkv, ("img", "seq"), axis=0, tiled=True),
        lax.all_gather(q_bias, ("img", "seq"), axis=0, tiled=True),
        lax.all_gather(v_bias, ("img", "seq"), axis=0, tiled=True),
        lax.all_gather(w_proj, ("img", "seq"), axis=0, tiled=True),
        lax.all_gather(proj_bias, ("img", "seq"), axis=0, tiled=True),
        lax.all_gather(gamma1, ("img", "seq"), axis=0, tiled=True),
        lax.all_gather(norm2_gain, ("img", "seq"), axis=0, tiled=True),
        lax.all_gather(norm2_shift, ("img", "seq"), axis=0, tiled=True),
        lax.all_gather(w_fc1, ("img", "seq"), axis=0, tiled=True),
        lax.all_gather(fc1_bias, ("img", "seq"), axis=0, tiled=True),
        lax.all_gather(w_fc2, ("img", "seq"), axis=0, tiled=True),
        lax.all_gather(fc2_bias, ("img", "seq"), axis=0, tiled=True),
        lax.all_gather(gamma2, ("img", "seq"), axis=0, tiled=True),
    )
    (
        gain_one,
        shift_one,
        qkv_weight,
        query_bias,
        value_bias,
        proj_weight,
        proj_shift,
        scale_one,
        gain_two,
        shift_two,
        fc1_weight,
        fc1_shift,
        fc2_weight,
        fc2_shift,
        scale_two,
    ) = fetched
    gain_one = gain_one.astype(jnp.float32)
    shift_one = shift_one.astype(jnp.float32)
    proj_shift = proj_shift.astype(jnp.float32)
    scale_one = scale_one.astype(jnp.float32)
    gain_two = gain_two.astype(jnp.float32)
    shift_two = shift_two.astype(jnp.float32)
    fc1_shift = fc1_shift.astype(jnp.float32)
    fc2_shift = fc2_shift.astype(jnp.float32)
    scale_two = scale_two.astype(jnp.float32)
    local_rows = tokens.shape[0]
    width_model = tokens.shape[1]
    seq_len = local_rows * lax.axis_size("seq")
    offset = lax.axis_index("seq") * local_rows
    row_span = (seq_len - 1) // (SIDE // 2) + 1
    table_rows = bias_table.shape[0]
    entries = -(-table_rows // (2 * LANES)) * 2 * LANES
    table_lines = jnp.pad(
        bias_table.T, ((0, HEAD_ROWS - HEADS), (0, entries - table_rows))
    )
    scalars = jnp.stack([widths[0], counts[0], offset.astype(jnp.int32)])
    smem = pl.BlockSpec(memory_space=pltpu.SMEM)
    vmem = pl.BlockSpec(memory_space=pltpu.VMEM)
    params = pltpu.CompilerParams(vmem_limit_bytes=40 << 20)

    inputs_f = tokens.astype(jnp.float32)
    normed_full, normed_one, inv_std_one = layer_norm(inputs_f, gain_one, shift_one)
    normed_low = normed_full.astype(jnp.bfloat16)
    qkv_shift = jnp.concatenate(
        [query_bias, jnp.zeros((width_model,), jnp.bfloat16), value_bias]
    ).astype(jnp.float32)
    projected = (
        jnp.dot(normed_low, qkv_weight, preferred_element_type=jnp.float32) + qkv_shift
    ).astype(jnp.bfloat16)
    queries = projected[:, :width_model]
    key_local = projected[:, width_model:]
    keys_all = lax.all_gather(key_local, "seq", axis=0, tiled=True)

    attn_low, probs = pl.pallas_call(
        partial(attend_kernel, row_span),
        out_shape=(
            jax.ShapeDtypeStruct((local_rows, width_model), BF16),
            jax.ShapeDtypeStruct((HEADS, local_rows, seq_len), F32),
        ),
        in_specs=[smem, vmem, vmem, vmem],
        out_specs=(vmem, vmem),
        scratch_shapes=[pltpu.VMEM((HEAD_ROWS, 2 * (local_rows + seq_len)), F32)],
        compiler_params=params,
    )(scalars, queries, keys_all, table_lines)
    branch_one = jnp.dot(attn_low, proj_weight, preferred_element_type=jnp.float32) + proj_shift
    residual_one = inputs_f + scale_one * branch_one
    normed_full_two, normed_two, inv_std_two = layer_norm(residual_one, gain_two, shift_two)
    normed_low_two = normed_full_two.astype(jnp.bfloat16)
    pre_act = jnp.dot(normed_low_two, fc1_weight, preferred_element_type=jnp.float32) + fc1_shift
    activated, gelu_pull = jax.vjp(partial(jax.nn.gelu, approximate=False), pre_act)
    hidden = activated.astype(jnp.bfloat16)
    branch_two = jnp.dot(hidden, fc2_weight, preferred_element_type=jnp.float32) + fc2_shift
    output = (residual_one + scale_two * branch_two).astype(jnp.bfloat16)
    grad_out = cotangent.astype(jnp.float32)
    grad_scale_two = jnp.sum(grad_out * branch_two, axis=0)
    grad_branch_two = (scale_two * grad_out).astype(jnp.bfloat16)
    grad_fc2_weight = jnp.einsum(
        "tf,td->fd", hidden, grad_branch_two, preferred_element_type=jnp.float32
    )
    grad_fc2_shift = row_sum(grad_branch_two)
    grad_hidden = jnp.einsum(
        "td,fd->tf", grad_branch_two, fc2_weight, preferred_element_type=jnp.float32
    )
    grad_pre = gelu_pull(grad_hidden)[0].astype(jnp.bfloat16)
    grad_fc1_weight = jnp.einsum(
        "td,tf->df", normed_low_two, grad_pre, preferred_element_type=jnp.float32
    )
    grad_fc1_shift = row_sum(grad_pre)
    grad_normed_two = jnp.einsum(
        "tf,df->td", grad_pre, fc1_weight, preferred_element_type=jnp.float32
    )
    grad_gain_two = jnp.sum(grad_normed_two * normed_two, axis=0)
    grad_shift_two = jnp.sum(grad_normed_two, axis=0)
    grad_resid = grad_out + norm_back(grad_normed_two, normed_two, inv_std_two, gain_two)
    grad_scale_one = jnp.sum(grad_resid * branch_one, axis=0)
    grad_branch_one = (scale_one * grad_resid).astype(jnp.bfloat16)
    grad_proj_weight = jnp.einsum(
        "td,te->de", attn_low, grad_branch_one, preferred_element_type=jnp.float32
    )
    grad_proj_shift = row_sum(grad_branch_one)
    grad_attn = jnp.einsum(
        "te,de->td", grad_branch_one, proj_weight, preferred_element_type=jnp.float32
    ).astype(jnp.bfloat16)
    grad_query, key_terms, table_grad = pl.pallas_call(
        partial(attend_back_kernel, row_span),
        out_shape=(
            jax.ShapeDtypeStruct((local_rows, width_model), BF16),
            jax.ShapeDtypeStruct((seq_len, 2 * width_model), BF16),
            jax.ShapeDtypeStruct((HEAD_ROWS, entries), F32),
        ),
        in_specs=[smem, vmem, vmem, vmem, vmem],
        out_specs=(vmem, vmem, vmem),
        scratch_shapes=[
            pltpu.VMEM(((local_rows + seq_len) // LANES, 2 * HEAD_ROWS * 8, LANES), F32)
        ],
        compiler_params=params,
    )(scalars, queries, keys_all, probs, grad_attn)
    own_terms = lax.psum_scatter(key_terms, "seq", scatter_dimension=0, tiled=True)
    grad_qkv = jnp.concatenate([grad_query, own_terms], axis=1)
    grad_qkv_weight = jnp.einsum(
        "td,te->de", normed_low, grad_qkv, preferred_element_type=jnp.float32
    )
    grad_query_bias = row_sum(grad_qkv[:, :width_model])
    grad_value_bias = row_sum(grad_qkv[:, 2 * width_model :])
    grad_normed_one = jnp.einsum(
        "te,de->td", grad_qkv, qkv_weight, preferred_element_type=jnp.float32
    )
    grad_gain_one = jnp.sum(grad_normed_one * normed_one, axis=0)
    grad_shift_one = jnp.sum(grad_normed_one, axis=0)
    grad_inputs = (
        grad_resid + norm_back(grad_normed_one, normed_one, inv_std_one, gain_one)
    ).astype(jnp.bfloat16)
    summed = (
        lax.psum_scatter(grad_gain_one, ("img", "seq"), scatter_dimension=0, tiled=True),
        lax.psum_scatter(grad_shift_one, ("img", "seq"), scatter_dimension=0, tiled=True),
        lax.psum_scatter(grad_qkv_weight, ("img", "seq"), scatter_dimension=0, tiled=True),
        lax.psum_scatter(grad_query_bias, ("img", "seq"), scatter_dimension=0, tiled=True),
        lax.psum_scatter(grad_value_bias, ("img", "seq"), scatter_dimension=0, tiled=True),
        lax.psum_scatter(grad_proj_weight, ("img", "seq"), scatter_dimension=0, tiled=True),
        lax.psum_scatter(grad_proj_shift, ("img", "seq"), scatter_dimension=0, tiled=True),
        lax.psum_scatter(grad_scale_one, ("img", "seq"), scatter_dimension=0, tiled=True),
        lax.psum_scatter(grad_gain_two, ("img", "seq"), scatter_dimension=0, tiled=True),
        lax.psum_scatter(grad_shift_two, ("img", "seq"), scatter_dimension=0, tiled=True),
        lax.psum_scatter(grad_fc1_weight, ("img", "seq"), scatter_dimension=0, tiled=True),
        lax.psum_scatter(grad_fc1_shift, ("img", "seq"), scatter_dimension=0, tiled=True),
        lax.psum_scatter(grad_fc2_weight, ("img", "seq"), scatter_dimension=0, tiled=True),
        lax.psum_scatter(grad_fc2_shift, ("img", "seq"), scatter_dimension=0, tiled=True),
        lax.psum_scatter(grad_scale_two, ("img", "seq"), scatter_dimension=0, tiled=True),
    )
    table_total = lax.psum(table_grad, ("img", "seq"))[:HEADS, :table_rows].T
    return (output, grad_inputs) + tuple(summed) + (table_total,)


def per_device_linked(
    tokens,
    cotangent,
    counts,
    widths,
    norm1_gain,
    norm1_shift,
    w_qkv,
    q_bias,
    v_bias,
    w_proj,
    proj_bias,
    gamma1,
    norm2_gain,
    norm2_shift,
    w_fc1,
    fc1_bias,
    w_fc2,
    fc2_bias,
    gamma2,
    bias_table,
):
    seq_len = tokens.shape[0] * lax.axis_size("seq")
    row_span = (seq_len - 1) // (SIDE // 2) + 1
    vectors = [
        norm1_gain, norm1_shift, q_bias, v_bias, proj_bias, gamma1, norm2_gain, norm2_shift, fc2_bias, gamma2, fc1_bias,
    ]
    output, grad_tokens, small, *sums = run_layer(
        row_span, widths, counts, tokens, cotangent, vectors, w_qkv, w_proj, w_fc1, w_fc2, bias_table.T
    )
    sizes = [vector.shape[0] for vector in vectors]
    output, grad_tokens, sum_qkv, sum_proj, sum_fc1, sum_fc2, table_total, *lines = hand_out(
        small, [output, grad_tokens, *sums], sizes
    )
    lines = [line.reshape(-1) for line in lines]
    return (
        output, grad_tokens, lines[GAIN_ONE], lines[SHIFT_ONE], sum_qkv, lines[QUERY_BIAS], lines[VALUE_BIAS],
        sum_proj, lines[PROJ_SHIFT], lines[SCALE_ONE], lines[GAIN_TWO], lines[SHIFT_TWO], sum_fc1,
        lines[HIDDEN_LINE], sum_fc2, lines[FC2_SHIFT], lines[SCALE_TWO], table_total.T,
    )


def per_device(*arrays):
    tokens, bias_table = arrays[0], arrays[19]
    linked = lax.axis_size("img") == 4 * Z_SIZE and lax.axis_size("seq") == 2
    linked = linked and arrays[6].shape[0] % 8 == 0 and tokens.shape[0] == LANES
    linked = linked and 15 * LANES < bias_table.shape[0] <= 4 * Z_SIZE * LANES
    return per_device_linked(*arrays) if linked else per_device_native(*arrays)


def solution(mesh):
    return jax.shard_map(
        per_device,
        mesh=mesh,
        in_specs=(
            P(("img", "seq"), None),
            P(("img", "seq"), None),
            P("img"),
            P("img"),
            P(("img", "seq")),
            P(("img", "seq")),
            P(("img", "seq"), None),
            P(("img", "seq")),
            P(("img", "seq")),
            P(("img", "seq"), None),
            P(("img", "seq")),
            P(("img", "seq")),
            P(("img", "seq")),
            P(("img", "seq")),
            P(("img", "seq"), None),
            P(("img", "seq")),
            P(("img", "seq"), None),
            P(("img", "seq")),
            P(("img", "seq")),
            P(),
        ),
        out_specs=(
            P(("img", "seq"), None),
            P(("img", "seq"), None),
            P(("img", "seq")),
            P(("img", "seq")),
            P(("img", "seq"), None),
            P(("img", "seq")),
            P(("img", "seq")),
            P(("img", "seq"), None),
            P(("img", "seq")),
            P(("img", "seq")),
            P(("img", "seq")),
            P(("img", "seq")),
            P(("img", "seq"), None),
            P(("img", "seq")),
            P(("img", "seq"), None),
            P(("img", "seq")),
            P(("img", "seq")),
            P(),
        ),
        check_vma=False,
    )
```
